32 devices in a mesh: rep: 8 (over z, core), exp: 4 (over y, x).
Axes of the slice: x: 2, y: 2, z: 4, core: 2. Of those that a mesh axis runs over, the one named last changes fastest.
Arguments:
- tokens: bfloat16 [12608, 768], P(('rep', 'exp')), may hold values from -6 to 6
- routes: int32 [12608, 2], P(('rep', 'exp')), may hold values from 0 to 3, all different within a row
- out_grad: bfloat16 [12608, 768], P(('rep', 'exp')), may hold values from -6 to 6
- attn_qkv: bfloat16 [768, 2304], P('exp'), may hold values from -0.21875 to 0.21875
- attn_out: bfloat16 [768, 768], P('exp'), may hold values from -1.5 to 1.5
- router: bfloat16 [768, 4], P('exp'), may hold values from -0.15625 to 0.15625
- norm_gains: bfloat16 [2, 768], P(None, 'exp'), may hold values from 0.25 to 1.75
- dense_biases: bfloat16 [5, 768], P(None, 'exp'), may hold values from -1.796875 to 1.796875
- expert_in: bfloat16 [4, 768, 3072], P('exp'), may hold values from -0.21875 to 0.21875
- expert_in_bias: bfloat16 [4, 3072], P('exp'), may hold values from -0.59765625 to 0.59765625
- expert_out: bfloat16 [4, 3072, 768], P('exp'), may hold values from -0.21875 to 0.21875
- expert_out_bias: bfloat16 [4, 768], P('exp'), may hold values from -3 to 3
Outputs:
- output: bfloat16 [12608, 768], P(('rep', 'exp'))
- grad_input: bfloat16 [12608, 768], P(('rep', 'exp'))
- grad_attn_qkv: float32 [768, 2304], P('exp')
- grad_attn_out: float32 [768, 768], P('exp')
- grad_router: float32 [768, 4], P('exp')
- grad_norm_gains: float32 [2, 768], P(None, 'exp')
- grad_dense_biases: float32 [5, 768], P(None, 'exp')
- grad_expert_in: float32 [4, 768, 3072], P('exp', None, 'rep')
- grad_expert_in_bias: float32 [4, 3072], P('exp', 'rep')
- grad_expert_out: float32 [4, 3072, 768], P('exp', 'rep')
- grad_expert_out_bias: float32 [4, 768], P('exp', 'rep')
The draws below stay inside these ranges and needn't reach their ends.
Inputs may be any that keep to these rules, and one draw needn't show every extreme that they name: `routes`: each row names two different experts; every expert is named by some row.
All inputs are finite; a program needn't handle non-finite values.
Results may differ from the reference program's by a relative error of at most 0.028.
Values may be sent and summed in bfloat16 or wider, within the bound.
A program may use at most 192 MiB of HBM per device.

```python
import math
import jax
import jax.numpy as jnp
from jax import lax

D = 768
HEADS = 12
HEAD_DIM = 64
FF = 3072
SEQ = 197
TOK_DEV = 394
EXPERTS = 4
CAPACITY = 222
TOKENS = 12608


def block_levels(key, shape, pieces, low, largest):
    level, own = 1.0, jax.random.fold_in(key, 6)
    for axis_at, shards_of in pieces:
        heights = jnp.exp(jax.random.uniform(jax.random.fold_in(own, axis_at), (shards_of,), jnp.float32, low / len(pieces), largest / len(pieces)))
        level = level * jnp.repeat(heights, shape[axis_at] // shards_of).reshape([-1 if axis == axis_at else 1 for axis in range(len(shape))])
    return level


def choose_distinct(key, rows, amount, top, lift):
    ranking = jax.random.permutation(jax.random.fold_in(key, 1), amount)
    pull = ranking
    for power in range(3):
        pull = pull * pull // amount
    pull = pull * lift // amount
    tickets = jax.random.randint(jax.random.fold_in(key, 2), (rows, amount), 0, 4096) + pull
    holders = jax.random.permutation(jax.random.fold_in(key, 3), rows)[jnp.arange(amount) % rows]
    tickets = jnp.where(jnp.arange(rows)[:, None] == holders[None, :], 1 << 14, tickets)
    score = tickets * amount + jnp.arange(amount)
    return lax.top_k(score.astype(jnp.int32), top)[1].astype(jnp.int32)


def bell_draw(stream_key, extent, width, most, shards=(), kind=jnp.bfloat16):
    drawn = width * jax.random.normal(stream_key, extent, jnp.float32)
    if shards:
        drawn = drawn * block_levels(stream_key, extent, shards, -0.22, 0.18)
    return jnp.clip(drawn, -most, most).astype(kind)


def setup_inputs(seed: int = 0) -> dict:
    splits = jax.random.split(jax.random.key(seed), 13)
    return {
        "tokens": bell_draw(splits[0], (TOKENS, D), 1.0, 6.0, ((0, 32),)),
        "routes": choose_distinct(splits[1], TOKENS, EXPERTS, 2, 4096),
        "out_grad": bell_draw(splits[2], (TOKENS, D), 1.0, 6.0, ((0, 32),)),
        "attn_qkv": bell_draw(splits[3], (D, 3 * D), D ** -0.5, 0.21875, ((0, 4),)),
        "attn_out": bell_draw(splits[4], (D, D), (max(4 * D // SEQ, 1)) ** -0.5, 1.5, ((0, 4),)),
        "router": bell_draw(splits[5], (D, EXPERTS), (2 * D) ** -0.5, 0.15625, ((0, 4),)),
        "norm_gains": jnp.clip(1.0 + 0.15 * jax.random.normal(splits[6], (2, D), jnp.float32), 0.25, 1.75).astype(jnp.bfloat16),
        "dense_biases": bell_draw(splits[7], (5, D), 0.3, 1.796875, ((1, 4),)),
        "expert_in": bell_draw(splits[8], (EXPERTS, D, FF), D ** -0.5, 0.21875, ((0, 4),)),
        "expert_in_bias": bell_draw(splits[9], (EXPERTS, FF), 0.1, 0.59765625, ((0, 4),)),
        "expert_out": bell_draw(splits[10], (EXPERTS, FF, D), (max(4 * FF // (EXPERTS * EXPERTS), 1)) ** -0.5, 0.21875, ((0, 4),)),
        "expert_out_bias": bell_draw(splits[11], (EXPERTS, D), 0.5, 3.0, ((0, 4),)),
    }


@jax.custom_vjp
def low(v):
    return lax.optimization_barrier(v.astype(jnp.bfloat16)).astype(jnp.float32)

@jax.custom_vjp
def low_back(v):
    return v

def low_keep(v):
    return (low(v), None)

def low_pass(kept, grad):
    return (grad,)

def back_keep(v):
    return (v, None)

def back_low(kept, grad):
    return (low(grad),)
low.defvjp(low_keep, low_pass)
low_back.defvjp(back_keep, back_low)
norm_eps = 1e-06
precise = lax.Precision.HIGHEST

def layer_norm(values, gain_row, shift_row):
    center = values - lax.optimization_barrier(jnp.mean(values, -1, keepdims=True))
    spread = lax.optimization_barrier(jnp.mean(center * center, -1, keepdims=True))
    return center * lax.rsqrt(spread + norm_eps) * gain_row + shift_row

def mat_prod(first_op, second_op):
    return jnp.dot(first_op, second_op, precision=precise, preferred_element_type=jnp.float32)

def group_layer(params, routes_group, tokens_group):
    w_qkv, w_proj, w_route, gains_all, biases_all, w_first, b_first, w_second, b_second = params
    model_width = tokens_group.shape[1]
    group_rows = tokens_group.shape[0]
    images = group_rows // SEQ
    blocks = group_rows // TOK_DEV
    experts = w_route.shape[1]
    scale = 1.0 / math.sqrt(HEAD_DIM)
    four_shape = (images, SEQ, HEADS, HEAD_DIM)
    normed = low(layer_norm(tokens_group, gains_all[0], biases_all[0]))
    qkv_all = mat_prod(normed, w_qkv)
    query = low(low_back(qkv_all[:, :model_width] + biases_all[1])).reshape(four_shape)
    key_rows = low(low_back(qkv_all[:, model_width:2 * model_width])).reshape(four_shape)
    value_rows = low(low_back(qkv_all[:, 2 * model_width:] + biases_all[2])).reshape(four_shape)
    scores = low_back(jnp.einsum('ishd,ithd->ihst', query, key_rows, precision=precise) * scale)
    probs_att = low(jax.nn.softmax(scores, -1))
    context = jnp.einsum('ihst,ithd->ishd', probs_att, value_rows, precision=precise)
    context = low(low_back(context)).reshape(group_rows, model_width)
    resid_one = tokens_group + low_back(mat_prod(context, w_proj) + biases_all[3])
    second = low(layer_norm(resid_one, gains_all[1], biases_all[4]))
    route_probs = jax.nn.softmax(low_back(mat_prod(second, w_route)), -1)
    gates = jnp.take_along_axis(route_probs, routes_group, 1)
    block_routes = routes_group.reshape(blocks, TOK_DEV, 2)
    pair_expert = jnp.concatenate([block_routes[:, :, 0], block_routes[:, :, 1]], 1)
    onehot = (pair_expert[:, :, None] == jnp.arange(experts, dtype=jnp.int32)[None, None, :]).astype(jnp.int32)
    position = lax.optimization_barrier(jnp.sum((jnp.cumsum(onehot, 1) - onehot) * onehot, 2))
    kept_pair = position < CAPACITY
    block_ids = jnp.arange(blocks, dtype=jnp.int32)[:, None]
    total_slots = experts * blocks * CAPACITY
    slot_index = jnp.where(kept_pair, pair_expert * (blocks * CAPACITY) + block_ids * CAPACITY + position, total_slots).reshape(-1)
    token_local = jnp.concatenate([jnp.arange(TOK_DEV, dtype=jnp.int32), jnp.arange(TOK_DEV, dtype=jnp.int32)])
    token_index = (token_local[None, :] + block_ids * TOK_DEV).reshape(-1)
    dispatch = jnp.zeros((total_slots, model_width), jnp.float32).at[slot_index].set(second[token_index], mode='drop')
    dispatch = low_back(dispatch).reshape(experts, blocks * CAPACITY, model_width)
    hidden = low_back(jnp.einsum('erd,edf->erf', dispatch, w_first, precision=precise) + b_first[:, None, :])
    active = low(jax.nn.gelu(hidden, approximate=False))
    result = jnp.einsum('erf,efd->erd', active, w_second, precision=precise) + b_second[:, None, :]
    result = low(low_back(result))
    pair_output = result.reshape(total_slots, model_width)[jnp.minimum(slot_index, total_slots - 1)]
    block_gates = gates.reshape(blocks, TOK_DEV, 2)
    pair_gate = jnp.concatenate([block_gates[:, :, 0], block_gates[:, :, 1]], 1)
    pair_weight = (pair_gate * kept_pair.astype(jnp.float32)).reshape(-1)
    contrib = (pair_weight[:, None] * pair_output).reshape(blocks, 2 * TOK_DEV, model_width)
    mixture = (contrib[:, :TOK_DEV] + contrib[:, TOK_DEV:]).reshape(group_rows, model_width)
    return resid_one + mixture

def reference(tokens, routes, out_grad, attn_qkv, attn_out, router, norm_gains, dense_biases, expert_in, expert_in_bias, expert_out, expert_out_bias):
    params = (attn_qkv.astype(jnp.float32), attn_out.astype(jnp.float32), router.astype(jnp.float32), norm_gains.astype(jnp.float32), dense_biases.astype(jnp.float32), expert_in.astype(jnp.float32), expert_in_bias.astype(jnp.float32), expert_out.astype(jnp.float32), expert_out_bias.astype(jnp.float32))
    group_rows = 4 * TOK_DEV
    groups = tokens.shape[0] // group_rows
    routes_groups = routes.reshape(groups, group_rows, 2)

    def forward(inputs, weights):
        tokens_groups = inputs.reshape(groups, group_rows, inputs.shape[1])
        group_step = jax.checkpoint(lambda operand_pair: group_layer(weights, operand_pair[0], operand_pair[1]))
        outputs = lax.map(group_step, (routes_groups, tokens_groups))
        return outputs.reshape(inputs.shape)
    result_all, pull_back = jax.vjp(forward, tokens.astype(jnp.float32), params)
    input_grad, weight_grads = pull_back(out_grad.astype(jnp.float32))
    return (result_all.astype(jnp.bfloat16), input_grad.astype(jnp.bfloat16), weight_grads[0], weight_grads[1], weight_grads[2], weight_grads[3], weight_grads[4], weight_grads[5], weight_grads[6], weight_grads[7], weight_grads[8])
```

```python
from functools import partial
import math

import jax
import jax.numpy as jnp
from jax import lax
from jax.experimental import pallas as pl
from jax.experimental.pallas import tpu as pltpu
from jax.sharding import PartitionSpec as P

HEAD_DIM = 64
SEQ = 197
EPS = 1e-06
BF = jnp.bfloat16
F32 = jnp.float32
MESH = pl.DeviceIdType.MESH


def up(value, step):
    return (value + step - 1) // step * step


def mm(a, b):
    return lax.dot_general(a, b, (((1,), (0,)), ((), ())), preferred_element_type=F32)


def mm_nt(a, b):
    return lax.dot_general(a, b, (((1,), (1,)), ((), ())), preferred_element_type=F32)


def mm_tn(a, b):
    return lax.dot_general(a, b, (((0,), (0,)), ((), ())), preferred_element_type=F32)


def iota(shape, dim):
    return lax.broadcasted_iota(jnp.int32, shape, dim)


def rows_at(index, size):
    return pl.ds(pl.multiple_of(index * size, size), size)


def normalize(values, gain, shift):
    center = values - jnp.mean(values, -1, keepdims=True)
    spread = jnp.mean(center * center, -1, keepdims=True)
    return center * lax.rsqrt(spread + EPS) * gain + shift


class Sizes:
    def __init__(self, mesh, tok_rows, width, ff):
        self.n_exp = mesh.shape["exp"]
        self.n_rep = mesh.shape["rep"]
        self.tok = tok_rows
        self.images = tok_rows // SEQ
        self.seq = up(SEQ, 16)
        self.rows = self.images * self.seq
        self.d = width
        self.ff = ff
        self.experts = self.n_exp
        self.cap = (18 * tok_rows + 8 * self.experts - 1) // (8 * self.experts)
        self.slots = up(self.cap, 16)
        self.all_slots = self.slots * self.experts
        self.shard = width // self.n_exp
        self.shard_pad = up(self.shard, 128)
        self.ep = up(self.experts, 8)
        self.small = up(8 + self.ep, 16)
        self.pairs = width // 128


def pad_matrix(sz):
    row = iota((sz.rows, sz.tok), 0)
    col = iota((sz.rows, sz.tok), 1)
    want = jnp.full((sz.rows, sz.tok), -1, jnp.int32)
    for image in range(sz.images):
        inside = (row >= image * sz.seq) & (row < image * sz.seq + SEQ)
        want = jnp.where(inside, row - image * (sz.seq - SEQ), want)
    return (want == col).astype(F32).astype(BF)


def front_kernel(
    sz,
    tok_ref,
    grad_ref,
    routes_ref,
    wq_shard,
    wp_shard,
    sm_shard,
    xr,
    gr,
    gater,
    qkv,
    pall,
    ctx,
    resid,
    second,
    normed,
    probs,
    wq,
    wp,
    smf,
    gpad,
    pmat,
    xs,
    gs,
    gates,
    smg,
    wq_sem,
    wp_sem,
    cq_sem,
    cp_sem,
    sm_sem,
    g_sem,
    x_sem,
    ga_sem,
):
    me_r = lax.axis_index("rep")
    me = lax.axis_index("exp")
    n = sz.n_exp
    core = lax.rem(me_r, 2)
    sibling = me_r + 1 - 2 * core

    barrier = pltpu.get_barrier_semaphore()
    for k in range(1, n):
        pl.semaphore_signal(
            barrier, inc=1, device_id=(me_r, lax.rem(me + k, n)), device_id_type=MESH
        )
    pl.semaphore_signal(barrier, inc=1, device_id=(sibling, me), device_id_type=MESH)
    pl.semaphore_wait(barrier, n)

    def to_peer(src, dst, sems, k):
        return pltpu.make_async_remote_copy(
            src_ref=src,
            dst_ref=dst,
            send_sem=sems.at[0, k],
            recv_sem=sems.at[1, k],
            device_id=(me_r, lax.rem(me + k, n)),
            device_id_type=MESH,
        )

    def to_sibling(ref, sems, k):
        return pltpu.make_async_remote_copy(
            src_ref=ref,
            dst_ref=ref,
            send_sem=sems.at[0, k],
            recv_sem=sems.at[1, k],
            device_id=(sibling, me),
            device_id_type=MESH,
        )

    hq, hp = 3 * sz.d // 2, sz.d // 2
    own = rows_at(me, sz.shard)
    half_q = pl.ds(pl.multiple_of(core * hq, 128), hq)
    half_p = pl.ds(pl.multiple_of(core * hp, 128), hp)
    other_q = pl.ds(pl.multiple_of((1 - core) * hq, 128), hq)
    other_p = pl.ds(pl.multiple_of((1 - core) * hp, 128), hp)

    smg[me] = sm_shard[...]
    for k in range(1, n):
        to_peer(sm_shard, smg.at[me], sm_sem, k).start()
    for k in range(1, n):
        to_peer(wq_shard.at[:, half_q], wq.at[own, half_q], wq_sem, k).start()
    for k in range(1, n):
        to_peer(wp_shard.at[:, half_p], wp.at[own, half_p], wp_sem, k).start()
    wq[own, :] = wq_shard[...]
    wp[own, :] = wp_shard[...]

    r1 = routes_ref[0:1, :]
    r2 = routes_ref[1:2, :]
    ids = iota((sz.ep, sz.rows), 0)
    oh1 = (r1 == ids).astype(F32)
    oh2 = (r2 == ids).astype(F32)
    before = (
        (iota((sz.rows, sz.rows), 0) < iota((sz.rows, sz.rows), 1))
        .astype(F32)
        .astype(BF)
    )
    pos1 = mm(oh1.astype(BF), before)
    pos2 = mm(oh2.astype(BF), before) + jnp.sum(oh1, 1, keepdims=True)
    place = oh1 * pos1 + oh2 * pos2
    kept = (oh1 + oh2 > 0.5) & (place < sz.cap - 0.5)
    slot = jnp.where(kept, place, -1.0).astype(jnp.int32)
    slot_ids = iota((sz.slots, sz.rows), 0)
    for e in range(sz.experts):
        pmat[e * sz.slots : (e + 1) * sz.slots, :] = (
            (slot_ids == slot[e : e + 1, :]).astype(F32).astype(BF)
        )

    spread = pad_matrix(sz)
    gpad[...] = mm(spread, grad_ref[...]).astype(BF)
    for e in range(sz.experts):
        block = slice(e * sz.slots, (e + 1) * sz.slots)
        gs[block, :] = mm(pmat[block, :], gpad[...]).astype(BF)
    slots_me = rows_at(me, sz.slots)
    for k in range(1, n):
        dst = rows_at(lax.rem(me + k, n), sz.slots)
        to_peer(gs.at[dst, :], gr.at[slots_me, :], g_sem, k).start()
    gr[slots_me, :] = gs[slots_me, :]

    x = mm(spread, tok_ref[...])
    for k in range(1, n):
        src = lax.rem(me + n - k, n)
        to_peer(sm_shard, smg.at[src], sm_sem, k).wait_recv()
    acc = jnp.zeros((sz.small, sz.d), F32)
    for j in range(n):
        r = iota((sz.shard_pad, sz.d), 0)
        c = iota((sz.shard_pad, sz.d), 1)
        pick = ((c == r + j * sz.shard) & (r < sz.shard)).astype(F32).astype(BF)
        acc = acc + mm(smg[j], pick)
    smf[...] = acc
    normed[...] = normalize(x, acc[0:1, :], acc[2:3, :]).astype(BF)

    for k in range(1, n):
        theirs = rows_at(lax.rem(me + n - k, n), sz.shard)
        part = wq.at[theirs, half_q]
        to_peer(wq_shard.at[:, half_q], part, wq_sem, k).wait_recv()
        to_sibling(part, cq_sem, k).start()
    for k in range(1, n):
        theirs = rows_at(lax.rem(me + n - k, n), sz.shard)
        to_sibling(wq.at[theirs, other_q], cq_sem, k).wait_recv()
    for j, bias_row in ((0, 3), (1, None), (2, 4)):
        cols = slice(j * sz.d, (j + 1) * sz.d)
        out = mm(normed[...], wq[:, cols])
        if bias_row is not None:
            out = out + smf[bias_row : bias_row + 1, :]
        qkv[:, cols] = out.astype(BF)

    scale = 1.0 / math.sqrt(HEAD_DIM)
    lane = iota((sz.seq, 128), 1)
    live = iota((sz.seq, sz.seq), 1) < SEQ

    def pair_step(pair, carry):
        for image in range(sz.images):
            rows = slice(image * sz.seq, (image + 1) * sz.seq)
            q2 = qkv[rows, pl.ds(pl.multiple_of(pair * 128, 128), 128)]
            k2 = qkv[rows, pl.ds(pl.multiple_of(sz.d + pair * 128, 128), 128)]
            v2 = qkv[rows, pl.ds(pl.multiple_of(2 * sz.d + pair * 128, 128), 128)]
            total = jnp.zeros((sz.seq, 128), F32)
            for half in range(2):
                mask = (lane >= half * 64) & (lane < half * 64 + 64)
                s = mm_nt(jnp.where(mask, q2, jnp.zeros_like(q2)), k2) * scale
                s = jnp.where(live, s, -1e30)
                e = jnp.exp(s - jnp.max(s, -1, keepdims=True))
                p = (e / jnp.sum(e, -1, keepdims=True)).astype(BF)
                pall[(image * sz.pairs + pair) * 2 + half] = p
                total = total + mm(p, jnp.where(mask, v2, jnp.zeros_like(v2)))
            ctx[rows, pl.ds(pl.multiple_of(pair * 128, 128), 128)] = total.astype(BF)
        return carry

    lax.fori_loop(0, sz.pairs, pair_step, 0)

    for k in range(1, n):
        theirs = rows_at(lax.rem(me + n - k, n), sz.shard)
        part = wp.at[theirs, half_p]
        to_peer(wp_shard.at[:, half_p], part, wp_sem, k).wait_recv()
        to_sibling(part, cp_sem, k).start()
    for k in range(1, n):
        theirs = rows_at(lax.rem(me + n - k, n), sz.shard)
        to_sibling(wp.at[theirs, other_p], cp_sem, k).wait_recv()
    res = (
        mm(spread, tok_ref[...])
        + mm(ctx[...], wp[...])
        + smf[5:6, :]
    )
    resid[...] = res
    low = normalize(res, smf[1:2, :], smf[6:7, :]).astype(BF)
    second[...] = low

    for e in range(sz.experts):
        block = slice(e * sz.slots, (e + 1) * sz.slots)
        xs[block, :] = mm(pmat[block, :], second[...]).astype(BF)
    for k in range(1, n):
        dst = rows_at(lax.rem(me + k, n), sz.slots)
        to_peer(xs.at[dst, :], xr.at[slots_me, :], x_sem, k).start()
    xr[slots_me, :] = xs[slots_me, :]

    small_low = smf[...].astype(BF)
    logit_rows = mm_nt(small_low, low)[8 : 8 + sz.ep, :]
    logit_rows = jnp.where(iota((sz.ep, sz.rows), 0) < sz.experts, logit_rows, -1e30)
    e_rows = jnp.exp(logit_rows - jnp.max(logit_rows, 0, keepdims=True))
    prob_rows = e_rows / jnp.sum(e_rows, 0, keepdims=True)
    hi = prob_rows.astype(BF)
    left = prob_rows - hi.astype(F32)
    mid = left.astype(BF)
    low3 = (left - mid.astype(F32)).astype(BF)
    for e in range(sz.experts):
        block = pmat[e * sz.slots : (e + 1) * sz.slots, :]
        gates[e] = mm_nt(hi, block) + mm_nt(mid, block) + mm_nt(low3, block)
    for k in range(1, n):
        to_peer(
            gates.at[lax.rem(me + k, n)], gater.at[me], ga_sem, k
        ).start()
    gater[me] = gates[me]
    logit_cols = mm_nt(low, small_low)
    col = iota((sz.rows, sz.small), 1)
    logit_cols = jnp.where((col >= 8) & (col < 8 + sz.experts), logit_cols, -1e30)
    e_cols = jnp.exp(logit_cols - jnp.max(logit_cols, 1, keepdims=True))
    probs[...] = e_cols / jnp.sum(e_cols, 1, keepdims=True)

    for k in range(1, n):
        src = lax.rem(me + n - k, n)
        dst = rows_at(lax.rem(me + k, n), sz.slots)
        theirs = rows_at(src, sz.slots)
        shard_rows = rows_at(src, sz.shard)
        to_peer(gs.at[dst, :], gr.at[theirs, :], g_sem, k).wait()
        to_peer(xs.at[dst, :], xr.at[theirs, :], x_sem, k).wait()
        to_peer(gates.at[lax.rem(me + k, n)], gater.at[src], ga_sem, k).wait()
        to_peer(sm_shard, smg.at[src], sm_sem, k).wait_send()
        to_peer(
            wq_shard.at[:, half_q], wq.at[shard_rows, half_q], wq_sem, k
        ).wait_send()
        to_peer(
            wp_shard.at[:, half_p], wp.at[shard_rows, half_p], wp_sem, k
        ).wait_send()
        to_sibling(wq.at[shard_rows, half_q], cq_sem, k).wait_send()
        to_sibling(wp.at[shard_rows, half_p], cp_sem, k).wait_send()


def front(sz, tokens, grad, routes, wq, wp, small):
    vmem = pl.BlockSpec(memory_space=pltpu.VMEM)
    rows, d, slots = sz.rows, sz.d, sz.all_slots
    outs = [
        ((slots, d), BF),
        ((slots, d), BF),
        ((sz.n_exp, sz.ep, sz.slots), F32),
        ((rows, 3 * d), BF),
        ((sz.images * sz.pairs * 2, sz.seq, sz.seq), BF),
        ((rows, d), BF),
        ((rows, d), F32),
        ((rows, d), BF),
        ((rows, d), BF),
        ((rows, sz.small), F32),
        ((d, 3 * d), BF),
        ((d, d), BF),
        ((sz.small, d), F32),
        ((rows, d), BF),
        ((slots, rows), BF),
    ]
    sems = pltpu.SemaphoreType.DMA((2, sz.n_exp))
    return pl.pallas_call(
        partial(front_kernel, sz),
        name="front",
        out_shape=[jax.ShapeDtypeStruct(s, t) for s, t in outs],
        in_specs=[vmem] * 6,
        out_specs=[vmem] * len(outs),
        scratch_shapes=[
            pltpu.VMEM((slots, d), BF),
            pltpu.VMEM((slots, d), BF),
            pltpu.VMEM((sz.n_exp, sz.ep, sz.slots), F32),
            pltpu.VMEM((sz.n_exp, sz.small, sz.shard_pad), BF),
        ]
        + [sems] * 8,
        compiler_params=pltpu.CompilerParams(
            collective_id=0, has_side_effects=True, vmem_limit_bytes=56 << 20
        ),
    )(tokens, grad, routes, wq, wp, small)


def on_device(
    mesh,
    tokens,
    routes,
    out_grad,
    attn_qkv,
    attn_out,
    router,
    norm_gains,
    dense_biases,
    expert_in,
    expert_in_bias,
    expert_out,
    expert_out_bias,
):
    sz = Sizes(mesh, tokens.shape[0], tokens.shape[1], expert_in.shape[2])
    d = sz.d
    scale = 1.0 / math.sqrt(HEAD_DIM)
    routes_pad = jnp.pad(
        routes.T.reshape(2, sz.images, SEQ),
        ((0, 6), (0, 0), (0, sz.seq - SEQ)),
        constant_values=-1,
    ).reshape(8, sz.rows)
    small = jnp.concatenate(
        [norm_gains, dense_biases, jnp.zeros((1, sz.shard), BF), router.T], 0
    )
    small = jnp.pad(
        small, ((0, sz.small - small.shape[0]), (0, sz.shard_pad - sz.shard))
    )
    (xr, gr, gater, qkv, pall, ctx, resid, second, normed, probs, wq, wp, smf, gpad, pmat) = front(
        sz, tokens, out_grad, routes_pad, attn_qkv, attn_out, small
    )
    me = lax.axis_index("exp")
    n = sz.n_exp
    gate_rows = lax.dynamic_index_in_dim(gater, me, 1, keepdims=False)
    d_res = (gate_rows.reshape(-1, 1) * gr.astype(F32)).astype(BF)
    w1, w2 = expert_in[0], expert_out[0]
    b1, b2 = expert_in_bias[0].astype(F32), expert_out_bias[0].astype(F32)
    hidden = mm(xr, w1) + b1
    act32, back = jax.vjp(partial(jax.nn.gelu, approximate=False), hidden)
    act = act32.astype(BF)
    result = (mm(act, w2) + b2).astype(BF)
    d_act = mm_nt(d_res, w2)
    d_hid = back(d_act)[0].astype(BF)
    gw2 = mm_tn(act, d_res)
    gb2 = jnp.sum(d_res.astype(F32), 0)
    gw1 = mm_tn(xr, d_hid)
    gb1 = jnp.sum(d_hid.astype(F32), 0)
    row_grad = mm_nt(d_hid, w1).astype(BF)
    ret = lax.all_to_all(result, "exp", split_axis=0, concat_axis=0, tiled=True)
    bck = lax.all_to_all(row_grad, "exp", split_axis=0, concat_axis=0, tiled=True)
    g32 = gpad.astype(F32)
    out = resid
    prob_grad = []
    p3 = probs[:, 8 : 8 + sz.experts]
    for e in range(sz.experts):
        blk = slice(e * sz.slots, (e + 1) * sz.slots)
        po = mm_tn(pmat[blk], ret[blk])
        out = out + p3[:, e : e + 1] * po
        prob_grad.append(jnp.sum(g32 * po, 1))
    pg = jnp.stack(prob_grad, 1)
    lg = (p3 * (pg - jnp.sum(pg * p3, 1, keepdims=True))).astype(BF)
    router_all = smf[8 : 8 + sz.experts].astype(BF)
    second_grad = mm_tn(pmat, bck) + mm(lg, router_all)
    g_router = mm_tn(second, lg)
    ln2 = jax.vjp(normalize, resid, smf[1], smf[6])[1](second_grad)
    resid_grad = g32 + ln2[0]
    pgd = resid_grad.astype(BF)
    gp = mm_tn(ctx, pgd)
    gbo = jnp.sum(pgd.astype(F32), 0)
    cg = mm_nt(pgd, wp).astype(BF)
    heads = d // HEAD_DIM
    four = (sz.images, sz.seq, heads, HEAD_DIM)
    q, k, v = (qkv[:, i * d : (i + 1) * d].reshape(four) for i in range(3))
    cg4 = cg.reshape(four)
    pa = pall.reshape(sz.images, heads, sz.seq, sz.seq)
    es = partial(jnp.einsum, preferred_element_type=F32)
    vg = es("ihst,ishd->ithd", pa, cg4).astype(BF)
    pb = es("ishd,ithd->ihst", cg4, v)
    p32 = pa.astype(F32)
    sg = (p32 * (pb - jnp.sum(pb * p32, -1, keepdims=True))).astype(BF)
    qg = (es("ihst,ithd->ishd", sg, k) * scale).astype(BF)
    kg = (es("ihst,ishd->ithd", sg, q) * scale).astype(BF)
    flat = lambda z: z.reshape(sz.rows, d)
    qkvg = jnp.concatenate([flat(qg), flat(kg), flat(vg)], 1)
    gq = mm_tn(normed, qkvg)
    ng = mm_nt(qkvg, wq)
    x = jnp.pad(tokens.astype(F32).reshape(sz.images, SEQ, d), ((0, 0), (0, sz.seq - SEQ), (0, 0))).reshape(sz.rows, d)
    ln1 = jax.vjp(normalize, x, smf[0], smf[2])[1](ng)
    gin = (resid_grad + ln1[0]).astype(BF)
    unpad = lambda z: z.reshape(sz.images, sz.seq, d)[:, :SEQ].reshape(sz.tok, d)
    gains = jnp.stack([ln1[1], ln2[1]])
    biases = jnp.stack([ln1[2], jnp.sum(flat(qg).astype(F32), 0), jnp.sum(flat(vg).astype(F32), 0), gbo, ln2[2]])
    smallg = jnp.concatenate([gains, biases, g_router.T], 0)
    def dense(z, dim):
        z = lax.psum(z.astype(BF), "rep")
        return lax.psum_scatter(z, "exp", scatter_dimension=dim, tiled=True).astype(F32)
    sg_out = dense(smallg, 1)
    def rsr(z, dim):
        return lax.psum_scatter(z[None].astype(BF), "rep", scatter_dimension=dim, tiled=True).astype(F32)
    return (
        unpad(out.astype(BF)), unpad(gin), dense(gq, 0), dense(gp, 0), sg_out[7:].T, sg_out[:2], sg_out[2:7],
        rsr(gw1, 2), rsr(gb1, 1), rsr(gw2, 1), rsr(gb2, 1),
    )


def solution(mesh):
    both = P(("rep", "exp"), None)
    rows = P("exp", None)
    cols = P(None, "exp")
    cube = P("exp", None, None)
    in_specs = (both, both, both, rows, rows, rows, cols, cols, cube, rows, cube, rows)
    out_specs = (
        both,
        both,
        rows,
        rows,
        rows,
        cols,
        cols,
        P("exp", None, "rep"),
        P("exp", "rep"),
        P("exp", "rep", None),
        P("exp", "rep"),
    )
    return jax.shard_map(
        partial(on_device, mesh),
        mesh=mesh,
        in_specs=in_specs,
        out_specs=out_specs,
        check_vma=False,
    )
```

```python
from functools import partial
import math

import jax
import jax.numpy as jnp
from jax import lax
from jax.experimental import pallas as pl
from jax.experimental.pallas import tpu as pltpu
from jax.sharding import PartitionSpec as P

HEAD_DIM = 64
SEQ = 197
EPS = 1e-06
BF = jnp.bfloat16
F32 = jnp.float32
MESH = pl.DeviceIdType.MESH


def up(value, step):
    return (value + step - 1) // step * step


def mm(a, b):
    return lax.dot_general(a, b, (((1,), (0,)), ((), ())), preferred_element_type=F32)


def mm_nt(a, b):
    return lax.dot_general(a, b, (((1,), (1,)), ((), ())), preferred_element_type=F32)


def mm_tn(a, b):
    return lax.dot_general(a, b, (((0,), (0,)), ((), ())), preferred_element_type=F32)


def iota(shape, dim):
    return lax.broadcasted_iota(jnp.int32, shape, dim)


def rows_at(index, size):
    return pl.ds(pl.multiple_of(index * size, size), size)


def normalize(values, gain, shift):
    center = values - jnp.mean(values, -1, keepdims=True)
    spread = jnp.mean(center * center, -1, keepdims=True)
    return center * lax.rsqrt(spread + EPS) * gain + shift


class Sizes:
    def __init__(self, mesh, tok_rows, width, ff):
        self.n_exp = mesh.shape["exp"]
        self.n_rep = mesh.shape["rep"]
        self.tok = tok_rows
        self.images = tok_rows // SEQ
        self.seq = up(SEQ, 16)
        self.rows = self.images * self.seq
        self.d = width
        self.ff = ff
        self.experts = self.n_exp
        self.cap = (18 * tok_rows + 8 * self.experts - 1) // (8 * self.experts)
        self.slots = up(self.cap, 16)
        self.all_slots = self.slots * self.experts
        self.shard = width // self.n_exp
        self.shard_pad = up(self.shard, 128)
        self.ep = up(self.experts, 8)
        self.small = up(8 + self.ep, 16)
        self.pairs = width // 128
        self.nz = self.n_rep // 2
        self.fs = ff // self.n_rep
        self.fs_rows = self.fs + 16
        self.blocks = 4
        self.row_block = self.all_slots // self.blocks
        self.part = 2 * self.shard // self.nz
        self.scatter = self.part % 16 == 0


def pad_matrix(sz):
    row = iota((sz.rows, sz.tok), 0)
    col = iota((sz.rows, sz.tok), 1)
    want = jnp.full((sz.rows, sz.tok), -1, jnp.int32)
    for image in range(sz.images):
        inside = (row >= image * sz.seq) & (row < image * sz.seq + SEQ)
        want = jnp.where(inside, row - image * (sz.seq - SEQ), want)
    return (want == col).astype(F32).astype(BF)


def front_kernel(
    sz,
    tok_ref,
    grad_ref,
    routes_ref,
    wq_shard,
    wp_shard,
    sm_shard,
    xr,
    dres,
    qkv,
    pall,
    ctx,
    resid,
    second,
    normed,
    probs,
    wq,
    wp,
    smf,
    gpad,
    comb,
    pmat,
    gr,
    gater,
    xs,
    gs,
    gates,
    smg,
    wq_sem,
    wp_sem,
    cq_sem,
    cp_sem,
    sm_sem,
    g_sem,
    x_sem,
    ga_sem,
):
    me_r = lax.axis_index("rep")
    me = lax.axis_index("exp")
    n = sz.n_exp
    core = lax.rem(me_r, 2)
    sibling = me_r + 1 - 2 * core

    barrier = pltpu.get_barrier_semaphore()
    for k in range(1, n):
        pl.semaphore_signal(
            barrier, inc=1, device_id=(me_r, lax.rem(me + k, n)), device_id_type=MESH
        )
    pl.semaphore_signal(barrier, inc=1, device_id=(sibling, me), device_id_type=MESH)
    pl.semaphore_wait(barrier, n)

    def to_peer(src, dst, sems, k):
        return pltpu.make_async_remote_copy(
            src_ref=src,
            dst_ref=dst,
            send_sem=sems.at[0, k],
            recv_sem=sems.at[1, k],
            device_id=(me_r, lax.rem(me + k, n)),
            device_id_type=MESH,
        )

    def to_sibling(ref, sems, k):
        return pltpu.make_async_remote_copy(
            src_ref=ref,
            dst_ref=ref,
            send_sem=sems.at[0, k],
            recv_sem=sems.at[1, k],
            device_id=(sibling, me),
            device_id_type=MESH,
        )

    hq, hp = 3 * sz.d // 2, sz.d // 2
    own = rows_at(me, sz.shard)
    half_q = pl.ds(pl.multiple_of(core * hq, 128), hq)
    half_p = pl.ds(pl.multiple_of(core * hp, 128), hp)
    other_q = pl.ds(pl.multiple_of((1 - core) * hq, 128), hq)
    other_p = pl.ds(pl.multiple_of((1 - core) * hp, 128), hp)

    smg[me] = sm_shard[...]
    for k in range(1, n):
        to_peer(sm_shard, smg.at[me], sm_sem, k).start()
    for k in range(1, n):
        to_peer(wq_shard.at[:, half_q], wq.at[own, half_q], wq_sem, k).start()
    for k in range(1, n):
        to_peer(wp_shard.at[:, half_p], wp.at[own, half_p], wp_sem, k).start()
    wq[own, :] = wq_shard[...]
    wp[own, :] = wp_shard[...]

    r1 = routes_ref[0:1, :]
    r2 = routes_ref[1:2, :]
    ids = iota((sz.ep, sz.rows), 0)
    oh1 = (r1 == ids).astype(F32)
    oh2 = (r2 == ids).astype(F32)
    before = (
        (iota((sz.rows, sz.rows), 0) < iota((sz.rows, sz.rows), 1))
        .astype(F32)
        .astype(BF)
    )
    pos1 = mm(oh1.astype(BF), before)
    pos2 = mm(oh2.astype(BF), before) + jnp.sum(oh1, 1, keepdims=True)
    place = oh1 * pos1 + oh2 * pos2
    kept = (oh1 + oh2 > 0.5) & (place < sz.cap - 0.5)
    slot = jnp.where(kept, place, -1.0).astype(jnp.int32)
    slot_ids = iota((sz.slots, sz.rows), 0)
    for e in range(sz.experts):
        pmat[e * sz.slots : (e + 1) * sz.slots, :] = (
            (slot_ids == slot[e : e + 1, :]).astype(F32).astype(BF)
        )

    eye = (iota((sz.rows, sz.rows), 0) == iota((sz.rows, sz.rows), 1)).astype(F32)
    slot_cols = mm_nt(eye.astype(BF), slot.astype(F32).astype(BF)).astype(jnp.int32)
    lane_ids = iota((sz.rows, sz.slots), 1)
    for e in range(sz.experts):
        comb[e] = (slot_cols[:, e : e + 1] == lane_ids).astype(F32).astype(BF)

    spread = pad_matrix(sz)
    gpad[...] = mm(spread, grad_ref[...]).astype(BF)
    for e in range(sz.experts):
        block = slice(e * sz.slots, (e + 1) * sz.slots)
        gs[block, :] = mm(pmat[block, :], gpad[...]).astype(BF)
    slots_me = rows_at(me, sz.slots)
    for k in range(1, n):
        dst = rows_at(lax.rem(me + k, n), sz.slots)
        to_peer(gs.at[dst, :], gr.at[slots_me, :], g_sem, k).start()
    gr[slots_me, :] = gs[slots_me, :]

    x = mm(spread, tok_ref[...])
    for k in range(1, n):
        src = lax.rem(me + n - k, n)
        to_peer(sm_shard, smg.at[src], sm_sem, k).wait_recv()
    acc = jnp.zeros((sz.small, sz.d), F32)
    for j in range(n):
        r = iota((sz.shard_pad, sz.d), 0)
        c = iota((sz.shard_pad, sz.d), 1)
        pick = ((c == r + j * sz.shard) & (r < sz.shard)).astype(F32).astype(BF)
        acc = acc + mm(smg[j], pick)
    smf[...] = acc
    normed[...] = normalize(x, acc[0:1, :], acc[2:3, :]).astype(BF)

    for k in range(1, n):
        theirs = rows_at(lax.rem(me + n - k, n), sz.shard)
        part = wq.at[theirs, half_q]
        to_peer(wq_shard.at[:, half_q], part, wq_sem, k).wait_recv()
        to_sibling(part, cq_sem, k).start()
    for k in range(1, n):
        theirs = rows_at(lax.rem(me + n - k, n), sz.shard)
        to_sibling(wq.at[theirs, other_q], cq_sem, k).wait_recv()
    for j, bias_row in ((0, 3), (1, None), (2, 4)):
        cols = slice(j * sz.d, (j + 1) * sz.d)
        out = mm(normed[...], wq[:, cols])
        if bias_row is not None:
            out = out + smf[bias_row : bias_row + 1, :]
        qkv[:, cols] = out.astype(BF)

    scale = 1.0 / math.sqrt(HEAD_DIM)
    lane = iota((sz.seq, 128), 1)
    live = iota((sz.seq, sz.seq), 1) < SEQ

    def pair_step(pair, carry):
        for image in range(sz.images):
            rows = slice(image * sz.seq, (image + 1) * sz.seq)
            q2 = qkv[rows, pl.ds(pl.multiple_of(pair * 128, 128), 128)]
            k2 = qkv[rows, pl.ds(pl.multiple_of(sz.d + pair * 128, 128), 128)]
            v2 = qkv[rows, pl.ds(pl.multiple_of(2 * sz.d + pair * 128, 128), 128)]
            total = jnp.zeros((sz.seq, 128), F32)
            for half in range(2):
                mask = (lane >= half * 64) & (lane < half * 64 + 64)
                s = mm_nt(jnp.where(mask, q2, jnp.zeros_like(q2)), k2) * scale
                s = jnp.where(live, s, -1e30)
                e = jnp.exp(s - jnp.max(s, -1, keepdims=True))
                p = (e / jnp.sum(e, -1, keepdims=True)).astype(BF)
                pall[pair, image * 2 + half] = p
                total = total + mm(p, jnp.where(mask, v2, jnp.zeros_like(v2)))
            ctx[rows, pl.ds(pl.multiple_of(pair * 128, 128), 128)] = total.astype(BF)
        return carry

    lax.fori_loop(0, sz.pairs, pair_step, 0)

    for k in range(1, n):
        theirs = rows_at(lax.rem(me + n - k, n), sz.shard)
        part = wp.at[theirs, half_p]
        to_peer(wp_shard.at[:, half_p], part, wp_sem, k).wait_recv()
        to_sibling(part, cp_sem, k).start()
    for k in range(1, n):
        theirs = rows_at(lax.rem(me + n - k, n), sz.shard)
        to_sibling(wp.at[theirs, other_p], cp_sem, k).wait_recv()
    res = (
        mm(spread, tok_ref[...])
        + mm(ctx[...], wp[...])
        + smf[5:6, :]
    )
    resid[...] = res
    low = normalize(res, smf[1:2, :], smf[6:7, :]).astype(BF)
    second[...] = low

    for e in range(sz.experts):
        block = slice(e * sz.slots, (e + 1) * sz.slots)
        xs[block, :] = mm(pmat[block, :], second[...]).astype(BF)
    for k in range(1, n):
        dst = rows_at(lax.rem(me + k, n), sz.slots)
        to_peer(xs.at[dst, :], xr.at[slots_me, :], x_sem, k).start()
    xr[slots_me, :] = xs[slots_me, :]

    small_low = smf[...].astype(BF)
    logit_rows = mm_nt(small_low, low)[8 : 8 + sz.ep, :]
    logit_rows = jnp.where(iota((sz.ep, sz.rows), 0) < sz.experts, logit_rows, -1e30)
    e_rows = jnp.exp(logit_rows - jnp.max(logit_rows, 0, keepdims=True))
    prob_rows = e_rows / jnp.sum(e_rows, 0, keepdims=True)
    hi = prob_rows.astype(BF)
    left = prob_rows - hi.astype(F32)
    mid = left.astype(BF)
    low3 = (left - mid.astype(F32)).astype(BF)
    for e in range(sz.experts):
        block = pmat[e * sz.slots : (e + 1) * sz.slots, :]
        gates[e] = mm_nt(hi, block) + mm_nt(mid, block) + mm_nt(low3, block)
    for k in range(1, n):
        to_peer(
            gates.at[lax.rem(me + k, n)], gater.at[me], ga_sem, k
        ).start()
    gater[me] = gates[me]
    logit_cols = mm_nt(low, small_low)
    col = iota((sz.rows, sz.small), 1)
    logit_cols = jnp.where((col >= 8) & (col < 8 + sz.experts), logit_cols, -1e30)
    e_cols = jnp.exp(logit_cols - jnp.max(logit_cols, 1, keepdims=True))
    probs[...] = e_cols / jnp.sum(e_cols, 1, keepdims=True)

    for k in range(1, n):
        src = lax.rem(me + n - k, n)
        dst = rows_at(lax.rem(me + k, n), sz.slots)
        theirs = rows_at(src, sz.slots)
        to_peer(gs.at[dst, :], gr.at[theirs, :], g_sem, k).wait()
        to_peer(gates.at[lax.rem(me + k, n)], gater.at[src], ga_sem, k).wait()
    square = iota((sz.slots, sz.slots), 0) == iota((sz.slots, sz.slots), 1)
    for j in range(n):
        block = slice(j * sz.slots, (j + 1) * sz.slots)
        row = gater[j, pl.ds(me, 1), :]
        gate = jnp.sum(jnp.where(square, row, 0.0), 1, keepdims=True)
        dres[block, :] = (gate * gr[block, :].astype(F32)).astype(BF)
    for k in range(1, n):
        src = lax.rem(me + n - k, n)
        dst = rows_at(lax.rem(me + k, n), sz.slots)
        theirs = rows_at(src, sz.slots)
        shard_rows = rows_at(src, sz.shard)
        to_peer(xs.at[dst, :], xr.at[theirs, :], x_sem, k).wait()
        to_peer(sm_shard, smg.at[src], sm_sem, k).wait_send()
        to_peer(
            wq_shard.at[:, half_q], wq.at[shard_rows, half_q], wq_sem, k
        ).wait_send()
        to_peer(
            wp_shard.at[:, half_p], wp.at[shard_rows, half_p], wp_sem, k
        ).wait_send()
        to_sibling(wq.at[shard_rows, half_q], cq_sem, k).wait_send()
        to_sibling(wp.at[shard_rows, half_p], cp_sem, k).wait_send()


def front(sz, tokens, grad, routes, wq, wp, small):
    vmem = pl.BlockSpec(memory_space=pltpu.VMEM)
    rows, d, slots = sz.rows, sz.d, sz.all_slots
    outs = [
        ((slots, d), BF),
        ((slots, d), BF),
        ((rows, 3 * d), BF),
        ((sz.pairs, sz.images * 2, sz.seq, sz.seq), BF),
        ((rows, d), BF),
        ((rows, d), F32),
        ((rows, d), BF),
        ((rows, d), BF),
        ((rows, sz.small), F32),
        ((d, 3 * d), BF),
        ((d, d), BF),
        ((sz.small, d), F32),
        ((rows, d), BF),
        ((sz.experts, rows, sz.slots), BF),
    ]
    sems = pltpu.SemaphoreType.DMA((2, sz.n_exp))
    return pl.pallas_call(
        partial(front_kernel, sz),
        name="front",
        out_shape=[jax.ShapeDtypeStruct(s, t) for s, t in outs],
        in_specs=[vmem] * 6,
        out_specs=[vmem] * len(outs),
        scratch_shapes=[
            pltpu.VMEM((slots, rows), BF),
            pltpu.VMEM((slots, d), BF),
            pltpu.VMEM((sz.n_exp, sz.ep, sz.slots), F32),
            pltpu.VMEM((slots, d), BF),
            pltpu.VMEM((slots, d), BF),
            pltpu.VMEM((sz.n_exp, sz.ep, sz.slots), F32),
            pltpu.VMEM((sz.n_exp, sz.small, sz.shard_pad), BF),
        ]
        + [sems] * 8,
        compiler_params=pltpu.CompilerParams(
            collective_id=0, has_side_effects=True, vmem_limit_bytes=56 << 20
        ),
    )(tokens, grad, routes, wq, wp, small)


def unpad_matrix(sz):
    row = iota((sz.tok, sz.rows), 0)
    col = iota((sz.tok, sz.rows), 1)
    want = row
    for image in range(1, sz.images):
        want = jnp.where(row >= image * SEQ, row + image * (sz.seq - SEQ), want)
    return (want == col).astype(F32).astype(BF)


def normalize_back(values, gain, cot):
    center = values - jnp.mean(values, -1, keepdims=True)
    spread = jnp.mean(center * center, -1, keepdims=True)
    inv = lax.rsqrt(spread + EPS)
    unit = center * inv
    scaled = cot * gain
    grad = inv * (
        scaled
        - jnp.mean(scaled, -1, keepdims=True)
        - unit * jnp.mean(scaled * unit, -1, keepdims=True)
    )
    return grad, jnp.sum(cot * unit, 0, keepdims=True), jnp.sum(cot, 0, keepdims=True)


def gelu_parts(h):
    t = 1.0 / (1.0 + (0.3275911 / math.sqrt(2.0)) * jnp.abs(h))
    bell = jnp.exp(-0.5 * h * h)
    poly = t * (
        0.127414796
        + t * (-0.142248368 + t * (0.7107068705 + t * (-0.7265760135 + t * 0.5307027145)))
    )
    tail = poly * bell
    return jnp.where(h >= 0, 1.0 - tail, tail), bell * (1.0 / math.sqrt(2.0 * math.pi))


def rest_kernel(
    sz,
    xr,
    dres,
    qkv,
    pall,
    ctx,
    resid,
    second,
    normed,
    probs,
    smf,
    gpad,
    comb,
    tok_ref,
    b1_ref,
    b2_ref,
    wq_hbm,
    wp_hbm,
    w1_hbm,
    w2_hbm,
    out_ref,
    gin_ref,
    o_w1,
    o_w2,
    o_dense,
    o_small,
    w1,
    w2,
    xt,
    act,
    dhid,
    res_acc,
    row_acc,
    res_send,
    row_send,
    ret,
    bck,
    t1,
    t2,
    v1,
    v2,
    u1,
    u2,
    pbuf,
    r1,
    r2,
    z1,
    z2,
    sm,
    smr,
    sme,
    sme_r,
    smz_r,
    wsem,
    psem,
    t_sem,
    u_sem,
    ret_sem,
    bck_sem,
    d1_sem,
    d2_sem,
    z1_sem,
    z2_sem,
    z3_sem,
    s1_sem,
    s2_sem,
    s3_sem,
):
    me_r = lax.axis_index("rep")
    me = lax.axis_index("exp")
    n, nz, fs, d = sz.n_exp, sz.nz, sz.fs, sz.d
    core = lax.rem(me_r, 2)
    z = lax.div(me_r, 2)
    sibling = me_r + 1 - 2 * core

    loads = []
    for i, (src, dst) in enumerate(((w1_hbm, w1), (w2_hbm, w2))):
        cp = pltpu.make_async_copy(src, dst, wsem.at[i])
        cp.start()
        loads.append(cp)

    barrier = pltpu.get_barrier_semaphore()
    for k in range(1, n):
        pl.semaphore_signal(
            barrier, inc=1, device_id=(me_r, lax.rem(me + k, n)), device_id_type=MESH
        )
    for k in range(1, nz):
        pl.semaphore_signal(
            barrier,
            inc=1,
            device_id=(lax.rem(me_r + 2 * k, 2 * nz), me),
            device_id_type=MESH,
        )
    pl.semaphore_signal(barrier, inc=1, device_id=(sibling, me), device_id_type=MESH)
    pl.semaphore_wait(barrier, n - 1 + nz)

    def remote(src, dst, send, recv, rep, exp):
        return pltpu.make_async_remote_copy(
            src_ref=src,
            dst_ref=dst,
            send_sem=send,
            recv_sem=recv,
            device_id=(rep, exp),
            device_id_type=MESH,
        )

    def to_peer(src, dst, sems, k):
        return remote(
            src, dst, sems.at[0, k], sems.at[1, k], me_r, lax.rem(me + k, n)
        )

    def to_z(src, dst, sems, k):
        return remote(
            src, dst, sems.at[0, k], sems.at[1, k], lax.rem(me_r + 2 * k, 2 * nz), me
        )

    cut = sz.d
    xta = res_send.at[0:d, :]
    xta[...] = xr[0:cut, :].T
    xt[...] = xr[cut:, :].T
    lower = 1 - lax.div(z, (nz + 1) // 2)
    bias2 = jnp.sum(dres[...].astype(F32), 0, keepdims=True)
    for cp in loads:
        cp.wait()

    def w1_part(f):
        return w1[:, pl.ds(pl.multiple_of(f * fs, 128), fs)]

    def compute(f):
        w2f_rows = pl.ds(pl.multiple_of(f * fs, 16), fs)
        bias = b1_ref[pl.ds(f, 1), :]
        for b in range(sz.blocks):
            rows = slice(b * sz.row_block, (b + 1) * sz.row_block)
            h = mm(xr[rows, :], w1_part(f)) + bias
            cdf, pdf = gelu_parts(h)
            da = mm_nt(dres[rows, :], w2[w2f_rows, :])
            a = (h * cdf).astype(BF)
            dh = (da * (cdf + h * pdf)).astype(BF)
            act[rows, :] = a
            dhid[rows, :] = dh
            res_acc[rows, :] += mm(a, w2[w2f_rows, :])
            row_acc[rows, :] += mm_nt(dh, w1_part(f))

    def grad1(rows):
        part = mm(xta[rows, :], dhid[0:cut, :])
        return part + mm(xt[rows, :], dhid[cut:, :])

    def grad2(cols):
        return mm_tn(act[:, cols], dres[...])

    def extra():
        gb = jnp.sum(dhid[...].astype(F32), 0, keepdims=True)
        row = iota((16, d), 0)
        wide = jnp.concatenate([gb, jnp.zeros((1, d - fs), F32)], 1)
        return jnp.where(row == 0, wide, jnp.where(row == 1, bias2, 0.0))

    def t_copies(dest):
        return (
            remote(t1, v1.at[dest], t_sem.at[0, 0, dest], t_sem.at[1, 0, dest], sibling, me),
            remote(t2, v2.at[dest], t_sem.at[0, 1, dest], t_sem.at[1, 1, dest], sibling, me),
        )

    def landing(way, step, at):
        if way == 0:
            return nz - 2 - step + at
        return at + step + 2 - nz if step < nz - 2 else nz

    def u_copies(src1, src2, way, step, target, slot):
        return (
            remote(src1, u1.at[slot], u_sem.at[0, 0, way, step], u_sem.at[1, 0, way, step], target, me),
            remote(src2, u2.at[slot], u_sem.at[0, 1, way, step], u_sem.at[1, 1, way, step], target, me),
        )

    res_acc[...] = jnp.zeros_like(res_acc)
    row_acc[...] = jnp.zeros_like(row_acc)

    parts1 = [slice(i, i + d // 2) for i in (0, d // 2)]
    parts2 = [slice(i, i + 128) for i in range(0, fs, 128)]

    def dest_of(i):
        return lower * (nz - 1 - i) + (1 - lower) * i

    def slice_step(i, carry):
        dest = dest_of(i)

        compute(dest * 2 + 1 - core)
        for rows in parts1:
            t1[rows, :] = grad1(rows).astype(BF)
        for rows in parts2:
            t2[rows, :] = grad2(rows).astype(BF)
        t2[fs:, :] = extra().astype(BF)
        for cp in t_copies(dest):
            cp.start()
        compute(dest * 2 + core)
        for cp in t_copies(dest):
            cp.wait()
        for rows in parts1:
            v1[dest, rows, :] = (v1[dest, rows, :].astype(F32) + grad1(rows)).astype(BF)
        for rows in parts2:
            v2[dest, rows, :] = (v2[dest, rows, :].astype(F32) + grad2(rows)).astype(BF)
        v2[dest, fs:, :] = (v2[dest, fs:, :].astype(F32) + extra()).astype(BF)

        @pl.when((z == 0) & (i <= nz - 2))
        def _():
            for cp in u_copies(v1.at[dest], v2.at[dest], 0, i, me_r + 2, dest):
                cp.start()

        @pl.when((z == nz - 1) & (i < nz - 2))
        def _():
            for cp in u_copies(v1.at[dest], v2.at[dest], 1, i, me_r - 2, dest):
                cp.start()

        @pl.when((z == nz - 1) & (i == nz - 2))
        def _():
            for cp in u_copies(v1.at[dest], v2.at[dest], 1, i, me_r - 2, nz):
                cp.start()

        return carry

    lax.fori_loop(0, nz, slice_step, 0)

    row_send[...] = row_acc[...].astype(BF)
    slots_me = rows_at(me, sz.slots)

    def peer_slots(k):
        return rows_at(lax.rem(me + k, n), sz.slots)

    for k in range(1, n):
        to_peer(row_send.at[peer_slots(k), :], bck.at[slots_me, :], bck_sem, k).start()
    bck[slots_me, :] = row_send[slots_me, :]
    res_send[...] = (res_acc[...] + b2_ref[...]).astype(BF)
    for k in range(1, n):
        to_peer(res_send.at[peer_slots(k), :], ret.at[slots_me, :], ret_sem, k).start()
    ret[slots_me, :] = res_send[slots_me, :]
    dense_loads = []
    for i, (src, cols) in enumerate(((wq_hbm, slice(0, 3 * d)), (wp_hbm, slice(3 * d, 4 * d)))):
        cp = pltpu.make_async_copy(src, w1.at[:, cols], wsem.at[i])
        cp.start()
        dense_loads.append(cp)

    def z_round(s):
        for way in range(2):
            zz = z if way == 0 else nz - 1 - z
            dest = nz - 1 - s + zz if way == 0 else z - (nz - 1 - s)
            target = me_r + 2 if way == 0 else me_r - 2

            @pl.when((zz >= 1) & (zz <= s))
            def _():
                here = landing(way, s - 1, z)
                there = landing(way, s, z + 1 if way == 0 else z - 1)
                a1, a2 = u1.at[here], u2.at[here]
                for cp in u_copies(a1, a2, way, s - 1, target, here):
                    cp.wait_recv()
                u1[here] = (u1[here].astype(F32) + v1[dest].astype(F32)).astype(BF)
                u2[here] = (u2[here].astype(F32) + v2[dest].astype(F32)).astype(BF)
                for cp in u_copies(a1, a2, way, s, target, there):
                    cp.start()

    if nz > 2:
        z_round(1)

    for k in range(1, n):
        theirs = rows_at(lax.rem(me + n - k, n), sz.slots)
        to_peer(row_send.at[peer_slots(k), :], bck.at[theirs, :], bck_sem, k).wait()
    for k in range(1, n):
        theirs = rows_at(lax.rem(me + n - k, n), sz.slots)
        to_peer(res_send.at[peer_slots(k), :], ret.at[theirs, :], ret_sem, k).wait()
    mixed = res_acc.at[0 : sz.rows, :]
    sgrad = res_acc.at[sz.rows : 2 * sz.rows, :]
    mixed[...] = resid[...]
    prob_grads = []
    total = jnp.zeros((sz.rows, 1), F32)
    for e in range(sz.experts):
        block = slice(e * sz.slots, (e + 1) * sz.slots)
        p = probs[:, 8 + e : 9 + e]
        rows_out = mm(comb[e], ret[block, :])
        mixed[...] += p * rows_out
        pg = jnp.sum(gpad[...].astype(F32) * rows_out, 1, keepdims=True)
        prob_grads.append(pg)
        total = total + pg * p
    out_ref[...] = mm(unpad_matrix(sz), mixed[...].astype(BF)).astype(BF)
    lane = iota((sz.rows, sz.small), 1)
    logit_grad = jnp.zeros((sz.rows, sz.small), F32)
    for e in range(sz.experts):
        logit_grad = jnp.where(lane == 8 + e, prob_grads[e] - total, logit_grad)
    logit_low = (probs[...] * logit_grad).astype(BF)
    sgrad[...] = mm(logit_low, smf[...].astype(BF))
    for e in range(sz.experts):
        sgrad[...] += mm(comb[e], bck[e * sz.slots : (e + 1) * sz.slots, :])
    back2, gain2, shift2 = normalize_back(resid[...], smf[1:2, :], sgrad[...])
    rgrad = row_acc.at[0 : sz.rows, :]
    rgrad[...] = gpad[...].astype(F32) + back2
    low = rgrad[...].astype(BF)
    bias_out = jnp.sum(low.astype(F32), 0, keepdims=True)
    dense = w2
    dense[3 * d : 4 * d, :] = mm_tn(ctx[...], low).astype(BF)
    for cp in dense_loads:
        cp.wait()
    dq_ref = res_send.at[0 : sz.rows, :]
    dk_ref = res_send.at[sz.rows : 2 * sz.rows, :]
    dv_ref = row_send.at[0 : sz.rows, :]
    cgrad = row_send.at[sz.rows : 2 * sz.rows, :]
    dqkv = (dq_ref, dk_ref, dv_ref)

    def load_probs(pair):
        slot = lax.rem(pair, 2)
        return pltpu.make_async_copy(pall.at[pair], pbuf.at[slot], psem.at[slot])

    cgrad[...] = mm_nt(low, w1[:, 3 * d : 4 * d]).astype(BF)
    sm[...] = mm_tn(logit_low, second[...])

    for s in range(2, nz - 1):
        z_round(s)

    scale = 1.0 / math.sqrt(HEAD_DIM)
    half_lane = iota((sz.seq, 128), 1)
    load_probs(0).start()

    def pair_step(pair, carry):
        load_probs(pair).wait()

        @pl.when(pair + 1 < sz.pairs)
        def _():
            load_probs(pair + 1).start()

        for image in range(sz.images):
            rows = slice(image * sz.seq, (image + 1) * sz.seq)
            at = [pl.ds(pl.multiple_of(j * d + pair * 128, 128), 128) for j in range(3)]
            q2, k2, v2_ = (qkv[rows, at[j]] for j in range(3))
            c2 = cgrad[rows, at[0]]
            dq = jnp.zeros((sz.seq, 128), F32)
            dk = jnp.zeros((sz.seq, 128), F32)
            dv = jnp.zeros((sz.seq, 128), F32)
            for half in range(2):
                mask = (half_lane >= half * 64) & (half_lane < half * 64 + 64)
                zero = jnp.zeros_like(q2)
                ch = jnp.where(mask, c2, zero)
                p = pbuf[lax.rem(pair, 2), image * 2 + half]
                dv = dv + mm_tn(p, ch)
                pb = mm_nt(ch, v2_)
                p32 = p.astype(F32)
                mix = jnp.sum(pb * p32, -1, keepdims=True)
                ds = (p32 * (pb - mix)).astype(BF)
                dq = dq + mm(ds, jnp.where(mask, k2, zero))
                dk = dk + mm_tn(ds, jnp.where(mask, q2, zero))
            dq_ref[rows, at[0]] = (dq * scale).astype(BF)
            dk_ref[rows, at[0]] = (dk * scale).astype(BF)
            dv_ref[rows, at[0]] = dv.astype(BF)
        return carry

    lax.fori_loop(0, sz.pairs, pair_step, 0)

    for j in range(3):
        cols = slice(j * d, (j + 1) * d)
        dense[cols, :] = mm_tn(normed[...], dqkv[j][...]).astype(BF)
    keep = pl.ds(pl.multiple_of(core * 2 * d, 16), 2 * d)
    give = pl.ds(pl.multiple_of((1 - core) * 2 * d, 16), 2 * d)
    first = remote(dense.at[give, :], r1, d1_sem.at[0], d1_sem.at[1], sibling, me)
    first.start()

    ngrad = mixed
    ngrad[...] = mm_nt(dq_ref[...], w1[:, 0:d])
    for j in range(1, 3):
        ngrad[...] += mm_nt(dqkv[j][...], w1[:, j * d : (j + 1) * d])
    x = mm(pad_matrix(sz), tok_ref[...])
    back1, gain1, shift1 = normalize_back(x, smf[0:1, :], ngrad[...])
    gin_ref[...] = mm(unpad_matrix(sz), (rgrad[...] + back1).astype(BF)).astype(BF)
    bias_q = jnp.sum(dq_ref[...].astype(F32), 0, keepdims=True)
    bias_v = jnp.sum(dv_ref[...].astype(F32), 0, keepdims=True)
    row = iota((sz.small, d), 0)
    small = sm[...]
    for i, value in enumerate((gain1, gain2, shift1, bias_q, bias_v, bias_out, shift2)):
        small = jnp.where(row == i, value, small)
    sm[...] = small
    smb = sme.at[n]
    smb[...] = small.astype(BF)
    s_first = remote(smb, smr, s1_sem.at[0], s1_sem.at[1], sibling, me)
    s_first.start()

    first.wait()
    dense[keep, :] = (dense[keep, :].astype(F32) + r1[...].astype(F32)).astype(BF)

    def block_rows(j, e):
        return pl.ds(pl.multiple_of(core * 2 * d + j * d + e * sz.shard, 16), sz.shard)

    def peer_blocks(k):
        e = lax.rem(me + k, n)
        return [
            remote(
                dense.at[block_rows(j, e), :],
                r2.at[k - 1, pl.ds(j * sz.shard, sz.shard), :],
                d2_sem.at[0, j, k],
                d2_sem.at[1, j, k],
                me_r,
                e,
            )
            for j in range(2)
        ]

    for k in range(1, n):
        for cp in peer_blocks(k):
            cp.start()
    s_first.wait()
    chip_small = (sm[...] + smr[...].astype(F32)).astype(BF)
    for e in range(n):
        r = iota((sz.shard_pad, d), 0)
        c = iota((sz.shard_pad, d), 1)
        pick = ((c == r + e * sz.shard) & (r < sz.shard)).astype(F32).astype(BF)
        sme[e, :, 0 : sz.shard_pad] = mm_nt(chip_small, pick).astype(BF)
    for k in range(1, n):
        to_peer(
            sme.at[lax.rem(me + k, n), :, 0 : sz.shard_pad], sme_r.at[k], s2_sem, k
        ).start()

    def z_last(way, sums):
        zz = z if way == 0 else nz - 1 - z
        target = me_r + 2 if way == 0 else me_r - 2

        @pl.when(zz >= 1)
        def _():
            here = landing(way, nz - 2, z)
            for cp in u_copies(u1.at[here], u2.at[here], way, nz - 2, target, here):
                cp.wait_recv()
            v1[z] = (v1[z].astype(F32) + u1[here].astype(F32)).astype(BF)
            v2[z] = (v2[z].astype(F32) + u2[here].astype(F32)).astype(BF)

    z_last(0, None)
    z_last(1, None)
    stores = [
        pltpu.make_async_copy(v1.at[z], o_w1, wsem.at[0]),
        pltpu.make_async_copy(v2.at[z], o_w2, wsem.at[1]),
    ]
    for cp in stores:
        cp.start()

    for k in range(1, n):
        for cp in peer_blocks(k):
            cp.wait()
    for j in range(2):
        part = slice(j * sz.shard, (j + 1) * sz.shard)
        acc = dense[block_rows(j, me), :].astype(F32)
        for k in range(1, n):
            acc = acc + r2[k - 1, part, :].astype(F32)
        z1[part, :] = acc.astype(BF)
    acc = sme[me, :, 0 : sz.shard_pad].astype(F32)
    for k in range(1, n):
        to_peer(
            sme.at[lax.rem(me + k, n), :, 0 : sz.shard_pad], sme_r.at[k], s2_sem, k
        ).wait()
        acc = acc + sme_r[k].astype(F32)
    smz_r[0] = acc.astype(BF)
    for k in range(1, nz):
        to_z(smz_r.at[0], smz_r.at[k], s3_sem, k).start()

    half = pl.ds(pl.multiple_of(core * 2 * sz.shard, 16), 2 * sz.shard)
    base = core * 2 * sz.shard
    if sz.scatter:
        part = sz.part

        def part_rows(zi):
            return pl.ds(pl.multiple_of(zi * part, 16), part)

        def out_rows(zi):
            return pl.ds(pl.multiple_of(base + zi * part, 16), part)

        for k in range(1, nz):
            to_z(z1.at[part_rows(lax.rem(z + k, nz)), :], z2.at[k - 1], z1_sem, k).start()
        acc = z1[part_rows(z), :].astype(F32)
        for k in range(1, nz):
            to_z(z1.at[part_rows(lax.rem(z + k, nz)), :], z2.at[k - 1], z1_sem, k).wait()
            acc = acc + z2[k - 1].astype(F32)
        o_dense[out_rows(z), :] = acc.astype(BF)
        for k in range(1, nz):
            to_z(o_dense.at[out_rows(z), :], o_dense.at[out_rows(z), :], z2_sem, k).start()
        for k in range(1, nz):
            theirs = lax.rem(z + nz - k, nz)
            to_z(o_dense.at[out_rows(theirs), :], o_dense.at[out_rows(theirs), :], z2_sem, k).wait()
    else:
        for k in range(1, nz):
            to_z(z1, z2.at[k - 1], z1_sem, k).start()
        acc = z1[...].astype(F32)
        for k in range(1, nz):
            to_z(z1, z2.at[k - 1], z1_sem, k).wait()
            acc = acc + z2[k - 1].astype(F32)
        o_dense[half, :] = acc.astype(BF)
    last = remote(o_dense.at[half, :], o_dense.at[half, :], z3_sem.at[0], z3_sem.at[1], sibling, me)
    last.start()
    acc = smz_r[0].astype(F32)
    for k in range(1, nz):
        to_z(smz_r.at[0], smz_r.at[k], s3_sem, k).wait()
        acc = acc + smz_r[k].astype(F32)
    o_small[...] = acc
    other = pl.ds(pl.multiple_of((1 - core) * 2 * sz.shard, 16), 2 * sz.shard)
    last.wait_send()
    remote(o_dense.at[other, :], o_dense.at[other, :], z3_sem.at[0], z3_sem.at[1], sibling, me).wait_recv()

    for cp in stores:
        cp.wait()
    for s in range(nz - 1):
        for way in range(2):
            zz = z if way == 0 else nz - 1 - z
            target = me_r + 2 if way == 0 else me_r - 2

            @pl.when(zz <= s)
            def _():
                for cp in u_copies(v1.at[0], v2.at[0], way, s, target, 0):
                    cp.wait_send()


def rest(sz, state, tokens, b1, b2, wq, wp, w1, w2):
    vmem = pl.BlockSpec(memory_space=pltpu.VMEM)
    hbm = pl.BlockSpec(memory_space=pl.ANY)
    rows, d, slots, fs, nz, n = sz.rows, sz.d, sz.all_slots, sz.fs, sz.nz, sz.n_exp
    dma = pltpu.SemaphoreType.DMA
    outs = [
        ((sz.tok, d), BF),
        ((sz.tok, d), BF),
        ((d, fs), BF),
        ((sz.fs_rows, d), BF),
        ((4 * sz.shard, d), BF),
        ((sz.small, sz.shard_pad), F32),
    ]
    scratch = [
        pltpu.VMEM(w1.shape, BF),
        pltpu.VMEM(w2.shape, BF),
        pltpu.VMEM((d, slots - d), BF),
        pltpu.VMEM((slots, fs), BF),
        pltpu.VMEM((slots, fs), BF),
        pltpu.VMEM((slots, d), F32),
        pltpu.VMEM((slots, d), F32),
        pltpu.VMEM((slots, d), BF),
        pltpu.VMEM((slots, d), BF),
        pltpu.VMEM((slots, d), BF),
        pltpu.VMEM((slots, d), BF),
        pltpu.VMEM((d, fs), BF),
        pltpu.VMEM((sz.fs_rows, d), BF),
        pltpu.VMEM((nz, d, fs), BF),
        pltpu.VMEM((nz, sz.fs_rows, d), BF),
        pltpu.VMEM((nz + 1, d, fs), BF),
        pltpu.VMEM((nz + 1, sz.fs_rows, d), BF),
        pltpu.VMEM((2, 2 * sz.images, sz.seq, sz.seq), BF),
        pltpu.VMEM((2 * d, d), BF),
        pltpu.VMEM((n - 1, 2 * sz.shard, d), BF),
        pltpu.VMEM((2 * sz.shard, d), BF),
        pltpu.VMEM((nz - 1, sz.part if sz.scatter else 2 * sz.shard, d), BF),
        pltpu.VMEM((sz.small, d), F32),
        pltpu.VMEM((sz.small, d), BF),
        pltpu.VMEM((n + 1, sz.small, d), BF),
        pltpu.VMEM((n, sz.small, sz.shard_pad), BF),
        pltpu.VMEM((nz, sz.small, sz.shard_pad), BF),
        dma((2,)),
        dma((2,)),
        dma((2, 2, nz)),
        dma((2, 2, 2, nz - 1)),
        dma((2, n)),
        dma((2, n)),
        dma((2,)),
        dma((2, 2, n)),
        dma((2, nz)),
        dma((2, nz)),
        dma((2,)),
        dma((2,)),
        dma((2, n)),
        dma((2, nz)),
    ]
    return pl.pallas_call(
        partial(rest_kernel, sz),
        name="rest",
        out_shape=[jax.ShapeDtypeStruct(s, t) for s, t in outs],
        in_specs=[vmem] * 3 + [hbm] + [vmem] * (len(state) - 1) + [hbm] * 4,
        out_specs=[vmem, vmem, hbm, hbm, vmem, vmem],
        scratch_shapes=scratch,
        compiler_params=pltpu.CompilerParams(
            collective_id=1, has_side_effects=True, vmem_limit_bytes=62 << 20
        ),
    )(*state, tokens, b1, b2, wq, wp, w1, w2)


def plain_rest(sz, state, tokens, w1, b1, w2, b2):
    xr, dres, qkv, pall, ctx, resid, second, normed, probs, smf, gpad, comb, wq, wp = state
    d, n = sz.d, sz.experts
    scale = 1.0 / math.sqrt(HEAD_DIM)
    h = mm(xr, w1) + b1
    cdf, pdf = gelu_parts(h)
    act = (h * cdf).astype(BF)
    result = (mm(act, w2) + b2).astype(BF)
    dhid = (mm_nt(dres, w2) * (cdf + h * pdf)).astype(BF)
    row_grad = mm_nt(dhid, w1).astype(BF)
    swap = partial(
        lax.all_to_all, axis_name="exp", split_axis=0, concat_axis=0, tiled=True
    )
    ret = swap(result).reshape(n, sz.slots, d)
    bck = swap(row_grad).reshape(n, sz.slots, d)
    g32 = gpad.astype(F32)
    p = probs[:, 8 : 8 + n]
    picked = jnp.einsum("ets,esd->etd", comb, ret, preferred_element_type=F32)
    mixed = resid + jnp.einsum("te,etd->td", p, picked, precision="highest")
    pg = jnp.sum(g32[None] * picked, -1).T
    lg = (p * (pg - jnp.sum(pg * p, 1, keepdims=True))).astype(BF)
    sgrad = mm(lg, smf[8 : 8 + n].astype(BF))
    sgrad = sgrad + jnp.einsum("ets,esd->td", comb, bck, preferred_element_type=F32)
    back2, gain2, shift2 = normalize_back(resid, smf[1:2], sgrad)
    rgrad = g32 + back2
    low = rgrad.astype(BF)
    cgrad = mm_nt(low, wp).astype(BF)
    four = (sz.images, sz.seq, d // HEAD_DIM, HEAD_DIM)
    q, k, v, c = (
        a.reshape(four)
        for a in (qkv[:, :d], qkv[:, d : 2 * d], qkv[:, 2 * d :], cgrad)
    )
    prob = pall.reshape(sz.pairs, sz.images, 2, sz.seq, sz.seq)
    prob = prob.transpose(1, 0, 2, 3, 4).reshape(sz.images, -1, sz.seq, sz.seq)
    product = partial(jnp.einsum, preferred_element_type=F32)
    dv = product("ihst,ishd->ithd", prob, c).astype(BF)
    pb = product("ishd,ithd->ihst", c, v)
    p32 = prob.astype(F32)
    ds = (p32 * (pb - jnp.sum(pb * p32, -1, keepdims=True))).astype(BF)
    dq = (product("ihst,ithd->ishd", ds, k) * scale).astype(BF)
    dk = (product("ihst,ishd->ithd", ds, q) * scale).astype(BF)
    dqkv = jnp.concatenate([a.reshape(sz.rows, d) for a in (dq, dk, dv)], 1)
    x = mm(pad_matrix(sz), tokens)
    back1, gain1, shift1 = normalize_back(x, smf[0:1], mm_nt(dqkv, wq))
    gin = (rgrad + back1).astype(BF)
    sums = jnp.sum(dqkv.astype(F32), 0, keepdims=True)
    small = jnp.concatenate(
        [gain1, gain2, shift1, sums[:, :d], sums[:, 2 * d :]]
        + [jnp.sum(low.astype(F32), 0, keepdims=True), shift2, mm_tn(lg, second)]
    )

    def dense(grad, dim):
        total = lax.psum(grad.astype(BF), "rep")
        total = lax.psum_scatter(total, "exp", scatter_dimension=dim, tiled=True)
        return total.astype(F32)

    def owned(grad, dim):
        total = lax.psum_scatter(
            grad[None].astype(BF), "rep", scatter_dimension=dim, tiled=True
        )
        return total.astype(F32)

    def unpad(rows):
        return rows.reshape(sz.images, sz.seq, d)[:, :SEQ].reshape(sz.tok, d)

    sums = dense(small, 1)
    return (
        unpad(mixed.astype(BF)),
        unpad(gin),
        dense(mm_tn(normed, dqkv), 0),
        dense(mm_tn(ctx, low), 0),
        sums[7:].T,
        sums[0:2],
        sums[2:7],
        owned(mm_tn(xr, dhid), 2),
        owned(jnp.sum(dhid.astype(F32), 0), 1),
        owned(mm_tn(act, dres), 1),
        owned(jnp.sum(dres.astype(F32), 0), 1),
    )


def on_device(
    mesh,
    tokens,
    routes,
    out_grad,
    attn_qkv,
    attn_out,
    router,
    norm_gains,
    dense_biases,
    expert_in,
    expert_in_bias,
    expert_out,
    expert_out_bias,
):
    sz = Sizes(mesh, tokens.shape[0], tokens.shape[1], expert_in.shape[2])
    d, fs = sz.d, sz.fs
    routes_pad = jnp.pad(
        routes.T.reshape(2, sz.images, SEQ),
        ((0, 6), (0, 0), (0, sz.seq - SEQ)),
        constant_values=-1,
    ).reshape(8, sz.rows)
    small = jnp.concatenate(
        [norm_gains, dense_biases, jnp.zeros((1, sz.shard), BF), router.T], 0
    )
    small = jnp.pad(
        small, ((0, sz.small - small.shape[0]), (0, sz.shard_pad - sz.shard))
    )
    (xr, dres, qkv, pall, ctx, resid, second, normed, probs, wq, wp, smf, gpad, comb) = front(
        sz, tokens, out_grad, routes_pad, attn_qkv, attn_out, small
    )
    w1, w2 = expert_in[0], expert_out[0]
    if fs % 128 or sz.all_slots % 128 or sz.all_slots <= d:
        state = (xr, dres, qkv, pall, ctx, resid, second, normed, probs, smf, gpad, comb, wq, wp)
        bias1, bias2 = expert_in_bias.astype(F32), expert_out_bias.astype(F32)
        return plain_rest(sz, state, tokens, w1, bias1, w2, bias2)
    b1 = expert_in_bias.astype(F32).reshape(sz.n_rep, fs)
    out, gin, g1, g2, dense, sg = rest(
        sz,
        (xr, dres, qkv, pall, ctx, resid, second, normed, probs, smf, gpad, comb),
        tokens,
        b1,
        expert_out_bias.astype(F32),
        wq,
        wp,
        w1,
        w2,
    )
    me_r = lax.axis_index("rep")
    sh = sz.shard
    dense = dense.astype(F32).reshape(4, sh, d)
    g2 = g2.astype(F32)
    own = d // sz.n_rep
    return (
        out,
        gin,
        jnp.concatenate([dense[0], dense[1], dense[2]], 1),
        dense[3],
        sg[8 : 8 + sz.experts, :sh].T,
        sg[0:2, :sh],
        sg[2:7, :sh],
        g1[None].astype(F32),
        g2[fs : fs + 1, : fs],
        g2[None, : fs],
        lax.dynamic_slice(g2, (fs + 1, me_r * own), (1, own)),
    )


def solution(mesh):
    both = P(("rep", "exp"), None)
    rows = P("exp", None)
    cols = P(None, "exp")
    cube = P("exp", None, None)
    in_specs = (both, both, both, rows, rows, rows, cols, cols, cube, rows, cube, rows)
    out_specs = (
        both,
        both,
        rows,
        rows,
        rows,
        cols,
        cols,
        P("exp", None, "rep"),
        P("exp", "rep"),
        P("exp", "rep", None),
        P("exp", "rep"),
    )
    return jax.shard_map(
        partial(on_device, mesh),
        mesh=mesh,
        in_specs=in_specs,
        out_specs=out_specs,
        check_vma=False,
    )
```

```python
from functools import partial
import math

import jax
import jax.numpy as jnp
from jax import lax
from jax.experimental import pallas as pl
from jax.experimental.pallas import tpu as pltpu
from jax.sharding import PartitionSpec as P

HEAD_DIM = 64
SEQ = 197
EPS = 1e-06
BF = jnp.bfloat16
F32 = jnp.float32
MESH = pl.DeviceIdType.MESH


def up(value, step):
    return (value + step - 1) // step * step


def mm(a, b):
    return lax.dot_general(a, b, (((1,), (0,)), ((), ())), preferred_element_type=F32)


def mm_nt(a, b):
    return lax.dot_general(a, b, (((1,), (1,)), ((), ())), preferred_element_type=F32)


def mm_tn(a, b):
    return lax.dot_general(a, b, (((0,), (0,)), ((), ())), preferred_element_type=F32)


def iota(shape, dim):
    return lax.broadcasted_iota(jnp.int32, shape, dim)


def rows_at(index, size):
    return pl.ds(pl.multiple_of(index * size, size), size)


def normalize(values, gain, shift):
    center = values - jnp.mean(values, -1, keepdims=True)
    spread = jnp.mean(center * center, -1, keepdims=True)
    return center * lax.rsqrt(spread + EPS) * gain + shift


class Sizes:
    def __init__(self, mesh, tok_rows, width, ff):
        self.n_exp = mesh.shape["exp"]
        self.n_rep = mesh.shape["rep"]
        self.tok = tok_rows
        self.images = tok_rows // SEQ
        self.seq = up(SEQ, 16)
        self.rows = self.images * self.seq
        self.d = width
        self.ff = ff
        self.experts = self.n_exp
        self.cap = (18 * tok_rows + 8 * self.experts - 1) // (8 * self.experts)
        self.slots = up(self.cap, 16)
        self.all_slots = self.slots * self.experts
        self.shard = width // self.n_exp
        self.shard_pad = up(self.shard, 128)
        self.ep = up(self.experts, 8)
        self.small = up(8 + self.ep, 16)
        self.pairs = width // 128
        self.nz = self.n_rep // 2
        self.fs = ff // self.n_rep
        self.fs_rows = self.fs + 16
        self.part = self.shard // self.nz
        self.groups = self.pairs // 2
        self.chunks = self.groups + 1


def pad_matrix(sz):
    row = iota((sz.rows, sz.tok), 0)
    col = iota((sz.rows, sz.tok), 1)
    want = jnp.full((sz.rows, sz.tok), -1, jnp.int32)
    for image in range(sz.images):
        inside = (row >= image * sz.seq) & (row < image * sz.seq + SEQ)
        want = jnp.where(inside, row - image * (sz.seq - SEQ), want)
    return (want == col).astype(F32).astype(BF)


def unpad_matrix(sz):
    row = iota((sz.tok, sz.rows), 0)
    col = iota((sz.tok, sz.rows), 1)
    want = row
    for image in range(1, sz.images):
        want = jnp.where(row >= image * SEQ, row + image * (sz.seq - SEQ), want)
    return (want == col).astype(F32).astype(BF)


def front_kernel(
    sz,
    tok_ref,
    grad_ref,
    routes_ref,
    wq_shard,
    wp_shard,
    router_ref,
    gains_ref,
    biases_ref,
    xr,
    dres,
    qkv,
    pall,
    ctx_t,
    resid,
    second,
    normed_t,
    probs,
    wq,
    wp,
    smf,
    gpad,
    comb,
    ctx,
    normed,
    pmat,
    gr,
    gater,
    xs,
    gs,
    gates,
    routers,
    gains,
    biases,
    wq_sem,
    wp_sem,
    zq_sem,
    zp_sem,
    cq_sem,
    cp_sem,
    sm_sem,
    g_sem,
    x_sem,
    ga_sem,
):
    me_r = lax.axis_index("rep")
    me = lax.axis_index("exp")
    n = sz.n_exp
    core = lax.rem(me_r, 2)
    sibling = me_r + 1 - 2 * core
    odd = lax.rem(lax.div(me_r, 2), 2)
    partner = me_r + 2 - 4 * odd

    barrier = pltpu.get_barrier_semaphore()
    for k in range(1, n):
        pl.semaphore_signal(
            barrier, inc=1, device_id=(me_r, lax.rem(me + k, n)), device_id_type=MESH
        )
    for rep in (sibling, partner):
        pl.semaphore_signal(barrier, inc=1, device_id=(rep, me), device_id_type=MESH)
    pl.semaphore_wait(barrier, n + 1)

    def remote(src, dst, send, recv, rep, exp):
        return pltpu.make_async_remote_copy(
            src_ref=src,
            dst_ref=dst,
            send_sem=send,
            recv_sem=recv,
            device_id=(rep, exp),
            device_id_type=MESH,
        )

    def to_peer(src, dst, sems, k):
        return remote(
            src, dst, sems.at[0, k], sems.at[1, k], me_r, lax.rem(me + k, n)
        )

    class Gather:
        def __init__(self, shard, full, width, peer_sem, layer_sem, twin_sem):
            self.shard, self.full = shard, full
            self.piece = width // 6
            self.peer_sem, self.layer_sem, self.twin_sem = peer_sem, layer_sem, twin_sem

        def cols(self, side, first, count):
            start = side * 3 * self.piece + first * self.piece
            return pl.ds(pl.multiple_of(start, 128), count * self.piece)

        def rows(self, k):
            return rows_at(lax.rem(me + n - k, n), sz.shard)

        def peer(self, k):
            cols = self.cols(core, odd, 2)
            return to_peer(
                self.shard.at[:, cols],
                self.full.at[rows_at(me, sz.shard), cols],
                self.peer_sem,
                k,
            )

        def layer(self, k, mine=True):
            part = 2 * odd if mine else 2 - 2 * odd
            piece = self.full.at[self.rows(k), self.cols(core, part, 1)]
            sem = self.layer_sem
            return remote(piece, piece, sem.at[0, k], sem.at[1, k], partner, me)

        def twin(self, k, late, side):
            first, count = (2 - 2 * odd, 1) if late else (odd, 2)
            piece = self.full.at[self.rows(k), self.cols(side, first, count)]
            sem = self.twin_sem
            return remote(
                piece, piece, sem.at[0, late, k], sem.at[1, late, k], sibling, me
            )

        def start(self):
            for k in range(1, n):
                self.peer(k).start()
            self.full[rows_at(me, sz.shard), :] = self.shard[...]

        def forward(self):
            for k in range(1, n):
                self.peer(k).wait_recv()
                self.layer(k).start()
                self.twin(k, 0, core).start()

        def finish(self):
            for k in range(1, n):
                self.layer(k, False).wait_recv()
                self.twin(k, 1, core).start()
            for k in range(1, n):
                for late in range(2):
                    self.twin(k, late, 1 - core).wait_recv()

        def drain(self):
            for k in range(1, n):
                self.peer(k).wait_send()
                self.layer(k).wait_send()
                for late in range(2):
                    self.twin(k, late, core).wait_send()

    gather_q = Gather(wq_shard, wq, 3 * sz.d, wq_sem, zq_sem, cq_sem)
    gather_p = Gather(wp_shard, wp, sz.d, wp_sem, zp_sem, cp_sem)

    def small_sends(k):
        return [
            to_peer(src, dst.at[me], sm_sem.at[i], k)
            for i, (src, dst) in enumerate(
                ((gains_ref, gains), (biases_ref, biases), (router_ref, routers))
            )
        ]

    for k in range(1, n):
        for cp in small_sends(k):
            cp.start()
    gather_q.start()
    gains[me] = gains_ref[...]
    biases[me] = biases_ref[...]
    routers[me] = router_ref[...]

    choice = (routes_ref[...].astype(F32) + 1.0).astype(BF)
    lines = mm_nt(choice, pad_matrix(sz)).astype(jnp.int32) - 1
    ids = iota((sz.ep, sz.rows), 0)
    oh1 = (lines[0:1, :] == ids).astype(F32)
    oh2 = (lines[1:2, :] == ids).astype(F32)
    before = (
        (iota((sz.rows, sz.rows), 0) < iota((sz.rows, sz.rows), 1))
        .astype(F32)
        .astype(BF)
    )
    pos1 = mm(oh1.astype(BF), before)
    pos2 = mm(oh2.astype(BF), before) + jnp.sum(oh1, 1, keepdims=True)
    place = oh1 * pos1 + oh2 * pos2
    kept = (oh1 + oh2 > 0.5) & (place < sz.cap - 0.5)
    slot = jnp.where(kept, place, -1.0).astype(jnp.int32)
    slot_ids = iota((sz.slots, sz.rows), 0)
    for e in range(sz.experts):
        pmat[e * sz.slots : (e + 1) * sz.slots, :] = (
            (slot_ids == slot[e : e + 1, :]).astype(F32).astype(BF)
        )
    eye = (iota((sz.rows, sz.rows), 0) == iota((sz.rows, sz.rows), 1)).astype(F32)
    slot_cols = mm_nt(eye.astype(BF), slot.astype(F32).astype(BF)).astype(jnp.int32)
    lane_ids = iota((sz.rows, sz.slots), 1)
    for e in range(sz.experts):
        comb[e] = (slot_cols[:, e : e + 1] == lane_ids).astype(F32).astype(BF)

    spread = pad_matrix(sz)
    gpad[...] = mm(spread, grad_ref[...]).astype(BF)
    for e in range(sz.experts):
        block = slice(e * sz.slots, (e + 1) * sz.slots)
        gs[block, :] = mm(pmat[block, :], gpad[...]).astype(BF)
    slots_me = rows_at(me, sz.slots)
    gr[slots_me, :] = gs[slots_me, :]

    x = mm(spread, tok_ref[...])
    for k in range(1, n):
        for cp in small_sends(k):
            cp.wait_recv()
    smf[...] = jnp.zeros_like(smf)
    for j in range(n):
        r = iota((sz.shard, sz.d), 0)
        c = iota((sz.shard, sz.d), 1)
        pick = (c == r + j * sz.shard).astype(F32).astype(BF)
        smf[0:2, :] += mm(gains[j], pick)
        smf[2:7, :] += mm(biases[j], pick)
        smf[8 : 8 + sz.experts, :] += mm(routers[j], pick)
    normed[...] = normalize(x, smf[0:1, :], smf[2:3, :]).astype(BF)
    normed_t[...] = normed[...].T

    gather_q.forward()
    gather_p.start()
    gather_q.finish()
    for j, bias_row in ((0, 3), (1, None), (2, 4)):
        cols = slice(j * sz.d, (j + 1) * sz.d)
        out = mm(normed[...], wq[:, cols])
        if bias_row is not None:
            out = out + smf[bias_row : bias_row + 1, :]
        qkv[:, cols] = out.astype(BF)
    for k in range(1, n):
        dst = rows_at(lax.rem(me + k, n), sz.slots)
        to_peer(gs.at[dst, :], gr.at[slots_me, :], g_sem, k).start()

    scale = 1.0 / math.sqrt(HEAD_DIM)
    lane = iota((sz.seq, 128), 1)
    live = iota((sz.seq, sz.seq), 1) < SEQ

    def pair_step(pair, carry):
        for image in range(sz.images):
            rows = slice(image * sz.seq, (image + 1) * sz.seq)
            q2 = qkv[rows, pl.ds(pl.multiple_of(pair * 128, 128), 128)]
            k2 = qkv[rows, pl.ds(pl.multiple_of(sz.d + pair * 128, 128), 128)]
            v2 = qkv[rows, pl.ds(pl.multiple_of(2 * sz.d + pair * 128, 128), 128)]
            total = jnp.zeros((sz.seq, 128), F32)
            for half in range(2):
                mask = (lane >= half * 64) & (lane < half * 64 + 64)
                s = mm_nt(jnp.where(mask, q2, jnp.zeros_like(q2)), k2) * scale
                s = jnp.where(live, s, -1e30)
                e = jnp.exp(s - jnp.max(s, -1, keepdims=True))
                p = (e / jnp.sum(e, -1, keepdims=True)).astype(BF)
                pall[pair, image * 2 + half] = p
                total = total + mm(p, jnp.where(mask, v2, jnp.zeros_like(v2)))
            ctx[rows, pl.ds(pl.multiple_of(pair * 128, 128), 128)] = total.astype(BF)
        return carry

    lax.fori_loop(0, sz.pairs, pair_step, 0)

    gather_p.forward()
    gather_p.finish()
    res = (
        mm(spread, tok_ref[...])
        + mm(ctx[...], wp[...])
        + smf[5:6, :]
    )
    resid[...] = res
    low = normalize(res, smf[1:2, :], smf[6:7, :]).astype(BF)
    second[...] = low

    for e in range(sz.experts):
        block = slice(e * sz.slots, (e + 1) * sz.slots)
        xs[block, :] = mm(pmat[block, :], second[...]).astype(BF)
    for k in range(1, n):
        dst = rows_at(lax.rem(me + k, n), sz.slots)
        to_peer(xs.at[dst, :], xr.at[slots_me, :], x_sem, k).start()
    xr[slots_me, :] = xs[slots_me, :]

    small_low = smf[...].astype(BF)
    logit_rows = mm_nt(small_low, low)[8 : 8 + sz.ep, :]
    logit_rows = jnp.where(iota((sz.ep, sz.rows), 0) < sz.experts, logit_rows, -1e30)
    e_rows = jnp.exp(logit_rows - jnp.max(logit_rows, 0, keepdims=True))
    prob_rows = e_rows / jnp.sum(e_rows, 0, keepdims=True)
    hi = prob_rows.astype(BF)
    left = prob_rows - hi.astype(F32)
    mid = left.astype(BF)
    low3 = (left - mid.astype(F32)).astype(BF)
    for e in range(sz.experts):
        block = pmat[e * sz.slots : (e + 1) * sz.slots, :]
        gates[e] = mm_nt(hi, block) + mm_nt(mid, block) + mm_nt(low3, block)
    for k in range(1, n):
        to_peer(
            gates.at[lax.rem(me + k, n)], gater.at[me], ga_sem, k
        ).start()
    gater[me] = gates[me]
    logit_cols = mm_nt(low, small_low)
    col = iota((sz.rows, sz.small), 1)
    logit_cols = jnp.where((col >= 8) & (col < 8 + sz.experts), logit_cols, -1e30)
    e_cols = jnp.exp(logit_cols - jnp.max(logit_cols, 1, keepdims=True))
    probs[...] = e_cols / jnp.sum(e_cols, 1, keepdims=True)

    ctx_t[...] = ctx[...].T

    for k in range(1, n):
        src = lax.rem(me + n - k, n)
        dst = rows_at(lax.rem(me + k, n), sz.slots)
        theirs = rows_at(src, sz.slots)
        to_peer(gs.at[dst, :], gr.at[theirs, :], g_sem, k).wait()
        to_peer(gates.at[lax.rem(me + k, n)], gater.at[src], ga_sem, k).wait()
    square = iota((sz.slots, sz.slots), 0) == iota((sz.slots, sz.slots), 1)
    for j in range(n):
        block = slice(j * sz.slots, (j + 1) * sz.slots)
        row = gater[j, pl.ds(me, 1), :]
        gate = jnp.sum(jnp.where(square, row, 0.0), 1, keepdims=True)
        dres[block, :] = (gate * gr[block, :].astype(F32)).astype(BF)
    for k in range(1, n):
        src = lax.rem(me + n - k, n)
        dst = rows_at(lax.rem(me + k, n), sz.slots)
        theirs = rows_at(src, sz.slots)
        to_peer(xs.at[dst, :], xr.at[theirs, :], x_sem, k).wait()
        for cp in small_sends(k):
            cp.wait_send()
    gather_q.drain()
    gather_p.drain()


def front(sz, tokens, grad, routes, wq, wp, router, gains, biases):
    vmem = pl.BlockSpec(memory_space=pltpu.VMEM)
    rows, d, slots, n = sz.rows, sz.d, sz.all_slots, sz.n_exp
    outs = [
        ((slots, d), BF),
        ((slots, d), BF),
        ((rows, 3 * d), BF),
        ((sz.pairs, sz.images * 2, sz.seq, sz.seq), BF),
        ((d, rows), BF),
        ((rows, d), F32),
        ((rows, d), BF),
        ((d, rows), BF),
        ((rows, sz.small), F32),
        ((d, 3 * d), BF),
        ((d, d), BF),
        ((sz.small, d), F32),
        ((rows, d), BF),
        ((sz.experts, rows, sz.slots), BF),
    ]
    dma = pltpu.SemaphoreType.DMA
    sems = [dma((2, n))] * 4 + [dma((2, 2, n))] * 2 + [dma((3, 2, n))] + [dma((2, n))] * 3
    return pl.pallas_call(
        partial(front_kernel, sz),
        name="front",
        out_shape=[jax.ShapeDtypeStruct(s, t) for s, t in outs],
        in_specs=[vmem] * 8,
        out_specs=[vmem] * len(outs),
        scratch_shapes=[
            pltpu.VMEM((rows, d), BF),
            pltpu.VMEM((rows, d), BF),
            pltpu.VMEM((slots, rows), BF),
            pltpu.VMEM((slots, d), BF),
            pltpu.VMEM((n, sz.ep, sz.slots), F32),
            pltpu.VMEM((slots, d), BF),
            pltpu.VMEM((slots, d), BF),
            pltpu.VMEM((n, sz.ep, sz.slots), F32),
            pltpu.VMEM((n, *router.shape), BF),
            pltpu.VMEM((n, *gains.shape), BF),
            pltpu.VMEM((n, *biases.shape), BF),
        ]
        + sems,
        compiler_params=pltpu.CompilerParams(
            collective_id=0, has_side_effects=True, vmem_limit_bytes=56 << 20
        ),
    )(tokens, grad, routes, wq, wp, router, gains, biases)


def finish_kernel(sz, out, gin, g1, g2, dense, sg, *refs):
    o_out, o_gin, o_qkv, o_proj, o_router, o_gains, o_biases, o_w1, o_b1, o_w2, o_b2 = refs
    o_out[...] = out[...]
    o_gin[...] = gin[...]
    fs, sh = sz.fs, sz.shard
    o_w1[0] = g1[...].astype(F32)
    o_w2[0] = g2[0:fs, :].astype(F32)
    o_b1[...] = g2[fs : fs + 16, :].astype(F32)[0:1, 0:fs]
    own = o_b2.shape[1]
    first = lax.axis_index("rep") * own
    pick = iota((sz.d, own), 0) == iota((sz.d, own), 1) + first
    o_b2[...] = mm(g2[fs : fs + 16, :], pick.astype(F32).astype(BF))[1:2, :]
    o_proj[...] = dense[0].astype(F32)
    for g in range(sz.groups):
        for j in range(3):
            cols = slice(j * sz.d + g * 256, j * sz.d + (g + 1) * 256)
            o_qkv[:, cols] = dense[g + 1, :, j * 256 : (j + 1) * 256].astype(F32)
    o_router[...] = sg[8 : 8 + sz.experts, 0:sh]
    o_gains[...] = sg[0:2, 0:sh]
    o_biases[...] = sg[2:7, 0:sh]


def finish(sz, out, gin, g1, g2, dense, sg):
    vmem = pl.BlockSpec(memory_space=pltpu.VMEM)
    d, fs, sh = sz.d, sz.fs, sz.shard
    outs = [
        ((sz.tok, d), BF),
        ((sz.tok, d), BF),
        ((sh, 3 * d), F32),
        ((sh, d), F32),
        ((sz.experts, sh), F32),
        ((2, sh), F32),
        ((5, sh), F32),
        ((1, d, fs), F32),
        ((1, fs), F32),
        ((1, fs, d), F32),
        ((1, d // sz.n_rep), F32),
    ]
    grads = pl.pallas_call(
        partial(finish_kernel, sz),
        name="finish",
        out_shape=[jax.ShapeDtypeStruct(s, t) for s, t in outs],
        in_specs=[vmem] * 6,
        out_specs=[vmem] * len(outs),
        compiler_params=pltpu.CompilerParams(vmem_limit_bytes=62 << 20),
    )(out, gin, g1, g2, dense, sg)
    return (*grads[:4], grads[4].T, *grads[5:])


def normalize_back(values, gain, cot):
    center = values - jnp.mean(values, -1, keepdims=True)
    spread = jnp.mean(center * center, -1, keepdims=True)
    inv = lax.rsqrt(spread + EPS)
    unit = center * inv
    scaled = cot * gain
    grad = inv * (
        scaled
        - jnp.mean(scaled, -1, keepdims=True)
        - unit * jnp.mean(scaled * unit, -1, keepdims=True)
    )
    return grad, jnp.sum(cot * unit, 0, keepdims=True), jnp.sum(cot, 0, keepdims=True)


def gelu_parts(h):
    t = 1.0 / (1.0 + (0.3275911 / math.sqrt(2.0)) * jnp.abs(h))
    bell = jnp.exp(-0.5 * h * h)
    poly = t * (
        0.127414796
        + t * (-0.142248368 + t * (0.7107068705 + t * (-0.7265760135 + t * 0.5307027145)))
    )
    tail = poly * bell
    return jnp.where(h >= 0, 1.0 - tail, tail), bell * (1.0 / math.sqrt(2.0 * math.pi))


def block_kernel(
    sz,
    tok_ref,
    routes_ref,
    router_ref,
    gains_ref,
    biases_ref,
    b1_ref,
    b2_ref,
    grad_hbm,
    wq_shard,
    wp_shard,
    w1_hbm,
    w2_hbm,
    o_dense,
    o_small,
    o_out,
    o_gin,
    o_w1,
    o_w2,
    o_probs,
    o_save,
    dw,
    w2,
    stage,
    xr,
    dres,
    qkv,
    ctx_t,
    resid,
    second,
    normed_t,
    probs,
    smf,
    gpad,
    comb,
    gater,
    gates,
    routers,
    gains,
    biases,
    bias2,
    xt,
    act,
    dhid,
    res_acc,
    row_acc,
    res_send,
    row_send,
    ret,
    bck,
    qs,
    qr,
    t1,
    t2,
    v1,
    v2,
    u1,
    u2,
    pbuf,
    r1,
    r2,
    z1,
    z2,
    sm,
    smr,
    sme,
    sme_r,
    smz_r,
    wsem,
    psem,
    wq_sem,
    wp_sem,
    zq_sem,
    zp_sem,
    cq_sem,
    cp_sem,
    sm_sem,
    g_sem,
    x_sem,
    ga_sem,
    t_sem,
    u_sem,
    ret_sem,
    bck_sem,
    q_sem,
    d1_sem,
    d2_sem,
    z1_sem,
    z2_sem,
    z3_sem,
    s1_sem,
    s2_sem,
    s3_sem,
):
    me_r = lax.axis_index("rep")
    me = lax.axis_index("exp")
    n, nz, fs, d = sz.n_exp, sz.nz, sz.fs, sz.d
    core = lax.rem(me_r, 2)
    z = lax.div(me_r, 2)
    sibling = me_r + 1 - 2 * core
    odd = lax.rem(z, 2)
    partner = me_r + 2 - 4 * odd

    load_grad = pltpu.make_async_copy(grad_hbm, stage, wsem.at[0])
    load_grad.start()
    load_w2 = pltpu.make_async_copy(w2_hbm, w2, wsem.at[1])
    load_w2.start()

    barrier = pltpu.get_barrier_semaphore()
    for k in range(1, n):
        pl.semaphore_signal(
            barrier, inc=1, device_id=(me_r, lax.rem(me + k, n)), device_id_type=MESH
        )
    for k in range(1, nz):
        pl.semaphore_signal(
            barrier,
            inc=1,
            device_id=(lax.rem(me_r + 2 * k, 2 * nz), me),
            device_id_type=MESH,
        )
    pl.semaphore_signal(barrier, inc=1, device_id=(sibling, me), device_id_type=MESH)
    pl.semaphore_wait(barrier, n - 1 + nz)

    def remote(src, dst, send, recv, rep, exp):
        return pltpu.make_async_remote_copy(
            src_ref=src,
            dst_ref=dst,
            send_sem=send,
            recv_sem=recv,
            device_id=(rep, exp),
            device_id_type=MESH,
        )

    def to_peer(src, dst, sems, k):
        return remote(
            src, dst, sems.at[0, k], sems.at[1, k], me_r, lax.rem(me + k, n)
        )

    def to_z(src, dst, sems, k):
        return remote(
            src, dst, sems.at[0, k], sems.at[1, k], lax.rem(me_r + 2 * k, 2 * nz), me
        )

    normed = bck.at[0 : sz.rows, :]
    ctx = bck.at[sz.rows : 2 * sz.rows, :]
    xs, gs = res_send, row_send

    class Gather:
        def __init__(self, shard, base, width, own_sem, peer_sem, layer_sem, twin_sem):
            self.shard = shard
            self.base, self.width = base, width
            self.piece = width // 6
            self.own_sem = own_sem
            self.peer_sem, self.layer_sem, self.twin_sem = peer_sem, layer_sem, twin_sem

        def cols(self, side, first, count, base=0):
            start = base + side * 3 * self.piece + first * self.piece
            return pl.ds(pl.multiple_of(start, 128), count * self.piece)

        def own(self):
            return pltpu.make_async_copy(
                self.shard,
                dw.at[rows_at(me, sz.shard), self.base : self.base + self.width],
                self.own_sem,
            )

        def save(self):
            cols = slice(self.base, self.base + self.width)
            return pltpu.make_async_copy(dw.at[:, cols], o_save.at[:, cols], self.own_sem)

        def rows(self, k):
            return rows_at(lax.rem(me + n - k, n), sz.shard)

        def peer(self, k):
            return to_peer(
                self.shard.at[:, self.cols(core, odd, 2)],
                dw.at[rows_at(me, sz.shard), self.cols(core, odd, 2, self.base)],
                self.peer_sem,
                k,
            )

        def layer(self, k, mine=True):
            part = 2 * odd if mine else 2 - 2 * odd
            piece = dw.at[self.rows(k), self.cols(core, part, 1, self.base)]
            sem = self.layer_sem
            return remote(piece, piece, sem.at[0, k], sem.at[1, k], partner, me)

        def twin(self, k, late, side):
            first, count = (2 - 2 * odd, 1) if late else (odd, 2)
            piece = dw.at[self.rows(k), self.cols(side, first, count, self.base)]
            sem = self.twin_sem
            return remote(
                piece, piece, sem.at[0, late, k], sem.at[1, late, k], sibling, me
            )

        def start(self):
            for k in range(1, n):
                self.peer(k).start()
            self.own().start()

        def forward(self):
            for k in range(1, n):
                self.peer(k).wait_recv()
                self.layer(k).start()
                self.twin(k, 0, core).start()

        def finish(self):
            self.own().wait()
            for k in range(1, n):
                self.layer(k, False).wait_recv()
                self.twin(k, 1, core).start()
            for k in range(1, n):
                for late in range(2):
                    self.twin(k, late, 1 - core).wait_recv()

        def drain(self):
            for k in range(1, n):
                self.peer(k).wait_send()
                self.layer(k).wait_send()
                for late in range(2):
                    self.twin(k, late, core).wait_send()

    gather_q = Gather(wq_shard, 0, 3 * d, wsem.at[2], wq_sem, zq_sem, cq_sem)
    gather_p = Gather(wp_shard, 3 * d, d, wsem.at[3], wp_sem, zp_sem, cp_sem)

    def small_sends(k):
        return [
            to_peer(src, dst.at[me], sm_sem.at[i], k)
            for i, (src, dst) in enumerate(
                ((gains_ref, gains), (biases_ref, biases), (router_ref, routers))
            )
        ]

    for k in range(1, n):
        for cp in small_sends(k):
            cp.start()
    gather_q.start()
    gains[me] = gains_ref[...]
    biases[me] = biases_ref[...]
    routers[me] = router_ref[...]

    choice = (routes_ref[...].astype(F32) + 1.0).astype(BF)
    lines = mm_nt(choice, pad_matrix(sz)).astype(jnp.int32) - 1
    ids = iota((sz.ep, sz.rows), 0)
    oh1 = (lines[0:1, :] == ids).astype(F32)
    oh2 = (lines[1:2, :] == ids).astype(F32)
    before = (
        (iota((sz.rows, sz.rows), 0) < iota((sz.rows, sz.rows), 1))
        .astype(F32)
        .astype(BF)
    )
    pos1 = mm(oh1.astype(BF), before)
    pos2 = mm(oh2.astype(BF), before) + jnp.sum(oh1, 1, keepdims=True)
    place = oh1 * pos1 + oh2 * pos2
    kept = (oh1 + oh2 > 0.5) & (place < sz.cap - 0.5)
    slot = jnp.where(kept, place, -1.0).astype(jnp.int32)
    slot_ids = iota((sz.slots, sz.rows), 0)

    def picks(e):
        return (slot_ids == slot[e : e + 1, :]).astype(F32).astype(BF)

    eye = (iota((sz.rows, sz.rows), 0) == iota((sz.rows, sz.rows), 1)).astype(F32)
    slot_cols = mm_nt(eye.astype(BF), slot.astype(F32).astype(BF)).astype(jnp.int32)
    lane_ids = iota((sz.rows, sz.slots), 1)
    for e in range(sz.experts):
        comb[e] = (slot_cols[:, e : e + 1] == lane_ids).astype(F32).astype(BF)

    x = mm(pad_matrix(sz), tok_ref[...])
    load_grad.wait()
    gpad[...] = mm(pad_matrix(sz), stage[...]).astype(BF)
    for e in range(sz.experts):
        gs[e * sz.slots : (e + 1) * sz.slots, :] = mm(picks(e), gpad[...]).astype(BF)
    slots_me = rows_at(me, sz.slots)
    dres[slots_me, :] = gs[slots_me, :]

    for k in range(1, n):
        for cp in small_sends(k):
            cp.wait_recv()
    smf[...] = jnp.zeros_like(smf)
    for j in range(n):
        r = iota((sz.shard, d), 0)
        c = iota((sz.shard, d), 1)
        pick = (c == r + j * sz.shard).astype(F32).astype(BF)
        smf[0:2, :] += mm(gains[j], pick)
        smf[2:7, :] += mm(biases[j], pick)
        smf[8 : 8 + sz.experts, :] += mm(routers[j], pick)
    normed[...] = normalize(x, smf[0:1, :], smf[2:3, :]).astype(BF)
    normed_t[...] = normed[...].T

    gather_q.forward()
    gather_p.start()
    gather_q.finish()
    gather_q.save().start()
    for j, bias_row in ((0, 3), (1, None), (2, 4)):
        cols = slice(j * d, (j + 1) * d)
        value = mm(normed[...], dw[:, cols])
        if bias_row is not None:
            value = value + smf[bias_row : bias_row + 1, :]
        qkv[:, cols] = value.astype(BF)
    for k in range(1, n):
        dst = rows_at(lax.rem(me + k, n), sz.slots)
        to_peer(gs.at[dst, :], dres.at[slots_me, :], g_sem, k).start()

    scale = 1.0 / math.sqrt(HEAD_DIM)
    half_lane = iota((sz.seq, 128), 1)
    live = iota((sz.seq, sz.seq), 1) < SEQ

    def save_probs(pair):
        slot = lax.rem(pair, 2)
        return pltpu.make_async_copy(pbuf.at[slot], o_probs.at[pair], psem.at[slot])

    def forward_pair(pair, carry):
        @pl.when(pair >= 2)
        def _():
            save_probs(pair - 2).wait()

        for image in range(sz.images):
            rows = slice(image * sz.seq, (image + 1) * sz.seq)
            at = [pl.ds(pl.multiple_of(j * d + pair * 128, 128), 128) for j in range(3)]
            q2, k2, v2_ = (qkv[rows, at[j]] for j in range(3))
            total = jnp.zeros((sz.seq, 128), F32)
            for half in range(2):
                mask = (half_lane >= half * 64) & (half_lane < half * 64 + 64)
                zero = jnp.zeros_like(q2)
                s = mm_nt(jnp.where(mask, q2, zero), k2) * scale
                s = jnp.where(live, s, -1e30)
                e = jnp.exp(s - jnp.max(s, -1, keepdims=True))
                p = (e / jnp.sum(e, -1, keepdims=True)).astype(BF)
                pbuf[lax.rem(pair, 2), image * 2 + half] = p
                total = total + mm(p, jnp.where(mask, v2_, zero))
            ctx[rows, at[0]] = total.astype(BF)
        save_probs(pair).start()
        return carry

    lax.fori_loop(0, sz.pairs, forward_pair, 0)

    gather_p.forward()
    gather_p.finish()
    gather_p.save().start()
    res = (
        mm(pad_matrix(sz), tok_ref[...])
        + mm(ctx[...], dw[:, 3 * d : 4 * d])
        + smf[5:6, :]
    )
    resid[...] = res
    second[...] = normalize(res, smf[1:2, :], smf[6:7, :]).astype(BF)
    ctx_t[...] = ctx[...].T
    for k in [*range(1, n), 0]:
        rows = rows_at(lax.rem(me + k, n), sz.slots)
        line = slot[0:1, :]
        for e in range(1, sz.experts):
            line = jnp.where(lax.rem(me + k, n) == e, slot[e : e + 1, :], line)
        pick = (slot_ids == line).astype(F32).astype(BF)
        xs[rows, :] = mm(pick, second[...]).astype(BF)
        if k:
            to_peer(xs.at[rows, :], xr.at[slots_me, :], x_sem, k).start()
        else:
            xr[slots_me, :] = xs[slots_me, :]
    for gather in (gather_q, gather_p):
        gather.drain()
        gather.save().wait()
    load_w1 = pltpu.make_async_copy(w1_hbm, dw, wsem.at[0])
    load_w1.start()

    small_low = smf[...].astype(BF)
    low = second[...]
    logit_rows = mm_nt(small_low, low)[8 : 8 + sz.ep, :]
    logit_rows = jnp.where(iota((sz.ep, sz.rows), 0) < sz.experts, logit_rows, -1e30)
    e_rows = jnp.exp(logit_rows - jnp.max(logit_rows, 0, keepdims=True))
    prob_rows = e_rows / jnp.sum(e_rows, 0, keepdims=True)
    hi = prob_rows.astype(BF)
    left = prob_rows - hi.astype(F32)
    mid = left.astype(BF)
    rest_low = (left - mid.astype(F32)).astype(BF)
    for e in range(sz.experts):
        block = picks(e)
        gates[e] = mm_nt(hi, block) + mm_nt(mid, block) + mm_nt(rest_low, block)
    for k in range(1, n):
        to_peer(gates.at[lax.rem(me + k, n)], gater.at[me], ga_sem, k).start()
    gater[me] = gates[me]
    logit_cols = mm_nt(low, small_low)
    col = iota((sz.rows, sz.small), 1)
    logit_cols = jnp.where((col >= 8) & (col < 8 + sz.experts), logit_cols, -1e30)
    e_cols = jnp.exp(logit_cols - jnp.max(logit_cols, 1, keepdims=True))
    probs[...] = e_cols / jnp.sum(e_cols, 1, keepdims=True)
    for pair in range(max(sz.pairs - 2, 0), sz.pairs):
        save_probs(pair).wait()

    lower = 1 - lax.div(z, (nz + 1) // 2)
    xta = res_send.at[0:d, :]
    bias2[...] = jnp.zeros_like(bias2)
    load_w2.wait()
    load_w1.wait()

    def w1_part(f):
        return dw[:, pl.ds(pl.multiple_of(f * fs, 128), fs)]

    square = iota((sz.slots, sz.slots), 0) == iota((sz.slots, sz.slots), 1)

    def peer_slots(k):
        return rows_at(lax.rem(me + k, n), sz.slots)

    def send_back(k):
        rows = peer_slots(k)
        row_send[rows, :] = row_acc[rows, :].astype(BF)
        out = (res_acc[rows, :] + b2_ref[...].astype(F32)).astype(BF).astype(F32)
        column = jnp.sum(out * dres[rows, :].astype(F32), 1, keepdims=True)
        line = jnp.sum(jnp.where(square, column, 0.0), 0, keepdims=True)
        qs[k] = jnp.broadcast_to(line, (8, sz.slots))
        if k == 0:
            bck[slots_me, :] = row_send[rows, :]
            qr[me] = qs[k]
        else:
            to_peer(row_send.at[rows, :], bck.at[slots_me, :], bck_sem, k).start()
            to_peer(qs.at[k], qr.at[me], q_sem, k).start()

    def prepare(k):
        src = lax.rem(me + k, n)
        rows = rows_at(src, sz.slots)
        if k:
            at = n - k
            to_peer(gs.at[peer_slots(at), :], dres.at[rows, :], g_sem, at).wait()
            to_peer(gates.at[lax.rem(me + at, n)], gater.at[src], ga_sem, at).wait()
        row = gater[src, pl.ds(me, 1), :]
        gate = jnp.sum(jnp.where(square, row, 0.0), 1, keepdims=True)
        value = (gate * dres[rows, :].astype(F32)).astype(BF)
        dres[rows, :] = value
        bias2[...] += jnp.sum(value.astype(F32), 0, keepdims=True)
        if k:
            to_peer(xs.at[peer_slots(at), :], xr.at[rows, :], x_sem, at).wait()

    def compute(f, order, flag, ahead=None, behind=None):
        w2f_rows = pl.ds(pl.multiple_of(f * fs, 16), fs)
        bias = b1_ref[:, pl.ds(pl.multiple_of(f * fs, 128), fs)].astype(F32)
        for k in order:
            rows = peer_slots(k)
            if ahead is not None:
                pl.when(flag)(partial(ahead, k))
            h = mm(xr[rows, :], w1_part(f)) + bias
            cdf, pdf = gelu_parts(h)
            da = mm_nt(dres[rows, :], w2[w2f_rows, :])
            a = (h * cdf).astype(BF)
            dh = (da * (cdf + h * pdf)).astype(BF)
            act[rows, :] = a
            dhid[rows, :] = dh
            res_acc[rows, :] += mm(a, w2[w2f_rows, :])
            row_acc[rows, :] += mm_nt(dh, w1_part(f))
            if behind is not None:
                pl.when(flag)(partial(behind, k))

    def grad1(rows):
        part = mm(xta[rows, :], dhid[0:d, :])
        return part + mm(xt[rows, :], dhid[d:, :])

    def grad2(cols):
        return mm_tn(act[:, cols], dres[...])

    def extra():
        gb = jnp.sum(dhid[...].astype(F32), 0, keepdims=True)
        row = iota((16, d), 0)
        line = jnp.concatenate([gb, jnp.zeros((1, d - fs), F32)], 1)
        return jnp.where(row == 0, line, jnp.where(row == 1, bias2[...], 0.0))

    def t_copies(dest):
        return (
            remote(t1, v1.at[dest], t_sem.at[0, 0, dest], t_sem.at[1, 0, dest], sibling, me),
            remote(t2, v2.at[dest], t_sem.at[0, 1, dest], t_sem.at[1, 1, dest], sibling, me),
        )

    def landing(way, step, at):
        if way == 0:
            return nz - 2 - step + at
        return at + step + 2 - nz if step < nz - 2 else nz

    def u_copies(src1, src2, way, step, target, slot):
        return (
            remote(src1, u1.at[slot], u_sem.at[0, 0, way, step], u_sem.at[1, 0, way, step], target, me),
            remote(src2, u2.at[slot], u_sem.at[0, 1, way, step], u_sem.at[1, 1, way, step], target, me),
        )

    res_acc[...] = jnp.zeros_like(res_acc)
    row_acc[...] = jnp.zeros_like(row_acc)

    parts1 = [slice(i, i + d // 2) for i in (0, d // 2)]
    parts2 = [slice(i, i + 128) for i in range(0, fs, 128)]

    def dest_of(i):
        return lower * (nz - 1 - i) + (1 - lower) * i

    def slice_step(i, carry):
        dest = dest_of(i)

        compute(dest * 2 + 1 - core, range(n), i == 0, prepare)

        @pl.when(i == 0)
        def _():
            xta[...] = xr[0:d, :].T
            xt[...] = xr[d:, :].T

        for rows in parts1:
            t1[rows, :] = grad1(rows).astype(BF)
        for rows in parts2:
            t2[rows, :] = grad2(rows).astype(BF)
        t2[fs:, :] = extra().astype(BF)
        for cp in t_copies(dest):
            cp.start()
        compute(dest * 2 + core, [*range(1, n), 0], i == nz - 1, None, send_back)
        for cp in t_copies(dest):
            cp.wait()
        for rows in parts1:
            v1[dest, rows, :] = (v1[dest, rows, :].astype(F32) + grad1(rows)).astype(BF)
        for rows in parts2:
            v2[dest, rows, :] = (v2[dest, rows, :].astype(F32) + grad2(rows)).astype(BF)
        v2[dest, fs:, :] = (v2[dest, fs:, :].astype(F32) + extra()).astype(BF)

        @pl.when((z == 0) & (i <= nz - 2))
        def _():
            for cp in u_copies(v1.at[dest], v2.at[dest], 0, i, me_r + 2, dest):
                cp.start()

        @pl.when((z == nz - 1) & (i < nz - 2))
        def _():
            for cp in u_copies(v1.at[dest], v2.at[dest], 1, i, me_r - 2, dest):
                cp.start()

        @pl.when((z == nz - 1) & (i == nz - 2))
        def _():
            for cp in u_copies(v1.at[dest], v2.at[dest], 1, i, me_r - 2, nz):
                cp.start()

        return carry

    lax.fori_loop(0, nz, slice_step, 0)

    res_send[...] = (res_acc[...] + b2_ref[...].astype(F32)).astype(BF)
    for k in range(1, n):
        to_peer(res_send.at[peer_slots(k), :], ret.at[slots_me, :], ret_sem, k).start()
    ret[slots_me, :] = res_send[slots_me, :]
    dense_load = pltpu.make_async_copy(o_save, dw, wsem.at[0])
    dense_load.start()

    def z_round(s):
        for way in range(2):
            zz = z if way == 0 else nz - 1 - z
            dest = nz - 1 - s + zz if way == 0 else z - (nz - 1 - s)
            target = me_r + 2 if way == 0 else me_r - 2

            @pl.when((zz >= 1) & (zz <= s))
            def _():
                here = landing(way, s - 1, z)
                there = landing(way, s, z + 1 if way == 0 else z - 1)
                a1, a2 = u1.at[here], u2.at[here]
                for cp in u_copies(a1, a2, way, s - 1, target, here):
                    cp.wait_recv()
                u1[here] = (u1[here].astype(F32) + v1[dest].astype(F32)).astype(BF)
                u2[here] = (u2[here].astype(F32) + v2[dest].astype(F32)).astype(BF)
                for cp in u_copies(a1, a2, way, s, target, there):
                    cp.start()

    if nz > 2:
        z_round(1)

    for k in range(1, n):
        src = lax.rem(me + n - k, n)
        theirs = rows_at(src, sz.slots)
        to_peer(row_send.at[peer_slots(k), :], bck.at[theirs, :], bck_sem, k).wait()
        to_peer(qs.at[k], qr.at[src], q_sem, k).wait()
    mixed = res_acc.at[0 : sz.rows, :]
    sgrad = res_acc.at[sz.rows : 2 * sz.rows, :]
    lane = iota((sz.rows, sz.small), 1)
    weighted = jnp.zeros((sz.rows, sz.small), F32)
    for e in range(sz.experts):
        q = jnp.sum(comb[e].astype(F32) * qr[e, 0:1, :], 1, keepdims=True)
        weighted = jnp.where(lane == 8 + e, q, weighted)
    total = jnp.sum(weighted, 1, keepdims=True)
    logit_low = (weighted - probs[...] * total).astype(BF)
    sgrad[...] = mm(logit_low, smf[...].astype(BF))
    for e in range(sz.experts):
        sgrad[...] += mm(comb[e], bck[e * sz.slots : (e + 1) * sz.slots, :])
    back2, gain2, shift2 = normalize_back(resid[...], smf[1:2, :], sgrad[...])
    rgrad = row_acc.at[0 : sz.rows, :]
    rgrad[...] = gpad[...].astype(F32) + back2
    low = rgrad[...].astype(BF)
    bias_out = jnp.sum(low.astype(F32), 0, keepdims=True)

    dense = w2
    wide = d // 2
    keep = pl.ds(pl.multiple_of(core * wide, 128), wide)
    give = pl.ds(pl.multiple_of((1 - core) * wide, 128), wide)
    part = sz.part

    def chunk_rows(j, start, size):
        return pl.ds(pl.multiple_of(j * d + start, 16), size)

    def part_rows(zi):
        return pl.ds(pl.multiple_of(zi * part, 16), part)

    def to_sibling(j):
        return remote(
            dense.at[chunk_rows(j, 0, d), give],
            r1.at[j],
            d1_sem.at[0, j],
            d1_sem.at[1, j],
            sibling,
            me,
        )

    def to_owner(j, k):
        e = lax.rem(me + k, n)
        return remote(
            dense.at[chunk_rows(j, e * sz.shard, sz.shard), keep],
            r2.at[k - 1, j],
            d2_sem.at[0, j, k],
            d2_sem.at[1, j, k],
            me_r,
            e,
        )

    def to_layer(j, k):
        return remote(
            z1.at[j, part_rows(lax.rem(z + k, nz)), :],
            z2.at[k - 1, j],
            z1_sem.at[0, j, k],
            z1_sem.at[1, j, k],
            lax.rem(me_r + 2 * k, 2 * nz),
            me,
        )

    def from_layer(j, k, owner):
        piece = o_dense.at[j, part_rows(owner), keep]
        return remote(
            piece,
            piece,
            z2_sem.at[0, j, k],
            z2_sem.at[1, j, k],
            lax.rem(me_r + 2 * k, 2 * nz),
            me,
        )

    def to_twin(j, cols):
        piece = o_dense.at[j, :, cols]
        return remote(piece, piece, z3_sem.at[0, j], z3_sem.at[1, j], sibling, me)

    def stage1(j):
        to_sibling(j).wait()
        rows = chunk_rows(j, 0, d)
        dense[rows, keep] = (dense[rows, keep].astype(F32) + r1[j].astype(F32)).astype(BF)
        for k in range(1, n):
            to_owner(j, k).start()

    def stage2(j):
        acc = dense[chunk_rows(j, me * sz.shard, sz.shard), keep].astype(F32)
        for k in range(1, n):
            to_owner(j, k).wait()
            acc = acc + r2[k - 1, j].astype(F32)
        z1[j] = acc.astype(BF)
        for k in range(1, nz):
            to_layer(j, k).start()

    def stage3(j):
        acc = z1[j, part_rows(z), :].astype(F32)
        for k in range(1, nz):
            to_layer(j, k).wait()
            acc = acc + z2[k - 1, j].astype(F32)
        o_dense[j, part_rows(z), keep] = acc.astype(BF)
        for k in range(1, nz):
            from_layer(j, k, z).start()

    def stage4(j):
        for k in range(1, nz):
            from_layer(j, k, z).wait_send()
            from_layer(j, k, lax.rem(z + nz - k, nz)).wait_recv()
        to_twin(j, keep).start()

    def stage5(j):
        to_twin(j, keep).wait_send()
        to_twin(j, give).wait_recv()

    dense[chunk_rows(0, 0, d), :] = mm(ctx_t[...], low).astype(BF)
    to_sibling(0).start()
    dense_load.wait()
    for k in range(1, n):
        theirs = rows_at(lax.rem(me + n - k, n), sz.slots)
        to_peer(res_send.at[peer_slots(k), :], ret.at[theirs, :], ret_sem, k).wait()
    dq_ref = res_send.at[0 : sz.rows, :]
    dk_ref = res_send.at[sz.rows : 2 * sz.rows, :]
    dv_ref = row_send.at[0 : sz.rows, :]
    cgrad = row_send.at[sz.rows : 2 * sz.rows, :]
    dqkv = (dq_ref, dk_ref, dv_ref)

    def load_probs(pair):
        slot = lax.rem(pair, 2)
        return pltpu.make_async_copy(o_probs.at[pair], pbuf.at[slot], psem.at[slot])

    load_probs(0).start()
    cgrad[...] = mm_nt(low, dw[:, 3 * d : 4 * d]).astype(BF)
    sm[...] = mm_tn(logit_low, second[...])

    for s in range(2, nz - 1):
        z_round(s)

    scale = 1.0 / math.sqrt(HEAD_DIM)
    half_lane = iota((sz.seq, 128), 1)

    def pair_step(pair, carry):
        load_probs(pair).wait()

        @pl.when(pair + 1 < sz.pairs)
        def _():
            load_probs(pair + 1).start()

        for image in range(sz.images):
            rows = slice(image * sz.seq, (image + 1) * sz.seq)
            at = [pl.ds(pl.multiple_of(j * d + pair * 128, 128), 128) for j in range(3)]
            q2, k2, v2_ = (qkv[rows, at[j]] for j in range(3))
            c2 = cgrad[rows, at[0]]
            dq = jnp.zeros((sz.seq, 128), F32)
            dk = jnp.zeros((sz.seq, 128), F32)
            dv = jnp.zeros((sz.seq, 128), F32)
            for half in range(2):
                mask = (half_lane >= half * 64) & (half_lane < half * 64 + 64)
                zero = jnp.zeros_like(q2)
                ch = jnp.where(mask, c2, zero)
                p = pbuf[lax.rem(pair, 2), image * 2 + half]
                dv = dv + mm_tn(p, ch)
                pb = mm_nt(ch, v2_)
                p32 = p.astype(F32)
                mix = jnp.sum(pb * p32, -1, keepdims=True)
                ds = (p32 * (pb - mix)).astype(BF)
                dq = dq + mm(ds, jnp.where(mask, k2, zero))
                dk = dk + mm_tn(ds, jnp.where(mask, q2, zero))
            dq_ref[rows, at[0]] = (dq * scale).astype(BF)
            dk_ref[rows, at[0]] = (dk * scale).astype(BF)
            dv_ref[rows, at[0]] = dv.astype(BF)
        return carry

    def group_step(g, carry):
        lax.fori_loop(2 * g, 2 * g + 2, pair_step, 0)
        cols = pl.ds(pl.multiple_of(g * 256, 128), 256)
        for j in range(3):
            dense[chunk_rows(g + 1, 0, d), j * 256 : (j + 1) * 256] = mm(
                normed_t[...], dqkv[j][:, cols]
            ).astype(BF)
        to_sibling(g + 1).start()
        stage1(g)
        return carry

    lax.fori_loop(0, sz.groups, group_step, 0)
    stage1(sz.groups)

    ngrad = sgrad
    ngrad[...] = mm_nt(dq_ref[...], dw[:, 0:d])
    for j in range(1, 3):
        ngrad[...] += mm_nt(dqkv[j][...], dw[:, j * d : (j + 1) * d])
    stage2(0)
    x = mm(pad_matrix(sz), tok_ref[...])
    back1, gain1, shift1 = normalize_back(x, smf[0:1, :], ngrad[...])
    stage[...] = mm(unpad_matrix(sz), (rgrad[...] + back1).astype(BF)).astype(BF)
    store = pltpu.make_async_copy(stage, o_gin, wsem.at[2])
    store.start()
    bias_q = jnp.sum(dq_ref[...].astype(F32), 0, keepdims=True)
    bias_v = jnp.sum(dv_ref[...].astype(F32), 0, keepdims=True)
    row = iota((sz.small, d), 0)
    small = sm[...]
    for i, value in enumerate((gain1, gain2, shift1, bias_q, bias_v, bias_out, shift2)):
        small = jnp.where(row == i, value, small)
    sm[...] = small
    smb = sme.at[n]
    smb[...] = small.astype(BF)
    s_first = remote(smb, smr, s1_sem.at[0], s1_sem.at[1], sibling, me)
    s_first.start()

    stage2(1)
    stage3(0)
    mixed[...] = resid[...]
    for e in range(sz.experts):
        block = slice(e * sz.slots, (e + 1) * sz.slots)
        mixed[...] += probs[:, 8 + e : 9 + e] * mm(comb[e], ret[block, :])
    store.wait()
    stage[...] = mm(unpad_matrix(sz), mixed[...].astype(BF)).astype(BF)
    store = pltpu.make_async_copy(stage, o_out, wsem.at[2])
    store.start()

    s_first.wait()
    chip_small = (sm[...] + smr[...].astype(F32)).astype(BF)
    for e in range(n):
        r = iota((sz.shard_pad, d), 0)
        c = iota((sz.shard_pad, d), 1)
        pick = ((c == r + e * sz.shard) & (r < sz.shard)).astype(F32).astype(BF)
        sme[e, :, 0 : sz.shard_pad] = mm_nt(chip_small, pick).astype(BF)

    def small_peer(k):
        piece = sme.at[lax.rem(me + k, n), :, 0 : sz.shard_pad]
        return to_peer(piece, sme_r.at[k], s2_sem, k)

    for k in range(1, n):
        small_peer(k).start()
    stage2(2)
    stage3(1)
    stage4(0)
    acc = sme[me, :, 0 : sz.shard_pad].astype(F32)
    for k in range(1, n):
        small_peer(k).wait()
        acc = acc + sme_r[k].astype(F32)
    smz_r[0] = acc.astype(BF)
    for k in range(1, nz):
        to_z(smz_r.at[0], smz_r.at[k], s3_sem, k).start()
    stage2(3)
    stage3(2)
    stage4(1)

    for way in range(2):
        zz = z if way == 0 else nz - 1 - z
        target = me_r + 2 if way == 0 else me_r - 2

        @pl.when(zz >= 1)
        def _():
            here = landing(way, nz - 2, z)
            for cp in u_copies(u1.at[here], u2.at[here], way, nz - 2, target, here):
                cp.wait_recv()
            v1[z] = (v1[z].astype(F32) + u1[here].astype(F32)).astype(BF)
            v2[z] = (v2[z].astype(F32) + u2[here].astype(F32)).astype(BF)

    stores = [
        pltpu.make_async_copy(v1.at[z], o_w1, wsem.at[0]),
        pltpu.make_async_copy(v2.at[z], o_w2, wsem.at[1]),
    ]
    for cp in stores:
        cp.start()
    stage3(3)
    stage4(2)
    acc = smz_r[0].astype(F32)
    for k in range(1, nz):
        to_z(smz_r.at[0], smz_r.at[k], s3_sem, k).wait()
        acc = acc + smz_r[k].astype(F32)
    o_small[...] = acc
    stage4(3)
    for j in range(sz.chunks):
        stage5(j)

    for cp in stores:
        cp.wait()
    store.wait()
    for s in range(nz - 1):
        for way in range(2):
            zz = z if way == 0 else nz - 1 - z
            target = me_r + 2 if way == 0 else me_r - 2

            @pl.when(zz <= s)
            def _():
                for cp in u_copies(v1.at[0], v2.at[0], way, s, target, 0):
                    cp.wait_send()
    for k in range(1, n):
        for cp in small_sends(k):
            cp.wait_send()


def block(sz, tokens, routes, router, gains, biases, b1, b2, grad, wq, wp, w1, w2):
    vmem = pl.BlockSpec(memory_space=pltpu.VMEM)
    hbm = pl.BlockSpec(memory_space=pl.ANY)
    rows, d, slots, fs, nz, n = sz.rows, sz.d, sz.all_slots, sz.fs, sz.nz, sz.n_exp
    half = d // 2
    dma = pltpu.SemaphoreType.DMA
    outs = [
        ((sz.chunks, sz.shard, d), BF),
        ((sz.small, sz.shard_pad), F32),
        ((sz.tok, d), BF),
        ((sz.tok, d), BF),
        ((d, fs), BF),
        ((sz.fs_rows, d), BF),
        ((sz.pairs, sz.images * 2, sz.seq, sz.seq), BF),
        ((d, 4 * d), BF),
    ]
    buffers = [
        ((d, 4 * d), BF),
        (w2.shape, BF),
        ((sz.tok, d), BF),
        ((slots, d), BF),
        ((slots, d), BF),
        ((rows, 3 * d), BF),
        ((d, rows), BF),
        ((rows, d), F32),
        ((rows, d), BF),
        ((d, rows), BF),
        ((rows, sz.small), F32),
        ((sz.small, d), F32),
        ((rows, d), BF),
        ((sz.experts, rows, sz.slots), BF),
        ((n, sz.ep, sz.slots), F32),
        ((n, sz.ep, sz.slots), F32),
        ((n, *router.shape), BF),
        ((n, *gains.shape), BF),
        ((n, *biases.shape), BF),
        ((1, d), F32),
        ((d, slots - d), BF),
        ((slots, fs), BF),
        ((slots, fs), BF),
        ((slots, d), F32),
        ((slots, d), F32),
        ((slots, d), BF),
        ((slots, d), BF),
        ((slots, d), BF),
        ((slots, d), BF),
        ((n, 8, sz.slots), F32),
        ((n, 8, sz.slots), F32),
        ((d, fs), BF),
        ((sz.fs_rows, d), BF),
        ((nz, d, fs), BF),
        ((nz, sz.fs_rows, d), BF),
        ((nz + 1, d, fs), BF),
        ((nz + 1, sz.fs_rows, d), BF),
        ((2, 2 * sz.images, sz.seq, sz.seq), BF),
        ((sz.chunks, d, half), BF),
        ((n - 1, sz.chunks, sz.shard, half), BF),
        ((sz.chunks, sz.shard, half), BF),
        ((nz - 1, sz.chunks, sz.part, half), BF),
        ((sz.small, d), F32),
        ((sz.small, d), BF),
        ((n + 1, sz.small, d), BF),
        ((n, sz.small, sz.shard_pad), BF),
        ((nz, sz.small, sz.shard_pad), BF),
    ]
    sems = (
        [dma((4,)), dma((2,))]
        + [dma((2, n))] * 4
        + [dma((2, 2, n))] * 2
        + [dma((3, 2, n))]
        + [dma((2, n))] * 3
        + [dma((2, 2, nz)), dma((2, 2, 2, nz - 1))]
        + [dma((2, n))] * 3
        + [dma((2, sz.chunks)), dma((2, sz.chunks, n))]
        + [dma((2, sz.chunks, nz))] * 2
        + [dma((2, sz.chunks)), dma((2,)), dma((2, n)), dma((2, nz))]
    )
    return pl.pallas_call(
        partial(block_kernel, sz),
        name="block",
        out_shape=[jax.ShapeDtypeStruct(s, t) for s, t in outs],
        in_specs=[vmem] * 7 + [hbm] * 5,
        out_specs=[vmem] * 2 + [hbm] * 6,
        scratch_shapes=[pltpu.VMEM(s, t) for s, t in buffers] + sems,
        compiler_params=pltpu.CompilerParams(
            collective_id=1, has_side_effects=True, vmem_limit_bytes=62 << 20
        ),
    )(tokens, routes, router, gains, biases, b1, b2, grad, wq, wp, w1, w2)


def plain_rest(sz, state, tokens, w1, b1, w2, b2):
    xr, dres, qkv, pall, ctx_t, resid, second, normed_t, probs, wq, wp, smf, gpad, comb = state
    d, n = sz.d, sz.experts
    scale = 1.0 / math.sqrt(HEAD_DIM)
    h = mm(xr, w1) + b1
    cdf, pdf = gelu_parts(h)
    act = (h * cdf).astype(BF)
    result = (mm(act, w2) + b2).astype(BF)
    dhid = (mm_nt(dres, w2) * (cdf + h * pdf)).astype(BF)
    row_grad = mm_nt(dhid, w1).astype(BF)
    swap = partial(
        lax.all_to_all, axis_name="exp", split_axis=0, concat_axis=0, tiled=True
    )
    ret = swap(result).reshape(n, sz.slots, d)
    bck = swap(row_grad).reshape(n, sz.slots, d)
    g32 = gpad.astype(F32)
    p = probs[:, 8 : 8 + n]
    picked = jnp.einsum("ets,esd->etd", comb, ret, preferred_element_type=F32)
    mixed = resid + jnp.einsum("te,etd->td", p, picked, precision="highest")
    pg = jnp.sum(g32[None] * picked, -1).T
    lg = (p * (pg - jnp.sum(pg * p, 1, keepdims=True))).astype(BF)
    sgrad = mm(lg, smf[8 : 8 + n].astype(BF))
    sgrad = sgrad + jnp.einsum("ets,esd->td", comb, bck, preferred_element_type=F32)
    back2, gain2, shift2 = normalize_back(resid, smf[1:2], sgrad)
    rgrad = g32 + back2
    low = rgrad.astype(BF)
    cgrad = mm_nt(low, wp).astype(BF)
    four = (sz.images, sz.seq, d // HEAD_DIM, HEAD_DIM)
    q, k, v, c = (
        a.reshape(four)
        for a in (qkv[:, :d], qkv[:, d : 2 * d], qkv[:, 2 * d :], cgrad)
    )
    prob = pall.reshape(sz.pairs, sz.images, 2, sz.seq, sz.seq)
    prob = prob.transpose(1, 0, 2, 3, 4).reshape(sz.images, -1, sz.seq, sz.seq)
    product = partial(jnp.einsum, preferred_element_type=F32)
    dv = product("ihst,ishd->ithd", prob, c).astype(BF)
    pb = product("ishd,ithd->ihst", c, v)
    p32 = prob.astype(F32)
    ds = (p32 * (pb - jnp.sum(pb * p32, -1, keepdims=True))).astype(BF)
    dq = (product("ihst,ithd->ishd", ds, k) * scale).astype(BF)
    dk = (product("ihst,ishd->ithd", ds, q) * scale).astype(BF)
    dqkv = jnp.concatenate([a.reshape(sz.rows, d) for a in (dq, dk, dv)], 1)
    x = mm(pad_matrix(sz), tokens)
    back1, gain1, shift1 = normalize_back(x, smf[0:1], mm_nt(dqkv, wq))
    gin = (rgrad + back1).astype(BF)
    sums = jnp.sum(dqkv.astype(F32), 0, keepdims=True)
    small = jnp.concatenate(
        [gain1, gain2, shift1, sums[:, :d], sums[:, 2 * d :]]
        + [jnp.sum(low.astype(F32), 0, keepdims=True), shift2, mm_tn(lg, second)]
    )

    def dense(grad, dim):
        total = lax.psum(grad.astype(BF), "rep")
        total = lax.psum_scatter(total, "exp", scatter_dimension=dim, tiled=True)
        return total.astype(F32)

    def owned(grad, dim):
        total = lax.psum_scatter(
            grad[None].astype(BF), "rep", scatter_dimension=dim, tiled=True
        )
        return total.astype(F32)

    def unpad(rows):
        return rows.reshape(sz.images, sz.seq, d)[:, :SEQ].reshape(sz.tok, d)

    sums = dense(small, 1)
    return (
        unpad(mixed.astype(BF)),
        unpad(gin),
        dense(mm(normed_t, dqkv), 0),
        dense(mm(ctx_t, low), 0),
        sums[7:].T,
        sums[0:2],
        sums[2:7],
        owned(mm_tn(xr, dhid), 2),
        owned(jnp.sum(dhid.astype(F32), 0), 1),
        owned(mm_tn(act, dres), 1),
        owned(jnp.sum(dres.astype(F32), 0), 1),
    )


def on_device(
    mesh,
    tokens,
    routes,
    out_grad,
    attn_qkv,
    attn_out,
    router,
    norm_gains,
    dense_biases,
    expert_in,
    expert_in_bias,
    expert_out,
    expert_out_bias,
):
    sz = Sizes(mesh, tokens.shape[0], tokens.shape[1], expert_in.shape[2])
    d, fs = sz.d, sz.fs
    w1, w2 = expert_in[0], expert_out[0]
    small = (router.T, norm_gains, dense_biases)
    if fs % 128 or sz.all_slots % 128 or sz.all_slots < 2 * sz.rows or sz.part % 16:
        state = front(sz, tokens, out_grad, routes.T, attn_qkv, attn_out, *small)
        bias1, bias2 = expert_in_bias.astype(F32), expert_out_bias.astype(F32)
        return plain_rest(sz, state, tokens, w1, bias1, w2, bias2)
    dense, sums, out, gin, g1, g2, _, _ = block(
        sz,
        tokens,
        routes.T,
        *small,
        expert_in_bias,
        expert_out_bias,
        out_grad,
        attn_qkv,
        attn_out,
        w1,
        w2,
    )
    return finish(sz, out, gin, g1, g2, dense, sums)


def solution(mesh):
    both = P(("rep", "exp"), None)
    rows = P("exp", None)
    cols = P(None, "exp")
    cube = P("exp", None, None)
    in_specs = (both, both, both, rows, rows, rows, cols, cols, cube, rows, cube, rows)
    out_specs = (
        both,
        both,
        rows,
        rows,
        rows,
        cols,
        cols,
        P("exp", None, "rep"),
        P("exp", "rep"),
        P("exp", "rep", None),
        P("exp", "rep"),
    )
    return jax.shard_map(
        partial(on_device, mesh),
        mesh=mesh,
        in_specs=in_specs,
        out_specs=out_specs,
        check_vma=False,
    )
```

```python
from functools import partial
import math

import jax
import jax.numpy as jnp
from jax import lax
from jax.experimental import pallas as pl
from jax.experimental.pallas import tpu as pltpu
from jax.sharding import PartitionSpec as P

HEAD_DIM = 64
SEQ = 197
EPS = 1e-06
BF = jnp.bfloat16
F32 = jnp.float32
MESH = pl.DeviceIdType.MESH


def up(value, step):
    return (value + step - 1) // step * step


def mm(a, b):
    return lax.dot_general(a, b, (((1,), (0,)), ((), ())), preferred_element_type=F32)


def mm_nt(a, b):
    return lax.dot_general(a, b, (((1,), (1,)), ((), ())), preferred_element_type=F32)


def mm_tn(a, b):
    return lax.dot_general(a, b, (((0,), (0,)), ((), ())), preferred_element_type=F32)


def iota(shape, dim):
    return lax.broadcasted_iota(jnp.int32, shape, dim)


def rows_at(index, size):
    return pl.ds(pl.multiple_of(index * size, size), size)


def normalize(values, gain, shift):
    center = values - jnp.mean(values, -1, keepdims=True)
    spread = jnp.mean(center * center, -1, keepdims=True)
    return center * lax.rsqrt(spread + EPS) * gain + shift


class Sizes:
    def __init__(self, mesh, tok_rows, width, ff):
        self.n_exp = mesh.shape["exp"]
        self.n_rep = mesh.shape["rep"]
        self.tok = tok_rows
        self.images = tok_rows // SEQ
        self.seq = up(SEQ, 16)
        self.rows = self.images * self.seq
        self.d = width
        self.ff = ff
        self.experts = self.n_exp
        self.cap = (18 * tok_rows + 8 * self.experts - 1) // (8 * self.experts)
        self.slots = up(self.cap, 16)
        self.all_slots = self.slots * self.experts
        self.shard = width // self.n_exp
        self.shard_pad = up(self.shard, 128)
        self.ep = up(self.experts, 8)
        self.small = up(8 + self.ep, 16)
        self.pairs = width // 128
        self.nz = self.n_rep // 2
        self.fs = ff // self.n_rep
        self.fs_rows = self.fs + 16
        self.part = self.shard // self.nz
        self.groups = self.pairs // 2
        self.chunks = self.groups + 1


def pad_matrix(sz):
    row = iota((sz.rows, sz.tok), 0)
    col = iota((sz.rows, sz.tok), 1)
    want = jnp.full((sz.rows, sz.tok), -1, jnp.int32)
    for image in range(sz.images):
        inside = (row >= image * sz.seq) & (row < image * sz.seq + SEQ)
        want = jnp.where(inside, row - image * (sz.seq - SEQ), want)
    return (want == col).astype(F32).astype(BF)


def unpad_matrix(sz):
    row = iota((sz.tok, sz.rows), 0)
    col = iota((sz.tok, sz.rows), 1)
    want = row
    for image in range(1, sz.images):
        want = jnp.where(row >= image * SEQ, row + image * (sz.seq - SEQ), want)
    return (want == col).astype(F32).astype(BF)


def front_kernel(
    sz,
    tok_ref,
    grad_ref,
    routes_ref,
    wq_shard,
    wp_shard,
    router_ref,
    gains_ref,
    biases_ref,
    xr,
    dres,
    qkv,
    pall,
    ctx_t,
    resid,
    second,
    normed_t,
    probs,
    wq,
    wp,
    smf,
    gpad,
    comb,
    ctx,
    normed,
    pmat,
    gr,
    gater,
    xs,
    gs,
    gates,
    routers,
    gains,
    biases,
    wq_sem,
    wp_sem,
    zq_sem,
    zp_sem,
    cq_sem,
    cp_sem,
    sm_sem,
    g_sem,
    x_sem,
    ga_sem,
):
    me_r = lax.axis_index("rep")
    me = lax.axis_index("exp")
    n = sz.n_exp
    core = lax.rem(me_r, 2)
    sibling = me_r + 1 - 2 * core
    odd = lax.rem(lax.div(me_r, 2), 2)
    partner = me_r + 2 - 4 * odd

    barrier = pltpu.get_barrier_semaphore()
    for k in range(1, n):
        pl.semaphore_signal(
            barrier, inc=1, device_id=(me_r, lax.rem(me + k, n)), device_id_type=MESH
        )
    for rep in (sibling, partner):
        pl.semaphore_signal(barrier, inc=1, device_id=(rep, me), device_id_type=MESH)
    pl.semaphore_wait(barrier, n + 1)

    def remote(src, dst, send, recv, rep, exp):
        return pltpu.make_async_remote_copy(
            src_ref=src,
            dst_ref=dst,
            send_sem=send,
            recv_sem=recv,
            device_id=(rep, exp),
            device_id_type=MESH,
        )

    def to_peer(src, dst, sems, k):
        return remote(
            src, dst, sems.at[0, k], sems.at[1, k], me_r, lax.rem(me + k, n)
        )

    class Gather:
        def __init__(self, shard, full, width, peer_sem, layer_sem, twin_sem):
            self.shard, self.full = shard, full
            self.piece = width // 6
            self.peer_sem, self.layer_sem, self.twin_sem = peer_sem, layer_sem, twin_sem

        def cols(self, side, first, count):
            start = side * 3 * self.piece + first * self.piece
            return pl.ds(pl.multiple_of(start, 128), count * self.piece)

        def rows(self, k):
            return rows_at(lax.rem(me + n - k, n), sz.shard)

        def peer(self, k):
            cols = self.cols(core, odd, 2)
            return to_peer(
                self.shard.at[:, cols],
                self.full.at[rows_at(me, sz.shard), cols],
                self.peer_sem,
                k,
            )

        def layer(self, k, mine=True):
            part = 2 * odd if mine else 2 - 2 * odd
            piece = self.full.at[self.rows(k), self.cols(core, part, 1)]
            sem = self.layer_sem
            return remote(piece, piece, sem.at[0, k], sem.at[1, k], partner, me)

        def twin(self, k, late, side):
            first, count = (2 - 2 * odd, 1) if late else (odd, 2)
            piece = self.full.at[self.rows(k), self.cols(side, first, count)]
            sem = self.twin_sem
            return remote(
                piece, piece, sem.at[0, late, k], sem.at[1, late, k], sibling, me
            )

        def start(self):
            for k in range(1, n):
                self.peer(k).start()
            self.full[rows_at(me, sz.shard), :] = self.shard[...]

        def forward(self):
            for k in range(1, n):
                self.peer(k).wait_recv()
                self.layer(k).start()
                self.twin(k, 0, core).start()

        def finish(self):
            for k in range(1, n):
                self.layer(k, False).wait_recv()
                self.twin(k, 1, core).start()
            for k in range(1, n):
                for late in range(2):
                    self.twin(k, late, 1 - core).wait_recv()

        def drain(self):
            for k in range(1, n):
                self.peer(k).wait_send()
                self.layer(k).wait_send()
                for late in range(2):
                    self.twin(k, late, core).wait_send()

    gather_q = Gather(wq_shard, wq, 3 * sz.d, wq_sem, zq_sem, cq_sem)
    gather_p = Gather(wp_shard, wp, sz.d, wp_sem, zp_sem, cp_sem)

    def small_sends(k):
        return [
            to_peer(src, dst.at[me], sm_sem.at[i], k)
            for i, (src, dst) in enumerate(
                ((gains_ref, gains), (biases_ref, biases), (router_ref, routers))
            )
        ]

    for k in range(1, n):
        for cp in small_sends(k):
            cp.start()
    gather_q.start()
    gains[me] = gains_ref[...]
    biases[me] = biases_ref[...]
    routers[me] = router_ref[...]

    choice = (routes_ref[...].astype(F32) + 1.0).astype(BF)
    lines = mm_nt(choice, pad_matrix(sz)).astype(jnp.int32) - 1
    ids = iota((sz.ep, sz.rows), 0)
    oh1 = (lines[0:1, :] == ids).astype(F32)
    oh2 = (lines[1:2, :] == ids).astype(F32)
    before = (
        (iota((sz.rows, sz.rows), 0) < iota((sz.rows, sz.rows), 1))
        .astype(F32)
        .astype(BF)
    )
    pos1 = mm(oh1.astype(BF), before)
    pos2 = mm(oh2.astype(BF), before) + jnp.sum(oh1, 1, keepdims=True)
    place = oh1 * pos1 + oh2 * pos2
    kept = (oh1 + oh2 > 0.5) & (place < sz.cap - 0.5)
    slot = jnp.where(kept, place, -1.0).astype(jnp.int32)
    slot_ids = iota((sz.slots, sz.rows), 0)
    for e in range(sz.experts):
        pmat[e * sz.slots : (e + 1) * sz.slots, :] = (
            (slot_ids == slot[e : e + 1, :]).astype(F32).astype(BF)
        )
    eye = (iota((sz.rows, sz.rows), 0) == iota((sz.rows, sz.rows), 1)).astype(F32)
    slot_cols = mm_nt(eye.astype(BF), slot.astype(F32).astype(BF)).astype(jnp.int32)
    lane_ids = iota((sz.rows, sz.slots), 1)
    for e in range(sz.experts):
        comb[e] = (slot_cols[:, e : e + 1] == lane_ids).astype(F32).astype(BF)

    spread = pad_matrix(sz)
    gpad[...] = mm(spread, grad_ref[...]).astype(BF)
    for e in range(sz.experts):
        block = slice(e * sz.slots, (e + 1) * sz.slots)
        gs[block, :] = mm(pmat[block, :], gpad[...]).astype(BF)
    slots_me = rows_at(me, sz.slots)
    gr[slots_me, :] = gs[slots_me, :]

    x = mm(spread, tok_ref[...])
    for k in range(1, n):
        for cp in small_sends(k):
            cp.wait_recv()
    smf[...] = jnp.zeros_like(smf)
    for j in range(n):
        r = iota((sz.shard, sz.d), 0)
        c = iota((sz.shard, sz.d), 1)
        pick = (c == r + j * sz.shard).astype(F32).astype(BF)
        smf[0:2, :] += mm(gains[j], pick)
        smf[2:7, :] += mm(biases[j], pick)
        smf[8 : 8 + sz.experts, :] += mm(routers[j], pick)
    normed[...] = normalize(x, smf[0:1, :], smf[2:3, :]).astype(BF)
    normed_t[...] = normed[...].T

    gather_q.forward()
    gather_p.start()
    gather_q.finish()
    for j, bias_row in ((0, 3), (1, None), (2, 4)):
        cols = slice(j * sz.d, (j + 1) * sz.d)
        out = mm(normed[...], wq[:, cols])
        if bias_row is not None:
            out = out + smf[bias_row : bias_row + 1, :]
        qkv[:, cols] = out.astype(BF)
    for k in range(1, n):
        dst = rows_at(lax.rem(me + k, n), sz.slots)
        to_peer(gs.at[dst, :], gr.at[slots_me, :], g_sem, k).start()

    scale = 1.0 / math.sqrt(HEAD_DIM)
    lane = iota((sz.seq, 128), 1)
    live = iota((sz.seq, sz.seq), 1) < SEQ

    def pair_step(pair, carry):
        for image in range(sz.images):
            rows = slice(image * sz.seq, (image + 1) * sz.seq)
            q2 = qkv[rows, pl.ds(pl.multiple_of(pair * 128, 128), 128)]
            k2 = qkv[rows, pl.ds(pl.multiple_of(sz.d + pair * 128, 128), 128)]
            v2 = qkv[rows, pl.ds(pl.multiple_of(2 * sz.d + pair * 128, 128), 128)]
            total = jnp.zeros((sz.seq, 128), F32)
            for half in range(2):
                mask = (lane >= half * 64) & (lane < half * 64 + 64)
                s = mm_nt(jnp.where(mask, q2, jnp.zeros_like(q2)), k2) * scale
                s = jnp.where(live, s, -1e30)
                e = jnp.exp(s - jnp.max(s, -1, keepdims=True))
                p = (e / jnp.sum(e, -1, keepdims=True)).astype(BF)
                pall[pair, image * 2 + half] = p
                total = total + mm(p, jnp.where(mask, v2, jnp.zeros_like(v2)))
            ctx[rows, pl.ds(pl.multiple_of(pair * 128, 128), 128)] = total.astype(BF)
        return carry

    lax.fori_loop(0, sz.pairs, pair_step, 0)

    gather_p.forward()
    gather_p.finish()
    res = (
        mm(spread, tok_ref[...])
        + mm(ctx[...], wp[...])
        + smf[5:6, :]
    )
    resid[...] = res
    low = normalize(res, smf[1:2, :], smf[6:7, :]).astype(BF)
    second[...] = low

    for e in range(sz.experts):
        block = slice(e * sz.slots, (e + 1) * sz.slots)
        xs[block, :] = mm(pmat[block, :], second[...]).astype(BF)
    for k in range(1, n):
        dst = rows_at(lax.rem(me + k, n), sz.slots)
        to_peer(xs.at[dst, :], xr.at[slots_me, :], x_sem, k).start()
    xr[slots_me, :] = xs[slots_me, :]

    small_low = smf[...].astype(BF)
    logit_rows = mm_nt(small_low, low)[8 : 8 + sz.ep, :]
    logit_rows = jnp.where(iota((sz.ep, sz.rows), 0) < sz.experts, logit_rows, -1e30)
    e_rows = jnp.exp(logit_rows - jnp.max(logit_rows, 0, keepdims=True))
    prob_rows = e_rows / jnp.sum(e_rows, 0, keepdims=True)
    hi = prob_rows.astype(BF)
    left = prob_rows - hi.astype(F32)
    mid = left.astype(BF)
    low3 = (left - mid.astype(F32)).astype(BF)
    for e in range(sz.experts):
        block = pmat[e * sz.slots : (e + 1) * sz.slots, :]
        gates[e] = mm_nt(hi, block) + mm_nt(mid, block) + mm_nt(low3, block)
    for k in range(1, n):
        to_peer(
            gates.at[lax.rem(me + k, n)], gater.at[me], ga_sem, k
        ).start()
    gater[me] = gates[me]
    logit_cols = mm_nt(low, small_low)
    col = iota((sz.rows, sz.small), 1)
    logit_cols = jnp.where((col >= 8) & (col < 8 + sz.experts), logit_cols, -1e30)
    e_cols = jnp.exp(logit_cols - jnp.max(logit_cols, 1, keepdims=True))
    probs[...] = e_cols / jnp.sum(e_cols, 1, keepdims=True)

    ctx_t[...] = ctx[...].T

    for k in range(1, n):
        src = lax.rem(me + n - k, n)
        dst = rows_at(lax.rem(me + k, n), sz.slots)
        theirs = rows_at(src, sz.slots)
        to_peer(gs.at[dst, :], gr.at[theirs, :], g_sem, k).wait()
        to_peer(gates.at[lax.rem(me + k, n)], gater.at[src], ga_sem, k).wait()
    square = iota((sz.slots, sz.slots), 0) == iota((sz.slots, sz.slots), 1)
    for j in range(n):
        block = slice(j * sz.slots, (j + 1) * sz.slots)
        row = gater[j, pl.ds(me, 1), :]
        gate = jnp.sum(jnp.where(square, row, 0.0), 1, keepdims=True)
        dres[block, :] = (gate * gr[block, :].astype(F32)).astype(BF)
    for k in range(1, n):
        src = lax.rem(me + n - k, n)
        dst = rows_at(lax.rem(me + k, n), sz.slots)
        theirs = rows_at(src, sz.slots)
        to_peer(xs.at[dst, :], xr.at[theirs, :], x_sem, k).wait()
        for cp in small_sends(k):
            cp.wait_send()
    gather_q.drain()
    gather_p.drain()


def front(sz, tokens, grad, routes, wq, wp, router, gains, biases):
    vmem = pl.BlockSpec(memory_space=pltpu.VMEM)
    rows, d, slots, n = sz.rows, sz.d, sz.all_slots, sz.n_exp
    outs = [
        ((slots, d), BF),
        ((slots, d), BF),
        ((rows, 3 * d), BF),
        ((sz.pairs, sz.images * 2, sz.seq, sz.seq), BF),
        ((d, rows), BF),
        ((rows, d), F32),
        ((rows, d), BF),
        ((d, rows), BF),
        ((rows, sz.small), F32),
        ((d, 3 * d), BF),
        ((d, d), BF),
        ((sz.small, d), F32),
        ((rows, d), BF),
        ((sz.experts, rows, sz.slots), BF),
    ]
    dma = pltpu.SemaphoreType.DMA
    sems = [dma((2, n))] * 4 + [dma((2, 2, n))] * 2 + [dma((3, 2, n))] + [dma((2, n))] * 3
    return pl.pallas_call(
        partial(front_kernel, sz),
        name="front",
        out_shape=[jax.ShapeDtypeStruct(s, t) for s, t in outs],
        in_specs=[vmem] * 8,
        out_specs=[vmem] * len(outs),
        scratch_shapes=[
            pltpu.VMEM((rows, d), BF),
            pltpu.VMEM((rows, d), BF),
            pltpu.VMEM((slots, rows), BF),
            pltpu.VMEM((slots, d), BF),
            pltpu.VMEM((n, sz.ep, sz.slots), F32),
            pltpu.VMEM((slots, d), BF),
            pltpu.VMEM((slots, d), BF),
            pltpu.VMEM((n, sz.ep, sz.slots), F32),
            pltpu.VMEM((n, *router.shape), BF),
            pltpu.VMEM((n, *gains.shape), BF),
            pltpu.VMEM((n, *biases.shape), BF),
        ]
        + sems,
        compiler_params=pltpu.CompilerParams(
            collective_id=0, has_side_effects=True, vmem_limit_bytes=56 << 20
        ),
    )(tokens, grad, routes, wq, wp, router, gains, biases)


def finish_kernel(sz, out, gin, g1, g2, dense, sg, *refs):
    o_out, o_gin, o_qkv, o_proj, o_router, o_gains, o_biases, o_w1, o_b1, o_w2, o_b2 = refs
    o_out[...] = out[...]
    o_gin[...] = gin[...]
    fs, sh = sz.fs, sz.shard
    o_w1[0] = g1[...].astype(F32)
    o_w2[0] = g2[0:fs, :].astype(F32)
    o_b1[...] = g2[fs : fs + 16, :].astype(F32)[0:1, 0:fs]
    own = o_b2.shape[1]
    first = lax.axis_index("rep") * own
    pick = iota((sz.d, own), 0) == iota((sz.d, own), 1) + first
    o_b2[...] = mm(g2[fs : fs + 16, :], pick.astype(F32).astype(BF))[1:2, :]
    o_proj[...] = dense[0].astype(F32)
    for g in range(sz.groups):
        for j in range(3):
            cols = slice(j * sz.d + g * 256, j * sz.d + (g + 1) * 256)
            o_qkv[:, cols] = dense[g + 1, :, j * 256 : (j + 1) * 256].astype(F32)
    o_router[...] = sg[8 : 8 + sz.experts, 0:sh]
    o_gains[...] = sg[0:2, 0:sh]
    o_biases[...] = sg[2:7, 0:sh]


def finish(sz, out, gin, g1, g2, dense, sg):
    vmem = pl.BlockSpec(memory_space=pltpu.VMEM)
    d, fs, sh = sz.d, sz.fs, sz.shard
    outs = [
        ((sz.tok, d), BF),
        ((sz.tok, d), BF),
        ((sh, 3 * d), F32),
        ((sh, d), F32),
        ((sz.experts, sh), F32),
        ((2, sh), F32),
        ((5, sh), F32),
        ((1, d, fs), F32),
        ((1, fs), F32),
        ((1, fs, d), F32),
        ((1, d // sz.n_rep), F32),
    ]
    grads = pl.pallas_call(
        partial(finish_kernel, sz),
        name="finish",
        out_shape=[jax.ShapeDtypeStruct(s, t) for s, t in outs],
        in_specs=[vmem] * 6,
        out_specs=[vmem] * len(outs),
        compiler_params=pltpu.CompilerParams(vmem_limit_bytes=62 << 20),
    )(out, gin, g1, g2, dense, sg)
    return (*grads[:4], grads[4].T, *grads[5:])


def normalize_back(values, gain, cot):
    center = values - jnp.mean(values, -1, keepdims=True)
    spread = jnp.mean(center * center, -1, keepdims=True)
    inv = lax.rsqrt(spread + EPS)
    unit = center * inv
    scaled = cot * gain
    grad = inv * (
        scaled
        - jnp.mean(scaled, -1, keepdims=True)
        - unit * jnp.mean(scaled * unit, -1, keepdims=True)
    )
    return grad, jnp.sum(cot * unit, 0, keepdims=True), jnp.sum(cot, 0, keepdims=True)


def gelu_parts(h):
    t = 1.0 / (1.0 + (0.3275911 / math.sqrt(2.0)) * jnp.abs(h))
    bell = jnp.exp(-0.5 * h * h)
    poly = t * (
        0.127414796
        + t * (-0.142248368 + t * (0.7107068705 + t * (-0.7265760135 + t * 0.5307027145)))
    )
    tail = poly * bell
    return jnp.where(h >= 0, 1.0 - tail, tail), bell * (1.0 / math.sqrt(2.0 * math.pi))


def block_kernel(
    sz,
    tok_ref,
    routes_ref,
    router_ref,
    gains_ref,
    biases_ref,
    b1_ref,
    b2_ref,
    grad_hbm,
    wq_shard,
    wp_shard,
    w1_hbm,
    w2_hbm,
    o_dense,
    o_small,
    o_out,
    o_gin,
    o_w1,
    o_w2,
    o_probs,
    o_save,
    dw,
    w2,
    stage,
    xr,
    dres,
    qkv,
    ctx_t,
    resid,
    second,
    normed_t,
    probs,
    smf,
    gpad,
    comb,
    gater,
    gates,
    routers,
    gains,
    biases,
    bias2,
    xt,
    xta,
    acts,
    dhids,
    wide1,
    wide2,
    sends,
    ret,
    bck,
    qs,
    qr,
    t2,
    v1,
    v2,
    u1,
    u2,
    pbuf,
    r2,
    z1,
    z2,
    sm,
    smr,
    sme,
    sme_r,
    smz_r,
    wsem,
    psem,
    f_sem,
    l_sem,
    c_sem,
    o_sem,
    sm_sem,
    g_sem,
    x_sem,
    ga_sem,
    t_sem,
    u_sem,
    ret_sem,
    bck_sem,
    q_sem,
    d1_sem,
    d2_sem,
    z1_sem,
    z2_sem,
    z3_sem,
    s1_sem,
    s2_sem,
    s3_sem,
):
    me_r = lax.axis_index("rep")
    me = lax.axis_index("exp")
    n, nz, fs, d = sz.n_exp, sz.nz, sz.fs, sz.d
    core = lax.rem(me_r, 2)
    z = lax.div(me_r, 2)
    sibling = me_r + 1 - 2 * core
    odd = lax.rem(z, 2)
    partner = me_r + 2 - 4 * odd

    load_grad = pltpu.make_async_copy(grad_hbm, stage, wsem.at[0])
    load_grad.start()
    load_w2 = pltpu.make_async_copy(w2_hbm, w2, wsem.at[1])
    load_w2.start()

    barrier = pltpu.get_barrier_semaphore()
    for k in range(1, n):
        pl.semaphore_signal(
            barrier, inc=1, device_id=(me_r, lax.rem(me + k, n)), device_id_type=MESH
        )
    for k in range(1, nz):
        pl.semaphore_signal(
            barrier,
            inc=1,
            device_id=(lax.rem(me_r + 2 * k, 2 * nz), me),
            device_id_type=MESH,
        )
    pl.semaphore_signal(barrier, inc=1, device_id=(sibling, me), device_id_type=MESH)
    pl.semaphore_wait(barrier, n - 1 + nz)

    def remote(src, dst, send, recv, rep, exp):
        return pltpu.make_async_remote_copy(
            src_ref=src,
            dst_ref=dst,
            send_sem=send,
            recv_sem=recv,
            device_id=(rep, exp),
            device_id_type=MESH,
        )

    def to_peer(src, dst, sems, k):
        return remote(
            src, dst, sems.at[0, k], sems.at[1, k], me_r, lax.rem(me + k, n)
        )

    def to_z(src, dst, sems, k):
        return remote(
            src, dst, sems.at[0, k], sems.at[1, k], lax.rem(me_r + 2 * k, 2 * nz), me
        )

    normed = bck.at[0 : sz.rows, :]
    ctx = bck.at[sz.rows : 2 * sz.rows, :]
    res_send = sends.at[0 : sz.all_slots, :]
    row_send = sends.at[sz.all_slots : 2 * sz.all_slots, :]
    xs, gs = res_send, row_send

    piece = 128

    def shard_cols(g, tile):
        if isinstance(g, int) and g == sz.groups:
            return wp_shard, tile * piece
        return wq_shard, lax.div(tile, 2) * d + g * 256 + lax.rem(tile, 2) * piece

    def dw_cols(g, tile, count):
        return pl.ds(pl.multiple_of(g * d + tile * piece, 128), count * piece)

    def dw_rows(k):
        return rows_at(lax.rem(me + n - k, n), sz.shard)

    def fetch(g, i, k):
        tile = 3 * core + odd + i
        shard, start = shard_cols(g, tile)
        return remote(
            shard.at[:, pl.ds(pl.multiple_of(start, 128), piece)],
            dw.at[rows_at(me, sz.shard), dw_cols(g, tile, 1)],
            f_sem.at[0, g, i, k],
            f_sem.at[1, g, i, k],
            me_r,
            lax.rem(me + k, n),
        )

    def fetched(g, i, k):
        ref = dw.at[dw_rows(k), dw_cols(g, 3 * core + odd + i, 1)]
        return remote(
            ref,
            ref,
            f_sem.at[0, g, i, k],
            f_sem.at[1, g, i, k],
            me_r,
            lax.rem(me + k, n),
        )

    def layer(g, k, mine):
        part = 2 * odd if mine else 2 - 2 * odd
        ref = dw.at[dw_rows(k), dw_cols(g, 3 * core + part, 1)]
        return remote(ref, ref, l_sem.at[0, g, k], l_sem.at[1, g, k], partner, me)

    def twin(g, k, late, side):
        first, count = (2 - 2 * odd, 1) if late else (odd, 2)
        ref = dw.at[dw_rows(k), dw_cols(g, 3 * side + first, count)]
        return remote(
            ref, ref, c_sem.at[0, g, late, k], c_sem.at[1, g, late, k], sibling, me
        )

    def own_part(g, j):
        if isinstance(g, int) and g == sz.groups:
            src = wp_shard.at[:, j * 256 : (j + 1) * 256]
        else:
            src = wq_shard.at[:, pl.ds(pl.multiple_of(j * d + g * 256, 128), 256)]
        dst = dw.at[
            rows_at(me, sz.shard), pl.ds(pl.multiple_of(g * d + j * 256, 128), 256)
        ]
        return pltpu.make_async_copy(src, dst, o_sem.at[g, j])

    def start_weights(g):
        for k in range(1, n):
            for i in range(2):
                fetch(g, i, k).start()
        for j in range(3):
            own_part(g, j).start()

    def forward_weights(g):
        for k in range(1, n):
            for i in range(2):
                fetched(g, i, k).wait_recv()
            layer(g, k, True).start()
            twin(g, k, 0, core).start()

    def finish_weights(g):
        for j in range(3):
            own_part(g, j).wait()
        for k in range(1, n):
            layer(g, k, False).wait_recv()
            twin(g, k, 1, core).start()
        for k in range(1, n):
            for late in range(2):
                twin(g, k, late, 1 - core).wait_recv()

    def drain_weights(g):
        for k in range(1, n):
            for i in range(2):
                fetch(g, i, k).wait_send()
            layer(g, k, True).wait_send()
            for late in range(2):
                twin(g, k, late, core).wait_send()

    def small_sends(k):
        return [
            to_peer(src, dst.at[me], sm_sem.at[i], k)
            for i, (src, dst) in enumerate(
                ((gains_ref, gains), (biases_ref, biases), (router_ref, routers))
            )
        ]

    for k in range(1, n):
        for cp in small_sends(k):
            cp.start()
    for g in range(sz.groups):
        start_weights(g)
    gains[me] = gains_ref[...]
    biases[me] = biases_ref[...]
    routers[me] = router_ref[...]

    choice = (routes_ref[...].astype(F32) + 1.0).astype(BF)
    lines = mm_nt(choice, pad_matrix(sz)).astype(jnp.int32) - 1
    ids = iota((sz.ep, sz.rows), 0)
    oh1 = (lines[0:1, :] == ids).astype(F32)
    oh2 = (lines[1:2, :] == ids).astype(F32)
    before = (
        (iota((sz.rows, sz.rows), 0) < iota((sz.rows, sz.rows), 1))
        .astype(F32)
        .astype(BF)
    )
    pos1 = mm(oh1.astype(BF), before)
    pos2 = mm(oh2.astype(BF), before) + jnp.sum(oh1, 1, keepdims=True)
    place = oh1 * pos1 + oh2 * pos2
    kept = (oh1 + oh2 > 0.5) & (place < sz.cap - 0.5)
    slot = jnp.where(kept, place, -1.0).astype(jnp.int32)
    slot_ids = iota((sz.slots, sz.rows), 0)

    def picks(e):
        return (slot_ids == slot[e : e + 1, :]).astype(F32).astype(BF)

    eye = (iota((sz.rows, sz.rows), 0) == iota((sz.rows, sz.rows), 1)).astype(F32)
    slot_cols = mm_nt(eye.astype(BF), slot.astype(F32).astype(BF)).astype(jnp.int32)
    lane_ids = iota((sz.rows, sz.slots), 1)
    for e in range(sz.experts):
        comb[e] = (slot_cols[:, e : e + 1] == lane_ids).astype(F32).astype(BF)

    x = mm(pad_matrix(sz), tok_ref[...])
    load_grad.wait()
    gpad[...] = mm(pad_matrix(sz), stage[...]).astype(BF)
    slots_me = rows_at(me, sz.slots)

    def at_peer(k):
        return slice(k * sz.slots, (k + 1) * sz.slots)

    def picks_for(k):
        line = slot[0:1, :]
        for e in range(1, sz.experts):
            line = jnp.where(lax.rem(me + k, n) == e, slot[e : e + 1, :], line)
        return (slot_ids == line).astype(F32).astype(BF)

    for k in range(n):
        gs[at_peer(k), :] = mm(picks_for(k), gpad[...]).astype(BF)
    dres[at_peer(0), :] = gs[at_peer(0), :]

    for k in range(1, n):
        for cp in small_sends(k):
            cp.wait_recv()
    smf[...] = jnp.zeros_like(smf)
    for j in range(n):
        r = iota((sz.shard, d), 0)
        c = iota((sz.shard, d), 1)
        pick = (c == r + j * sz.shard).astype(F32).astype(BF)
        smf[0:2, :] += mm(gains[j], pick)
        smf[2:7, :] += mm(biases[j], pick)
        smf[8 : 8 + sz.experts, :] += mm(routers[j], pick)
    normed[...] = normalize(x, smf[0:1, :], smf[2:3, :]).astype(BF)
    normed_t[...] = normed[...].T

    scale = 1.0 / math.sqrt(HEAD_DIM)
    half_lane = iota((sz.seq, 128), 1)
    live = iota((sz.seq, sz.seq), 1) < SEQ

    def pair_cols(pair, j, base=None):
        group = lax.div(pair, 2) * d if base is None else base
        start = group + j * 256 + lax.rem(pair, 2) * 128
        return pl.ds(pl.multiple_of(start, 128), 128)

    def save_probs(pair):
        slot = lax.rem(pair, 2)
        return pltpu.make_async_copy(pbuf.at[slot], o_probs.at[pair], psem.at[slot])

    def forward_pair(pair, carry):
        @pl.when(pair >= 2)
        def _():
            save_probs(pair - 2).wait()

        for image in range(sz.images):
            rows = slice(image * sz.seq, (image + 1) * sz.seq)
            q2, k2, v2_ = (qkv[rows, pair_cols(pair, j)] for j in range(3))
            total = jnp.zeros((sz.seq, 128), F32)
            for half in range(2):
                mask = (half_lane >= half * 64) & (half_lane < half * 64 + 64)
                zero = jnp.zeros_like(q2)
                s = mm_nt(jnp.where(mask, q2, zero), k2) * scale
                s = jnp.where(live, s, -1e30)
                e = jnp.exp(s - jnp.max(s, -1, keepdims=True))
                p = (e / jnp.sum(e, -1, keepdims=True)).astype(BF)
                pbuf[lax.rem(pair, 2), image * 2 + half] = p
                total = total + mm(p, jnp.where(mask, v2_, zero))
            ctx[rows, pl.ds(pl.multiple_of(pair * 128, 128), 128)] = total.astype(BF)
        save_probs(pair).start()
        return carry

    def forward_group(g, carry):
        finish_weights(g)
        cols = pl.ds(pl.multiple_of(g * d, 128), d)
        of_bias = pl.ds(pl.multiple_of(g * 256, 128), 256)
        bias = jnp.concatenate(
            [smf[3:4, of_bias], jnp.zeros((1, 256), F32), smf[4:5, of_bias]], 1
        )
        qkv[:, cols] = (mm(normed[...], dw[:, cols]) + bias).astype(BF)
        lax.fori_loop(2 * g, 2 * g + 2, forward_pair, 0)

        @pl.when(g + 2 < sz.groups)
        def _():
            forward_weights(g + 2)

        return carry

    forward_weights(0)
    forward_weights(1)
    start_weights(sz.groups)
    for k in range(1, n):
        to_peer(gs.at[at_peer(k), :], dres.at[at_peer(n - k), :], g_sem, k).start()
    lax.fori_loop(0, sz.groups, forward_group, 0)
    forward_weights(sz.groups)
    finish_weights(sz.groups)
    save = pltpu.make_async_copy(dw, o_save, wsem.at[2])
    save.start()
    res = (
        mm(pad_matrix(sz), tok_ref[...])
        + mm(ctx[...], dw[:, 3 * d : 4 * d])
        + smf[5:6, :]
    )
    resid[...] = res
    second[...] = normalize(res, smf[1:2, :], smf[6:7, :]).astype(BF)
    ctx_t[...] = ctx[...].T
    for k in [*range(1, n), 0]:
        xs[at_peer(k), :] = mm(picks_for(k), second[...]).astype(BF)
        if k:
            to_peer(xs.at[at_peer(k), :], xr.at[at_peer(n - k), :], x_sem, k).start()
        else:
            xr[at_peer(0), :] = xs[at_peer(0), :]
    for g in range(sz.groups + 1):
        drain_weights(g)
    save.wait()
    load_w1 = pltpu.make_async_copy(w1_hbm, dw, wsem.at[0])
    load_w1.start()

    small_low = smf[...].astype(BF)
    low = second[...]
    logit_rows = mm_nt(small_low, low)[8 : 8 + sz.ep, :]
    logit_rows = jnp.where(iota((sz.ep, sz.rows), 0) < sz.experts, logit_rows, -1e30)
    e_rows = jnp.exp(logit_rows - jnp.max(logit_rows, 0, keepdims=True))
    prob_rows = e_rows / jnp.sum(e_rows, 0, keepdims=True)
    hi = prob_rows.astype(BF)
    left = prob_rows - hi.astype(F32)
    mid = left.astype(BF)
    rest_low = (left - mid.astype(F32)).astype(BF)
    for e in range(sz.experts):
        block = picks(e)
        gates[e] = mm_nt(hi, block) + mm_nt(mid, block) + mm_nt(rest_low, block)
    for k in range(1, n):
        to_peer(gates.at[lax.rem(me + k, n)], gater.at[n - k], ga_sem, k).start()
    gater[0] = gates[me]
    logit_cols = mm_nt(low, small_low)
    col = iota((sz.rows, sz.small), 1)
    logit_cols = jnp.where((col >= 8) & (col < 8 + sz.experts), logit_cols, -1e30)
    e_cols = jnp.exp(logit_cols - jnp.max(logit_cols, 1, keepdims=True))
    probs[...] = e_cols / jnp.sum(e_cols, 1, keepdims=True)
    for pair in range(max(sz.pairs - 2, 0), sz.pairs):
        save_probs(pair).wait()

    lower = 1 - lax.div(z, (nz + 1) // 2)
    span = 2 * fs
    per = span // 256
    everyone, others = slice(0, sz.all_slots), slice(sz.slots, sz.all_slots)
    square = iota((sz.slots, sz.slots), 0) == iota((sz.slots, sz.slots), 1)
    bias2[...] = jnp.zeros_like(bias2)
    half_own = pl.ds(pl.multiple_of(core * fs, 128), fs)
    half_other = pl.ds(pl.multiple_of((1 - core) * fs, 128), fs)

    def dest_of(i):
        return lower * (nz - 1 - i) + (1 - lower) * i

    def hidden_at(i, first, size):
        return pl.ds(pl.multiple_of(dest_of(i) * span + first, 128), size)

    def prepare(k):
        rows = at_peer(k)
        if k:
            j = n - k
            to_peer(gs.at[at_peer(j), :], dres.at[rows, :], g_sem, j).wait()
            to_peer(gates.at[lax.rem(me + j, n)], gater.at[k], ga_sem, j).wait()
        row = gater[k, pl.ds(me, 1), :]
        gate = jnp.sum(jnp.where(square, row, 0.0), 1, keepdims=True)
        value = (gate * dres[rows, :].astype(F32)).astype(BF)
        dres[rows, :] = value
        bias2[...] += jnp.sum(value.astype(F32), 0, keepdims=True)
        if k:
            to_peer(xs.at[at_peer(j), :], xr.at[rows, :], x_sem, j).wait()

    def cell(t, rows):
        i, c = lax.div(t, per), lax.rem(t, per)
        hidden = hidden_at(i, c * 256, 256)
        here = pl.ds(pl.multiple_of(c * 256, 128), 256)
        h = mm(xr[rows, :], dw[:, hidden]) + b1_ref[:, hidden].astype(F32)
        cdf, pdf = gelu_parts(h)
        da = mm_nt(dres[rows, :], w2[hidden, :])
        acts[i, rows, here] = (h * cdf).astype(BF)
        dhids[i, rows, here] = (da * (cdf + h * pdf)).astype(BF)

    def cells(first, last, rows):
        lax.fori_loop(first * per, last * per, lambda t, c: (cell(t, rows), c)[1], 0)

    def row_copy(c, k, land):
        cols = pl.ds(pl.multiple_of(c * 256, 128), 256)
        return remote(
            row_send.at[at_peer(k), cols],
            bck.at[land, cols],
            bck_sem.at[0, c, k],
            bck_sem.at[1, c, k],
            me_r,
            lax.rem(me + k, n),
        )

    def back_rows(c, carry):
        cols = pl.ds(pl.multiple_of(c * 256, 128), 256)
        total = mm_nt(dhids[0], dw[cols, hidden_at(0, 0, span)])
        for i in range(1, nz):
            total = total + mm_nt(dhids[i], dw[cols, hidden_at(i, 0, span)])
        row_send[:, cols] = total.astype(BF)
        for k in range(1, n):
            row_copy(c, k, slots_me).start()
        bck[slots_me, cols] = row_send[at_peer(0), cols]
        return carry

    def back_results(c, column):
        cols = pl.ds(pl.multiple_of(c * 256, 128), 256)
        total = mm(acts[0], w2[hidden_at(0, 0, span), cols])
        for i in range(1, nz):
            total = total + mm(acts[i], w2[hidden_at(i, 0, span), cols])
        out = (total + b2_ref[:, cols].astype(F32)).astype(BF)
        res_send[:, cols] = out
        return column + jnp.sum(
            out.astype(F32) * dres[:, cols].astype(F32), 1, keepdims=True
        )

    parts1 = [slice(i, i + d // 2) for i in (0, d // 2)]
    parts2 = range(0, fs, 128)

    def grad1(i, half, rows):
        part = mm(xta[rows, :], dhids[i, 0:d, half])
        return part + mm(xt[rows, :], dhids[i, d:, half])

    def grad2(i, start, first):
        cols = pl.ds(pl.multiple_of(start + first, 128), 128)
        return mm_tn(acts[i, :, cols], dres[...])

    def extra(i, half):
        gb = jnp.sum(dhids[i, :, half].astype(F32), 0, keepdims=True)
        row = iota((16, d), 0)
        line = jnp.concatenate([gb, jnp.zeros((1, d - fs), F32)], 1)
        return jnp.where(row == 0, line, jnp.where(row == 1, bias2[...], 0.0))

    def leaving(i):
        return r2.at[0] if isinstance(i, int) else acts.at[i, 0:d, half_other]

    def t_copies(i):
        dest = dest_of(i)
        return (
            remote(leaving(i), v1.at[dest], t_sem.at[0, 0, dest], t_sem.at[1, 0, dest], sibling, me),
            remote(t2, v2.at[dest], t_sem.at[0, 1, dest], t_sem.at[1, 1, dest], sibling, me),
        )

    def landing(way, step, at):
        if way == 0:
            return nz - 2 - step + at
        return at + step + 2 - nz if step < nz - 2 else nz

    def u_copies(src1, src2, way, step, target, slot):
        return (
            remote(src1, u1.at[slot], u_sem.at[0, 0, way, step], u_sem.at[1, 0, way, step], target, me),
            remote(src2, u2.at[slot], u_sem.at[0, 1, way, step], u_sem.at[1, 1, way, step], target, me),
        )

    def other_grads(i):
        for first in parts2:
            value = grad2(i, (1 - core) * fs, first)
            t2[first : first + 128, :] = value.astype(BF)
        t2[fs:, :] = extra(i, half_other).astype(BF)
        t_copies(i)[1].start()
        if isinstance(i, int):
            xta[...] = xr[0:d, :].T
            xt[...] = xr[d:, :].T
        for rows in parts1:
            leaving(i)[rows, :] = grad1(i, half_other, rows).astype(BF)
        t_copies(i)[0].start()

    def own_grads(i):
        dest = dest_of(i)
        t_copies(i)[1].wait()
        for first in parts2:
            rows = slice(first, first + 128)
            value = v2[dest, rows, :].astype(F32) + grad2(i, core * fs, first)
            v2[dest, rows, :] = value.astype(BF)
        v2[dest, fs:, :] = (v2[dest, fs:, :].astype(F32) + extra(i, half_own)).astype(BF)
        leave(i, 1)
        t_copies(i)[0].wait()
        for rows in parts1:
            value = v1[dest, rows, :].astype(F32) + grad1(i, half_own, rows)
            v1[dest, rows, :] = value.astype(BF)
        leave(i, 0)

    def leave(i, which):
        dest = dest_of(i)

        @pl.when((z == 0) & (i <= nz - 2))
        def _():
            u_copies(v1.at[dest], v2.at[dest], 0, i, me_r + 2, dest)[which].start()

        @pl.when((z == nz - 1) & (i < nz - 2))
        def _():
            u_copies(v1.at[dest], v2.at[dest], 1, i, me_r - 2, dest)[which].start()

        @pl.when((z == nz - 1) & (i == nz - 2))
        def _():
            u_copies(v1.at[dest], v2.at[dest], 1, i, me_r - 2, nz)[which].start()

    prepare(0)
    load_w2.wait()
    load_w1.wait()
    cells(0, nz, at_peer(0))
    for k in range(1, n):
        prepare(k)
    cells(0, 1, others)
    other_grads(0)
    own_grads(0)
    cells(1, nz, others)
    lax.fori_loop(0, d // 256, back_rows, 0)
    column = lax.fori_loop(
        0, d // 256, back_results, jnp.zeros((sz.all_slots, 1), F32)
    )
    for k in range(n):
        line = jnp.where(square, column[at_peer(k), :], 0.0)
        qs[k] = jnp.broadcast_to(jnp.sum(line, 0, keepdims=True), (8, sz.slots))
    qr[me] = qs[0]
    ret[slots_me, :] = res_send[at_peer(0), :]
    for k in range(1, n):
        to_peer(qs.at[k], qr.at[me], q_sem, k).start()
    for k in range(1, n):
        to_peer(res_send.at[at_peer(k), :], ret.at[slots_me, :], ret_sem, k).start()

    def slice_step(i, carry):
        other_grads(i)
        own_grads(i)
        return carry

    lax.fori_loop(1, nz, slice_step, 0)
    dense_load = pltpu.make_async_copy(o_save, dw, wsem.at[0])
    dense_load.start()

    def z_round(s):
        for way in range(2):
            zz = z if way == 0 else nz - 1 - z
            dest = nz - 1 - s + zz if way == 0 else z - (nz - 1 - s)
            target = me_r + 2 if way == 0 else me_r - 2

            @pl.when((zz >= 1) & (zz <= s))
            def _():
                here = landing(way, s - 1, z)
                there = landing(way, s, z + 1 if way == 0 else z - 1)
                a1, a2 = u1.at[here], u2.at[here]
                for cp in u_copies(a1, a2, way, s - 1, target, here):
                    cp.wait_recv()
                u1[here] = (u1[here].astype(F32) + v1[dest].astype(F32)).astype(BF)
                u2[here] = (u2[here].astype(F32) + v2[dest].astype(F32)).astype(BF)
                for cp in u_copies(a1, a2, way, s, target, there):
                    cp.start()

    if nz > 2:
        z_round(1)

    for k in range(1, n):
        src = lax.rem(me + n - k, n)
        for c in range(d // 256):
            row_copy(c, k, rows_at(src, sz.slots)).wait()
        to_peer(qs.at[k], qr.at[src], q_sem, k).wait()
    mixed = sgrad = wide2
    lane = iota((sz.rows, sz.small), 1)
    weighted = jnp.zeros((sz.rows, sz.small), F32)
    for e in range(sz.experts):
        q = jnp.sum(comb[e].astype(F32) * qr[e, 0:1, :], 1, keepdims=True)
        weighted = jnp.where(lane == 8 + e, q, weighted)
    total = jnp.sum(weighted, 1, keepdims=True)
    logit_low = (weighted - probs[...] * total).astype(BF)
    sgrad[...] = mm(logit_low, smf[...].astype(BF))
    for e in range(sz.experts):
        sgrad[...] += mm(comb[e], bck[e * sz.slots : (e + 1) * sz.slots, :])
    back2, gain2, shift2 = normalize_back(resid[...], smf[1:2, :], sgrad[...])
    rgrad = wide1
    rgrad[...] = gpad[...].astype(F32) + back2
    low = rgrad[...].astype(BF)
    bias_out = jnp.sum(low.astype(F32), 0, keepdims=True)

    dense = w2
    wide = d // 2
    keep = pl.ds(pl.multiple_of(core * wide, 128), wide)
    give = pl.ds(pl.multiple_of((1 - core) * wide, 128), wide)
    part = sz.part

    def chunk_rows(j, start, size):
        return pl.ds(pl.multiple_of(j * d + start, 16), size)

    def part_rows(zi):
        return pl.ds(pl.multiple_of(zi * part, 16), part)

    def parked(j):
        cols = pl.ds(pl.multiple_of(lax.rem(j, 2) * wide, 128), wide)
        return acts.at[lax.div(j, 2), 0:d, cols]

    def to_sibling(j):
        return remote(
            dense.at[chunk_rows(j, 0, d), give],
            parked(j),
            d1_sem.at[0, j],
            d1_sem.at[1, j],
            sibling,
            me,
        )

    def to_owner(j, k):
        e = lax.rem(me + k, n)
        return remote(
            dense.at[chunk_rows(j, e * sz.shard, sz.shard), keep],
            r2.at[k - 1, pl.ds(pl.multiple_of(j * sz.shard, 16), sz.shard), :],
            d2_sem.at[0, j, k],
            d2_sem.at[1, j, k],
            me_r,
            e,
        )

    def to_layer(j, k):
        return remote(
            z1.at[j, part_rows(lax.rem(z + k, nz)), :],
            z2.at[k - 1, j],
            z1_sem.at[0, j, k],
            z1_sem.at[1, j, k],
            lax.rem(me_r + 2 * k, 2 * nz),
            me,
        )

    def from_layer(j, k, owner):
        piece = o_dense.at[j, part_rows(owner), keep]
        return remote(
            piece,
            piece,
            z2_sem.at[0, j, k],
            z2_sem.at[1, j, k],
            lax.rem(me_r + 2 * k, 2 * nz),
            me,
        )

    def to_twin(j, cols):
        piece = o_dense.at[j, :, cols]
        return remote(piece, piece, z3_sem.at[0, j], z3_sem.at[1, j], sibling, me)

    def stage1(j):
        to_sibling(j).wait()
        rows = chunk_rows(j, 0, d)
        dense[rows, keep] = (dense[rows, keep].astype(F32) + parked(j)[...].astype(F32)).astype(BF)
        for k in range(1, n):
            to_owner(j, k).start()

    def stage2(j):
        acc = dense[chunk_rows(j, me * sz.shard, sz.shard), keep].astype(F32)
        for k in range(1, n):
            to_owner(j, k).wait()
            acc = acc + r2[k - 1, j * sz.shard : (j + 1) * sz.shard, :].astype(F32)
        z1[j] = acc.astype(BF)
        for k in range(1, nz):
            to_layer(j, k).start()

    def stage3(j):
        acc = z1[j, part_rows(z), :].astype(F32)
        for k in range(1, nz):
            to_layer(j, k).wait()
            acc = acc + z2[k - 1, j].astype(F32)
        o_dense[j, part_rows(z), keep] = acc.astype(BF)
        for k in range(1, nz):
            from_layer(j, k, z).start()

    def stage4(j):
        for k in range(1, nz):
            from_layer(j, k, z).wait_send()
            from_layer(j, k, lax.rem(z + nz - k, nz)).wait_recv()
        to_twin(j, keep).start()

    def stage5(j):
        to_twin(j, keep).wait_send()
        to_twin(j, give).wait_recv()

    dense[chunk_rows(0, 0, d), :] = mm(ctx_t[...], low).astype(BF)
    to_sibling(0).start()
    dense_load.wait()
    for k in range(1, n):
        theirs = rows_at(lax.rem(me + n - k, n), sz.slots)
        to_peer(res_send.at[at_peer(k), :], ret.at[theirs, :], ret_sem, k).wait()
    cgrad = sends.at[3 * sz.rows : 4 * sz.rows, :]

    def load_probs(pair):
        slot = lax.rem(pair, 2)
        return pltpu.make_async_copy(o_probs.at[pair], pbuf.at[slot], psem.at[slot])

    load_probs(0).start()
    cgrad[...] = mm_nt(low, dw[:, 3 * d : 4 * d]).astype(BF)
    sm[...] = mm_tn(logit_low, second[...])

    scale = 1.0 / math.sqrt(HEAD_DIM)
    half_lane = iota((sz.seq, 128), 1)

    def pair_step(pair, carry):
        load_probs(pair).wait()

        @pl.when(pair + 1 < sz.pairs)
        def _():
            load_probs(pair + 1).start()

        for image in range(sz.images):
            rows = slice(image * sz.seq, (image + 1) * sz.seq)
            q2, k2, v2_ = (qkv[rows, pair_cols(pair, j)] for j in range(3))
            c2 = cgrad[rows, pl.ds(pl.multiple_of(pair * 128, 128), 128)]
            there = pl.ds(
                pl.multiple_of(lax.div(pair, 2) * sz.rows + image * sz.seq, 16), sz.seq
            )
            dq = jnp.zeros((sz.seq, 128), F32)
            dk = jnp.zeros((sz.seq, 128), F32)
            dv = jnp.zeros((sz.seq, 128), F32)
            for half in range(2):
                mask = (half_lane >= half * 64) & (half_lane < half * 64 + 64)
                zero = jnp.zeros_like(q2)
                ch = jnp.where(mask, c2, zero)
                p = pbuf[lax.rem(pair, 2), image * 2 + half]
                dv = dv + mm_tn(p, ch)
                pb = mm_nt(ch, v2_)
                p32 = p.astype(F32)
                mix = jnp.sum(pb * p32, -1, keepdims=True)
                ds = (p32 * (pb - mix)).astype(BF)
                dq = dq + mm(ds, jnp.where(mask, k2, zero))
                dk = dk + mm_tn(ds, jnp.where(mask, q2, zero))
            sends[there, pair_cols(pair, 0, 0)] = (dq * scale).astype(BF)
            sends[there, pair_cols(pair, 1, 0)] = (dk * scale).astype(BF)
            sends[there, pair_cols(pair, 2, 0)] = dv.astype(BF)
        return carry

    def group_step(g, carry):
        lax.fori_loop(2 * g, 2 * g + 2, pair_step, 0)
        dense[chunk_rows(g + 1, 0, d), :] = mm(
            normed_t[...], sends[rows_at(g, sz.rows), :]
        ).astype(BF)
        to_sibling(g + 1).start()
        stage1(g)
        return carry

    lax.fori_loop(0, sz.groups, group_step, 0)
    for s in range(2, nz - 1):
        z_round(s)
    stage1(sz.groups)

    ngrad = sgrad
    ngrad[...] = mm_nt(sends[0 : sz.rows, :], dw[:, 0:d])
    for g in range(1, sz.groups):
        grads = sends[g * sz.rows : (g + 1) * sz.rows, :]
        ngrad[...] += mm_nt(grads, dw[:, g * d : (g + 1) * d])
    stage2(0)
    x = mm(pad_matrix(sz), tok_ref[...])
    back1, gain1, shift1 = normalize_back(x, smf[0:1, :], ngrad[...])
    stage[...] = mm(unpad_matrix(sz), (rgrad[...] + back1).astype(BF)).astype(BF)
    store = pltpu.make_async_copy(stage, o_gin, wsem.at[2])
    store.start()
    sums = [
        jnp.sum(sends[g * sz.rows : (g + 1) * sz.rows, :].astype(F32), 0, keepdims=True)
        for g in range(sz.groups)
    ]
    bias_q = jnp.concatenate([total[:, 0:256] for total in sums], 1)
    bias_v = jnp.concatenate([total[:, 512:768] for total in sums], 1)
    row = iota((sz.small, d), 0)
    small = sm[...]
    for i, value in enumerate((gain1, gain2, shift1, bias_q, bias_v, bias_out, shift2)):
        small = jnp.where(row == i, value, small)
    sm[...] = small
    smb = sme.at[n]
    smb[...] = small.astype(BF)
    s_first = remote(smb, smr, s1_sem.at[0], s1_sem.at[1], sibling, me)
    s_first.start()

    stage2(1)
    stage3(0)
    mixed[...] = resid[...]
    for e in range(sz.experts):
        block = slice(e * sz.slots, (e + 1) * sz.slots)
        mixed[...] += probs[:, 8 + e : 9 + e] * mm(comb[e], ret[block, :])
    store.wait()
    stage[...] = mm(unpad_matrix(sz), mixed[...].astype(BF)).astype(BF)
    store = pltpu.make_async_copy(stage, o_out, wsem.at[2])
    store.start()

    s_first.wait()
    chip_small = (sm[...] + smr[...].astype(F32)).astype(BF)
    for e in range(n):
        r = iota((sz.shard_pad, d), 0)
        c = iota((sz.shard_pad, d), 1)
        pick = ((c == r + e * sz.shard) & (r < sz.shard)).astype(F32).astype(BF)
        sme[e, :, 0 : sz.shard_pad] = mm_nt(chip_small, pick).astype(BF)

    def small_peer(k):
        piece = sme.at[lax.rem(me + k, n), :, 0 : sz.shard_pad]
        return to_peer(piece, sme_r.at[k], s2_sem, k)

    for k in range(1, n):
        small_peer(k).start()
    stage2(2)
    stage3(1)
    stage4(0)
    acc = sme[me, :, 0 : sz.shard_pad].astype(F32)
    for k in range(1, n):
        small_peer(k).wait()
        acc = acc + sme_r[k].astype(F32)
    smz_r[0] = acc.astype(BF)
    for k in range(1, nz):
        to_z(smz_r.at[0], smz_r.at[k], s3_sem, k).start()
    stage2(3)
    stage3(2)
    stage4(1)

    for way in range(2):
        zz = z if way == 0 else nz - 1 - z
        target = me_r + 2 if way == 0 else me_r - 2

        @pl.when(zz >= 1)
        def _():
            here = landing(way, nz - 2, z)
            for cp in u_copies(u1.at[here], u2.at[here], way, nz - 2, target, here):
                cp.wait_recv()
            v1[z] = (v1[z].astype(F32) + u1[here].astype(F32)).astype(BF)
            v2[z] = (v2[z].astype(F32) + u2[here].astype(F32)).astype(BF)

    stores = [
        pltpu.make_async_copy(v1.at[z], o_w1, wsem.at[0]),
        pltpu.make_async_copy(v2.at[z], o_w2, wsem.at[1]),
    ]
    for cp in stores:
        cp.start()
    stage3(3)
    stage4(2)
    acc = smz_r[0].astype(F32)
    for k in range(1, nz):
        to_z(smz_r.at[0], smz_r.at[k], s3_sem, k).wait()
        acc = acc + smz_r[k].astype(F32)
    o_small[...] = acc
    stage4(3)
    for j in range(sz.chunks):
        stage5(j)

    for cp in stores:
        cp.wait()
    store.wait()
    for s in range(nz - 1):
        for way in range(2):
            zz = z if way == 0 else nz - 1 - z
            target = me_r + 2 if way == 0 else me_r - 2

            @pl.when(zz <= s)
            def _():
                for cp in u_copies(v1.at[0], v2.at[0], way, s, target, 0):
                    cp.wait_send()
    for k in range(1, n):
        for cp in small_sends(k):
            cp.wait_send()


def block(sz, tokens, routes, router, gains, biases, b1, b2, grad, wq, wp, w1, w2):
    vmem = pl.BlockSpec(memory_space=pltpu.VMEM)
    hbm = pl.BlockSpec(memory_space=pl.ANY)
    rows, d, slots, fs, nz, n = sz.rows, sz.d, sz.all_slots, sz.fs, sz.nz, sz.n_exp
    half = d // 2
    dma = pltpu.SemaphoreType.DMA
    outs = [
        ((sz.chunks, sz.shard, d), BF),
        ((sz.small, sz.shard_pad), F32),
        ((sz.tok, d), BF),
        ((sz.tok, d), BF),
        ((d, fs), BF),
        ((sz.fs_rows, d), BF),
        ((sz.pairs, sz.images * 2, sz.seq, sz.seq), BF),
        ((d, 4 * d), BF),
    ]
    buffers = [
        ((d, 4 * d), BF),
        (w2.shape, BF),
        ((sz.tok, d), BF),
        ((slots, d), BF),
        ((slots, d), BF),
        ((rows, 3 * d), BF),
        ((d, rows), BF),
        ((rows, d), F32),
        ((rows, d), BF),
        ((d, rows), BF),
        ((rows, sz.small), F32),
        ((sz.small, d), F32),
        ((rows, d), BF),
        ((sz.experts, rows, sz.slots), BF),
        ((n, sz.ep, sz.slots), F32),
        ((n, sz.ep, sz.slots), F32),
        ((n, *router.shape), BF),
        ((n, *gains.shape), BF),
        ((n, *biases.shape), BF),
        ((1, d), F32),
        ((d, slots - d), BF),
        ((d, d), BF),
        ((nz, slots, 2 * fs), BF),
        ((nz, slots, 2 * fs), BF),
        ((rows, d), F32),
        ((rows, d), F32),
        ((2 * slots, d), BF),
        ((slots, d), BF),
        ((slots, d), BF),
        ((n, 8, sz.slots), F32),
        ((n, 8, sz.slots), F32),
        ((sz.fs_rows, d), BF),
        ((nz, d, fs), BF),
        ((nz, sz.fs_rows, d), BF),
        ((nz + 1, d, fs), BF),
        ((nz + 1, sz.fs_rows, d), BF),
        ((2, 2 * sz.images, sz.seq, sz.seq), BF),
        ((n - 1, d, half), BF),
        ((sz.chunks, sz.shard, half), BF),
        ((nz - 1, sz.chunks, sz.part, half), BF),
        ((sz.small, d), F32),
        ((sz.small, d), BF),
        ((n + 1, sz.small, d), BF),
        ((n, sz.small, sz.shard_pad), BF),
        ((nz, sz.small, sz.shard_pad), BF),
    ]
    sems = (
        [dma((4,)), dma((2,))]
        + [dma((2, sz.chunks, 2, n)), dma((2, sz.chunks, n))]
        + [dma((2, sz.chunks, 2, n)), dma((sz.chunks, 3))]
        + [dma((3, 2, n))]
        + [dma((2, n))] * 3
        + [dma((2, 2, nz)), dma((2, 2, 2, nz - 1))]
        + [dma((2, n)), dma((2, d // 256, n)), dma((2, n))]
        + [dma((2, sz.chunks)), dma((2, sz.chunks, n))]
        + [dma((2, sz.chunks, nz))] * 2
        + [dma((2, sz.chunks)), dma((2,)), dma((2, n)), dma((2, nz))]
    )
    return pl.pallas_call(
        partial(block_kernel, sz),
        name="block",
        out_shape=[jax.ShapeDtypeStruct(s, t) for s, t in outs],
        in_specs=[vmem] * 7 + [hbm] * 5,
        out_specs=[vmem] * 2 + [hbm] * 6,
        scratch_shapes=[pltpu.VMEM(s, t) for s, t in buffers] + sems,
        compiler_params=pltpu.CompilerParams(
            collective_id=1, has_side_effects=True, vmem_limit_bytes=62 << 20
        ),
    )(tokens, routes, router, gains, biases, b1, b2, grad, wq, wp, w1, w2)


def plain_rest(sz, state, tokens, w1, b1, w2, b2):
    xr, dres, qkv, pall, ctx_t, resid, second, normed_t, probs, wq, wp, smf, gpad, comb = state
    d, n = sz.d, sz.experts
    scale = 1.0 / math.sqrt(HEAD_DIM)
    h = mm(xr, w1) + b1
    cdf, pdf = gelu_parts(h)
    act = (h * cdf).astype(BF)
    result = (mm(act, w2) + b2).astype(BF)
    dhid = (mm_nt(dres, w2) * (cdf + h * pdf)).astype(BF)
    row_grad = mm_nt(dhid, w1).astype(BF)
    swap = partial(
        lax.all_to_all, axis_name="exp", split_axis=0, concat_axis=0, tiled=True
    )
    ret = swap(result).reshape(n, sz.slots, d)
    bck = swap(row_grad).reshape(n, sz.slots, d)
    g32 = gpad.astype(F32)
    p = probs[:, 8 : 8 + n]
    picked = jnp.einsum("ets,esd->etd", comb, ret, preferred_element_type=F32)
    mixed = resid + jnp.einsum("te,etd->td", p, picked, precision="highest")
    pg = jnp.sum(g32[None] * picked, -1).T
    lg = (p * (pg - jnp.sum(pg * p, 1, keepdims=True))).astype(BF)
    sgrad = mm(lg, smf[8 : 8 + n].astype(BF))
    sgrad = sgrad + jnp.einsum("ets,esd->td", comb, bck, preferred_element_type=F32)
    back2, gain2, shift2 = normalize_back(resid, smf[1:2], sgrad)
    rgrad = g32 + back2
    low = rgrad.astype(BF)
    cgrad = mm_nt(low, wp).astype(BF)
    four = (sz.images, sz.seq, d // HEAD_DIM, HEAD_DIM)
    q, k, v, c = (
        a.reshape(four)
        for a in (qkv[:, :d], qkv[:, d : 2 * d], qkv[:, 2 * d :], cgrad)
    )
    prob = pall.reshape(sz.pairs, sz.images, 2, sz.seq, sz.seq)
    prob = prob.transpose(1, 0, 2, 3, 4).reshape(sz.images, -1, sz.seq, sz.seq)
    product = partial(jnp.einsum, preferred_element_type=F32)
    dv = product("ihst,ishd->ithd", prob, c).astype(BF)
    pb = product("ishd,ithd->ihst", c, v)
    p32 = prob.astype(F32)
    ds = (p32 * (pb - jnp.sum(pb * p32, -1, keepdims=True))).astype(BF)
    dq = (product("ihst,ithd->ishd", ds, k) * scale).astype(BF)
    dk = (product("ihst,ishd->ithd", ds, q) * scale).astype(BF)
    dqkv = jnp.concatenate([a.reshape(sz.rows, d) for a in (dq, dk, dv)], 1)
    x = mm(pad_matrix(sz), tokens)
    back1, gain1, shift1 = normalize_back(x, smf[0:1], mm_nt(dqkv, wq))
    gin = (rgrad + back1).astype(BF)
    sums = jnp.sum(dqkv.astype(F32), 0, keepdims=True)
    small = jnp.concatenate(
        [gain1, gain2, shift1, sums[:, :d], sums[:, 2 * d :]]
        + [jnp.sum(low.astype(F32), 0, keepdims=True), shift2, mm_tn(lg, second)]
    )

    def dense(grad, dim):
        total = lax.psum(grad.astype(BF), "rep")
        total = lax.psum_scatter(total, "exp", scatter_dimension=dim, tiled=True)
        return total.astype(F32)

    def owned(grad, dim):
        total = lax.psum_scatter(
            grad[None].astype(BF), "rep", scatter_dimension=dim, tiled=True
        )
        return total.astype(F32)

    def unpad(rows):
        return rows.reshape(sz.images, sz.seq, d)[:, :SEQ].reshape(sz.tok, d)

    sums = dense(small, 1)
    return (
        unpad(mixed.astype(BF)),
        unpad(gin),
        dense(mm(normed_t, dqkv), 0),
        dense(mm(ctx_t, low), 0),
        sums[7:].T,
        sums[0:2],
        sums[2:7],
        owned(mm_tn(xr, dhid), 2),
        owned(jnp.sum(dhid.astype(F32), 0), 1),
        owned(mm_tn(act, dres), 1),
        owned(jnp.sum(dres.astype(F32), 0), 1),
    )


def on_device(
    mesh,
    tokens,
    routes,
    out_grad,
    attn_qkv,
    attn_out,
    router,
    norm_gains,
    dense_biases,
    expert_in,
    expert_in_bias,
    expert_out,
    expert_out_bias,
):
    sz = Sizes(mesh, tokens.shape[0], tokens.shape[1], expert_in.shape[2])
    d, fs = sz.d, sz.fs
    w1, w2 = expert_in[0], expert_out[0]
    small = (router.T, norm_gains, dense_biases)
    if fs % 128 or sz.all_slots % 128 or sz.all_slots < 2 * sz.rows or sz.part % 16:
        state = front(sz, tokens, out_grad, routes.T, attn_qkv, attn_out, *small)
        bias1, bias2 = expert_in_bias.astype(F32), expert_out_bias.astype(F32)
        return plain_rest(sz, state, tokens, w1, bias1, w2, bias2)
    dense, sums, out, gin, g1, g2, _, _ = block(
        sz,
        tokens,
        routes.T,
        *small,
        expert_in_bias,
        expert_out_bias,
        out_grad,
        attn_qkv,
        attn_out,
        w1,
        w2,
    )
    return finish(sz, out, gin, g1, g2, dense, sums)


def solution(mesh):
    both = P(("rep", "exp"), None)
    rows = P("exp", None)
    cols = P(None, "exp")
    cube = P("exp", None, None)
    in_specs = (both, both, both, rows, rows, rows, cols, cols, cube, rows, cube, rows)
    out_specs = (
        both,
        both,
        rows,
        rows,
        rows,
        cols,
        cols,
        P("exp", None, "rep"),
        P("exp", "rep"),
        P("exp", "rep", None),
        P("exp", "rep"),
    )
    return jax.shard_map(
        partial(on_device, mesh),
        mesh=mesh,
        in_specs=in_specs,
        out_specs=out_specs,
        check_vma=False,
    )
```

```python
from functools import partial
import math

import jax
import jax.numpy as jnp
from jax import lax
from jax.experimental import pallas as pl
from jax.experimental.pallas import tpu as pltpu
from jax.sharding import PartitionSpec as P

HEAD_DIM = 64
SEQ = 197
EPS = 1e-06
BF = jnp.bfloat16
F32 = jnp.float32
MESH = pl.DeviceIdType.MESH


def up(value, step):
    return (value + step - 1) // step * step


def mm(a, b):
    return lax.dot_general(a, b, (((1,), (0,)), ((), ())), preferred_element_type=F32)


def mm_nt(a, b):
    return lax.dot_general(a, b, (((1,), (1,)), ((), ())), preferred_element_type=F32)


def mm_tn(a, b):
    return lax.dot_general(a, b, (((0,), (0,)), ((), ())), preferred_element_type=F32)


def iota(shape, dim):
    return lax.broadcasted_iota(jnp.int32, shape, dim)


def rows_at(index, size):
    return pl.ds(pl.multiple_of(index * size, size), size)


def normalize(values, gain, shift):
    center = values - jnp.mean(values, -1, keepdims=True)
    spread = jnp.mean(center * center, -1, keepdims=True)
    return center * lax.rsqrt(spread + EPS) * gain + shift


class Sizes:
    def __init__(self, mesh, tok_rows, width, ff):
        self.n_exp = mesh.shape["exp"]
        self.n_rep = mesh.shape["rep"]
        self.tok = tok_rows
        self.images = tok_rows // SEQ
        self.seq = up(SEQ, 16)
        self.rows = self.images * self.seq
        self.d = width
        self.ff = ff
        self.experts = self.n_exp
        self.cap = (18 * tok_rows + 8 * self.experts - 1) // (8 * self.experts)
        self.slots = up(self.cap, 16)
        self.all_slots = self.slots * self.experts
        self.shard = width // self.n_exp
        self.shard_pad = up(self.shard, 128)
        self.ep = up(self.experts, 8)
        self.small = up(8 + self.ep, 16)
        self.pairs = width // 128
        self.nz = self.n_rep // 2
        self.fs = ff // self.n_rep
        self.fs_rows = self.fs + 16
        self.groups = self.pairs // 2
        self.chunks = self.groups + 1


def pad_matrix(sz):
    row = iota((sz.rows, sz.tok), 0)
    col = iota((sz.rows, sz.tok), 1)
    want = jnp.full((sz.rows, sz.tok), -1, jnp.int32)
    for image in range(sz.images):
        inside = (row >= image * sz.seq) & (row < image * sz.seq + SEQ)
        want = jnp.where(inside, row - image * (sz.seq - SEQ), want)
    return (want == col).astype(F32).astype(BF)


def unpad_matrix(sz):
    row = iota((sz.tok, sz.rows), 0)
    col = iota((sz.tok, sz.rows), 1)
    want = row
    for image in range(1, sz.images):
        want = jnp.where(row >= image * SEQ, row + image * (sz.seq - SEQ), want)
    return (want == col).astype(F32).astype(BF)


def front_kernel(
    sz,
    tok_ref,
    grad_ref,
    routes_ref,
    wq_shard,
    wp_shard,
    router_ref,
    gains_ref,
    biases_ref,
    xr,
    dres,
    qkv,
    pall,
    ctx_t,
    resid,
    second,
    normed_t,
    probs,
    wq,
    wp,
    smf,
    gpad,
    comb,
    ctx,
    normed,
    pmat,
    gr,
    gater,
    xs,
    gs,
    gates,
    routers,
    gains,
    biases,
    wq_sem,
    wp_sem,
    zq_sem,
    zp_sem,
    cq_sem,
    cp_sem,
    sm_sem,
    g_sem,
    x_sem,
    ga_sem,
):
    me_r = lax.axis_index("rep")
    me = lax.axis_index("exp")
    n = sz.n_exp
    core = lax.rem(me_r, 2)
    sibling = me_r + 1 - 2 * core
    odd = lax.rem(lax.div(me_r, 2), 2)
    partner = me_r + 2 - 4 * odd

    barrier = pltpu.get_barrier_semaphore()
    for k in range(1, n):
        pl.semaphore_signal(
            barrier, inc=1, device_id=(me_r, lax.rem(me + k, n)), device_id_type=MESH
        )
    for rep in (sibling, partner):
        pl.semaphore_signal(barrier, inc=1, device_id=(rep, me), device_id_type=MESH)
    pl.semaphore_wait(barrier, n + 1)

    def remote(src, dst, send, recv, rep, exp):
        return pltpu.make_async_remote_copy(
            src_ref=src,
            dst_ref=dst,
            send_sem=send,
            recv_sem=recv,
            device_id=(rep, exp),
            device_id_type=MESH,
        )

    def to_peer(src, dst, sems, k):
        return remote(
            src, dst, sems.at[0, k], sems.at[1, k], me_r, lax.rem(me + k, n)
        )

    class Gather:
        def __init__(self, shard, full, width, peer_sem, layer_sem, twin_sem):
            self.shard, self.full = shard, full
            self.piece = width // 6
            self.peer_sem, self.layer_sem, self.twin_sem = peer_sem, layer_sem, twin_sem

        def cols(self, side, first, count):
            start = side * 3 * self.piece + first * self.piece
            return pl.ds(pl.multiple_of(start, 128), count * self.piece)

        def rows(self, k):
            return rows_at(lax.rem(me + n - k, n), sz.shard)

        def peer(self, k):
            cols = self.cols(core, odd, 2)
            return to_peer(
                self.shard.at[:, cols],
                self.full.at[rows_at(me, sz.shard), cols],
                self.peer_sem,
                k,
            )

        def layer(self, k, mine=True):
            part = 2 * odd if mine else 2 - 2 * odd
            piece = self.full.at[self.rows(k), self.cols(core, part, 1)]
            sem = self.layer_sem
            return remote(piece, piece, sem.at[0, k], sem.at[1, k], partner, me)

        def twin(self, k, late, side):
            first, count = (2 - 2 * odd, 1) if late else (odd, 2)
            piece = self.full.at[self.rows(k), self.cols(side, first, count)]
            sem = self.twin_sem
            return remote(
                piece, piece, sem.at[0, late, k], sem.at[1, late, k], sibling, me
            )

        def start(self):
            for k in range(1, n):
                self.peer(k).start()
            self.full[rows_at(me, sz.shard), :] = self.shard[...]

        def forward(self):
            for k in range(1, n):
                self.peer(k).wait_recv()
                self.layer(k).start()
                self.twin(k, 0, core).start()

        def finish(self):
            for k in range(1, n):
                self.layer(k, False).wait_recv()
                self.twin(k, 1, core).start()
            for k in range(1, n):
                for late in range(2):
                    self.twin(k, late, 1 - core).wait_recv()

        def drain(self):
            for k in range(1, n):
                self.peer(k).wait_send()
                self.layer(k).wait_send()
                for late in range(2):
                    self.twin(k, late, core).wait_send()

    gather_q = Gather(wq_shard, wq, 3 * sz.d, wq_sem, zq_sem, cq_sem)
    gather_p = Gather(wp_shard, wp, sz.d, wp_sem, zp_sem, cp_sem)

    def small_sends(k):
        return [
            to_peer(src, dst.at[me], sm_sem.at[i], k)
            for i, (src, dst) in enumerate(
                ((gains_ref, gains), (biases_ref, biases), (router_ref, routers))
            )
        ]

    for k in range(1, n):
        for cp in small_sends(k):
            cp.start()
    gather_q.start()
    gains[me] = gains_ref[...]
    biases[me] = biases_ref[...]
    routers[me] = router_ref[...]

    choice = (routes_ref[...].astype(F32) + 1.0).astype(BF)
    lines = mm_nt(choice, pad_matrix(sz)).astype(jnp.int32) - 1
    ids = iota((sz.ep, sz.rows), 0)
    oh1 = (lines[0:1, :] == ids).astype(F32)
    oh2 = (lines[1:2, :] == ids).astype(F32)
    before = (
        (iota((sz.rows, sz.rows), 0) < iota((sz.rows, sz.rows), 1))
        .astype(F32)
        .astype(BF)
    )
    pos1 = mm(oh1.astype(BF), before)
    pos2 = mm(oh2.astype(BF), before) + jnp.sum(oh1, 1, keepdims=True)
    place = oh1 * pos1 + oh2 * pos2
    kept = (oh1 + oh2 > 0.5) & (place < sz.cap - 0.5)
    slot = jnp.where(kept, place, -1.0).astype(jnp.int32)
    slot_ids = iota((sz.slots, sz.rows), 0)
    for e in range(sz.experts):
        pmat[e * sz.slots : (e + 1) * sz.slots, :] = (
            (slot_ids == slot[e : e + 1, :]).astype(F32).astype(BF)
        )
    eye = (iota((sz.rows, sz.rows), 0) == iota((sz.rows, sz.rows), 1)).astype(F32)
    slot_cols = mm_nt(eye.astype(BF), slot.astype(F32).astype(BF)).astype(jnp.int32)
    lane_ids = iota((sz.rows, sz.slots), 1)
    for e in range(sz.experts):
        comb[e] = (slot_cols[:, e : e + 1] == lane_ids).astype(F32).astype(BF)

    spread = pad_matrix(sz)
    gpad[...] = mm(spread, grad_ref[...]).astype(BF)
    for e in range(sz.experts):
        block = slice(e * sz.slots, (e + 1) * sz.slots)
        gs[block, :] = mm(pmat[block, :], gpad[...]).astype(BF)
    slots_me = rows_at(me, sz.slots)
    gr[slots_me, :] = gs[slots_me, :]

    x = mm(spread, tok_ref[...])
    for k in range(1, n):
        for cp in small_sends(k):
            cp.wait_recv()
    smf[...] = jnp.zeros_like(smf)
    for j in range(n):
        r = iota((sz.shard, sz.d), 0)
        c = iota((sz.shard, sz.d), 1)
        pick = (c == r + j * sz.shard).astype(F32).astype(BF)
        smf[0:2, :] += mm(gains[j], pick)
        smf[2:7, :] += mm(biases[j], pick)
        smf[8 : 8 + sz.experts, :] += mm(routers[j], pick)
    normed[...] = normalize(x, smf[0:1, :], smf[2:3, :]).astype(BF)
    normed_t[...] = normed[...].T

    gather_q.forward()
    gather_p.start()
    gather_q.finish()
    for j, bias_row in ((0, 3), (1, None), (2, 4)):
        cols = slice(j * sz.d, (j + 1) * sz.d)
        out = mm(normed[...], wq[:, cols])
        if bias_row is not None:
            out = out + smf[bias_row : bias_row + 1, :]
        qkv[:, cols] = out.astype(BF)
    for k in range(1, n):
        dst = rows_at(lax.rem(me + k, n), sz.slots)
        to_peer(gs.at[dst, :], gr.at[slots_me, :], g_sem, k).start()

    scale = 1.0 / math.sqrt(HEAD_DIM)
    lane = iota((sz.seq, 128), 1)
    live = iota((sz.seq, sz.seq), 1) < SEQ

    def pair_step(pair, carry):
        for image in range(sz.images):
            rows = slice(image * sz.seq, (image + 1) * sz.seq)
            q2 = qkv[rows, pl.ds(pl.multiple_of(pair * 128, 128), 128)]
            k2 = qkv[rows, pl.ds(pl.multiple_of(sz.d + pair * 128, 128), 128)]
            v2 = qkv[rows, pl.ds(pl.multiple_of(2 * sz.d + pair * 128, 128), 128)]
            total = jnp.zeros((sz.seq, 128), F32)
            for half in range(2):
                mask = (lane >= half * 64) & (lane < half * 64 + 64)
                s = mm_nt(jnp.where(mask, q2, jnp.zeros_like(q2)), k2) * scale
                s = jnp.where(live, s, -1e30)
                e = jnp.exp(s - jnp.max(s, -1, keepdims=True))
                p = (e / jnp.sum(e, -1, keepdims=True)).astype(BF)
                pall[pair, image * 2 + half] = p
                total = total + mm(p, jnp.where(mask, v2, jnp.zeros_like(v2)))
            ctx[rows, pl.ds(pl.multiple_of(pair * 128, 128), 128)] = total.astype(BF)
        return carry

    lax.fori_loop(0, sz.pairs, pair_step, 0)

    gather_p.forward()
    gather_p.finish()
    res = (
        mm(spread, tok_ref[...])
        + mm(ctx[...], wp[...])
        + smf[5:6, :]
    )
    resid[...] = res
    low = normalize(res, smf[1:2, :], smf[6:7, :]).astype(BF)
    second[...] = low

    for e in range(sz.experts):
        block = slice(e * sz.slots, (e + 1) * sz.slots)
        xs[block, :] = mm(pmat[block, :], second[...]).astype(BF)
    for k in range(1, n):
        dst = rows_at(lax.rem(me + k, n), sz.slots)
        to_peer(xs.at[dst, :], xr.at[slots_me, :], x_sem, k).start()
    xr[slots_me, :] = xs[slots_me, :]

    small_low = smf[...].astype(BF)
    logit_rows = mm_nt(small_low, low)[8 : 8 + sz.ep, :]
    logit_rows = jnp.where(iota((sz.ep, sz.rows), 0) < sz.experts, logit_rows, -1e30)
    e_rows = jnp.exp(logit_rows - jnp.max(logit_rows, 0, keepdims=True))
    prob_rows = e_rows / jnp.sum(e_rows, 0, keepdims=True)
    hi = prob_rows.astype(BF)
    left = prob_rows - hi.astype(F32)
    mid = left.astype(BF)
    low3 = (left - mid.astype(F32)).astype(BF)
    for e in range(sz.experts):
        block = pmat[e * sz.slots : (e + 1) * sz.slots, :]
        gates[e] = mm_nt(hi, block) + mm_nt(mid, block) + mm_nt(low3, block)
    for k in range(1, n):
        to_peer(
            gates.at[lax.rem(me + k, n)], gater.at[me], ga_sem, k
        ).start()
    gater[me] = gates[me]
    logit_cols = mm_nt(low, small_low)
    col = iota((sz.rows, sz.small), 1)
    logit_cols = jnp.where((col >= 8) & (col < 8 + sz.experts), logit_cols, -1e30)
    e_cols = jnp.exp(logit_cols - jnp.max(logit_cols, 1, keepdims=True))
    probs[...] = e_cols / jnp.sum(e_cols, 1, keepdims=True)

    ctx_t[...] = ctx[...].T

    for k in range(1, n):
        src = lax.rem(me + n - k, n)
        dst = rows_at(lax.rem(me + k, n), sz.slots)
        theirs = rows_at(src, sz.slots)
        to_peer(gs.at[dst, :], gr.at[theirs, :], g_sem, k).wait()
        to_peer(gates.at[lax.rem(me + k, n)], gater.at[src], ga_sem, k).wait()
    square = iota((sz.slots, sz.slots), 0) == iota((sz.slots, sz.slots), 1)
    for j in range(n):
        block = slice(j * sz.slots, (j + 1) * sz.slots)
        row = gater[j, pl.ds(me, 1), :]
        gate = jnp.sum(jnp.where(square, row, 0.0), 1, keepdims=True)
        dres[block, :] = (gate * gr[block, :].astype(F32)).astype(BF)
    for k in range(1, n):
        src = lax.rem(me + n - k, n)
        dst = rows_at(lax.rem(me + k, n), sz.slots)
        theirs = rows_at(src, sz.slots)
        to_peer(xs.at[dst, :], xr.at[theirs, :], x_sem, k).wait()
        for cp in small_sends(k):
            cp.wait_send()
    gather_q.drain()
    gather_p.drain()


def front(sz, tokens, grad, routes, wq, wp, router, gains, biases):
    vmem = pl.BlockSpec(memory_space=pltpu.VMEM)
    rows, d, slots, n = sz.rows, sz.d, sz.all_slots, sz.n_exp
    outs = [
        ((slots, d), BF),
        ((slots, d), BF),
        ((rows, 3 * d), BF),
        ((sz.pairs, sz.images * 2, sz.seq, sz.seq), BF),
        ((d, rows), BF),
        ((rows, d), F32),
        ((rows, d), BF),
        ((d, rows), BF),
        ((rows, sz.small), F32),
        ((d, 3 * d), BF),
        ((d, d), BF),
        ((sz.small, d), F32),
        ((rows, d), BF),
        ((sz.experts, rows, sz.slots), BF),
    ]
    dma = pltpu.SemaphoreType.DMA
    sems = [dma((2, n))] * 4 + [dma((2, 2, n))] * 2 + [dma((3, 2, n))] + [dma((2, n))] * 3
    return pl.pallas_call(
        partial(front_kernel, sz),
        name="front",
        out_shape=[jax.ShapeDtypeStruct(s, t) for s, t in outs],
        in_specs=[vmem] * 8,
        out_specs=[vmem] * len(outs),
        scratch_shapes=[
            pltpu.VMEM((rows, d), BF),
            pltpu.VMEM((rows, d), BF),
            pltpu.VMEM((slots, rows), BF),
            pltpu.VMEM((slots, d), BF),
            pltpu.VMEM((n, sz.ep, sz.slots), F32),
            pltpu.VMEM((slots, d), BF),
            pltpu.VMEM((slots, d), BF),
            pltpu.VMEM((n, sz.ep, sz.slots), F32),
            pltpu.VMEM((n, *router.shape), BF),
            pltpu.VMEM((n, *gains.shape), BF),
            pltpu.VMEM((n, *biases.shape), BF),
        ]
        + sems,
        compiler_params=pltpu.CompilerParams(
            collective_id=0, has_side_effects=True, vmem_limit_bytes=56 << 20
        ),
    )(tokens, grad, routes, wq, wp, router, gains, biases)


def finish_kernel(sz, out, gin, g1, g2, dense, sg, *refs):
    o_out, o_gin, o_qkv, o_proj, o_router, o_gains, o_biases, o_w1, o_b1, o_w2, o_b2 = refs
    o_out[...] = out[...]
    o_gin[...] = gin[...]
    fs, sh = sz.fs, sz.shard
    o_w1[0] = g1[...].astype(F32)
    o_w2[0] = g2[0:fs, :].astype(F32)
    o_b1[...] = g2[fs : fs + 16, :].astype(F32)[0:1, 0:fs]
    own = o_b2.shape[1]
    first = lax.axis_index("rep") * own
    pick = iota((sz.d, own), 0) == iota((sz.d, own), 1) + first
    o_b2[...] = mm(g2[fs : fs + 16, :], pick.astype(F32).astype(BF))[1:2, :]
    o_proj[...] = dense[0].astype(F32)
    for g in range(sz.groups):
        for j in range(3):
            cols = slice(j * sz.d + g * 256, j * sz.d + (g + 1) * 256)
            o_qkv[:, cols] = dense[g + 1, :, j * 256 : (j + 1) * 256].astype(F32)
    o_router[...] = sg[8 : 8 + sz.experts, 0:sh]
    o_gains[...] = sg[0:2, 0:sh]
    o_biases[...] = sg[2:7, 0:sh]


def finish(sz, out, gin, g1, g2, dense, sg):
    vmem = pl.BlockSpec(memory_space=pltpu.VMEM)
    d, fs, sh = sz.d, sz.fs, sz.shard
    outs = [
        ((sz.tok, d), BF),
        ((sz.tok, d), BF),
        ((sh, 3 * d), F32),
        ((sh, d), F32),
        ((sz.experts, sh), F32),
        ((2, sh), F32),
        ((5, sh), F32),
        ((1, d, fs), F32),
        ((1, fs), F32),
        ((1, fs, d), F32),
        ((1, d // sz.n_rep), F32),
    ]
    grads = pl.pallas_call(
        partial(finish_kernel, sz),
        name="finish",
        out_shape=[jax.ShapeDtypeStruct(s, t) for s, t in outs],
        in_specs=[vmem] * 6,
        out_specs=[vmem] * len(outs),
        compiler_params=pltpu.CompilerParams(vmem_limit_bytes=62 << 20),
    )(out, gin, g1, g2, dense, sg)
    return (*grads[:4], grads[4].T, *grads[5:])


def normalize_back(values, gain, cot):
    center = values - jnp.mean(values, -1, keepdims=True)
    spread = jnp.mean(center * center, -1, keepdims=True)
    inv = lax.rsqrt(spread + EPS)
    unit = center * inv
    scaled = cot * gain
    grad = inv * (
        scaled
        - jnp.mean(scaled, -1, keepdims=True)
        - unit * jnp.mean(scaled * unit, -1, keepdims=True)
    )
    return grad, jnp.sum(cot * unit, 0, keepdims=True), jnp.sum(cot, 0, keepdims=True)


def gelu_parts(h):
    t = 1.0 / (1.0 + (0.3275911 / math.sqrt(2.0)) * jnp.abs(h))
    bell = jnp.exp(-0.5 * h * h)
    poly = t * (
        0.127414796
        + t * (-0.142248368 + t * (0.7107068705 + t * (-0.7265760135 + t * 0.5307027145)))
    )
    tail = poly * bell
    return jnp.where(h >= 0, 1.0 - tail, tail), bell * (1.0 / math.sqrt(2.0 * math.pi))


def block_kernel(
    sz,
    tok_hbm,
    routes_hbm,
    router_ref,
    gains_ref,
    biases_ref,
    b1_hbm,
    b2_hbm,
    grad_hbm,
    wq_shard,
    wp_shard,
    w1_hbm,
    w2_hbm,
    o_dense,
    o_small,
    o_out,
    o_gin,
    o_w1,
    o_w2,
    o_probs,
    o_save,
    tok_ref,
    routes_ref,
    b1_ref,
    b2_ref,
    od,
    dw,
    w2,
    stage,
    xr,
    dres,
    qkv,
    ctx_t,
    resid,
    second,
    normed_t,
    probs,
    smf,
    gpad,
    comb,
    gater,
    gates,
    routers,
    gains,
    biases,
    bias2,
    xt,
    xta,
    acts,
    dhids,
    wide1,
    wide2,
    sends,
    ret,
    bck,
    qs,
    qr,
    t2,
    v1,
    v2,
    u1,
    u2,
    pbuf,
    r2,
    z1,
    z2,
    sm,
    smr,
    sme,
    sme_r,
    smz_r,
    isem,
    wsem,
    psem,
    f_sem,
    l_sem,
    c_sem,
    o_sem,
    sm_sem,
    g_sem,
    x_sem,
    ga_sem,
    t_sem,
    u_sem,
    ret_sem,
    bck_sem,
    q_sem,
    d1_sem,
    d2_sem,
    z1_sem,
    z2_sem,
    z3_sem,
    s1_sem,
    s2_sem,
    s3_sem,
):
    me_r = lax.axis_index("rep")
    me = lax.axis_index("exp")
    n, nz, fs, d = sz.n_exp, sz.nz, sz.fs, sz.d
    core = lax.rem(me_r, 2)
    z = lax.div(me_r, 2)
    sibling = me_r + 1 - 2 * core
    odd = lax.rem(z, 2)
    partner = me_r + 2 - 4 * odd

    loads = [
        pltpu.make_async_copy(src, dst, isem.at[i])
        for i, (src, dst) in enumerate(
            (
                (tok_hbm, tok_ref),
                (gains_ref, gains.at[me]),
                (biases_ref, biases.at[me]),
                (router_ref, routers.at[me]),
                (routes_hbm, routes_ref),
                (b1_hbm, b1_ref),
                (b2_hbm, b2_ref),
            )
        )
    ]
    for cp in loads:
        cp.start()
    load_grad = pltpu.make_async_copy(grad_hbm, stage, wsem.at[0])
    load_grad.start()
    load_w2 = pltpu.make_async_copy(w2_hbm, w2, wsem.at[1])
    load_w2.start()

    barrier = pltpu.get_barrier_semaphore()
    for k in range(1, n):
        pl.semaphore_signal(
            barrier, inc=1, device_id=(me_r, lax.rem(me + k, n)), device_id_type=MESH
        )
    for k in range(1, nz):
        pl.semaphore_signal(
            barrier,
            inc=1,
            device_id=(lax.rem(me_r + 2 * k, 2 * nz), me),
            device_id_type=MESH,
        )
    pl.semaphore_signal(barrier, inc=1, device_id=(sibling, me), device_id_type=MESH)
    pl.semaphore_wait(barrier, n - 1 + nz)

    def remote(src, dst, send, recv, rep, exp):
        return pltpu.make_async_remote_copy(
            src_ref=src,
            dst_ref=dst,
            send_sem=send,
            recv_sem=recv,
            device_id=(rep, exp),
            device_id_type=MESH,
        )

    def to_peer(src, dst, sems, k):
        return remote(
            src, dst, sems.at[0, k], sems.at[1, k], me_r, lax.rem(me + k, n)
        )

    def to_z(src, dst, sems, k):
        return remote(
            src, dst, sems.at[0, k], sems.at[1, k], lax.rem(me_r + 2 * k, 2 * nz), me
        )

    normed = acts.at[nz - 1, sz.slots : sz.slots + sz.rows, :]
    ctx = xta.at[0 : sz.rows, :]
    res_send = sends.at[0 : sz.all_slots, :]
    row_send = sends.at[sz.all_slots : 2 * sz.all_slots, :]
    xs, gs = res_send, row_send

    piece = 128

    def shard_cols(g, tile):
        if isinstance(g, int) and g == sz.groups:
            return wp_shard, tile * piece
        return wq_shard, lax.div(tile, 2) * d + g * 256 + lax.rem(tile, 2) * piece

    def dw_cols(g, tile, count):
        return pl.ds(pl.multiple_of(g * d + tile * piece, 128), count * piece)

    def dw_rows(k):
        return rows_at(lax.rem(me + n - k, n), sz.shard)

    def fetch(g, i, k):
        tile = 3 * core + odd + i
        shard, start = shard_cols(g, tile)
        return remote(
            shard.at[:, pl.ds(pl.multiple_of(start, 128), piece)],
            dw.at[rows_at(me, sz.shard), dw_cols(g, tile, 1)],
            f_sem.at[0, g, i, k],
            f_sem.at[1, g, i, k],
            me_r,
            lax.rem(me + k, n),
        )

    def fetched(g, i, k):
        ref = dw.at[dw_rows(k), dw_cols(g, 3 * core + odd + i, 1)]
        return remote(
            ref,
            ref,
            f_sem.at[0, g, i, k],
            f_sem.at[1, g, i, k],
            me_r,
            lax.rem(me + k, n),
        )

    def layer(g, k, mine):
        part = 2 * odd if mine else 2 - 2 * odd
        ref = dw.at[dw_rows(k), dw_cols(g, 3 * core + part, 1)]
        return remote(ref, ref, l_sem.at[0, g, k], l_sem.at[1, g, k], partner, me)

    def twin(g, k, late, side):
        first, count = (2 - 2 * odd, 1) if late else (odd, 2)
        ref = dw.at[dw_rows(k), dw_cols(g, 3 * side + first, count)]
        return remote(
            ref, ref, c_sem.at[0, g, late, k], c_sem.at[1, g, late, k], sibling, me
        )

    def own_part(g, j):
        if isinstance(g, int) and g == sz.groups:
            src = wp_shard.at[:, j * 256 : (j + 1) * 256]
        else:
            src = wq_shard.at[:, pl.ds(pl.multiple_of(j * d + g * 256, 128), 256)]
        dst = dw.at[
            rows_at(me, sz.shard), pl.ds(pl.multiple_of(g * d + j * 256, 128), 256)
        ]
        return pltpu.make_async_copy(src, dst, o_sem.at[g, j])

    def start_weights(g):
        for k in range(1, n):
            for i in range(2):
                fetch(g, i, k).start()
        for j in range(3):
            own_part(g, j).start()

    def forward_weights(g):
        for k in range(1, n):
            for i in range(2):
                fetched(g, i, k).wait_recv()
            layer(g, k, True).start()
            twin(g, k, 0, core).start()

    def finish_weights(g):
        for j in range(3):
            own_part(g, j).wait()
        for k in range(1, n):
            layer(g, k, False).wait_recv()
            twin(g, k, 1, core).start()
        for k in range(1, n):
            for late in range(2):
                twin(g, k, late, 1 - core).wait_recv()

    def drain_weights(g):
        for k in range(1, n):
            for i in range(2):
                fetch(g, i, k).wait_send()
            layer(g, k, True).wait_send()
            for late in range(2):
                twin(g, k, late, core).wait_send()

    def small_sends(k):
        return [
            to_peer(src, dst.at[me], sm_sem.at[i], k)
            for i, (src, dst) in enumerate(
                ((gains_ref, gains), (biases_ref, biases), (router_ref, routers))
            )
        ]

    for k in range(1, n):
        for cp in small_sends(k):
            cp.start()
    for g in range(sz.groups + 1):
        start_weights(g)
    loads[0].wait()
    wide1[...] = mm(pad_matrix(sz), tok_ref[...])
    for cp in loads[1:]:
        cp.wait()
    for k in range(1, n):
        for cp in small_sends(k):
            cp.wait_recv()
    smf[...] = jnp.zeros_like(smf)
    for j in range(n):
        r = iota((sz.shard, d), 0)
        c = iota((sz.shard, d), 1)
        pick = (c == r + j * sz.shard).astype(F32).astype(BF)
        smf[0:2, :] += mm(gains[j], pick)
        smf[2:7, :] += mm(biases[j], pick)
        smf[8 : 8 + sz.experts, :] += mm(routers[j], pick)
    normed[...] = normalize(wide1[...], smf[0:1, :], smf[2:3, :]).astype(BF)
    forward_weights(0)
    choice = (routes_ref[...].astype(F32) + 1.0).astype(BF)
    lines = mm_nt(choice, pad_matrix(sz)).astype(jnp.int32) - 1
    ids = iota((sz.ep, sz.rows), 0)
    oh1 = (lines[0:1, :] == ids).astype(F32)
    oh2 = (lines[1:2, :] == ids).astype(F32)
    before = (
        (iota((sz.rows, sz.rows), 0) < iota((sz.rows, sz.rows), 1))
        .astype(F32)
        .astype(BF)
    )
    pos1 = mm(oh1.astype(BF), before)
    pos2 = mm(oh2.astype(BF), before) + jnp.sum(oh1, 1, keepdims=True)
    place = oh1 * pos1 + oh2 * pos2
    kept = (oh1 + oh2 > 0.5) & (place < sz.cap - 0.5)
    slot = jnp.where(kept, place, -1.0).astype(jnp.int32)
    slot_ids = iota((sz.slots, sz.rows), 0)

    def picks(e):
        return (slot_ids == slot[e : e + 1, :]).astype(F32).astype(BF)

    forward_weights(1)

    load_grad.wait()
    gpad[...] = mm(pad_matrix(sz), stage[...]).astype(BF)
    slots_me = rows_at(me, sz.slots)

    def at_peer(k):
        return slice(k * sz.slots, (k + 1) * sz.slots)

    def picks_for(k):
        line = slot[0:1, :]
        for e in range(1, sz.experts):
            line = jnp.where(lax.rem(me + k, n) == e, slot[e : e + 1, :], line)
        return (slot_ids == line).astype(F32).astype(BF)

    for k in range(n):
        gs[at_peer(k), :] = mm(picks_for(k), gpad[...]).astype(BF)
    dres[at_peer(0), :] = gs[at_peer(0), :]
    forward_weights(2)
    for k in range(1, n):
        to_peer(gs.at[at_peer(k), :], dres.at[at_peer(n - k), :], g_sem, k).start()

    scale = 1.0 / math.sqrt(HEAD_DIM)
    half_lane = iota((sz.seq, 128), 1)
    live = iota((sz.seq, sz.seq), 1) < SEQ

    def pair_cols(pair, j, base=None):
        group = lax.div(pair, 2) * d if base is None else base
        start = group + j * 256 + lax.rem(pair, 2) * 128
        return pl.ds(pl.multiple_of(start, 128), 128)

    def save_probs(pair):
        slot = lax.rem(pair, 2)
        return pltpu.make_async_copy(pbuf.at[slot], o_probs.at[pair], psem.at[slot])

    def forward_pair(pair, carry):
        @pl.when(pair >= 2)
        def _():
            save_probs(pair - 2).wait()

        for image in range(sz.images):
            rows = slice(image * sz.seq, (image + 1) * sz.seq)
            q2, k2, v2_ = (qkv[rows, pair_cols(pair, j)] for j in range(3))
            total = jnp.zeros((sz.seq, 128), F32)
            for half in range(2):
                mask = (half_lane >= half * 64) & (half_lane < half * 64 + 64)
                zero = jnp.zeros_like(q2)
                s = mm_nt(jnp.where(mask, q2 * jnp.asarray(scale, BF), zero), k2)
                s = jnp.where(live, s, -1e30)
                e = jnp.exp(s - jnp.max(s, -1, keepdims=True))
                p = (e * (1.0 / jnp.sum(e, -1, keepdims=True))).astype(BF)
                pbuf[lax.rem(pair, 2), image * 2 + half] = p
                total = total + mm(p, jnp.where(mask, v2_, zero))
            ctx[rows, pl.ds(pl.multiple_of(pair * 128, 128), 128)] = total.astype(BF)
        save_probs(pair).start()
        return carry

    def forward_group(g, carry):
        finish_weights(g)
        cols = pl.ds(pl.multiple_of(g * d, 128), d)
        of_bias = pl.ds(pl.multiple_of(g * 256, 128), 256)
        bias = jnp.concatenate(
            [smf[3:4, of_bias], jnp.zeros((1, 256), F32), smf[4:5, of_bias]], 1
        )
        qkv[:, cols] = (mm(normed[...], dw[:, cols]) + bias).astype(BF)
        lax.fori_loop(2 * g, 2 * g + 2, forward_pair, 0)

        @pl.when(g == 0)
        def _():
            forward_weights(sz.groups)

        return carry

    lax.fori_loop(0, sz.groups, forward_group, 0)
    finish_weights(sz.groups)
    save = pltpu.make_async_copy(dw, o_save, wsem.at[2])
    save.start()
    res = (
        wide1[...]
        + mm(ctx[...], dw[:, 3 * d : 4 * d])
        + smf[5:6, :]
    )
    resid[...] = res
    second[...] = normalize(res, smf[1:2, :], smf[6:7, :]).astype(BF)
    for k in [*range(1, n), 0]:
        xs[at_peer(k), :] = mm(picks_for(k), second[...]).astype(BF)
        if k:
            to_peer(xs.at[at_peer(k), :], xr.at[at_peer(n - k), :], x_sem, k).start()
        else:
            xr[at_peer(0), :] = xs[at_peer(0), :]
    small_low = smf[...].astype(BF)
    low = second[...]
    logit_rows = mm_nt(small_low, low)[8 : 8 + sz.ep, :]
    logit_rows = jnp.where(iota((sz.ep, sz.rows), 0) < sz.experts, logit_rows, -1e30)
    e_rows = jnp.exp(logit_rows - jnp.max(logit_rows, 0, keepdims=True))
    prob_rows = e_rows / jnp.sum(e_rows, 0, keepdims=True)
    hi = prob_rows.astype(BF)
    left = prob_rows - hi.astype(F32)
    mid = left.astype(BF)
    rest_low = (left - mid.astype(F32)).astype(BF)
    for e in range(sz.experts):
        block = picks(e)
        gates[e] = mm_nt(hi, block) + mm_nt(mid, block) + mm_nt(rest_low, block)
    for k in range(1, n):
        to_peer(gates.at[lax.rem(me + k, n)], gater.at[n - k], ga_sem, k).start()
    gater[0] = gates[me]
    for g in range(sz.groups + 1):
        drain_weights(g)
    save.wait()
    load_w1 = pltpu.make_async_copy(w1_hbm, dw, wsem.at[0])
    load_w1.start()
    normed_t[...] = normed[...].T
    ctx_t[...] = ctx[...].T
    eye = (iota((sz.rows, sz.rows), 0) == iota((sz.rows, sz.rows), 1)).astype(F32)
    slot_cols = mm_nt(eye.astype(BF), slot.astype(F32).astype(BF)).astype(jnp.int32)
    lane_ids = iota((sz.rows, sz.slots), 1)
    for e in range(sz.experts):
        comb[e] = (slot_cols[:, e : e + 1] == lane_ids).astype(F32).astype(BF)
    logit_cols = mm_nt(low, small_low)
    col = iota((sz.rows, sz.small), 1)
    logit_cols = jnp.where((col >= 8) & (col < 8 + sz.experts), logit_cols, -1e30)
    e_cols = jnp.exp(logit_cols - jnp.max(logit_cols, 1, keepdims=True))
    probs[...] = e_cols / jnp.sum(e_cols, 1, keepdims=True)
    for pair in range(max(sz.pairs - 2, 0), sz.pairs):
        save_probs(pair).wait()

    lower = 1 - lax.div(z, (nz + 1) // 2)
    span = 2 * fs
    per = span // 256
    everyone, others = slice(0, sz.all_slots), slice(sz.slots, sz.all_slots)
    square = iota((sz.slots, sz.slots), 0) == iota((sz.slots, sz.slots), 1)
    bias2[...] = jnp.zeros_like(bias2)
    half_own = pl.ds(pl.multiple_of(core * fs, 128), fs)
    half_other = pl.ds(pl.multiple_of((1 - core) * fs, 128), fs)

    def dest_of(i):
        return lower * (nz - 1 - i) + (1 - lower) * i

    def hidden_at(i, first, size):
        return pl.ds(pl.multiple_of(dest_of(i) * span + first, 128), size)

    def prepare(k):
        rows = at_peer(k)
        if k:
            j = n - k
            to_peer(gs.at[at_peer(j), :], dres.at[rows, :], g_sem, j).wait()
            to_peer(gates.at[lax.rem(me + j, n)], gater.at[k], ga_sem, j).wait()
        row = gater[k, pl.ds(me, 1), :]
        gate = jnp.sum(jnp.where(square, row, 0.0), 1, keepdims=True)
        value = (gate * dres[rows, :].astype(F32)).astype(BF)
        dres[rows, :] = value
        bias2[...] += jnp.sum(value.astype(F32), 0, keepdims=True)

    def cell(t, rows):
        i, c = lax.div(t, per), lax.rem(t, per)
        hidden = hidden_at(i, c * 256, 256)
        here = pl.ds(pl.multiple_of(c * 256, 128), 256)
        h = mm(xr[rows, :], dw[:, hidden]) + b1_ref[:, hidden].astype(F32)
        cdf, pdf = gelu_parts(h)
        da = mm_nt(dres[rows, :], w2[hidden, :])
        acts[i, rows, here] = (h * cdf).astype(BF)
        dhids[i, rows, here] = (da * (cdf + h * pdf)).astype(BF)

    def cells(first, last, rows):
        lax.fori_loop(first * per, last * per, lambda t, c: (cell(t, rows), c)[1], 0)

    def row_copy(c, k, land):
        cols = pl.ds(pl.multiple_of(c * 256, 128), 256)
        return remote(
            row_send.at[at_peer(k), cols],
            bck.at[land, cols],
            bck_sem.at[0, c, k],
            bck_sem.at[1, c, k],
            me_r,
            lax.rem(me + k, n),
        )

    def back_rows(c, carry):
        cols = pl.ds(pl.multiple_of(c * 256, 128), 256)
        total = mm_nt(dhids[0], dw[cols, hidden_at(0, 0, span)])
        for i in range(1, nz):
            total = total + mm_nt(dhids[i], dw[cols, hidden_at(i, 0, span)])
        row_send[:, cols] = total.astype(BF)
        for k in range(1, n):
            row_copy(c, k, slots_me).start()
        bck[slots_me, cols] = row_send[at_peer(0), cols]
        return carry

    def back_results(c, column):
        cols = pl.ds(pl.multiple_of(c * 256, 128), 256)
        total = mm(acts[0], w2[hidden_at(0, 0, span), cols])
        for i in range(1, nz):
            total = total + mm(acts[i], w2[hidden_at(i, 0, span), cols])
        out = (total + b2_ref[:, cols].astype(F32)).astype(BF)
        res_send[:, cols] = out
        return column + jnp.sum(
            out.astype(F32) * dres[:, cols].astype(F32), 1, keepdims=True
        )

    parts1 = [slice(i, i + d // 2) for i in (0, d // 2)]
    parts2 = range(0, fs, 128)

    def grad1(i, half, rows):
        part = mm(xta[rows, :], dhids[i, 0:d, half])
        return part + mm(xt[rows, :], dhids[i, d:, half])

    def grad2(i, start, first):
        cols = pl.ds(pl.multiple_of(start + first, 128), 128)
        return mm_tn(acts[i, :, cols], dres[...])

    def extra(i, half):
        gb = jnp.sum(dhids[i, :, half].astype(F32), 0, keepdims=True)
        row = iota((16, d), 0)
        line = jnp.concatenate([gb, jnp.zeros((1, d - fs), F32)], 1)
        return jnp.where(row == 0, line, jnp.where(row == 1, bias2[...], 0.0))

    def leaving(i):
        return r2.at[0] if isinstance(i, int) else acts.at[i, 0:d, half_other]

    def t_copies(i):
        dest = dest_of(i)
        return (
            remote(leaving(i), v1.at[dest], t_sem.at[0, 0, dest], t_sem.at[1, 0, dest], sibling, me),
            remote(t2, v2.at[dest], t_sem.at[0, 1, dest], t_sem.at[1, 1, dest], sibling, me),
        )

    def landing(way, step, at):
        if way == 0:
            return nz - 2 - step + at
        return at + step + 2 - nz if step < nz - 2 else nz

    def u_copies(src1, src2, way, step, target, slot):
        return (
            remote(src1, u1.at[slot], u_sem.at[0, 0, way, step], u_sem.at[1, 0, way, step], target, me),
            remote(src2, u2.at[slot], u_sem.at[0, 1, way, step], u_sem.at[1, 1, way, step], target, me),
        )

    def other_grads(i):
        for first in parts2:
            value = grad2(i, (1 - core) * fs, first)
            t2[first : first + 128, :] = value.astype(BF)
        t2[fs:, :] = extra(i, half_other).astype(BF)
        t_copies(i)[1].start()
        if isinstance(i, int):
            xta[...] = xr[0:d, :].T
            xt[...] = xr[d:, :].T
        for rows in parts1:
            leaving(i)[rows, :] = grad1(i, half_other, rows).astype(BF)
        t_copies(i)[0].start()

    def own_grads(i):
        dest = dest_of(i)
        t_copies(i)[1].wait()
        for first in parts2:
            rows = slice(first, first + 128)
            value = v2[dest, rows, :].astype(F32) + grad2(i, core * fs, first)
            v2[dest, rows, :] = value.astype(BF)
        v2[dest, fs:, :] = (v2[dest, fs:, :].astype(F32) + extra(i, half_own)).astype(BF)
        leave(i, 1)
        t_copies(i)[0].wait()
        for rows in parts1:
            value = v1[dest, rows, :].astype(F32) + grad1(i, half_own, rows)
            v1[dest, rows, :] = value.astype(BF)
        leave(i, 0)

    def leave(i, which):
        dest = dest_of(i)

        @pl.when((z == 0) & (i <= nz - 2))
        def _():
            u_copies(v1.at[dest], v2.at[dest], 0, i, me_r + 2, dest)[which].start()

        @pl.when((z == nz - 1) & (i < nz - 2))
        def _():
            u_copies(v1.at[dest], v2.at[dest], 1, i, me_r - 2, dest)[which].start()

        @pl.when((z == nz - 1) & (i == nz - 2))
        def _():
            u_copies(v1.at[dest], v2.at[dest], 1, i, me_r - 2, nz)[which].start()

    def z_round(s, which):
        v, u = ((v1, u1), (v2, u2))[which]
        for way in range(2):
            zz = z if way == 0 else nz - 1 - z
            dest = nz - 1 - s + zz if way == 0 else z - (nz - 1 - s)
            target = me_r + 2 if way == 0 else me_r - 2

            @pl.when((zz >= 1) & (zz <= s))
            def _():
                here = landing(way, s - 1, z)
                there = landing(way, s, z + 1 if way == 0 else z - 1)
                at_here, at_there = (u1.at[here], u2.at[here]), there
                u_copies(*at_here, way, s - 1, target, here)[which].wait_recv()
                u[here] = (u[here].astype(F32) + v[dest].astype(F32)).astype(BF)
                u_copies(*at_here, way, s, target, at_there)[which].start()

    prepare(0)
    load_w2.wait()
    load_w1.wait()
    cells(0, nz, at_peer(0))
    for k in range(1, n):
        prepare(k)
    for k in range(1, n):
        to_peer(xs.at[at_peer(k), :], xr.at[at_peer(n - k), :], x_sem, k).wait_send()
        to_peer(xs.at[at_peer(n - k), :], xr.at[at_peer(k), :], x_sem, n - k).wait_recv()
    cells(0, 1, others)
    other_grads(0)
    own_grads(0)
    cells(1, nz, others)
    lax.fori_loop(0, d // 256, back_rows, 0)
    column = lax.fori_loop(
        0, d // 256, back_results, jnp.zeros((sz.all_slots, 1), F32)
    )
    for k in range(n):
        line = jnp.where(square, column[at_peer(k), :], 0.0)
        qs[k] = jnp.broadcast_to(jnp.sum(line, 0, keepdims=True), (8, sz.slots))
    qr[me] = qs[0]
    ret[slots_me, :] = res_send[at_peer(0), :]
    for k in range(1, n):
        to_peer(qs.at[k], qr.at[me], q_sem, k).start()
    for k in range(1, n):
        to_peer(res_send.at[at_peer(k), :], ret.at[slots_me, :], ret_sem, k).start()

    def slice_step(i, carry):
        other_grads(i)
        own_grads(i)
        return carry

    if nz > 2:
        z_round(1, 1)
    lax.fori_loop(1, nz, slice_step, 0)
    if nz > 2:
        z_round(1, 0)
    dense_load = pltpu.make_async_copy(o_save, dw, wsem.at[0])
    dense_load.start()

    for k in range(1, n):
        src = lax.rem(me + n - k, n)
        for c in range(d // 256):
            row_copy(c, k, rows_at(src, sz.slots)).wait()
        to_peer(qs.at[k], qr.at[src], q_sem, k).wait()
    mixed = sgrad = wide2
    lane = iota((sz.rows, sz.small), 1)
    weighted = jnp.zeros((sz.rows, sz.small), F32)
    for e in range(sz.experts):
        q = jnp.sum(comb[e].astype(F32) * qr[e, 0:1, :], 1, keepdims=True)
        weighted = jnp.where(lane == 8 + e, q, weighted)
    total = jnp.sum(weighted, 1, keepdims=True)
    logit_low = (weighted - probs[...] * total).astype(BF)
    sgrad[...] = mm(logit_low, smf[...].astype(BF))
    for e in range(sz.experts):
        sgrad[...] += mm(comb[e], bck[e * sz.slots : (e + 1) * sz.slots, :])
    back2, gain2, shift2 = normalize_back(resid[...], smf[1:2, :], sgrad[...])
    rgrad = wide1
    rgrad[...] = gpad[...].astype(F32) + back2
    low = rgrad[...].astype(BF)
    bias_out = jnp.sum(low.astype(F32), 0, keepdims=True)

    dense = w2
    wide = d // 2
    keep = pl.ds(pl.multiple_of(core * wide, 128), wide)
    give = pl.ds(pl.multiple_of((1 - core) * wide, 128), wide)

    def chunk_rows(j, start, size):
        return pl.ds(pl.multiple_of(j * d + start, 16), size)

    def parked(j):
        cols = pl.ds(pl.multiple_of(lax.rem(j, 2) * wide, 128), wide)
        return acts.at[lax.div(j, 2), 0:d, cols]

    def to_sibling(j):
        return remote(
            dense.at[chunk_rows(j, 0, d), give],
            parked(j),
            d1_sem.at[0, j],
            d1_sem.at[1, j],
            sibling,
            me,
        )

    def to_owner(j, k):
        e = lax.rem(me + k, n)
        return remote(
            dense.at[chunk_rows(j, e * sz.shard, sz.shard), keep],
            r2.at[k - 1, pl.ds(pl.multiple_of(j * sz.shard, 16), sz.shard), :],
            d2_sem.at[0, j, k],
            d2_sem.at[1, j, k],
            me_r,
            e,
        )

    outer = (z == 0) | (z == nz - 1)
    across = me_r - 2 + 4 * odd

    def inward(j):
        return remote(
            z1.at[j], z2.at[0, j], z1_sem.at[0, 0, j], z1_sem.at[1, 0, j], partner, me
        )

    def swap(j):
        return remote(
            z1.at[j], z2.at[1, j], z1_sem.at[0, 1, j], z1_sem.at[1, 1, j], across, me
        )

    def outward(j):
        piece = od.at[j, :, keep]
        return remote(piece, piece, z2_sem.at[0, j], z2_sem.at[1, j], partner, me)

    def to_twin(j, cols):
        piece = od.at[j, :, cols]
        return remote(piece, piece, z3_sem.at[0, j], z3_sem.at[1, j], sibling, me)

    def stage1(j):
        to_sibling(j).wait()
        rows = chunk_rows(j, 0, d)
        dense[rows, keep] = (dense[rows, keep].astype(F32) + parked(j)[...].astype(F32)).astype(BF)
        for k in range(1, n):
            to_owner(j, k).start()

    def stage2(j):
        acc = dense[chunk_rows(j, me * sz.shard, sz.shard), keep].astype(F32)
        for k in range(1, n):
            to_owner(j, k).wait()
            acc = acc + r2[k - 1, j * sz.shard : (j + 1) * sz.shard, :].astype(F32)
        z1[j] = acc.astype(BF)
        pl.when(outer)(lambda: inward(j).start())

    def stage3(j):
        @pl.when(jnp.logical_not(outer))
        def _():
            inward(j).wait_recv()
            z1[j] = (z1[j].astype(F32) + z2[0, j].astype(F32)).astype(BF)
            swap(j).start()

    def stage4(j):
        @pl.when(jnp.logical_not(outer))
        def _():
            swap(j).wait()
            od[j, :, keep] = (z1[j].astype(F32) + z2[1, j].astype(F32)).astype(BF)
            outward(j).start()
            to_twin(j, keep).start()

    def stage5(j):
        @pl.when(outer)
        def _():
            inward(j).wait_send()
            outward(j).wait_recv()
            to_twin(j, keep).start()

    def stage6(j):
        pl.when(jnp.logical_not(outer))(lambda: outward(j).wait_send())
        to_twin(j, keep).wait_send()
        to_twin(j, give).wait_recv()
        pltpu.make_async_copy(od.at[j], o_dense.at[j], isem.at[j]).start()

    dense[chunk_rows(0, 0, d), :] = mm(ctx_t[...], low).astype(BF)
    to_sibling(0).start()
    dense_load.wait()
    for k in range(1, n):
        theirs = rows_at(lax.rem(me + n - k, n), sz.slots)
        to_peer(res_send.at[at_peer(k), :], ret.at[theirs, :], ret_sem, k).wait()
    cgrad = sends.at[3 * sz.rows : 4 * sz.rows, :]

    def load_probs(pair):
        slot = lax.rem(pair, 2)
        return pltpu.make_async_copy(o_probs.at[pair], pbuf.at[slot], psem.at[slot])

    load_probs(0).start()
    cgrad[...] = mm_nt(low, dw[:, 3 * d : 4 * d]).astype(BF)
    sm[...] = mm_tn(logit_low, second[...])

    scale = 1.0 / math.sqrt(HEAD_DIM)
    half_lane = iota((sz.seq, 128), 1)

    def pair_step(pair, carry):
        load_probs(pair).wait()

        @pl.when(pair + 1 < sz.pairs)
        def _():
            load_probs(pair + 1).start()

        for image in range(sz.images):
            rows = slice(image * sz.seq, (image + 1) * sz.seq)
            q2, k2, v2_ = (qkv[rows, pair_cols(pair, j)] for j in range(3))
            c2 = cgrad[rows, pl.ds(pl.multiple_of(pair * 128, 128), 128)]
            there = pl.ds(
                pl.multiple_of(lax.div(pair, 2) * sz.rows + image * sz.seq, 16), sz.seq
            )
            dq = jnp.zeros((sz.seq, 128), F32)
            dk = jnp.zeros((sz.seq, 128), F32)
            dv = jnp.zeros((sz.seq, 128), F32)
            for half in range(2):
                mask = (half_lane >= half * 64) & (half_lane < half * 64 + 64)
                zero = jnp.zeros_like(q2)
                ch = jnp.where(mask, c2, zero)
                p = pbuf[lax.rem(pair, 2), image * 2 + half]
                dv = dv + mm_tn(p, ch)
                pb = mm_nt(ch, v2_)
                p32 = p.astype(F32)
                mix = jnp.sum(pb * p32, -1, keepdims=True)
                ds = (p32 * (pb - mix)).astype(BF)
                dq = dq + mm(ds, jnp.where(mask, k2, zero))
                dk = dk + mm_tn(ds, jnp.where(mask, q2, zero))
            sends[there, pair_cols(pair, 0, 0)] = (dq * scale).astype(BF)
            sends[there, pair_cols(pair, 1, 0)] = (dk * scale).astype(BF)
            sends[there, pair_cols(pair, 2, 0)] = dv.astype(BF)
        return carry

    def group_step(g, carry):
        lax.fori_loop(2 * g, 2 * g + 2, pair_step, 0)
        dense[chunk_rows(g + 1, 0, d), :] = mm(
            normed_t[...], sends[rows_at(g, sz.rows), :]
        ).astype(BF)
        to_sibling(g + 1).start()
        stage1(g)
        return carry

    lax.fori_loop(0, sz.groups, group_step, 0)
    for s in range(2, nz - 1):
        z_round(s, 1)
        z_round(s, 0)
    stage1(sz.groups)

    ngrad = sgrad
    ngrad[...] = mm_nt(sends[0 : sz.rows, :], dw[:, 0:d])
    for g in range(1, sz.groups):
        grads = sends[g * sz.rows : (g + 1) * sz.rows, :]
        ngrad[...] += mm_nt(grads, dw[:, g * d : (g + 1) * d])
    stage2(0)
    x = mm(pad_matrix(sz), tok_ref[...])
    back1, gain1, shift1 = normalize_back(x, smf[0:1, :], ngrad[...])
    stage[...] = mm(unpad_matrix(sz), (rgrad[...] + back1).astype(BF)).astype(BF)
    store = pltpu.make_async_copy(stage, o_gin, wsem.at[2])
    store.start()
    sums = [
        jnp.sum(sends[g * sz.rows : (g + 1) * sz.rows, :].astype(F32), 0, keepdims=True)
        for g in range(sz.groups)
    ]
    bias_q = jnp.concatenate([total[:, 0:256] for total in sums], 1)
    bias_v = jnp.concatenate([total[:, 512:768] for total in sums], 1)
    row = iota((sz.small, d), 0)
    small = sm[...]
    for i, value in enumerate((gain1, gain2, shift1, bias_q, bias_v, bias_out, shift2)):
        small = jnp.where(row == i, value, small)
    sm[...] = small
    smb = sme.at[n]
    smb[...] = small.astype(BF)
    s_first = remote(smb, smr, s1_sem.at[0], s1_sem.at[1], sibling, me)
    s_first.start()

    stage2(1)
    stage3(0)
    mixed[...] = resid[...]
    for e in range(sz.experts):
        block = slice(e * sz.slots, (e + 1) * sz.slots)
        mixed[...] += probs[:, 8 + e : 9 + e] * mm(comb[e], ret[block, :])
    store.wait()
    stage[...] = mm(unpad_matrix(sz), mixed[...].astype(BF)).astype(BF)
    store = pltpu.make_async_copy(stage, o_out, wsem.at[2])
    store.start()

    s_first.wait()
    chip_small = (sm[...] + smr[...].astype(F32)).astype(BF)
    for e in range(n):
        r = iota((sz.shard_pad, d), 0)
        c = iota((sz.shard_pad, d), 1)
        pick = ((c == r + e * sz.shard) & (r < sz.shard)).astype(F32).astype(BF)
        sme[e, :, 0 : sz.shard_pad] = mm_nt(chip_small, pick).astype(BF)

    def small_peer(k):
        piece = sme.at[lax.rem(me + k, n), :, 0 : sz.shard_pad]
        return to_peer(piece, sme_r.at[k], s2_sem, k)

    for k in range(1, n):
        small_peer(k).start()
    stage2(2)
    stage3(1)
    stage4(0)
    acc = sme[me, :, 0 : sz.shard_pad].astype(F32)
    for k in range(1, n):
        small_peer(k).wait()
        acc = acc + sme_r[k].astype(F32)
    smz_r[0] = acc.astype(BF)
    for k in range(1, nz):
        to_z(smz_r.at[0], smz_r.at[k], s3_sem, k).start()
    stage2(3)
    stage3(2)
    stage4(1)

    for way in range(2):
        zz = z if way == 0 else nz - 1 - z
        target = me_r + 2 if way == 0 else me_r - 2

        @pl.when(zz >= 1)
        def _():
            here = landing(way, nz - 2, z)
            for cp in u_copies(u1.at[here], u2.at[here], way, nz - 2, target, here):
                cp.wait_recv()
            v1[z] = (v1[z].astype(F32) + u1[here].astype(F32)).astype(BF)
            v2[z] = (v2[z].astype(F32) + u2[here].astype(F32)).astype(BF)

    stores = [
        pltpu.make_async_copy(v1.at[z], o_w1, wsem.at[0]),
        pltpu.make_async_copy(v2.at[z], o_w2, wsem.at[1]),
    ]
    for cp in stores:
        cp.start()
    stage3(3)
    stage4(2)
    acc = smz_r[0].astype(F32)
    for k in range(1, nz):
        to_z(smz_r.at[0], smz_r.at[k], s3_sem, k).wait()
        acc = acc + smz_r[k].astype(F32)
    o_small[...] = acc
    stage4(3)
    for j in range(sz.chunks):
        stage5(j)
    for j in range(sz.chunks):
        stage6(j)
    for j in range(sz.chunks):
        pltpu.make_async_copy(od.at[j], o_dense.at[j], isem.at[j]).wait()

    for cp in stores:
        cp.wait()
    store.wait()
    for s in range(nz - 1):
        for way in range(2):
            zz = z if way == 0 else nz - 1 - z
            target = me_r + 2 if way == 0 else me_r - 2

            @pl.when(zz <= s)
            def _():
                for cp in u_copies(v1.at[0], v2.at[0], way, s, target, 0):
                    cp.wait_send()
    for k in range(1, n):
        for cp in small_sends(k):
            cp.wait_send()


def block(sz, tokens, routes, router, gains, biases, b1, b2, grad, wq, wp, w1, w2):
    vmem = pl.BlockSpec(memory_space=pltpu.VMEM)
    hbm = pl.BlockSpec(memory_space=pl.ANY)
    rows, d, slots, fs, nz, n = sz.rows, sz.d, sz.all_slots, sz.fs, sz.nz, sz.n_exp
    half = d // 2
    dma = pltpu.SemaphoreType.DMA
    outs = [
        ((sz.chunks, sz.shard, d), BF),
        ((sz.small, sz.shard_pad), F32),
        ((sz.tok, d), BF),
        ((sz.tok, d), BF),
        ((d, fs), BF),
        ((sz.fs_rows, d), BF),
        ((sz.pairs, sz.images * 2, sz.seq, sz.seq), BF),
        ((d, 4 * d), BF),
    ]
    buffers = [
        (tokens.shape, BF),
        (b1.shape, BF),
        (b2.shape, BF),
        ((sz.chunks, sz.shard, d), BF),
        ((d, 4 * d), BF),
        (w2.shape, BF),
        ((sz.tok, d), BF),
        ((slots, d), BF),
        ((slots, d), BF),
        ((rows, 3 * d), BF),
        ((d, rows), BF),
        ((rows, d), F32),
        ((rows, d), BF),
        ((d, rows), BF),
        ((rows, sz.small), F32),
        ((sz.small, d), F32),
        ((rows, d), BF),
        ((sz.experts, rows, sz.slots), BF),
        ((n, sz.ep, sz.slots), F32),
        ((n, sz.ep, sz.slots), F32),
        ((n, *router.shape), BF),
        ((n, *gains.shape), BF),
        ((n, *biases.shape), BF),
        ((1, d), F32),
        ((d, slots - d), BF),
        ((d, d), BF),
        ((nz, slots, 2 * fs), BF),
        ((nz, slots, 2 * fs), BF),
        ((rows, d), F32),
        ((rows, d), F32),
        ((2 * slots, d), BF),
        ((slots, d), BF),
        ((slots, d), BF),
        ((n, 8, sz.slots), F32),
        ((n, 8, sz.slots), F32),
        ((sz.fs_rows, d), BF),
        ((nz, d, fs), BF),
        ((nz, sz.fs_rows, d), BF),
        ((nz + 1, d, fs), BF),
        ((nz + 1, sz.fs_rows, d), BF),
        ((2, 2 * sz.images, sz.seq, sz.seq), BF),
        ((n - 1, d, half), BF),
        ((sz.chunks, sz.shard, half), BF),
        ((2, sz.chunks, sz.shard, half), BF),
        ((sz.small, d), F32),
        ((sz.small, d), BF),
        ((n + 1, sz.small, d), BF),
        ((n, sz.small, sz.shard_pad), BF),
        ((nz, sz.small, sz.shard_pad), BF),
    ]
    sems = (
        [dma((7,)), dma((4,)), dma((2,))]
        + [dma((2, sz.chunks, 2, n)), dma((2, sz.chunks, n))]
        + [dma((2, sz.chunks, 2, n)), dma((sz.chunks, 3))]
        + [dma((3, 2, n))]
        + [dma((2, n))] * 3
        + [dma((2, 2, nz)), dma((2, 2, 2, nz - 1))]
        + [dma((2, n)), dma((2, d // 256, n)), dma((2, n))]
        + [dma((2, sz.chunks)), dma((2, sz.chunks, n))]
        + [dma((2, 2, sz.chunks)), dma((2, sz.chunks))]
        + [dma((2, sz.chunks)), dma((2,)), dma((2, n)), dma((2, nz))]
    )
    return pl.pallas_call(
        partial(block_kernel, sz),
        name="block",
        out_shape=[jax.ShapeDtypeStruct(s, t) for s, t in outs],
        in_specs=[hbm] * 12,
        out_specs=[hbm, vmem] + [hbm] * 6,
        scratch_shapes=[pltpu.VMEM(s, t) for s, t in buffers[:1]]
        + [pltpu.VMEM(routes.shape, jnp.int32)]
        + [pltpu.VMEM(s, t) for s, t in buffers[1:]]
        + sems,
        compiler_params=pltpu.CompilerParams(
            collective_id=1, has_side_effects=True, vmem_limit_bytes=62 << 20
        ),
    )(tokens, routes, router, gains, biases, b1, b2, grad, wq, wp, w1, w2)


def plain_rest(sz, state, tokens, w1, b1, w2, b2):
    xr, dres, qkv, pall, ctx_t, resid, second, normed_t, probs, wq, wp, smf, gpad, comb = state
    d, n = sz.d, sz.experts
    scale = 1.0 / math.sqrt(HEAD_DIM)
    h = mm(xr, w1) + b1
    cdf, pdf = gelu_parts(h)
    act = (h * cdf).astype(BF)
    result = (mm(act, w2) + b2).astype(BF)
    dhid = (mm_nt(dres, w2) * (cdf + h * pdf)).astype(BF)
    row_grad = mm_nt(dhid, w1).astype(BF)
    swap = partial(
        lax.all_to_all, axis_name="exp", split_axis=0, concat_axis=0, tiled=True
    )
    ret = swap(result).reshape(n, sz.slots, d)
    bck = swap(row_grad).reshape(n, sz.slots, d)
    g32 = gpad.astype(F32)
    p = probs[:, 8 : 8 + n]
    picked = jnp.einsum("ets,esd->etd", comb, ret, preferred_element_type=F32)
    mixed = resid + jnp.einsum("te,etd->td", p, picked, precision="highest")
    pg = jnp.sum(g32[None] * picked, -1).T
    lg = (p * (pg - jnp.sum(pg * p, 1, keepdims=True))).astype(BF)
    sgrad = mm(lg, smf[8 : 8 + n].astype(BF))
    sgrad = sgrad + jnp.einsum("ets,esd->td", comb, bck, preferred_element_type=F32)
    back2, gain2, shift2 = normalize_back(resid, smf[1:2], sgrad)
    rgrad = g32 + back2
    low = rgrad.astype(BF)
    cgrad = mm_nt(low, wp).astype(BF)
    four = (sz.images, sz.seq, d // HEAD_DIM, HEAD_DIM)
    q, k, v, c = (
        a.reshape(four)
        for a in (qkv[:, :d], qkv[:, d : 2 * d], qkv[:, 2 * d :], cgrad)
    )
    prob = pall.reshape(sz.pairs, sz.images, 2, sz.seq, sz.seq)
    prob = prob.transpose(1, 0, 2, 3, 4).reshape(sz.images, -1, sz.seq, sz.seq)
    product = partial(jnp.einsum, preferred_element_type=F32)
    dv = product("ihst,ishd->ithd", prob, c).astype(BF)
    pb = product("ishd,ithd->ihst", c, v)
    p32 = prob.astype(F32)
    ds = (p32 * (pb - jnp.sum(pb * p32, -1, keepdims=True))).astype(BF)
    dq = (product("ihst,ithd->ishd", ds, k) * scale).astype(BF)
    dk = (product("ihst,ishd->ithd", ds, q) * scale).astype(BF)
    dqkv = jnp.concatenate([a.reshape(sz.rows, d) for a in (dq, dk, dv)], 1)
    x = mm(pad_matrix(sz), tokens)
    back1, gain1, shift1 = normalize_back(x, smf[0:1], mm_nt(dqkv, wq))
    gin = (rgrad + back1).astype(BF)
    sums = jnp.sum(dqkv.astype(F32), 0, keepdims=True)
    small = jnp.concatenate(
        [gain1, gain2, shift1, sums[:, :d], sums[:, 2 * d :]]
        + [jnp.sum(low.astype(F32), 0, keepdims=True), shift2, mm_tn(lg, second)]
    )

    def dense(grad, dim):
        total = lax.psum(grad.astype(BF), "rep")
        total = lax.psum_scatter(total, "exp", scatter_dimension=dim, tiled=True)
        return total.astype(F32)

    def owned(grad, dim):
        total = lax.psum_scatter(
            grad[None].astype(BF), "rep", scatter_dimension=dim, tiled=True
        )
        return total.astype(F32)

    def unpad(rows):
        return rows.reshape(sz.images, sz.seq, d)[:, :SEQ].reshape(sz.tok, d)

    sums = dense(small, 1)
    return (
        unpad(mixed.astype(BF)),
        unpad(gin),
        dense(mm(normed_t, dqkv), 0),
        dense(mm(ctx_t, low), 0),
        sums[7:].T,
        sums[0:2],
        sums[2:7],
        owned(mm_tn(xr, dhid), 2),
        owned(jnp.sum(dhid.astype(F32), 0), 1),
        owned(mm_tn(act, dres), 1),
        owned(jnp.sum(dres.astype(F32), 0), 1),
    )


def on_device(
    mesh,
    tokens,
    routes,
    out_grad,
    attn_qkv,
    attn_out,
    router,
    norm_gains,
    dense_biases,
    expert_in,
    expert_in_bias,
    expert_out,
    expert_out_bias,
):
    sz = Sizes(mesh, tokens.shape[0], tokens.shape[1], expert_in.shape[2])
    d, fs = sz.d, sz.fs
    w1, w2 = expert_in[0], expert_out[0]
    small = (router.T, norm_gains, dense_biases)
    if (sz.nz, sz.chunks * sz.shard, 2 * fs) != (4, d, d) or sz.all_slots < 2 * sz.rows:
        state = front(sz, tokens, out_grad, routes.T, attn_qkv, attn_out, *small)
        bias1, bias2 = expert_in_bias.astype(F32), expert_out_bias.astype(F32)
        return plain_rest(sz, state, tokens, w1, bias1, w2, bias2)
    dense, sums, out, gin, g1, g2, _, _ = block(
        sz,
        tokens,
        routes.T,
        *small,
        expert_in_bias,
        expert_out_bias,
        out_grad,
        attn_qkv,
        attn_out,
        w1,
        w2,
    )
    return finish(sz, out, gin, g1, g2, dense, sums)


def solution(mesh):
    both = P(("rep", "exp"), None)
    rows = P("exp", None)
    cols = P(None, "exp")
    cube = P("exp", None, None)
    in_specs = (both, both, both, rows, rows, rows, cols, cols, cube, rows, cube, rows)
    out_specs = (
        both,
        both,
        rows,
        rows,
        rows,
        cols,
        cols,
        P("exp", None, "rep"),
        P("exp", "rep"),
        P("exp", "rep", None),
        P("exp", "rep"),
    )
    return jax.shard_map(
        partial(on_device, mesh),
        mesh=mesh,
        in_specs=in_specs,
        out_specs=out_specs,
        check_vma=False,
    )
```

```python
from functools import partial
import math

import jax
import jax.numpy as jnp
from jax import lax
from jax.experimental import pallas as pl
from jax.experimental.pallas import tpu as pltpu
from jax.sharding import PartitionSpec as P

HEAD_DIM = 64
SEQ = 197
EPS = 1e-06
BF = jnp.bfloat16
F32 = jnp.float32
MESH = pl.DeviceIdType.MESH


def up(value, step):
    return (value + step - 1) // step * step


def mm(a, b):
    return lax.dot_general(a, b, (((1,), (0,)), ((), ())), preferred_element_type=F32)


def mm_nt(a, b):
    return lax.dot_general(a, b, (((1,), (1,)), ((), ())), preferred_element_type=F32)


def mm_tn(a, b):
    return lax.dot_general(a, b, (((0,), (0,)), ((), ())), preferred_element_type=F32)


def iota(shape, dim):
    return lax.broadcasted_iota(jnp.int32, shape, dim)


def rows_at(index, size):
    return pl.ds(pl.multiple_of(index * size, size), size)


def normalize(values, gain, shift):
    center = values - jnp.mean(values, -1, keepdims=True)
    spread = jnp.mean(center * center, -1, keepdims=True)
    return center * lax.rsqrt(spread + EPS) * gain + shift


class Sizes:
    def __init__(self, mesh, tok_rows, width, ff):
        self.n_exp = mesh.shape["exp"]
        self.n_rep = mesh.shape["rep"]
        self.tok = tok_rows
        self.images = tok_rows // SEQ
        self.seq = up(SEQ, 16)
        self.rows = self.images * self.seq
        self.d = width
        self.ff = ff
        self.experts = self.n_exp
        self.cap = (18 * tok_rows + 8 * self.experts - 1) // (8 * self.experts)
        self.slots = up(self.cap, 16)
        self.all_slots = self.slots * self.experts
        self.shard = width // self.n_exp
        self.shard_pad = up(self.shard, 128)
        self.ep = up(self.experts, 8)
        self.small = up(8 + self.ep, 16)
        self.pairs = width // 128
        self.nz = self.n_rep // 2
        self.fs = ff // self.n_rep
        self.fs_rows = self.fs + 16
        self.groups = self.pairs // 2
        self.chunks = self.groups + 1


def pad_matrix(sz):
    row = iota((sz.rows, sz.tok), 0)
    col = iota((sz.rows, sz.tok), 1)
    want = jnp.full((sz.rows, sz.tok), -1, jnp.int32)
    for image in range(sz.images):
        inside = (row >= image * sz.seq) & (row < image * sz.seq + SEQ)
        want = jnp.where(inside, row - image * (sz.seq - SEQ), want)
    return (want == col).astype(F32).astype(BF)


def unpad_matrix(sz):
    row = iota((sz.tok, sz.rows), 0)
    col = iota((sz.tok, sz.rows), 1)
    want = row
    for image in range(1, sz.images):
        want = jnp.where(row >= image * SEQ, row + image * (sz.seq - SEQ), want)
    return (want == col).astype(F32).astype(BF)


def front_kernel(
    sz,
    tok_ref,
    grad_ref,
    routes_ref,
    wq_shard,
    wp_shard,
    router_ref,
    gains_ref,
    biases_ref,
    xr,
    dres,
    qkv,
    pall,
    ctx_t,
    resid,
    second,
    normed_t,
    probs,
    wq,
    wp,
    smf,
    gpad,
    comb,
    ctx,
    normed,
    pmat,
    gr,
    gater,
    xs,
    gs,
    gates,
    routers,
    gains,
    biases,
    wq_sem,
    wp_sem,
    zq_sem,
    zp_sem,
    cq_sem,
    cp_sem,
    sm_sem,
    g_sem,
    x_sem,
    ga_sem,
):
    me_r = lax.axis_index("rep")
    me = lax.axis_index("exp")
    n = sz.n_exp
    core = lax.rem(me_r, 2)
    sibling = me_r + 1 - 2 * core
    odd = lax.rem(lax.div(me_r, 2), 2)
    partner = me_r + 2 - 4 * odd

    barrier = pltpu.get_barrier_semaphore()
    for k in range(1, n):
        pl.semaphore_signal(
            barrier, inc=1, device_id=(me_r, lax.rem(me + k, n)), device_id_type=MESH
        )
    for rep in (sibling, partner):
        pl.semaphore_signal(barrier, inc=1, device_id=(rep, me), device_id_type=MESH)
    pl.semaphore_wait(barrier, n + 1)

    def remote(src, dst, send, recv, rep, exp):
        return pltpu.make_async_remote_copy(
            src_ref=src,
            dst_ref=dst,
            send_sem=send,
            recv_sem=recv,
            device_id=(rep, exp),
            device_id_type=MESH,
        )

    def to_peer(src, dst, sems, k):
        return remote(
            src, dst, sems.at[0, k], sems.at[1, k], me_r, lax.rem(me + k, n)
        )

    class Gather:
        def __init__(self, shard, full, width, peer_sem, layer_sem, twin_sem):
            self.shard, self.full = shard, full
            self.piece = width // 6
            self.peer_sem, self.layer_sem, self.twin_sem = peer_sem, layer_sem, twin_sem

        def cols(self, side, first, count):
            start = side * 3 * self.piece + first * self.piece
            return pl.ds(pl.multiple_of(start, 128), count * self.piece)

        def rows(self, k):
            return rows_at(lax.rem(me + n - k, n), sz.shard)

        def peer(self, k):
            cols = self.cols(core, odd, 2)
            return to_peer(
                self.shard.at[:, cols],
                self.full.at[rows_at(me, sz.shard), cols],
                self.peer_sem,
                k,
            )

        def layer(self, k, mine=True):
            part = 2 * odd if mine else 2 - 2 * odd
            piece = self.full.at[self.rows(k), self.cols(core, part, 1)]
            sem = self.layer_sem
            return remote(piece, piece, sem.at[0, k], sem.at[1, k], partner, me)

        def twin(self, k, late, side):
            first, count = (2 - 2 * odd, 1) if late else (odd, 2)
            piece = self.full.at[self.rows(k), self.cols(side, first, count)]
            sem = self.twin_sem
            return remote(
                piece, piece, sem.at[0, late, k], sem.at[1, late, k], sibling, me
            )

        def start(self):
            for k in range(1, n):
                self.peer(k).start()
            self.full[rows_at(me, sz.shard), :] = self.shard[...]

        def forward(self):
            for k in range(1, n):
                self.peer(k).wait_recv()
                self.layer(k).start()
                self.twin(k, 0, core).start()

        def finish(self):
            for k in range(1, n):
                self.layer(k, False).wait_recv()
                self.twin(k, 1, core).start()
            for k in range(1, n):
                for late in range(2):
                    self.twin(k, late, 1 - core).wait_recv()

        def drain(self):
            for k in range(1, n):
                self.peer(k).wait_send()
                self.layer(k).wait_send()
                for late in range(2):
                    self.twin(k, late, core).wait_send()

    gather_q = Gather(wq_shard, wq, 3 * sz.d, wq_sem, zq_sem, cq_sem)
    gather_p = Gather(wp_shard, wp, sz.d, wp_sem, zp_sem, cp_sem)

    def small_sends(k):
        return [
            to_peer(src, dst.at[me], sm_sem.at[i], k)
            for i, (src, dst) in enumerate(
                ((gains_ref, gains), (biases_ref, biases), (router_ref, routers))
            )
        ]

    for k in range(1, n):
        for cp in small_sends(k):
            cp.start()
    gather_q.start()
    gains[me] = gains_ref[...]
    biases[me] = biases_ref[...]
    routers[me] = router_ref[...]

    choice = (routes_ref[...].astype(F32) + 1.0).astype(BF)
    lines = mm_nt(choice, pad_matrix(sz)).astype(jnp.int32) - 1
    ids = iota((sz.ep, sz.rows), 0)
    oh1 = (lines[0:1, :] == ids).astype(F32)
    oh2 = (lines[1:2, :] == ids).astype(F32)
    before = (
        (iota((sz.rows, sz.rows), 0) < iota((sz.rows, sz.rows), 1))
        .astype(F32)
        .astype(BF)
    )
    pos1 = mm(oh1.astype(BF), before)
    pos2 = mm(oh2.astype(BF), before) + jnp.sum(oh1, 1, keepdims=True)
    place = oh1 * pos1 + oh2 * pos2
    kept = (oh1 + oh2 > 0.5) & (place < sz.cap - 0.5)
    slot = jnp.where(kept, place, -1.0).astype(jnp.int32)
    slot_ids = iota((sz.slots, sz.rows), 0)
    for e in range(sz.experts):
        pmat[e * sz.slots : (e + 1) * sz.slots, :] = (
            (slot_ids == slot[e : e + 1, :]).astype(F32).astype(BF)
        )
    eye = (iota((sz.rows, sz.rows), 0) == iota((sz.rows, sz.rows), 1)).astype(F32)
    slot_cols = mm_nt(eye.astype(BF), slot.astype(F32).astype(BF)).astype(jnp.int32)
    lane_ids = iota((sz.rows, sz.slots), 1)
    for e in range(sz.experts):
        comb[e] = (slot_cols[:, e : e + 1] == lane_ids).astype(F32).astype(BF)

    spread = pad_matrix(sz)
    gpad[...] = mm(spread, grad_ref[...]).astype(BF)
    for e in range(sz.experts):
        block = slice(e * sz.slots, (e + 1) * sz.slots)
        gs[block, :] = mm(pmat[block, :], gpad[...]).astype(BF)
    slots_me = rows_at(me, sz.slots)
    gr[slots_me, :] = gs[slots_me, :]

    x = mm(spread, tok_ref[...])
    for k in range(1, n):
        for cp in small_sends(k):
            cp.wait_recv()
    smf[...] = jnp.zeros_like(smf)
    for j in range(n):
        r = iota((sz.shard, sz.d), 0)
        c = iota((sz.shard, sz.d), 1)
        pick = (c == r + j * sz.shard).astype(F32).astype(BF)
        smf[0:2, :] += mm(gains[j], pick)
        smf[2:7, :] += mm(biases[j], pick)
        smf[8 : 8 + sz.experts, :] += mm(routers[j], pick)
    normed[...] = normalize(x, smf[0:1, :], smf[2:3, :]).astype(BF)
    normed_t[...] = normed[...].T

    gather_q.forward()
    gather_p.start()
    gather_q.finish()
    for j, bias_row in ((0, 3), (1, None), (2, 4)):
        cols = slice(j * sz.d, (j + 1) * sz.d)
        out = mm(normed[...], wq[:, cols])
        if bias_row is not None:
            out = out + smf[bias_row : bias_row + 1, :]
        qkv[:, cols] = out.astype(BF)
    for k in range(1, n):
        dst = rows_at(lax.rem(me + k, n), sz.slots)
        to_peer(gs.at[dst, :], gr.at[slots_me, :], g_sem, k).start()

    scale = 1.0 / math.sqrt(HEAD_DIM)
    lane = iota((sz.seq, 128), 1)
    live = iota((sz.seq, sz.seq), 1) < SEQ

    def pair_step(pair, carry):
        for image in range(sz.images):
            rows = slice(image * sz.seq, (image + 1) * sz.seq)
            q2 = qkv[rows, pl.ds(pl.multiple_of(pair * 128, 128), 128)]
            k2 = qkv[rows, pl.ds(pl.multiple_of(sz.d + pair * 128, 128), 128)]
            v2 = qkv[rows, pl.ds(pl.multiple_of(2 * sz.d + pair * 128, 128), 128)]
            total = jnp.zeros((sz.seq, 128), F32)
            for half in range(2):
                mask = (lane >= half * 64) & (lane < half * 64 + 64)
                s = mm_nt(jnp.where(mask, q2, jnp.zeros_like(q2)), k2) * scale
                s = jnp.where(live, s, -1e30)
                e = jnp.exp(s - jnp.max(s, -1, keepdims=True))
                p = (e / jnp.sum(e, -1, keepdims=True)).astype(BF)
                pall[pair, image * 2 + half] = p
                total = total + mm(p, jnp.where(mask, v2, jnp.zeros_like(v2)))
            ctx[rows, pl.ds(pl.multiple_of(pair * 128, 128), 128)] = total.astype(BF)
        return carry

    lax.fori_loop(0, sz.pairs, pair_step, 0)

    gather_p.forward()
    gather_p.finish()
    res = (
        mm(spread, tok_ref[...])
        + mm(ctx[...], wp[...])
        + smf[5:6, :]
    )
    resid[...] = res
    low = normalize(res, smf[1:2, :], smf[6:7, :]).astype(BF)
    second[...] = low

    for e in range(sz.experts):
        block = slice(e * sz.slots, (e + 1) * sz.slots)
        xs[block, :] = mm(pmat[block, :], second[...]).astype(BF)
    for k in range(1, n):
        dst = rows_at(lax.rem(me + k, n), sz.slots)
        to_peer(xs.at[dst, :], xr.at[slots_me, :], x_sem, k).start()
    xr[slots_me, :] = xs[slots_me, :]

    small_low = smf[...].astype(BF)
    logit_rows = mm_nt(small_low, low)[8 : 8 + sz.ep, :]
    logit_rows = jnp.where(iota((sz.ep, sz.rows), 0) < sz.experts, logit_rows, -1e30)
    e_rows = jnp.exp(logit_rows - jnp.max(logit_rows, 0, keepdims=True))
    prob_rows = e_rows / jnp.sum(e_rows, 0, keepdims=True)
    hi = prob_rows.astype(BF)
    left = prob_rows - hi.astype(F32)
    mid = left.astype(BF)
    low3 = (left - mid.astype(F32)).astype(BF)
    for e in range(sz.experts):
        block = pmat[e * sz.slots : (e + 1) * sz.slots, :]
        gates[e] = mm_nt(hi, block) + mm_nt(mid, block) + mm_nt(low3, block)
    for k in range(1, n):
        to_peer(
            gates.at[lax.rem(me + k, n)], gater.at[me], ga_sem, k
        ).start()
    gater[me] = gates[me]
    logit_cols = mm_nt(low, small_low)
    col = iota((sz.rows, sz.small), 1)
    logit_cols = jnp.where((col >= 8) & (col < 8 + sz.experts), logit_cols, -1e30)
    e_cols = jnp.exp(logit_cols - jnp.max(logit_cols, 1, keepdims=True))
    probs[...] = e_cols / jnp.sum(e_cols, 1, keepdims=True)

    ctx_t[...] = ctx[...].T

    for k in range(1, n):
        src = lax.rem(me + n - k, n)
        dst = rows_at(lax.rem(me + k, n), sz.slots)
        theirs = rows_at(src, sz.slots)
        to_peer(gs.at[dst, :], gr.at[theirs, :], g_sem, k).wait()
        to_peer(gates.at[lax.rem(me + k, n)], gater.at[src], ga_sem, k).wait()
    square = iota((sz.slots, sz.slots), 0) == iota((sz.slots, sz.slots), 1)
    for j in range(n):
        block = slice(j * sz.slots, (j + 1) * sz.slots)
        row = gater[j, pl.ds(me, 1), :]
        gate = jnp.sum(jnp.where(square, row, 0.0), 1, keepdims=True)
        dres[block, :] = (gate * gr[block, :].astype(F32)).astype(BF)
    for k in range(1, n):
        src = lax.rem(me + n - k, n)
        dst = rows_at(lax.rem(me + k, n), sz.slots)
        theirs = rows_at(src, sz.slots)
        to_peer(xs.at[dst, :], xr.at[theirs, :], x_sem, k).wait()
        for cp in small_sends(k):
            cp.wait_send()
    gather_q.drain()
    gather_p.drain()


def front(sz, tokens, grad, routes, wq, wp, router, gains, biases):
    vmem = pl.BlockSpec(memory_space=pltpu.VMEM)
    rows, d, slots, n = sz.rows, sz.d, sz.all_slots, sz.n_exp
    outs = [
        ((slots, d), BF),
        ((slots, d), BF),
        ((rows, 3 * d), BF),
        ((sz.pairs, sz.images * 2, sz.seq, sz.seq), BF),
        ((d, rows), BF),
        ((rows, d), F32),
        ((rows, d), BF),
        ((d, rows), BF),
        ((rows, sz.small), F32),
        ((d, 3 * d), BF),
        ((d, d), BF),
        ((sz.small, d), F32),
        ((rows, d), BF),
        ((sz.experts, rows, sz.slots), BF),
    ]
    dma = pltpu.SemaphoreType.DMA
    sems = [dma((2, n))] * 4 + [dma((2, 2, n))] * 2 + [dma((3, 2, n))] + [dma((2, n))] * 3
    return pl.pallas_call(
        partial(front_kernel, sz),
        name="front",
        out_shape=[jax.ShapeDtypeStruct(s, t) for s, t in outs],
        in_specs=[vmem] * 8,
        out_specs=[vmem] * len(outs),
        scratch_shapes=[
            pltpu.VMEM((rows, d), BF),
            pltpu.VMEM((rows, d), BF),
            pltpu.VMEM((slots, rows), BF),
            pltpu.VMEM((slots, d), BF),
            pltpu.VMEM((n, sz.ep, sz.slots), F32),
            pltpu.VMEM((slots, d), BF),
            pltpu.VMEM((slots, d), BF),
            pltpu.VMEM((n, sz.ep, sz.slots), F32),
            pltpu.VMEM((n, *router.shape), BF),
            pltpu.VMEM((n, *gains.shape), BF),
            pltpu.VMEM((n, *biases.shape), BF),
        ]
        + sems,
        compiler_params=pltpu.CompilerParams(
            collective_id=0, has_side_effects=True, vmem_limit_bytes=56 << 20
        ),
    )(tokens, grad, routes, wq, wp, router, gains, biases)


def finish_kernel(sz, *refs):
    sources, targets = refs[:6], refs[6:17]
    ins, outs = refs[17:23], refs[23:32]
    in_sem, out_sem = refs[32:]
    out, gin, g1, g2, dense, sg = ins
    o_qkv, o_proj, o_router, o_gains, o_biases, o_w1, o_b1, o_w2, o_b2 = outs
    loads = [
        pltpu.make_async_copy(src, dst, in_sem.at[i])
        for i, (src, dst) in enumerate(zip(sources, ins))
    ]
    stores = [
        pltpu.make_async_copy(src, dst, out_sem.at[i])
        for i, (src, dst) in enumerate(zip((out, gin, *outs), targets))
    ]
    for i in (2, 3, 4, 0, 1, 5):
        loads[i].start()
    fs, sh = sz.fs, sz.shard
    loads[2].wait()
    o_w1[0] = g1[...].astype(F32)
    stores[7].start()
    loads[3].wait()
    o_w2[0] = g2[0:fs, :].astype(F32)
    stores[9].start()
    loads[4].wait()
    for g in range(sz.groups):
        for j in range(3):
            cols = slice(j * sz.d + g * 256, j * sz.d + (g + 1) * 256)
            o_qkv[:, cols] = dense[g + 1, :, j * 256 : (j + 1) * 256].astype(F32)
    stores[2].start()
    o_proj[...] = dense[0].astype(F32)
    stores[3].start()
    for i in range(2):
        loads[i].wait()
        stores[i].start()
    loads[5].wait()
    o_router[...] = sg[8 : 8 + sz.experts, 0:sh]
    o_gains[...] = sg[0:2, 0:sh]
    o_biases[...] = sg[2:7, 0:sh]
    o_b1[...] = g2[fs : fs + 16, :].astype(F32)[0:1, 0:fs]
    own = o_b2.shape[1]
    first = lax.axis_index("rep") * own
    pick = iota((sz.d, own), 0) == iota((sz.d, own), 1) + first
    o_b2[...] = mm(g2[fs : fs + 16, :], pick.astype(F32).astype(BF))[1:2, :]
    for i in (4, 5, 6, 8, 10):
        stores[i].start()
    for store in stores:
        store.wait()


def finish(sz, out, gin, g1, g2, dense, sg):
    d, fs, sh = sz.d, sz.fs, sz.shard
    outs = [
        ((sz.tok, d), BF),
        ((sz.tok, d), BF),
        ((sh, 3 * d), F32),
        ((sh, d), F32),
        ((sz.experts, sh), F32),
        ((2, sh), F32),
        ((5, sh), F32),
        ((1, d, fs), F32),
        ((1, fs), F32),
        ((1, fs, d), F32),
        ((1, d // sz.n_rep), F32),
    ]
    sources = (out, gin, g1, g2, dense, sg)
    hbm = pl.BlockSpec(memory_space=pl.ANY)
    grads = pl.pallas_call(
        partial(finish_kernel, sz),
        name="finish",
        out_shape=[jax.ShapeDtypeStruct(s, t) for s, t in outs],
        in_specs=[hbm] * 6,
        out_specs=[hbm] * len(outs),
        scratch_shapes=[pltpu.VMEM(a.shape, a.dtype) for a in sources]
        + [pltpu.VMEM(s, t) for s, t in outs[2:]]
        + [pltpu.SemaphoreType.DMA((6,)), pltpu.SemaphoreType.DMA((11,))],
        compiler_params=pltpu.CompilerParams(vmem_limit_bytes=62 << 20),
    )(*sources)
    return (*grads[:4], grads[4].T, *grads[5:])


def normalize_back(values, gain, cot):
    center = values - jnp.mean(values, -1, keepdims=True)
    spread = jnp.mean(center * center, -1, keepdims=True)
    inv = lax.rsqrt(spread + EPS)
    unit = center * inv
    scaled = cot * gain
    grad = inv * (
        scaled
        - jnp.mean(scaled, -1, keepdims=True)
        - unit * jnp.mean(scaled * unit, -1, keepdims=True)
    )
    return grad, jnp.sum(cot * unit, 0, keepdims=True), jnp.sum(cot, 0, keepdims=True)


def gelu_parts(h):
    t = 1.0 / (1.0 + (0.3275911 / math.sqrt(2.0)) * jnp.abs(h))
    bell = jnp.exp(-0.5 * h * h)
    poly = t * (
        0.127414796
        + t * (-0.142248368 + t * (0.7107068705 + t * (-0.7265760135 + t * 0.5307027145)))
    )
    tail = poly * bell
    return jnp.where(h >= 0, 1.0 - tail, tail), bell * (1.0 / math.sqrt(2.0 * math.pi))


def block_kernel(
    sz,
    tok_hbm,
    routes_hbm,
    router_ref,
    gains_ref,
    biases_ref,
    b1_hbm,
    b2_hbm,
    grad_hbm,
    wq_shard,
    wp_shard,
    w1_hbm,
    w2_hbm,
    o_dense,
    o_small,
    o_out,
    o_gin,
    o_w1,
    o_w2,
    o_probs,
    o_save,
    tok_ref,
    routes_ref,
    b1_ref,
    b2_ref,
    od,
    dw,
    w2,
    stage,
    xr,
    dres,
    qkv,
    ctx_t,
    resid,
    second,
    normed_t,
    probs,
    smf,
    gpad,
    comb,
    gater,
    gates,
    routers,
    gains,
    biases,
    bias2,
    xt,
    xta,
    acts,
    dhids,
    wide1,
    wide2,
    sends,
    ret,
    bck,
    qs,
    qr,
    t2,
    v1,
    v2,
    u1,
    u2,
    pbuf,
    r2,
    z1,
    z2,
    sm,
    smr,
    sme,
    sme_r,
    smz_r,
    isem,
    wsem,
    psem,
    f_sem,
    l_sem,
    c_sem,
    o_sem,
    sm_sem,
    g_sem,
    x_sem,
    ga_sem,
    t_sem,
    u_sem,
    ret_sem,
    bck_sem,
    q_sem,
    d1_sem,
    d2_sem,
    z1_sem,
    z2_sem,
    z3_sem,
    s1_sem,
    s2_sem,
    s3_sem,
):
    me_r = lax.axis_index("rep")
    me = lax.axis_index("exp")
    n, nz, fs, d = sz.n_exp, sz.nz, sz.fs, sz.d
    core = lax.rem(me_r, 2)
    z = lax.div(me_r, 2)
    sibling = me_r + 1 - 2 * core
    odd = lax.rem(z, 2)
    partner = me_r + 2 - 4 * odd

    loads = [
        pltpu.make_async_copy(src, dst, isem.at[i])
        for i, (src, dst) in enumerate(
            (
                (tok_hbm, tok_ref),
                (gains_ref, gains.at[me]),
                (biases_ref, biases.at[me]),
                (router_ref, routers.at[me]),
                (routes_hbm, routes_ref),
                (b1_hbm, b1_ref),
                (b2_hbm, b2_ref),
            )
        )
    ]
    for cp in loads:
        cp.start()
    load_grad = pltpu.make_async_copy(grad_hbm, stage, wsem.at[0])
    load_grad.start()
    load_w2 = pltpu.make_async_copy(w2_hbm, w2, wsem.at[1])
    load_w2.start()

    barrier = pltpu.get_barrier_semaphore()
    for k in range(1, n):
        pl.semaphore_signal(
            barrier, inc=1, device_id=(me_r, lax.rem(me + k, n)), device_id_type=MESH
        )
    for k in range(1, nz):
        pl.semaphore_signal(
            barrier,
            inc=1,
            device_id=(lax.rem(me_r + 2 * k, 2 * nz), me),
            device_id_type=MESH,
        )
    pl.semaphore_signal(barrier, inc=1, device_id=(sibling, me), device_id_type=MESH)
    pl.semaphore_wait(barrier, n - 1 + nz)

    def remote(src, dst, send, recv, rep, exp):
        return pltpu.make_async_remote_copy(
            src_ref=src,
            dst_ref=dst,
            send_sem=send,
            recv_sem=recv,
            device_id=(rep, exp),
            device_id_type=MESH,
        )

    def to_peer(src, dst, sems, k):
        return remote(
            src, dst, sems.at[0, k], sems.at[1, k], me_r, lax.rem(me + k, n)
        )

    def to_z(src, dst, sems, k):
        return remote(
            src, dst, sems.at[0, k], sems.at[1, k], lax.rem(me_r + 2 * k, 2 * nz), me
        )

    normed = acts.at[nz - 1, sz.slots : sz.slots + sz.rows, :]
    ctx = xta.at[0 : sz.rows, :]
    res_send = sends.at[0 : sz.all_slots, :]
    row_send = sends.at[sz.all_slots : 2 * sz.all_slots, :]
    xs, gs = res_send, row_send

    piece = 128

    def shard_cols(g, tile):
        if isinstance(g, int) and g == sz.groups:
            return wp_shard, tile * piece
        return wq_shard, lax.div(tile, 2) * d + g * 256 + lax.rem(tile, 2) * piece

    def dw_cols(g, tile, count):
        return pl.ds(pl.multiple_of(g * d + tile * piece, 128), count * piece)

    def dw_rows(k):
        return rows_at(lax.rem(me + n - k, n), sz.shard)

    def fetch(g, i, k):
        tile = 3 * core + odd + i
        shard, start = shard_cols(g, tile)
        return remote(
            shard.at[:, pl.ds(pl.multiple_of(start, 128), piece)],
            dw.at[rows_at(me, sz.shard), dw_cols(g, tile, 1)],
            f_sem.at[0, g, i, k],
            f_sem.at[1, g, i, k],
            me_r,
            lax.rem(me + k, n),
        )

    def fetched(g, i, k):
        ref = dw.at[dw_rows(k), dw_cols(g, 3 * core + odd + i, 1)]
        return remote(
            ref,
            ref,
            f_sem.at[0, g, i, k],
            f_sem.at[1, g, i, k],
            me_r,
            lax.rem(me + k, n),
        )

    def layer(g, k, mine):
        part = 2 * odd if mine else 2 - 2 * odd
        ref = dw.at[dw_rows(k), dw_cols(g, 3 * core + part, 1)]
        return remote(ref, ref, l_sem.at[0, g, k], l_sem.at[1, g, k], partner, me)

    def twin(g, k, late, side):
        first, count = (2 - 2 * odd, 1) if late else (odd, 2)
        ref = dw.at[dw_rows(k), dw_cols(g, 3 * side + first, count)]
        return remote(
            ref, ref, c_sem.at[0, g, late, k], c_sem.at[1, g, late, k], sibling, me
        )

    def own_part(g, j):
        if isinstance(g, int) and g == sz.groups:
            src = wp_shard.at[:, j * 256 : (j + 1) * 256]
        else:
            src = wq_shard.at[:, pl.ds(pl.multiple_of(j * d + g * 256, 128), 256)]
        dst = dw.at[
            rows_at(me, sz.shard), pl.ds(pl.multiple_of(g * d + j * 256, 128), 256)
        ]
        return pltpu.make_async_copy(src, dst, o_sem.at[g, j])

    def start_weights(g):
        for k in range(1, n):
            for i in range(2):
                fetch(g, i, k).start()
        for j in range(3):
            own_part(g, j).start()

    def forward_weights(g):
        for k in range(1, n):
            for i in range(2):
                fetched(g, i, k).wait_recv()
            layer(g, k, True).start()
            twin(g, k, 0, core).start()

    def finish_weights(g):
        for j in range(3):
            own_part(g, j).wait()
        for k in range(1, n):
            layer(g, k, False).wait_recv()
            twin(g, k, 1, core).start()
        for k in range(1, n):
            for late in range(2):
                twin(g, k, late, 1 - core).wait_recv()

    def drain_weights(g):
        for k in range(1, n):
            for i in range(2):
                fetch(g, i, k).wait_send()
            layer(g, k, True).wait_send()
            for late in range(2):
                twin(g, k, late, core).wait_send()

    def small_sends(k):
        return [
            to_peer(src, dst.at[me], sm_sem.at[i], k)
            for i, (src, dst) in enumerate(
                ((gains_ref, gains), (biases_ref, biases), (router_ref, routers))
            )
        ]

    for k in range(1, n):
        for cp in small_sends(k):
            cp.start()
    for g in range(sz.groups + 1):
        start_weights(g)
    loads[0].wait()
    wide1[...] = mm(pad_matrix(sz), tok_ref[...])
    for cp in loads[1:]:
        cp.wait()
    for k in range(1, n):
        for cp in small_sends(k):
            cp.wait_recv()
    smf[...] = jnp.zeros_like(smf)
    for j in range(n):
        r = iota((sz.shard, d), 0)
        c = iota((sz.shard, d), 1)
        pick = (c == r + j * sz.shard).astype(F32).astype(BF)
        smf[0:2, :] += mm(gains[j], pick)
        smf[2:7, :] += mm(biases[j], pick)
        smf[8 : 8 + sz.experts, :] += mm(routers[j], pick)
    normed[...] = normalize(wide1[...], smf[0:1, :], smf[2:3, :]).astype(BF)
    forward_weights(0)
    choice = (routes_ref[...].astype(F32) + 1.0).astype(BF)
    lines = mm_nt(choice, pad_matrix(sz)).astype(jnp.int32) - 1
    ids = iota((sz.ep, sz.rows), 0)
    oh1 = (lines[0:1, :] == ids).astype(F32)
    oh2 = (lines[1:2, :] == ids).astype(F32)
    before = (
        (iota((sz.rows, sz.rows), 0) < iota((sz.rows, sz.rows), 1))
        .astype(F32)
        .astype(BF)
    )
    pos1 = mm(oh1.astype(BF), before)
    pos2 = mm(oh2.astype(BF), before) + jnp.sum(oh1, 1, keepdims=True)
    place = oh1 * pos1 + oh2 * pos2
    kept = (oh1 + oh2 > 0.5) & (place < sz.cap - 0.5)
    slot = jnp.where(kept, place, -1.0).astype(jnp.int32)
    slot_ids = iota((sz.slots, sz.rows), 0)

    def picks(e):
        return (slot_ids == slot[e : e + 1, :]).astype(F32).astype(BF)

    forward_weights(1)

    load_grad.wait()
    gpad[...] = mm(pad_matrix(sz), stage[...]).astype(BF)
    slots_me = rows_at(me, sz.slots)

    def at_peer(k):
        return slice(k * sz.slots, (k + 1) * sz.slots)

    def picks_for(k):
        line = slot[0:1, :]
        for e in range(1, sz.experts):
            line = jnp.where(lax.rem(me + k, n) == e, slot[e : e + 1, :], line)
        return (slot_ids == line).astype(F32).astype(BF)

    for k in range(n):
        gs[at_peer(k), :] = mm(picks_for(k), gpad[...]).astype(BF)
    dres[at_peer(0), :] = gs[at_peer(0), :]
    forward_weights(2)
    for k in range(1, n):
        to_peer(gs.at[at_peer(k), :], dres.at[at_peer(n - k), :], g_sem, k).start()

    scale = 1.0 / math.sqrt(HEAD_DIM)
    half_lane = iota((sz.seq, 128), 1)
    live = iota((sz.seq, sz.seq), 1) < SEQ

    def pair_cols(pair, j, base=None):
        group = lax.div(pair, 2) * d if base is None else base
        start = group + j * 256 + lax.rem(pair, 2) * 128
        return pl.ds(pl.multiple_of(start, 128), 128)

    def save_probs(pair):
        slot = lax.rem(pair, 2)
        return pltpu.make_async_copy(pbuf.at[slot], o_probs.at[pair], psem.at[slot])

    def forward_pair(pair, carry):
        @pl.when(pair >= 2)
        def _():
            save_probs(pair - 2).wait()

        for image in range(sz.images):
            rows = slice(image * sz.seq, (image + 1) * sz.seq)
            q2, k2, v2_ = (qkv[rows, pair_cols(pair, j)] for j in range(3))
            total = jnp.zeros((sz.seq, 128), F32)
            for half in range(2):
                mask = (half_lane >= half * 64) & (half_lane < half * 64 + 64)
                zero = jnp.zeros_like(q2)
                s = mm_nt(jnp.where(mask, q2 * jnp.asarray(scale, BF), zero), k2)
                s = jnp.where(live, s, -1e30)
                e = jnp.exp(s - jnp.max(s, -1, keepdims=True))
                p = (e * (1.0 / jnp.sum(e, -1, keepdims=True))).astype(BF)
                pbuf[lax.rem(pair, 2), image * 2 + half] = p
                total = total + mm(p, jnp.where(mask, v2_, zero))
            ctx[rows, pl.ds(pl.multiple_of(pair * 128, 128), 128)] = total.astype(BF)
        save_probs(pair).start()
        return carry

    def forward_group(g, carry):
        finish_weights(g)
        cols = pl.ds(pl.multiple_of(g * d, 128), d)
        of_bias = pl.ds(pl.multiple_of(g * 256, 128), 256)
        bias = jnp.concatenate(
            [smf[3:4, of_bias], jnp.zeros((1, 256), F32), smf[4:5, of_bias]], 1
        )
        qkv[:, cols] = (mm(normed[...], dw[:, cols]) + bias).astype(BF)
        lax.fori_loop(2 * g, 2 * g + 2, forward_pair, 0)

        @pl.when(g == 0)
        def _():
            forward_weights(sz.groups)

        return carry

    lax.fori_loop(0, sz.groups, forward_group, 0)
    finish_weights(sz.groups)
    save = pltpu.make_async_copy(dw, o_save, wsem.at[2])
    save.start()
    res = (
        wide1[...]
        + mm(ctx[...], dw[:, 3 * d : 4 * d])
        + smf[5:6, :]
    )
    resid[...] = res
    second[...] = normalize(res, smf[1:2, :], smf[6:7, :]).astype(BF)
    for k in [*range(1, n), 0]:
        xs[at_peer(k), :] = mm(picks_for(k), second[...]).astype(BF)
        if k:
            to_peer(xs.at[at_peer(k), :], xr.at[at_peer(n - k), :], x_sem, k).start()
        else:
            xr[at_peer(0), :] = xs[at_peer(0), :]
    small_low = smf[...].astype(BF)
    low = second[...]
    logit_rows = mm_nt(small_low, low)[8 : 8 + sz.ep, :]
    logit_rows = jnp.where(iota((sz.ep, sz.rows), 0) < sz.experts, logit_rows, -1e30)
    e_rows = jnp.exp(logit_rows - jnp.max(logit_rows, 0, keepdims=True))
    prob_rows = e_rows / jnp.sum(e_rows, 0, keepdims=True)
    hi = prob_rows.astype(BF)
    left = prob_rows - hi.astype(F32)
    mid = left.astype(BF)
    rest_low = (left - mid.astype(F32)).astype(BF)
    for e in range(sz.experts):
        block = picks(e)
        gates[e] = mm_nt(hi, block) + mm_nt(mid, block) + mm_nt(rest_low, block)
    for k in range(1, n):
        to_peer(gates.at[lax.rem(me + k, n)], gater.at[n - k], ga_sem, k).start()
    gater[0] = gates[me]
    for g in range(sz.groups + 1):
        drain_weights(g)
    save.wait()
    load_w1 = pltpu.make_async_copy(w1_hbm, dw, wsem.at[0])
    load_w1.start()
    normed_t[...] = normed[...].T
    ctx_t[...] = ctx[...].T
    eye = (iota((sz.rows, sz.rows), 0) == iota((sz.rows, sz.rows), 1)).astype(F32)
    slot_cols = mm_nt(eye.astype(BF), slot.astype(F32).astype(BF)).astype(jnp.int32)
    lane_ids = iota((sz.rows, sz.slots), 1)
    for e in range(sz.experts):
        comb[e] = (slot_cols[:, e : e + 1] == lane_ids).astype(F32).astype(BF)
    logit_cols = mm_nt(low, small_low)
    col = iota((sz.rows, sz.small), 1)
    logit_cols = jnp.where((col >= 8) & (col < 8 + sz.experts), logit_cols, -1e30)
    e_cols = jnp.exp(logit_cols - jnp.max(logit_cols, 1, keepdims=True))
    probs[...] = e_cols / jnp.sum(e_cols, 1, keepdims=True)
    for pair in range(max(sz.pairs - 2, 0), sz.pairs):
        save_probs(pair).wait()

    lower = 1 - lax.div(z, (nz + 1) // 2)
    span = 2 * fs
    per = span // 256
    everyone, others = slice(0, sz.all_slots), slice(sz.slots, sz.all_slots)
    square = iota((sz.slots, sz.slots), 0) == iota((sz.slots, sz.slots), 1)
    bias2[...] = jnp.zeros_like(bias2)
    half_own = pl.ds(pl.multiple_of(core * fs, 128), fs)
    half_other = pl.ds(pl.multiple_of((1 - core) * fs, 128), fs)

    def dest_of(i):
        return lower * (nz - 1 - i) + (1 - lower) * i

    def hidden_at(i, first, size):
        return pl.ds(pl.multiple_of(dest_of(i) * span + first, 128), size)

    def prepare(k):
        rows = at_peer(k)
        if k:
            j = n - k
            to_peer(gs.at[at_peer(j), :], dres.at[rows, :], g_sem, j).wait()
            to_peer(gates.at[lax.rem(me + j, n)], gater.at[k], ga_sem, j).wait()
        row = gater[k, pl.ds(me, 1), :]
        gate = jnp.sum(jnp.where(square, row, 0.0), 1, keepdims=True)
        value = (gate * dres[rows, :].astype(F32)).astype(BF)
        dres[rows, :] = value
        bias2[...] += jnp.sum(value.astype(F32), 0, keepdims=True)

    def cell(t, rows):
        i, c = lax.div(t, per), lax.rem(t, per)
        hidden = hidden_at(i, c * 256, 256)
        here = pl.ds(pl.multiple_of(c * 256, 128), 256)
        h = mm(xr[rows, :], dw[:, hidden]) + b1_ref[:, hidden].astype(F32)
        cdf, pdf = gelu_parts(h)
        da = mm_nt(dres[rows, :], w2[hidden, :])
        acts[i, rows, here] = (h * cdf).astype(BF)
        dhids[i, rows, here] = (da * (cdf + h * pdf)).astype(BF)

    def cells(first, last, rows):
        lax.fori_loop(first * per, last * per, lambda t, c: (cell(t, rows), c)[1], 0)

    def row_copy(c, k, land):
        cols = pl.ds(pl.multiple_of(c * 256, 128), 256)
        return remote(
            row_send.at[at_peer(k), cols],
            bck.at[land, cols],
            bck_sem.at[0, c, k],
            bck_sem.at[1, c, k],
            me_r,
            lax.rem(me + k, n),
        )

    def back_rows(c, carry):
        cols = pl.ds(pl.multiple_of(c * 256, 128), 256)
        total = mm_nt(dhids[0], dw[cols, hidden_at(0, 0, span)])
        for i in range(1, nz):
            total = total + mm_nt(dhids[i], dw[cols, hidden_at(i, 0, span)])
        row_send[:, cols] = total.astype(BF)
        for k in range(1, n):
            row_copy(c, k, slots_me).start()
        bck[slots_me, cols] = row_send[at_peer(0), cols]
        return carry

    def back_results(c, column):
        cols = pl.ds(pl.multiple_of(c * 256, 128), 256)
        total = mm(acts[0], w2[hidden_at(0, 0, span), cols])
        for i in range(1, nz):
            total = total + mm(acts[i], w2[hidden_at(i, 0, span), cols])
        out = (total + b2_ref[:, cols].astype(F32)).astype(BF)
        res_send[:, cols] = out
        return column + jnp.sum(
            out.astype(F32) * dres[:, cols].astype(F32), 1, keepdims=True
        )

    parts1 = [slice(i, i + d // 2) for i in (0, d // 2)]
    parts2 = range(0, fs, 128)

    def grad1(i, half, rows):
        part = mm(xta[rows, :], dhids[i, 0:d, half])
        return part + mm(xt[rows, :], dhids[i, d:, half])

    def grad2(i, start, first):
        cols = pl.ds(pl.multiple_of(start + first, 128), 128)
        return mm_tn(acts[i, :, cols], dres[...])

    def extra(i, half):
        gb = jnp.sum(dhids[i, :, half].astype(F32), 0, keepdims=True)
        row = iota((16, d), 0)
        line = jnp.concatenate([gb, jnp.zeros((1, d - fs), F32)], 1)
        return jnp.where(row == 0, line, jnp.where(row == 1, bias2[...], 0.0))

    def leaving(i):
        return r2.at[0] if isinstance(i, int) else acts.at[i, 0:d, half_other]

    def t_copies(i):
        dest = dest_of(i)
        return (
            remote(leaving(i), v1.at[dest], t_sem.at[0, 0, dest], t_sem.at[1, 0, dest], sibling, me),
            remote(t2, v2.at[dest], t_sem.at[0, 1, dest], t_sem.at[1, 1, dest], sibling, me),
        )

    def landing(way, step, at):
        if way == 0:
            return nz - 2 - step + at
        return at + step + 2 - nz if step < nz - 2 else nz

    def u_copies(src1, src2, way, step, target, slot):
        return (
            remote(src1, u1.at[slot], u_sem.at[0, 0, way, step], u_sem.at[1, 0, way, step], target, me),
            remote(src2, u2.at[slot], u_sem.at[0, 1, way, step], u_sem.at[1, 1, way, step], target, me),
        )

    def other_grads(i):
        for first in parts2:
            value = grad2(i, (1 - core) * fs, first)
            t2[first : first + 128, :] = value.astype(BF)
        t2[fs:, :] = extra(i, half_other).astype(BF)
        t_copies(i)[1].start()
        if isinstance(i, int):
            xta[...] = xr[0:d, :].T
            xt[...] = xr[d:, :].T
        for rows in parts1:
            leaving(i)[rows, :] = grad1(i, half_other, rows).astype(BF)
        t_copies(i)[0].start()

    def own_grads(i):
        dest = dest_of(i)
        t_copies(i)[1].wait()
        for first in parts2:
            rows = slice(first, first + 128)
            value = v2[dest, rows, :].astype(F32) + grad2(i, core * fs, first)
            v2[dest, rows, :] = value.astype(BF)
        v2[dest, fs:, :] = (v2[dest, fs:, :].astype(F32) + extra(i, half_own)).astype(BF)
        leave(i, 1)
        t_copies(i)[0].wait()
        for rows in parts1:
            value = v1[dest, rows, :].astype(F32) + grad1(i, half_own, rows)
            v1[dest, rows, :] = value.astype(BF)
        leave(i, 0)

    def leave(i, which):
        dest = dest_of(i)

        @pl.when((z == 0) & (i <= nz - 2))
        def _():
            u_copies(v1.at[dest], v2.at[dest], 0, i, me_r + 2, dest)[which].start()

        @pl.when((z == nz - 1) & (i < nz - 2))
        def _():
            u_copies(v1.at[dest], v2.at[dest], 1, i, me_r - 2, dest)[which].start()

        @pl.when((z == nz - 1) & (i == nz - 2))
        def _():
            u_copies(v1.at[dest], v2.at[dest], 1, i, me_r - 2, nz)[which].start()

    def z_round(s, which):
        v, u = ((v1, u1), (v2, u2))[which]
        pieces = [
            [slice(i, min(i + 128, size)) for i in range(0, size, 128)]
            for size in (d, sz.fs_rows)
        ]
        for way in range(2):
            zz = z if way == 0 else nz - 1 - z
            dest = nz - 1 - s + zz if way == 0 else z - (nz - 1 - s)
            target = me_r + 2 if way == 0 else me_r - 2

            @pl.when((zz >= 1) & (zz <= s))
            def _():
                here = landing(way, s - 1, z)
                there = landing(way, s, z + 1 if way == 0 else z - 1)
                at_here, at_there = (u1.at[here], u2.at[here]), there
                u_copies(*at_here, way, s - 1, target, here)[which].wait_recv()
                for rows in pieces[which]:
                    value = u[here, rows, :].astype(F32) + v[dest, rows, :].astype(F32)
                    u[here, rows, :] = value.astype(BF)
                u_copies(*at_here, way, s, target, at_there)[which].start()

    prepare(0)
    load_w2.wait()
    load_w1.wait()
    cells(0, nz, at_peer(0))
    for k in range(1, n):
        prepare(k)
    for k in range(1, n):
        to_peer(xs.at[at_peer(k), :], xr.at[at_peer(n - k), :], x_sem, k).wait_send()
        to_peer(xs.at[at_peer(n - k), :], xr.at[at_peer(k), :], x_sem, n - k).wait_recv()
    cells(0, 1, others)
    other_grads(0)
    own_grads(0)
    cells(1, nz, others)
    lax.fori_loop(0, d // 256, back_rows, 0)
    column = lax.fori_loop(
        0, d // 256, back_results, jnp.zeros((sz.all_slots, 1), F32)
    )
    for k in range(n):
        line = jnp.where(square, column[at_peer(k), :], 0.0)
        qs[k] = jnp.broadcast_to(jnp.sum(line, 0, keepdims=True), (8, sz.slots))
    qr[me] = qs[0]
    ret[slots_me, :] = res_send[at_peer(0), :]
    for k in range(1, n):
        to_peer(qs.at[k], qr.at[me], q_sem, k).start()
    for k in range(1, n):
        to_peer(res_send.at[at_peer(k), :], ret.at[slots_me, :], ret_sem, k).start()

    def slice_step(i, carry):
        other_grads(i)
        own_grads(i)
        return carry

    if nz > 2:
        z_round(1, 1)
    lax.fori_loop(1, nz, slice_step, 0)
    if nz > 2:
        z_round(1, 0)
    dense_load = pltpu.make_async_copy(o_save, dw, wsem.at[0])
    dense_load.start()

    for k in range(1, n):
        src = lax.rem(me + n - k, n)
        for c in range(d // 256):
            row_copy(c, k, rows_at(src, sz.slots)).wait()
        to_peer(qs.at[k], qr.at[src], q_sem, k).wait()
    mixed = sgrad = wide2
    lane = iota((sz.rows, sz.small), 1)
    weighted = jnp.zeros((sz.rows, sz.small), F32)
    for e in range(sz.experts):
        q = jnp.sum(comb[e].astype(F32) * qr[e, 0:1, :], 1, keepdims=True)
        weighted = jnp.where(lane == 8 + e, q, weighted)
    total = jnp.sum(weighted, 1, keepdims=True)
    logit_low = (weighted - probs[...] * total).astype(BF)
    sgrad[...] = mm(logit_low, smf[...].astype(BF))
    for e in range(sz.experts):
        sgrad[...] += mm(comb[e], bck[e * sz.slots : (e + 1) * sz.slots, :])
    back2, gain2, shift2 = normalize_back(resid[...], smf[1:2, :], sgrad[...])
    rgrad = wide1
    rgrad[...] = gpad[...].astype(F32) + back2
    low = rgrad[...].astype(BF)
    bias_out = jnp.sum(low.astype(F32), 0, keepdims=True)

    dense = w2
    wide = d // 2
    keep = pl.ds(pl.multiple_of(core * wide, 128), wide)
    give = pl.ds(pl.multiple_of((1 - core) * wide, 128), wide)

    def chunk_rows(j, start, size):
        return pl.ds(pl.multiple_of(j * d + start, 16), size)

    def parked(j):
        cols = pl.ds(pl.multiple_of(lax.rem(j, 2) * wide, 128), wide)
        return acts.at[lax.div(j, 2), 0:d, cols]

    def to_sibling(j):
        return remote(
            dense.at[chunk_rows(j, 0, d), give],
            parked(j),
            d1_sem.at[0, j],
            d1_sem.at[1, j],
            sibling,
            me,
        )

    def to_owner(j, k):
        e = lax.rem(me + k, n)
        return remote(
            dense.at[chunk_rows(j, e * sz.shard, sz.shard), keep],
            r2.at[k - 1, pl.ds(pl.multiple_of(j * sz.shard, 16), sz.shard), :],
            d2_sem.at[0, j, k],
            d2_sem.at[1, j, k],
            me_r,
            e,
        )

    outer = (z == 0) | (z == nz - 1)
    across = me_r - 2 + 4 * odd

    def inward(j):
        return remote(
            z1.at[j], z2.at[0, j], z1_sem.at[0, 0, j], z1_sem.at[1, 0, j], partner, me
        )

    def swap(j):
        return remote(
            z1.at[j], z2.at[1, j], z1_sem.at[0, 1, j], z1_sem.at[1, 1, j], across, me
        )

    def outward(j):
        piece = od.at[j, :, keep]
        return remote(piece, piece, z2_sem.at[0, j], z2_sem.at[1, j], partner, me)

    def to_twin(j, cols):
        piece = od.at[j, :, cols]
        return remote(piece, piece, z3_sem.at[0, j], z3_sem.at[1, j], sibling, me)

    def stage1(j):
        to_sibling(j).wait()
        rows = chunk_rows(j, 0, d)
        dense[rows, keep] = (dense[rows, keep].astype(F32) + parked(j)[...].astype(F32)).astype(BF)
        for k in range(1, n):
            to_owner(j, k).start()

    def stage2(j):
        acc = dense[chunk_rows(j, me * sz.shard, sz.shard), keep].astype(F32)
        for k in range(1, n):
            to_owner(j, k).wait()
            acc = acc + r2[k - 1, j * sz.shard : (j + 1) * sz.shard, :].astype(F32)
        z1[j] = acc.astype(BF)
        pl.when(outer)(lambda: inward(j).start())

    def stage3(j):
        @pl.when(jnp.logical_not(outer))
        def _():
            inward(j).wait_recv()
            z1[j] = (z1[j].astype(F32) + z2[0, j].astype(F32)).astype(BF)
            swap(j).start()

    def stage4(j):
        @pl.when(jnp.logical_not(outer))
        def _():
            swap(j).wait()
            od[j, :, keep] = (z1[j].astype(F32) + z2[1, j].astype(F32)).astype(BF)
            outward(j).start()
            to_twin(j, keep).start()

    def stage5(j):
        @pl.when(outer)
        def _():
            inward(j).wait_send()
            outward(j).wait_recv()
            to_twin(j, keep).start()

    def stage6(j):
        pl.when(jnp.logical_not(outer))(lambda: outward(j).wait_send())
        to_twin(j, keep).wait_send()
        to_twin(j, give).wait_recv()
        pltpu.make_async_copy(od.at[j], o_dense.at[j], isem.at[j]).start()

    dense[chunk_rows(0, 0, d), :] = mm(ctx_t[...], low).astype(BF)
    to_sibling(0).start()
    dense_load.wait()
    for k in range(1, n):
        theirs = rows_at(lax.rem(me + n - k, n), sz.slots)
        to_peer(res_send.at[at_peer(k), :], ret.at[theirs, :], ret_sem, k).wait()
    cgrad = sends.at[3 * sz.rows : 4 * sz.rows, :]

    def load_probs(pair):
        slot = lax.rem(pair, 2)
        return pltpu.make_async_copy(o_probs.at[pair], pbuf.at[slot], psem.at[slot])

    load_probs(0).start()
    cgrad[...] = mm_nt(low, dw[:, 3 * d : 4 * d]).astype(BF)
    sm[...] = mm_tn(logit_low, second[...])

    scale = 1.0 / math.sqrt(HEAD_DIM)
    half_lane = iota((sz.seq, 128), 1)

    def pair_step(pair, carry):
        load_probs(pair).wait()

        @pl.when(pair + 1 < sz.pairs)
        def _():
            load_probs(pair + 1).start()

        for image in range(sz.images):
            rows = slice(image * sz.seq, (image + 1) * sz.seq)
            q2, k2, v2_ = (qkv[rows, pair_cols(pair, j)] for j in range(3))
            c2 = cgrad[rows, pl.ds(pl.multiple_of(pair * 128, 128), 128)]
            there = pl.ds(
                pl.multiple_of(lax.div(pair, 2) * sz.rows + image * sz.seq, 16), sz.seq
            )
            dq = jnp.zeros((sz.seq, 128), F32)
            dk = jnp.zeros((sz.seq, 128), F32)
            dv = jnp.zeros((sz.seq, 128), F32)
            for half in range(2):
                mask = (half_lane >= half * 64) & (half_lane < half * 64 + 64)
                zero = jnp.zeros_like(q2)
                ch = jnp.where(mask, c2, zero)
                p = pbuf[lax.rem(pair, 2), image * 2 + half]
                dv = dv + mm_tn(p, ch)
                pb = mm_nt(ch, v2_)
                p32 = p.astype(F32)
                mix = jnp.sum(pb * p32, -1, keepdims=True)
                ds = (p32 * (pb - mix)).astype(BF)
                dq = dq + mm(ds, jnp.where(mask, k2, zero))
                dk = dk + mm_tn(ds, jnp.where(mask, q2, zero))
            sends[there, pair_cols(pair, 0, 0)] = (dq * scale).astype(BF)
            sends[there, pair_cols(pair, 1, 0)] = (dk * scale).astype(BF)
            sends[there, pair_cols(pair, 2, 0)] = dv.astype(BF)
        return carry

    def group_step(g, carry):
        lax.fori_loop(2 * g, 2 * g + 2, pair_step, 0)
        dense[chunk_rows(g + 1, 0, d), :] = mm(
            normed_t[...], sends[rows_at(g, sz.rows), :]
        ).astype(BF)
        to_sibling(g + 1).start()
        stage1(g)

        @pl.when(g == sz.groups - 2)
        def _():
            for s in range(2, nz - 1):
                z_round(s, 1)

        return carry

    lax.fori_loop(0, sz.groups, group_step, 0)
    for s in range(2, nz - 1):
        z_round(s, 0)
    stage1(sz.groups)

    ngrad = sgrad
    ngrad[...] = mm_nt(sends[0 : sz.rows, :], dw[:, 0:d])
    for g in range(1, sz.groups):
        grads = sends[g * sz.rows : (g + 1) * sz.rows, :]
        ngrad[...] += mm_nt(grads, dw[:, g * d : (g + 1) * d])
    stage2(0)
    x = mm(pad_matrix(sz), tok_ref[...])
    back1, gain1, shift1 = normalize_back(x, smf[0:1, :], ngrad[...])
    stage[...] = mm(unpad_matrix(sz), (rgrad[...] + back1).astype(BF)).astype(BF)
    store = pltpu.make_async_copy(stage, o_gin, wsem.at[2])
    store.start()
    sums = [
        jnp.sum(sends[g * sz.rows : (g + 1) * sz.rows, :].astype(F32), 0, keepdims=True)
        for g in range(sz.groups)
    ]
    bias_q = jnp.concatenate([total[:, 0:256] for total in sums], 1)
    bias_v = jnp.concatenate([total[:, 512:768] for total in sums], 1)
    row = iota((sz.small, d), 0)
    small = sm[...]
    for i, value in enumerate((gain1, gain2, shift1, bias_q, bias_v, bias_out, shift2)):
        small = jnp.where(row == i, value, small)
    sm[...] = small
    smb = sme.at[n]
    smb[...] = small.astype(BF)
    s_first = remote(smb, smr, s1_sem.at[0], s1_sem.at[1], sibling, me)
    s_first.start()

    stage2(1)
    stage3(0)
    mixed[...] = resid[...]
    for e in range(sz.experts):
        block = slice(e * sz.slots, (e + 1) * sz.slots)
        mixed[...] += probs[:, 8 + e : 9 + e] * mm(comb[e], ret[block, :])
    store.wait()
    stage[...] = mm(unpad_matrix(sz), mixed[...].astype(BF)).astype(BF)
    store = pltpu.make_async_copy(stage, o_out, wsem.at[2])
    store.start()

    s_first.wait()
    chip_small = (sm[...] + smr[...].astype(F32)).astype(BF)
    for e in range(n):
        r = iota((sz.shard_pad, d), 0)
        c = iota((sz.shard_pad, d), 1)
        pick = ((c == r + e * sz.shard) & (r < sz.shard)).astype(F32).astype(BF)
        sme[e, :, 0 : sz.shard_pad] = mm_nt(chip_small, pick).astype(BF)

    def small_peer(k):
        piece = sme.at[lax.rem(me + k, n), :, 0 : sz.shard_pad]
        return to_peer(piece, sme_r.at[k], s2_sem, k)

    for k in range(1, n):
        small_peer(k).start()
    stage2(2)
    stage3(1)
    stage4(0)
    acc = sme[me, :, 0 : sz.shard_pad].astype(F32)
    for k in range(1, n):
        small_peer(k).wait()
        acc = acc + sme_r[k].astype(F32)
    smz_r[0] = acc.astype(BF)
    for k in range(1, nz):
        to_z(smz_r.at[0], smz_r.at[k], s3_sem, k).start()
    stage2(3)
    stage3(2)
    stage4(1)

    for way in range(2):
        zz = z if way == 0 else nz - 1 - z
        target = me_r + 2 if way == 0 else me_r - 2

        @pl.when(zz >= 1)
        def _():
            here = landing(way, nz - 2, z)
            for cp in u_copies(u1.at[here], u2.at[here], way, nz - 2, target, here):
                cp.wait_recv()
            v1[z] = (v1[z].astype(F32) + u1[here].astype(F32)).astype(BF)
            v2[z] = (v2[z].astype(F32) + u2[here].astype(F32)).astype(BF)

    stores = [
        pltpu.make_async_copy(v1.at[z], o_w1, wsem.at[0]),
        pltpu.make_async_copy(v2.at[z], o_w2, wsem.at[1]),
    ]
    for cp in stores:
        cp.start()
    stage3(3)
    stage4(2)
    acc = smz_r[0].astype(F32)
    for k in range(1, nz):
        to_z(smz_r.at[0], smz_r.at[k], s3_sem, k).wait()
        acc = acc + smz_r[k].astype(F32)
    o_small[...] = acc
    stage4(3)
    for j in range(sz.chunks):
        stage5(j)
    for j in range(sz.chunks):
        stage6(j)
    for j in range(sz.chunks):
        pltpu.make_async_copy(od.at[j], o_dense.at[j], isem.at[j]).wait()

    for cp in stores:
        cp.wait()
    store.wait()
    for s in range(nz - 1):
        for way in range(2):
            zz = z if way == 0 else nz - 1 - z
            target = me_r + 2 if way == 0 else me_r - 2

            @pl.when(zz <= s)
            def _():
                for cp in u_copies(v1.at[0], v2.at[0], way, s, target, 0):
                    cp.wait_send()
    for k in range(1, n):
        for cp in small_sends(k):
            cp.wait_send()


def block(sz, tokens, routes, router, gains, biases, b1, b2, grad, wq, wp, w1, w2):
    vmem = pl.BlockSpec(memory_space=pltpu.VMEM)
    hbm = pl.BlockSpec(memory_space=pl.ANY)
    rows, d, slots, fs, nz, n = sz.rows, sz.d, sz.all_slots, sz.fs, sz.nz, sz.n_exp
    half = d // 2
    dma = pltpu.SemaphoreType.DMA
    outs = [
        ((sz.chunks, sz.shard, d), BF),
        ((sz.small, sz.shard_pad), F32),
        ((sz.tok, d), BF),
        ((sz.tok, d), BF),
        ((d, fs), BF),
        ((sz.fs_rows, d), BF),
        ((sz.pairs, sz.images * 2, sz.seq, sz.seq), BF),
        ((d, 4 * d), BF),
    ]
    buffers = [
        (tokens.shape, BF),
        (b1.shape, BF),
        (b2.shape, BF),
        ((sz.chunks, sz.shard, d), BF),
        ((d, 4 * d), BF),
        (w2.shape, BF),
        ((sz.tok, d), BF),
        ((slots, d), BF),
        ((slots, d), BF),
        ((rows, 3 * d), BF),
        ((d, rows), BF),
        ((rows, d), F32),
        ((rows, d), BF),
        ((d, rows), BF),
        ((rows, sz.small), F32),
        ((sz.small, d), F32),
        ((rows, d), BF),
        ((sz.experts, rows, sz.slots), BF),
        ((n, sz.ep, sz.slots), F32),
        ((n, sz.ep, sz.slots), F32),
        ((n, *router.shape), BF),
        ((n, *gains.shape), BF),
        ((n, *biases.shape), BF),
        ((1, d), F32),
        ((d, slots - d), BF),
        ((d, d), BF),
        ((nz, slots, 2 * fs), BF),
        ((nz, slots, 2 * fs), BF),
        ((rows, d), F32),
        ((rows, d), F32),
        ((2 * slots, d), BF),
        ((slots, d), BF),
        ((slots, d), BF),
        ((n, 8, sz.slots), F32),
        ((n, 8, sz.slots), F32),
        ((sz.fs_rows, d), BF),
        ((nz, d, fs), BF),
        ((nz, sz.fs_rows, d), BF),
        ((nz + 1, d, fs), BF),
        ((nz + 1, sz.fs_rows, d), BF),
        ((2, 2 * sz.images, sz.seq, sz.seq), BF),
        ((n - 1, d, half), BF),
        ((sz.chunks, sz.shard, half), BF),
        ((2, sz.chunks, sz.shard, half), BF),
        ((sz.small, d), F32),
        ((sz.small, d), BF),
        ((n + 1, sz.small, d), BF),
        ((n, sz.small, sz.shard_pad), BF),
        ((nz, sz.small, sz.shard_pad), BF),
    ]
    sems = (
        [dma((7,)), dma((4,)), dma((2,))]
        + [dma((2, sz.chunks, 2, n)), dma((2, sz.chunks, n))]
        + [dma((2, sz.chunks, 2, n)), dma((sz.chunks, 3))]
        + [dma((3, 2, n))]
        + [dma((2, n))] * 3
        + [dma((2, 2, nz)), dma((2, 2, 2, nz - 1))]
        + [dma((2, n)), dma((2, d // 256, n)), dma((2, n))]
        + [dma((2, sz.chunks)), dma((2, sz.chunks, n))]
        + [dma((2, 2, sz.chunks)), dma((2, sz.chunks))]
        + [dma((2, sz.chunks)), dma((2,)), dma((2, n)), dma((2, nz))]
    )
    return pl.pallas_call(
        partial(block_kernel, sz),
        name="block",
        out_shape=[jax.ShapeDtypeStruct(s, t) for s, t in outs],
        in_specs=[hbm] * 12,
        out_specs=[hbm, vmem] + [hbm] * 6,
        scratch_shapes=[pltpu.VMEM(s, t) for s, t in buffers[:1]]
        + [pltpu.VMEM(routes.shape, jnp.int32)]
        + [pltpu.VMEM(s, t) for s, t in buffers[1:]]
        + sems,
        compiler_params=pltpu.CompilerParams(
            collective_id=1, has_side_effects=True, vmem_limit_bytes=62 << 20
        ),
    )(tokens, routes, router, gains, biases, b1, b2, grad, wq, wp, w1, w2)


def plain_rest(sz, state, tokens, w1, b1, w2, b2):
    xr, dres, qkv, pall, ctx_t, resid, second, normed_t, probs, wq, wp, smf, gpad, comb = state
    d, n = sz.d, sz.experts
    scale = 1.0 / math.sqrt(HEAD_DIM)
    h = mm(xr, w1) + b1
    cdf, pdf = gelu_parts(h)
    act = (h * cdf).astype(BF)
    result = (mm(act, w2) + b2).astype(BF)
    dhid = (mm_nt(dres, w2) * (cdf + h * pdf)).astype(BF)
    row_grad = mm_nt(dhid, w1).astype(BF)
    swap = partial(
        lax.all_to_all, axis_name="exp", split_axis=0, concat_axis=0, tiled=True
    )
    ret = swap(result).reshape(n, sz.slots, d)
    bck = swap(row_grad).reshape(n, sz.slots, d)
    g32 = gpad.astype(F32)
    p = probs[:, 8 : 8 + n]
    picked = jnp.einsum("ets,esd->etd", comb, ret, preferred_element_type=F32)
    mixed = resid + jnp.einsum("te,etd->td", p, picked, precision="highest")
    pg = jnp.sum(g32[None] * picked, -1).T
    lg = (p * (pg - jnp.sum(pg * p, 1, keepdims=True))).astype(BF)
    sgrad = mm(lg, smf[8 : 8 + n].astype(BF))
    sgrad = sgrad + jnp.einsum("ets,esd->td", comb, bck, preferred_element_type=F32)
    back2, gain2, shift2 = normalize_back(resid, smf[1:2], sgrad)
    rgrad = g32 + back2
    low = rgrad.astype(BF)
    cgrad = mm_nt(low, wp).astype(BF)
    four = (sz.images, sz.seq, d // HEAD_DIM, HEAD_DIM)
    q, k, v, c = (
        a.reshape(four)
        for a in (qkv[:, :d], qkv[:, d : 2 * d], qkv[:, 2 * d :], cgrad)
    )
    prob = pall.reshape(sz.pairs, sz.images, 2, sz.seq, sz.seq)
    prob = prob.transpose(1, 0, 2, 3, 4).reshape(sz.images, -1, sz.seq, sz.seq)
    product = partial(jnp.einsum, preferred_element_type=F32)
    dv = product("ihst,ishd->ithd", prob, c).astype(BF)
    pb = product("ishd,ithd->ihst", c, v)
    p32 = prob.astype(F32)
    ds = (p32 * (pb - jnp.sum(pb * p32, -1, keepdims=True))).astype(BF)
    dq = (product("ihst,ithd->ishd", ds, k) * scale).astype(BF)
    dk = (product("ihst,ishd->ithd", ds, q) * scale).astype(BF)
    dqkv = jnp.concatenate([a.reshape(sz.rows, d) for a in (dq, dk, dv)], 1)
    x = mm(pad_matrix(sz), tokens)
    back1, gain1, shift1 = normalize_back(x, smf[0:1], mm_nt(dqkv, wq))
    gin = (rgrad + back1).astype(BF)
    sums = jnp.sum(dqkv.astype(F32), 0, keepdims=True)
    small = jnp.concatenate(
        [gain1, gain2, shift1, sums[:, :d], sums[:, 2 * d :]]
        + [jnp.sum(low.astype(F32), 0, keepdims=True), shift2, mm_tn(lg, second)]
    )

    def dense(grad, dim):
        total = lax.psum(grad.astype(BF), "rep")
        total = lax.psum_scatter(total, "exp", scatter_dimension=dim, tiled=True)
        return total.astype(F32)

    def owned(grad, dim):
        total = lax.psum_scatter(
            grad[None].astype(BF), "rep", scatter_dimension=dim, tiled=True
        )
        return total.astype(F32)

    def unpad(rows):
        return rows.reshape(sz.images, sz.seq, d)[:, :SEQ].reshape(sz.tok, d)

    sums = dense(small, 1)
    return (
        unpad(mixed.astype(BF)),
        unpad(gin),
        dense(mm(normed_t, dqkv), 0),
        dense(mm(ctx_t, low), 0),
        sums[7:].T,
        sums[0:2],
        sums[2:7],
        owned(mm_tn(xr, dhid), 2),
        owned(jnp.sum(dhid.astype(F32), 0), 1),
        owned(mm_tn(act, dres), 1),
        owned(jnp.sum(dres.astype(F32), 0), 1),
    )


def on_device(
    mesh,
    tokens,
    routes,
    out_grad,
    attn_qkv,
    attn_out,
    router,
    norm_gains,
    dense_biases,
    expert_in,
    expert_in_bias,
    expert_out,
    expert_out_bias,
):
    sz = Sizes(mesh, tokens.shape[0], tokens.shape[1], expert_in.shape[2])
    d, fs = sz.d, sz.fs
    w1, w2 = expert_in[0], expert_out[0]
    small = (router.T, norm_gains, dense_biases)
    if (sz.nz, sz.chunks * sz.shard, 2 * fs) != (4, d, d) or sz.all_slots < 2 * sz.rows:
        state = front(sz, tokens, out_grad, routes.T, attn_qkv, attn_out, *small)
        bias1, bias2 = expert_in_bias.astype(F32), expert_out_bias.astype(F32)
        return plain_rest(sz, state, tokens, w1, bias1, w2, bias2)
    dense, sums, out, gin, g1, g2, _, _ = block(
        sz,
        tokens,
        routes.T,
        *small,
        expert_in_bias,
        expert_out_bias,
        out_grad,
        attn_qkv,
        attn_out,
        w1,
        w2,
    )
    return finish(sz, out, gin, g1, g2, dense, sums)


def solution(mesh):
    both = P(("rep", "exp"), None)
    rows = P("exp", None)
    cols = P(None, "exp")
    cube = P("exp", None, None)
    in_specs = (both, both, both, rows, rows, rows, cols, cols, cube, rows, cube, rows)
    out_specs = (
        both,
        both,
        rows,
        rows,
        rows,
        cols,
        cols,
        P("exp", None, "rep"),
        P("exp", "rep"),
        P("exp", "rep", None),
        P("exp", "rep"),
    )
    return jax.shard_map(
        partial(on_device, mesh),
        mesh=mesh,
        in_specs=in_specs,
        out_specs=out_specs,
        check_vma=False,
    )
```

```python
from functools import partial
import math

import jax
import jax.numpy as jnp
from jax import lax
from jax.experimental import pallas as pl
from jax.experimental.pallas import tpu as pltpu
from jax.sharding import PartitionSpec as P

HEAD_DIM = 64
SEQ = 197
EPS = 1e-06
BF = jnp.bfloat16
F32 = jnp.float32
MESH = pl.DeviceIdType.MESH


def up(value, step):
    return (value + step - 1) // step * step


def mm(a, b):
    return lax.dot_general(a, b, (((1,), (0,)), ((), ())), preferred_element_type=F32)


def mm_nt(a, b):
    return lax.dot_general(a, b, (((1,), (1,)), ((), ())), preferred_element_type=F32)


def mm_tn(a, b):
    return lax.dot_general(a, b, (((0,), (0,)), ((), ())), preferred_element_type=F32)


def iota(shape, dim):
    return lax.broadcasted_iota(jnp.int32, shape, dim)


def rows_at(index, size):
    return pl.ds(pl.multiple_of(index * size, size), size)


def normalize(values, gain, shift):
    center = values - jnp.mean(values, -1, keepdims=True)
    spread = jnp.mean(center * center, -1, keepdims=True)
    return center * lax.rsqrt(spread + EPS) * gain + shift


class Sizes:
    def __init__(self, mesh, tok_rows, width, ff):
        self.n_exp = mesh.shape["exp"]
        self.n_rep = mesh.shape["rep"]
        self.tok = tok_rows
        self.images = tok_rows // SEQ
        self.seq = up(SEQ, 16)
        self.rows = self.images * self.seq
        self.d = width
        self.ff = ff
        self.experts = self.n_exp
        self.cap = (18 * tok_rows + 8 * self.experts - 1) // (8 * self.experts)
        self.slots = up(self.cap, 16)
        self.all_slots = self.slots * self.experts
        self.shard = width // self.n_exp
        self.shard_pad = up(self.shard, 128)
        self.ep = up(self.experts, 8)
        self.small = up(8 + self.ep, 16)
        self.pairs = width // 128
        self.nz = self.n_rep // 2
        self.fs = ff // self.n_rep
        self.fs_rows = self.fs + 16
        self.groups = self.pairs // 2
        self.chunks = self.groups + 1


def pad_matrix(sz):
    row = iota((sz.rows, sz.tok), 0)
    col = iota((sz.rows, sz.tok), 1)
    want = jnp.full((sz.rows, sz.tok), -1, jnp.int32)
    for image in range(sz.images):
        inside = (row >= image * sz.seq) & (row < image * sz.seq + SEQ)
        want = jnp.where(inside, row - image * (sz.seq - SEQ), want)
    return (want == col).astype(F32).astype(BF)


def unpad_matrix(sz):
    row = iota((sz.tok, sz.rows), 0)
    col = iota((sz.tok, sz.rows), 1)
    want = row
    for image in range(1, sz.images):
        want = jnp.where(row >= image * SEQ, row + image * (sz.seq - SEQ), want)
    return (want == col).astype(F32).astype(BF)


def front_kernel(
    sz,
    tok_ref,
    grad_ref,
    routes_ref,
    wq_shard,
    wp_shard,
    router_ref,
    gains_ref,
    biases_ref,
    xr,
    dres,
    qkv,
    pall,
    ctx_t,
    resid,
    second,
    normed_t,
    probs,
    wq,
    wp,
    smf,
    gpad,
    comb,
    ctx,
    normed,
    pmat,
    gr,
    gater,
    xs,
    gs,
    gates,
    routers,
    gains,
    biases,
    wq_sem,
    wp_sem,
    zq_sem,
    zp_sem,
    cq_sem,
    cp_sem,
    sm_sem,
    g_sem,
    x_sem,
    ga_sem,
):
    me_r = lax.axis_index("rep")
    me = lax.axis_index("exp")
    n = sz.n_exp
    core = lax.rem(me_r, 2)
    sibling = me_r + 1 - 2 * core
    odd = lax.rem(lax.div(me_r, 2), 2)
    partner = me_r + 2 - 4 * odd

    barrier = pltpu.get_barrier_semaphore()
    for k in range(1, n):
        pl.semaphore_signal(
            barrier, inc=1, device_id=(me_r, lax.rem(me + k, n)), device_id_type=MESH
        )
    for rep in (sibling, partner):
        pl.semaphore_signal(barrier, inc=1, device_id=(rep, me), device_id_type=MESH)
    pl.semaphore_wait(barrier, n + 1)

    def remote(src, dst, send, recv, rep, exp):
        return pltpu.make_async_remote_copy(
            src_ref=src,
            dst_ref=dst,
            send_sem=send,
            recv_sem=recv,
            device_id=(rep, exp),
            device_id_type=MESH,
        )

    def to_peer(src, dst, sems, k):
        return remote(
            src, dst, sems.at[0, k], sems.at[1, k], me_r, lax.rem(me + k, n)
        )

    class Gather:
        def __init__(self, shard, full, width, peer_sem, layer_sem, twin_sem):
            self.shard, self.full = shard, full
            self.piece = width // 6
            self.peer_sem, self.layer_sem, self.twin_sem = peer_sem, layer_sem, twin_sem

        def cols(self, side, first, count):
            start = side * 3 * self.piece + first * self.piece
            return pl.ds(pl.multiple_of(start, 128), count * self.piece)

        def rows(self, k):
            return rows_at(lax.rem(me + n - k, n), sz.shard)

        def peer(self, k):
            cols = self.cols(core, odd, 2)
            return to_peer(
                self.shard.at[:, cols],
                self.full.at[rows_at(me, sz.shard), cols],
                self.peer_sem,
                k,
            )

        def layer(self, k, mine=True):
            part = 2 * odd if mine else 2 - 2 * odd
            piece = self.full.at[self.rows(k), self.cols(core, part, 1)]
            sem = self.layer_sem
            return remote(piece, piece, sem.at[0, k], sem.at[1, k], partner, me)

        def twin(self, k, late, side):
            first, count = (2 - 2 * odd, 1) if late else (odd, 2)
            piece = self.full.at[self.rows(k), self.cols(side, first, count)]
            sem = self.twin_sem
            return remote(
                piece, piece, sem.at[0, late, k], sem.at[1, late, k], sibling, me
            )

        def start(self):
            for k in range(1, n):
                self.peer(k).start()
            self.full[rows_at(me, sz.shard), :] = self.shard[...]

        def forward(self):
            for k in range(1, n):
                self.peer(k).wait_recv()
                self.layer(k).start()
                self.twin(k, 0, core).start()

        def finish(self):
            for k in range(1, n):
                self.layer(k, False).wait_recv()
                self.twin(k, 1, core).start()
            for k in range(1, n):
                for late in range(2):
                    self.twin(k, late, 1 - core).wait_recv()

        def drain(self):
            for k in range(1, n):
                self.peer(k).wait_send()
                self.layer(k).wait_send()
                for late in range(2):
                    self.twin(k, late, core).wait_send()

    gather_q = Gather(wq_shard, wq, 3 * sz.d, wq_sem, zq_sem, cq_sem)
    gather_p = Gather(wp_shard, wp, sz.d, wp_sem, zp_sem, cp_sem)

    def small_sends(k):
        return [
            to_peer(src, dst.at[me], sm_sem.at[i], k)
            for i, (src, dst) in enumerate(
                ((gains_ref, gains), (biases_ref, biases), (router_ref, routers))
            )
        ]

    for k in range(1, n):
        for cp in small_sends(k):
            cp.start()
    gather_q.start()
    gains[me] = gains_ref[...]
    biases[me] = biases_ref[...]
    routers[me] = router_ref[...]

    choice = (routes_ref[...].astype(F32) + 1.0).astype(BF)
    lines = mm_nt(choice, pad_matrix(sz)).astype(jnp.int32) - 1
    ids = iota((sz.ep, sz.rows), 0)
    oh1 = (lines[0:1, :] == ids).astype(F32)
    oh2 = (lines[1:2, :] == ids).astype(F32)
    before = (
        (iota((sz.rows, sz.rows), 0) < iota((sz.rows, sz.rows), 1))
        .astype(F32)
        .astype(BF)
    )
    pos1 = mm(oh1.astype(BF), before)
    pos2 = mm(oh2.astype(BF), before) + jnp.sum(oh1, 1, keepdims=True)
    place = oh1 * pos1 + oh2 * pos2
    kept = (oh1 + oh2 > 0.5) & (place < sz.cap - 0.5)
    slot = jnp.where(kept, place, -1.0).astype(jnp.int32)
    slot_ids = iota((sz.slots, sz.rows), 0)
    for e in range(sz.experts):
        pmat[e * sz.slots : (e + 1) * sz.slots, :] = (
            (slot_ids == slot[e : e + 1, :]).astype(F32).astype(BF)
        )
    eye = (iota((sz.rows, sz.rows), 0) == iota((sz.rows, sz.rows), 1)).astype(F32)
    slot_cols = mm_nt(eye.astype(BF), slot.astype(F32).astype(BF)).astype(jnp.int32)
    lane_ids = iota((sz.rows, sz.slots), 1)
    for e in range(sz.experts):
        comb[e] = (slot_cols[:, e : e + 1] == lane_ids).astype(F32).astype(BF)

    spread = pad_matrix(sz)
    gpad[...] = mm(spread, grad_ref[...]).astype(BF)
    for e in range(sz.experts):
        block = slice(e * sz.slots, (e + 1) * sz.slots)
        gs[block, :] = mm(pmat[block, :], gpad[...]).astype(BF)
    slots_me = rows_at(me, sz.slots)
    gr[slots_me, :] = gs[slots_me, :]

    x = mm(spread, tok_ref[...])
    for k in range(1, n):
        for cp in small_sends(k):
            cp.wait_recv()
    smf[...] = jnp.zeros_like(smf)
    for j in range(n):
        r = iota((sz.shard, sz.d), 0)
        c = iota((sz.shard, sz.d), 1)
        pick = (c == r + j * sz.shard).astype(F32).astype(BF)
        smf[0:2, :] += mm(gains[j], pick)
        smf[2:7, :] += mm(biases[j], pick)
        smf[8 : 8 + sz.experts, :] += mm(routers[j], pick)
    normed[...] = normalize(x, smf[0:1, :], smf[2:3, :]).astype(BF)
    normed_t[...] = normed[...].T

    gather_q.forward()
    gather_p.start()
    gather_q.finish()
    for j, bias_row in ((0, 3), (1, None), (2, 4)):
        cols = slice(j * sz.d, (j + 1) * sz.d)
        out = mm(normed[...], wq[:, cols])
        if bias_row is not None:
            out = out + smf[bias_row : bias_row + 1, :]
        qkv[:, cols] = out.astype(BF)
    for k in range(1, n):
        dst = rows_at(lax.rem(me + k, n), sz.slots)
        to_peer(gs.at[dst, :], gr.at[slots_me, :], g_sem, k).start()

    scale = 1.0 / math.sqrt(HEAD_DIM)
    lane = iota((sz.seq, 128), 1)
    live = iota((sz.seq, sz.seq), 1) < SEQ

    def pair_step(pair, carry):
        for image in range(sz.images):
            rows = slice(image * sz.seq, (image + 1) * sz.seq)
            q2 = qkv[rows, pl.ds(pl.multiple_of(pair * 128, 128), 128)]
            k2 = qkv[rows, pl.ds(pl.multiple_of(sz.d + pair * 128, 128), 128)]
            v2 = qkv[rows, pl.ds(pl.multiple_of(2 * sz.d + pair * 128, 128), 128)]
            total = jnp.zeros((sz.seq, 128), F32)
            for half in range(2):
                mask = (lane >= half * 64) & (lane < half * 64 + 64)
                s = mm_nt(jnp.where(mask, q2, jnp.zeros_like(q2)), k2) * scale
                s = jnp.where(live, s, -1e30)
                e = jnp.exp(s - jnp.max(s, -1, keepdims=True))
                p = (e / jnp.sum(e, -1, keepdims=True)).astype(BF)
                pall[pair, image * 2 + half] = p
                total = total + mm(p, jnp.where(mask, v2, jnp.zeros_like(v2)))
            ctx[rows, pl.ds(pl.multiple_of(pair * 128, 128), 128)] = total.astype(BF)
        return carry

    lax.fori_loop(0, sz.pairs, pair_step, 0)

    gather_p.forward()
    gather_p.finish()
    res = (
        mm(spread, tok_ref[...])
        + mm(ctx[...], wp[...])
        + smf[5:6, :]
    )
    resid[...] = res
    low = normalize(res, smf[1:2, :], smf[6:7, :]).astype(BF)
    second[...] = low

    for e in range(sz.experts):
        block = slice(e * sz.slots, (e + 1) * sz.slots)
        xs[block, :] = mm(pmat[block, :], second[...]).astype(BF)
    for k in range(1, n):
        dst = rows_at(lax.rem(me + k, n), sz.slots)
        to_peer(xs.at[dst, :], xr.at[slots_me, :], x_sem, k).start()
    xr[slots_me, :] = xs[slots_me, :]

    small_low = smf[...].astype(BF)
    logit_rows = mm_nt(small_low, low)[8 : 8 + sz.ep, :]
    logit_rows = jnp.where(iota((sz.ep, sz.rows), 0) < sz.experts, logit_rows, -1e30)
    e_rows = jnp.exp(logit_rows - jnp.max(logit_rows, 0, keepdims=True))
    prob_rows = e_rows / jnp.sum(e_rows, 0, keepdims=True)
    hi = prob_rows.astype(BF)
    left = prob_rows - hi.astype(F32)
    mid = left.astype(BF)
    low3 = (left - mid.astype(F32)).astype(BF)
    for e in range(sz.experts):
        block = pmat[e * sz.slots : (e + 1) * sz.slots, :]
        gates[e] = mm_nt(hi, block) + mm_nt(mid, block) + mm_nt(low3, block)
    for k in range(1, n):
        to_peer(
            gates.at[lax.rem(me + k, n)], gater.at[me], ga_sem, k
        ).start()
    gater[me] = gates[me]
    logit_cols = mm_nt(low, small_low)
    col = iota((sz.rows, sz.small), 1)
    logit_cols = jnp.where((col >= 8) & (col < 8 + sz.experts), logit_cols, -1e30)
    e_cols = jnp.exp(logit_cols - jnp.max(logit_cols, 1, keepdims=True))
    probs[...] = e_cols / jnp.sum(e_cols, 1, keepdims=True)

    ctx_t[...] = ctx[...].T

    for k in range(1, n):
        src = lax.rem(me + n - k, n)
        dst = rows_at(lax.rem(me + k, n), sz.slots)
        theirs = rows_at(src, sz.slots)
        to_peer(gs.at[dst, :], gr.at[theirs, :], g_sem, k).wait()
        to_peer(gates.at[lax.rem(me + k, n)], gater.at[src], ga_sem, k).wait()
    square = iota((sz.slots, sz.slots), 0) == iota((sz.slots, sz.slots), 1)
    for j in range(n):
        block = slice(j * sz.slots, (j + 1) * sz.slots)
        row = gater[j, pl.ds(me, 1), :]
        gate = jnp.sum(jnp.where(square, row, 0.0), 1, keepdims=True)
        dres[block, :] = (gate * gr[block, :].astype(F32)).astype(BF)
    for k in range(1, n):
        src = lax.rem(me + n - k, n)
        dst = rows_at(lax.rem(me + k, n), sz.slots)
        theirs = rows_at(src, sz.slots)
        to_peer(xs.at[dst, :], xr.at[theirs, :], x_sem, k).wait()
        for cp in small_sends(k):
            cp.wait_send()
    gather_q.drain()
    gather_p.drain()


def front(sz, tokens, grad, routes, wq, wp, router, gains, biases):
    vmem = pl.BlockSpec(memory_space=pltpu.VMEM)
    rows, d, slots, n = sz.rows, sz.d, sz.all_slots, sz.n_exp
    outs = [
        ((slots, d), BF),
        ((slots, d), BF),
        ((rows, 3 * d), BF),
        ((sz.pairs, sz.images * 2, sz.seq, sz.seq), BF),
        ((d, rows), BF),
        ((rows, d), F32),
        ((rows, d), BF),
        ((d, rows), BF),
        ((rows, sz.small), F32),
        ((d, 3 * d), BF),
        ((d, d), BF),
        ((sz.small, d), F32),
        ((rows, d), BF),
        ((sz.experts, rows, sz.slots), BF),
    ]
    dma = pltpu.SemaphoreType.DMA
    sems = [dma((2, n))] * 4 + [dma((2, 2, n))] * 2 + [dma((3, 2, n))] + [dma((2, n))] * 3
    return pl.pallas_call(
        partial(front_kernel, sz),
        name="front",
        out_shape=[jax.ShapeDtypeStruct(s, t) for s, t in outs],
        in_specs=[vmem] * 8,
        out_specs=[vmem] * len(outs),
        scratch_shapes=[
            pltpu.VMEM((rows, d), BF),
            pltpu.VMEM((rows, d), BF),
            pltpu.VMEM((slots, rows), BF),
            pltpu.VMEM((slots, d), BF),
            pltpu.VMEM((n, sz.ep, sz.slots), F32),
            pltpu.VMEM((slots, d), BF),
            pltpu.VMEM((slots, d), BF),
            pltpu.VMEM((n, sz.ep, sz.slots), F32),
            pltpu.VMEM((n, *router.shape), BF),
            pltpu.VMEM((n, *gains.shape), BF),
            pltpu.VMEM((n, *biases.shape), BF),
        ]
        + sems,
        compiler_params=pltpu.CompilerParams(
            collective_id=0, has_side_effects=True, vmem_limit_bytes=56 << 20
        ),
    )(tokens, grad, routes, wq, wp, router, gains, biases)


def finish_kernel(sz, *refs):
    sources, targets = refs[:6], refs[6:17]
    ins, outs = refs[17:23], refs[23:32]
    in_sem, out_sem = refs[32:]
    out, gin, g1, g2, dense, sg = ins
    o_qkv, o_proj, o_router, o_gains, o_biases, o_w1, o_b1, o_w2, o_b2 = outs
    loads = [
        pltpu.make_async_copy(src, dst, in_sem.at[i])
        for i, (src, dst) in enumerate(zip(sources, ins))
    ]
    stores = [
        pltpu.make_async_copy(src, dst, out_sem.at[i])
        for i, (src, dst) in enumerate(zip((out, gin, *outs), targets))
    ]
    for i in (2, 3, 4, 0, 1, 5):
        loads[i].start()
    fs, sh = sz.fs, sz.shard
    loads[2].wait()
    o_w1[0] = g1[...].astype(F32)
    stores[7].start()
    loads[3].wait()
    o_w2[0] = g2[0:fs, :].astype(F32)
    stores[9].start()
    loads[4].wait()
    for g in range(sz.groups):
        for j in range(3):
            cols = slice(j * sz.d + g * 256, j * sz.d + (g + 1) * 256)
            o_qkv[:, cols] = dense[g + 1, :, j * 256 : (j + 1) * 256].astype(F32)
    stores[2].start()
    o_proj[...] = dense[0].astype(F32)
    stores[3].start()
    for i in range(2):
        loads[i].wait()
        stores[i].start()
    loads[5].wait()
    o_router[...] = sg[8 : 8 + sz.experts, 0:sh]
    o_gains[...] = sg[0:2, 0:sh]
    o_biases[...] = sg[2:7, 0:sh]
    o_b1[...] = g2[fs : fs + 16, :].astype(F32)[0:1, 0:fs]
    own = o_b2.shape[1]
    first = lax.axis_index("rep") * own
    pick = iota((sz.d, own), 0) == iota((sz.d, own), 1) + first
    o_b2[...] = mm(g2[fs : fs + 16, :], pick.astype(F32).astype(BF))[1:2, :]
    for i in (4, 5, 6, 8, 10):
        stores[i].start()
    for store in stores:
        store.wait()


def finish(sz, out, gin, g1, g2, dense, sg):
    d, fs, sh = sz.d, sz.fs, sz.shard
    outs = [
        ((sz.tok, d), BF),
        ((sz.tok, d), BF),
        ((sh, 3 * d), F32),
        ((sh, d), F32),
        ((sz.experts, sh), F32),
        ((2, sh), F32),
        ((5, sh), F32),
        ((1, d, fs), F32),
        ((1, fs), F32),
        ((1, fs, d), F32),
        ((1, d // sz.n_rep), F32),
    ]
    sources = (out, gin, g1, g2, dense, sg)
    hbm = pl.BlockSpec(memory_space=pl.ANY)
    grads = pl.pallas_call(
        partial(finish_kernel, sz),
        name="finish",
        out_shape=[jax.ShapeDtypeStruct(s, t) for s, t in outs],
        in_specs=[hbm] * 6,
        out_specs=[hbm] * len(outs),
        scratch_shapes=[pltpu.VMEM(a.shape, a.dtype) for a in sources]
        + [pltpu.VMEM(s, t) for s, t in outs[2:]]
        + [pltpu.SemaphoreType.DMA((6,)), pltpu.SemaphoreType.DMA((11,))],
        compiler_params=pltpu.CompilerParams(vmem_limit_bytes=62 << 20),
    )(*sources)
    return (*grads[:4], grads[4].T, *grads[5:])


def normalize_back(values, gain, cot):
    center = values - jnp.mean(values, -1, keepdims=True)
    spread = jnp.mean(center * center, -1, keepdims=True)
    inv = lax.rsqrt(spread + EPS)
    unit = center * inv
    scaled = cot * gain
    grad = inv * (
        scaled
        - jnp.mean(scaled, -1, keepdims=True)
        - unit * jnp.mean(scaled * unit, -1, keepdims=True)
    )
    return grad, jnp.sum(cot * unit, 0, keepdims=True), jnp.sum(cot, 0, keepdims=True)


def gelu_parts(h):
    t = 1.0 / (1.0 + (0.3275911 / math.sqrt(2.0)) * jnp.abs(h))
    bell = jnp.exp(-0.5 * h * h)
    poly = t * (
        0.127414796
        + t * (-0.142248368 + t * (0.7107068705 + t * (-0.7265760135 + t * 0.5307027145)))
    )
    tail = poly * bell
    return jnp.where(h >= 0, 1.0 - tail, tail), bell * (1.0 / math.sqrt(2.0 * math.pi))


def block_kernel(
    sz,
    tok_hbm,
    routes_hbm,
    router_ref,
    gains_ref,
    biases_ref,
    b1_hbm,
    b2_hbm,
    grad_hbm,
    wq_shard,
    wp_shard,
    w1_hbm,
    w2_hbm,
    o_dense,
    o_small,
    o_out,
    o_gin,
    o_w1,
    o_w2,
    o_probs,
    o_save,
    tok_ref,
    routes_ref,
    b1_ref,
    b2_ref,
    od,
    dw,
    w2,
    stage,
    xr,
    dres,
    qkv,
    ctx_t,
    resid,
    second,
    normed_t,
    probs,
    smf,
    gpad,
    comb,
    gater,
    gates,
    routers,
    gains,
    biases,
    bias2,
    xt,
    xta,
    acts,
    dhids,
    wide1,
    wide2,
    sends,
    ret,
    bck,
    qs,
    qr,
    t2,
    v1,
    v2,
    u1,
    u2,
    pbuf,
    r2,
    z1,
    z2,
    sm,
    smr,
    sme,
    sme_r,
    smz_r,
    isem,
    wsem,
    psem,
    f_sem,
    l_sem,
    c_sem,
    o_sem,
    sm_sem,
    g_sem,
    x_sem,
    ga_sem,
    t_sem,
    u_sem,
    ret_sem,
    bck_sem,
    q_sem,
    d1_sem,
    d2_sem,
    z1_sem,
    z2_sem,
    z3_sem,
    s1_sem,
    s2_sem,
    s3_sem,
):
    me_r = lax.axis_index("rep")
    me = lax.axis_index("exp")
    n, nz, fs, d = sz.n_exp, sz.nz, sz.fs, sz.d
    core = lax.rem(me_r, 2)
    z = lax.div(me_r, 2)
    sibling = me_r + 1 - 2 * core
    odd = lax.rem(z, 2)
    partner = me_r + 2 - 4 * odd

    loads = [
        pltpu.make_async_copy(src, dst, isem.at[i])
        for i, (src, dst) in enumerate(
            (
                (tok_hbm, tok_ref),
                (gains_ref, gains.at[me]),
                (biases_ref, biases.at[me]),
                (router_ref, routers.at[me]),
                (routes_hbm, routes_ref),
                (b1_hbm, b1_ref),
                (b2_hbm, b2_ref),
            )
        )
    ]
    for cp in loads:
        cp.start()
    load_grad = pltpu.make_async_copy(grad_hbm, stage, wsem.at[0])
    load_grad.start()
    load_w2 = pltpu.make_async_copy(w2_hbm, w2, wsem.at[1])
    load_w2.start()

    barrier = pltpu.get_barrier_semaphore()
    for k in range(1, n):
        pl.semaphore_signal(
            barrier, inc=1, device_id=(me_r, lax.rem(me + k, n)), device_id_type=MESH
        )
    for k in range(1, nz):
        pl.semaphore_signal(
            barrier,
            inc=1,
            device_id=(lax.rem(me_r + 2 * k, 2 * nz), me),
            device_id_type=MESH,
        )
    pl.semaphore_signal(barrier, inc=1, device_id=(sibling, me), device_id_type=MESH)
    pl.semaphore_wait(barrier, n - 1 + nz)

    def remote(src, dst, send, recv, rep, exp):
        return pltpu.make_async_remote_copy(
            src_ref=src,
            dst_ref=dst,
            send_sem=send,
            recv_sem=recv,
            device_id=(rep, exp),
            device_id_type=MESH,
        )

    def to_peer(src, dst, sems, k):
        return remote(
            src, dst, sems.at[0, k], sems.at[1, k], me_r, lax.rem(me + k, n)
        )

    def to_z(src, dst, sems, k):
        return remote(
            src, dst, sems.at[0, k], sems.at[1, k], lax.rem(me_r + 2 * k, 2 * nz), me
        )

    normed = acts.at[nz - 1, sz.slots : sz.slots + sz.rows, :]
    ctx = xta.at[0 : sz.rows, :]
    res_send = sends.at[0 : sz.all_slots, :]
    row_send = sends.at[sz.all_slots : 2 * sz.all_slots, :]
    xs, gs = res_send, row_send

    piece = 128

    def shard_cols(g, tile):
        if isinstance(g, int) and g == sz.groups:
            return wp_shard, tile * piece
        return wq_shard, lax.div(tile, 2) * d + g * 256 + lax.rem(tile, 2) * piece

    def dw_cols(g, tile, count):
        return pl.ds(pl.multiple_of(g * d + tile * piece, 128), count * piece)

    def dw_rows(k):
        return rows_at(lax.rem(me + n - k, n), sz.shard)

    def fetch(g, i, k):
        tile = 3 * core + odd + i
        shard, start = shard_cols(g, tile)
        return remote(
            shard.at[:, pl.ds(pl.multiple_of(start, 128), piece)],
            dw.at[rows_at(me, sz.shard), dw_cols(g, tile, 1)],
            f_sem.at[0, g, i, k],
            f_sem.at[1, g, i, k],
            me_r,
            lax.rem(me + k, n),
        )

    def fetched(g, i, k):
        ref = dw.at[dw_rows(k), dw_cols(g, 3 * core + odd + i, 1)]
        return remote(
            ref,
            ref,
            f_sem.at[0, g, i, k],
            f_sem.at[1, g, i, k],
            me_r,
            lax.rem(me + k, n),
        )

    def layer(g, k, mine):
        part = 2 * odd if mine else 2 - 2 * odd
        ref = dw.at[dw_rows(k), dw_cols(g, 3 * core + part, 1)]
        return remote(ref, ref, l_sem.at[0, g, k], l_sem.at[1, g, k], partner, me)

    def twin(g, k, late, side):
        first, count = (2 - 2 * odd, 1) if late else (odd, 2)
        ref = dw.at[dw_rows(k), dw_cols(g, 3 * side + first, count)]
        return remote(
            ref, ref, c_sem.at[0, g, late, k], c_sem.at[1, g, late, k], sibling, me
        )

    def own_part(g, j):
        if isinstance(g, int) and g == sz.groups:
            src = wp_shard.at[:, j * 256 : (j + 1) * 256]
        else:
            src = wq_shard.at[:, pl.ds(pl.multiple_of(j * d + g * 256, 128), 256)]
        dst = dw.at[
            rows_at(me, sz.shard), pl.ds(pl.multiple_of(g * d + j * 256, 128), 256)
        ]
        return pltpu.make_async_copy(src, dst, o_sem.at[g, j])

    def start_weights(g):
        for k in range(1, n):
            for i in range(2):
                fetch(g, i, k).start()
        for j in range(3):
            own_part(g, j).start()

    def forward_weights(g):
        for k in range(1, n):
            for i in range(2):
                fetched(g, i, k).wait_recv()
            layer(g, k, True).start()
            twin(g, k, 0, core).start()

    def finish_weights(g):
        for j in range(3):
            own_part(g, j).wait()
        for k in range(1, n):
            layer(g, k, False).wait_recv()
            twin(g, k, 1, core).start()
        for k in range(1, n):
            for late in range(2):
                twin(g, k, late, 1 - core).wait_recv()

    def drain_weights(g):
        for k in range(1, n):
            for i in range(2):
                fetch(g, i, k).wait_send()
            layer(g, k, True).wait_send()
            for late in range(2):
                twin(g, k, late, core).wait_send()

    def small_sends(k):
        return [
            to_peer(src, dst.at[me], sm_sem.at[i], k)
            for i, (src, dst) in enumerate(
                ((gains_ref, gains), (biases_ref, biases), (router_ref, routers))
            )
        ]

    for k in range(1, n):
        for cp in small_sends(k):
            cp.start()
    for g in range(sz.groups):
        start_weights(g)
    loads[0].wait()
    wide1[...] = mm(pad_matrix(sz), tok_ref[...])
    for cp in loads[1:]:
        cp.wait()
    for k in range(1, n):
        for cp in small_sends(k):
            cp.wait_recv()
    smf[...] = jnp.zeros_like(smf)
    for j in range(n):
        r = iota((sz.shard, d), 0)
        c = iota((sz.shard, d), 1)
        pick = (c == r + j * sz.shard).astype(F32).astype(BF)
        smf[0:2, :] += mm(gains[j], pick)
        smf[2:7, :] += mm(biases[j], pick)
        smf[8 : 8 + sz.experts, :] += mm(routers[j], pick)
    normed[...] = normalize(wide1[...], smf[0:1, :], smf[2:3, :]).astype(BF)
    forward_weights(0)
    choice = (routes_ref[...].astype(F32) + 1.0).astype(BF)
    lines = mm_nt(choice, pad_matrix(sz)).astype(jnp.int32) - 1
    ids = iota((sz.ep, sz.rows), 0)
    oh1 = (lines[0:1, :] == ids).astype(F32)
    oh2 = (lines[1:2, :] == ids).astype(F32)
    before = (
        (iota((sz.rows, sz.rows), 0) < iota((sz.rows, sz.rows), 1))
        .astype(F32)
        .astype(BF)
    )
    pos1 = mm(oh1.astype(BF), before)
    pos2 = mm(oh2.astype(BF), before) + jnp.sum(oh1, 1, keepdims=True)
    place = oh1 * pos1 + oh2 * pos2
    kept = (oh1 + oh2 > 0.5) & (place < sz.cap - 0.5)
    slot = jnp.where(kept, place, -1.0).astype(jnp.int32)
    slot_ids = iota((sz.slots, sz.rows), 0)

    def picks(e):
        return (slot_ids == slot[e : e + 1, :]).astype(F32).astype(BF)

    forward_weights(1)
    start_weights(sz.groups)

    load_grad.wait()
    gpad[...] = mm(pad_matrix(sz), stage[...]).astype(BF)
    slots_me = rows_at(me, sz.slots)

    def at_peer(k):
        return slice(k * sz.slots, (k + 1) * sz.slots)

    def picks_for(k):
        line = slot[0:1, :]
        for e in range(1, sz.experts):
            line = jnp.where(lax.rem(me + k, n) == e, slot[e : e + 1, :], line)
        return (slot_ids == line).astype(F32).astype(BF)

    for k in range(n):
        gs[at_peer(k), :] = mm(picks_for(k), gpad[...]).astype(BF)
    dres[at_peer(0), :] = gs[at_peer(0), :]
    for k in range(1, n):
        to_peer(gs.at[at_peer(k), :], dres.at[at_peer(n - k), :], g_sem, k).start()
    forward_weights(2)

    scale = 1.0 / math.sqrt(HEAD_DIM)
    half_lane = iota((sz.seq, 128), 1)
    live = iota((sz.seq, sz.seq), 1) < SEQ

    def pair_cols(pair, j, base=None):
        group = lax.div(pair, 2) * d if base is None else base
        start = group + j * 256 + lax.rem(pair, 2) * 128
        return pl.ds(pl.multiple_of(start, 128), 128)

    def save_probs(pair):
        slot = lax.rem(pair, 2)
        return pltpu.make_async_copy(pbuf.at[slot], o_probs.at[pair], psem.at[slot])

    def forward_pair(pair, carry):
        @pl.when(pair >= 2)
        def _():
            save_probs(pair - 2).wait()

        for image in range(sz.images):
            rows = slice(image * sz.seq, (image + 1) * sz.seq)
            q2, k2, v2_ = (qkv[rows, pair_cols(pair, j)] for j in range(3))
            total = jnp.zeros((sz.seq, 128), F32)
            for half in range(2):
                mask = (half_lane >= half * 64) & (half_lane < half * 64 + 64)
                zero = jnp.zeros_like(q2)
                s = mm_nt(jnp.where(mask, q2 * jnp.asarray(scale, BF), zero), k2)
                s = jnp.where(live, s, -1e30)
                e = jnp.exp(s - jnp.max(s, -1, keepdims=True))
                p = (e * (1.0 / jnp.sum(e, -1, keepdims=True))).astype(BF)
                pbuf[lax.rem(pair, 2), image * 2 + half] = p
                total = total + mm(p, jnp.where(mask, v2_, zero))
            ctx[rows, pl.ds(pl.multiple_of(pair * 128, 128), 128)] = total.astype(BF)
        save_probs(pair).start()
        return carry

    def forward_group(g, carry):
        finish_weights(g)
        cols = pl.ds(pl.multiple_of(g * d, 128), d)
        of_bias = pl.ds(pl.multiple_of(g * 256, 128), 256)
        bias = jnp.concatenate(
            [smf[3:4, of_bias], jnp.zeros((1, 256), F32), smf[4:5, of_bias]], 1
        )
        qkv[:, cols] = (mm(normed[...], dw[:, cols]) + bias).astype(BF)
        lax.fori_loop(2 * g, 2 * g + 2, forward_pair, 0)

        @pl.when(g == 0)
        def _():
            forward_weights(sz.groups)

        return carry

    lax.fori_loop(0, sz.groups, forward_group, 0)
    finish_weights(sz.groups)
    save = pltpu.make_async_copy(dw, o_save, wsem.at[2])
    save.start()
    res = (
        wide1[...]
        + mm(ctx[...], dw[:, 3 * d : 4 * d])
        + smf[5:6, :]
    )
    resid[...] = res
    second[...] = normalize(res, smf[1:2, :], smf[6:7, :]).astype(BF)
    for k in [*range(1, n), 0]:
        xs[at_peer(k), :] = mm(picks_for(k), second[...]).astype(BF)
        if k:
            to_peer(xs.at[at_peer(k), :], xr.at[at_peer(n - k), :], x_sem, k).start()
        else:
            xr[at_peer(0), :] = xs[at_peer(0), :]
    small_low = smf[...].astype(BF)
    low = second[...]
    logit_rows = mm_nt(small_low, low)[8 : 8 + sz.ep, :]
    logit_rows = jnp.where(iota((sz.ep, sz.rows), 0) < sz.experts, logit_rows, -1e30)
    e_rows = jnp.exp(logit_rows - jnp.max(logit_rows, 0, keepdims=True))
    prob_rows = e_rows / jnp.sum(e_rows, 0, keepdims=True)
    hi = prob_rows.astype(BF)
    left = prob_rows - hi.astype(F32)
    mid = left.astype(BF)
    rest_low = (left - mid.astype(F32)).astype(BF)
    for e in range(sz.experts):
        block = picks(e)
        gates[e] = mm_nt(hi, block) + mm_nt(mid, block) + mm_nt(rest_low, block)
    for k in range(1, n):
        to_peer(gates.at[lax.rem(me + k, n)], gater.at[n - k], ga_sem, k).start()
    gater[0] = gates[me]
    for g in range(sz.groups + 1):
        drain_weights(g)
    save.wait()
    load_w1 = pltpu.make_async_copy(w1_hbm, dw, wsem.at[0])
    load_w1.start()
    normed_t[...] = normed[...].T
    ctx_t[...] = ctx[...].T
    eye = (iota((sz.rows, sz.rows), 0) == iota((sz.rows, sz.rows), 1)).astype(F32)
    slot_cols = mm_nt(eye.astype(BF), slot.astype(F32).astype(BF)).astype(jnp.int32)
    lane_ids = iota((sz.rows, sz.slots), 1)
    for e in range(sz.experts):
        comb[e] = (slot_cols[:, e : e + 1] == lane_ids).astype(F32).astype(BF)
    logit_cols = mm_nt(low, small_low)
    col = iota((sz.rows, sz.small), 1)
    logit_cols = jnp.where((col >= 8) & (col < 8 + sz.experts), logit_cols, -1e30)
    e_cols = jnp.exp(logit_cols - jnp.max(logit_cols, 1, keepdims=True))
    probs[...] = e_cols / jnp.sum(e_cols, 1, keepdims=True)
    for pair in range(max(sz.pairs - 2, 0), sz.pairs):
        save_probs(pair).wait()

    lower = 1 - lax.div(z, (nz + 1) // 2)
    span = 2 * fs
    per = span // 256
    everyone, others = slice(0, sz.all_slots), slice(sz.slots, sz.all_slots)
    square = iota((sz.slots, sz.slots), 0) == iota((sz.slots, sz.slots), 1)
    bias2[...] = jnp.zeros_like(bias2)
    half_own = pl.ds(pl.multiple_of(core * fs, 128), fs)
    half_other = pl.ds(pl.multiple_of((1 - core) * fs, 128), fs)

    def dest_of(i):
        return lower * (nz - 1 - i) + (1 - lower) * i

    def hidden_at(i, first, size):
        return pl.ds(pl.multiple_of(dest_of(i) * span + first, 128), size)

    def prepare(k):
        rows = at_peer(k)
        if k:
            j = n - k
            to_peer(gs.at[at_peer(j), :], dres.at[rows, :], g_sem, j).wait()
            to_peer(gates.at[lax.rem(me + j, n)], gater.at[k], ga_sem, j).wait()
        row = gater[k, pl.ds(me, 1), :]
        gate = jnp.sum(jnp.where(square, row, 0.0), 1, keepdims=True)
        value = (gate * dres[rows, :].astype(F32)).astype(BF)
        dres[rows, :] = value
        bias2[...] += jnp.sum(value.astype(F32), 0, keepdims=True)

    def cell(t, rows):
        i, c = lax.div(t, per), lax.rem(t, per)
        hidden = hidden_at(i, c * 256, 256)
        here = pl.ds(pl.multiple_of(c * 256, 128), 256)
        h = mm(xr[rows, :], dw[:, hidden]) + b1_ref[:, hidden].astype(F32)
        cdf, pdf = gelu_parts(h)
        da = mm_nt(dres[rows, :], w2[hidden, :])
        acts[i, rows, here] = (h * cdf).astype(BF)
        dhids[i, rows, here] = (da * (cdf + h * pdf)).astype(BF)

    def cells(first, last, rows):
        lax.fori_loop(first * per, last * per, lambda t, c: (cell(t, rows), c)[1], 0)

    def row_copy(c, k, land):
        cols = pl.ds(pl.multiple_of(c * 256, 128), 256)
        return remote(
            row_send.at[at_peer(k), cols],
            bck.at[land, cols],
            bck_sem.at[0, c, k],
            bck_sem.at[1, c, k],
            me_r,
            lax.rem(me + k, n),
        )

    def back_rows(c, carry):
        cols = pl.ds(pl.multiple_of(c * 256, 128), 256)
        total = mm_nt(dhids[0], dw[cols, hidden_at(0, 0, span)])
        for i in range(1, nz):
            total = total + mm_nt(dhids[i], dw[cols, hidden_at(i, 0, span)])
        row_send[:, cols] = total.astype(BF)
        for k in range(1, n):
            row_copy(c, k, slots_me).start()
        bck[slots_me, cols] = row_send[at_peer(0), cols]
        return carry

    def back_results(c, column):
        cols = pl.ds(pl.multiple_of(c * 256, 128), 256)
        total = mm(acts[0], w2[hidden_at(0, 0, span), cols])
        for i in range(1, nz):
            total = total + mm(acts[i], w2[hidden_at(i, 0, span), cols])
        out = (total + b2_ref[:, cols].astype(F32)).astype(BF)
        res_send[:, cols] = out
        return column + jnp.sum(
            out.astype(F32) * dres[:, cols].astype(F32), 1, keepdims=True
        )

    parts1 = [slice(i, i + d // 2) for i in (0, d // 2)]
    parts2 = range(0, fs, 128)

    def grad1(i, half, rows):
        part = mm(xta[rows, :], dhids[i, 0:d, half])
        return part + mm(xt[rows, :], dhids[i, d:, half])

    def grad2(i, start, first):
        cols = pl.ds(pl.multiple_of(start + first, 128), 128)
        return mm_tn(acts[i, :, cols], dres[...])

    def extra(i, half):
        gb = jnp.sum(dhids[i, :, half].astype(F32), 0, keepdims=True)
        row = iota((16, d), 0)
        line = jnp.concatenate([gb, jnp.zeros((1, d - fs), F32)], 1)
        return jnp.where(row == 0, line, jnp.where(row == 1, bias2[...], 0.0))

    def leaving(i):
        return r2.at[0] if isinstance(i, int) else acts.at[i, 0:d, half_other]

    def t_copies(i):
        dest = dest_of(i)
        return (
            remote(leaving(i), v1.at[dest], t_sem.at[0, 0, dest], t_sem.at[1, 0, dest], sibling, me),
            remote(t2, v2.at[dest], t_sem.at[0, 1, dest], t_sem.at[1, 1, dest], sibling, me),
        )

    def landing(way, step, at):
        if way == 0:
            return nz - 2 - step + at
        return at + step + 2 - nz if step < nz - 2 else nz

    def u_copies(src1, src2, way, step, target, slot):
        return (
            remote(src1, u1.at[slot], u_sem.at[0, 0, way, step], u_sem.at[1, 0, way, step], target, me),
            remote(src2, u2.at[slot], u_sem.at[0, 1, way, step], u_sem.at[1, 1, way, step], target, me),
        )

    def other_grads(i):
        for first in parts2:
            value = grad2(i, (1 - core) * fs, first)
            t2[first : first + 128, :] = value.astype(BF)
        t2[fs:, :] = extra(i, half_other).astype(BF)
        t_copies(i)[1].start()
        if isinstance(i, int):
            xta[...] = xr[0:d, :].T
            xt[...] = xr[d:, :].T
        for rows in parts1:
            leaving(i)[rows, :] = grad1(i, half_other, rows).astype(BF)
        t_copies(i)[0].start()

    def own_grads(i):
        dest = dest_of(i)
        t_copies(i)[1].wait()
        for first in parts2:
            rows = slice(first, first + 128)
            value = v2[dest, rows, :].astype(F32) + grad2(i, core * fs, first)
            v2[dest, rows, :] = value.astype(BF)
        v2[dest, fs:, :] = (v2[dest, fs:, :].astype(F32) + extra(i, half_own)).astype(BF)
        leave(i, 1)
        t_copies(i)[0].wait()
        for rows in parts1:
            value = v1[dest, rows, :].astype(F32) + grad1(i, half_own, rows)
            v1[dest, rows, :] = value.astype(BF)
        leave(i, 0)

    def leave(i, which):
        dest = dest_of(i)

        @pl.when((z == 0) & (i <= nz - 2))
        def _():
            u_copies(v1.at[dest], v2.at[dest], 0, i, me_r + 2, dest)[which].start()

        @pl.when((z == nz - 1) & (i < nz - 2))
        def _():
            u_copies(v1.at[dest], v2.at[dest], 1, i, me_r - 2, dest)[which].start()

        @pl.when((z == nz - 1) & (i == nz - 2))
        def _():
            u_copies(v1.at[dest], v2.at[dest], 1, i, me_r - 2, nz)[which].start()

    def z_round(s, which):
        v, u = ((v1, u1), (v2, u2))[which]
        pieces = [
            [slice(i, min(i + 128, size)) for i in range(0, size, 128)]
            for size in (d, sz.fs_rows)
        ]
        for way in range(2):
            zz = z if way == 0 else nz - 1 - z
            dest = nz - 1 - s + zz if way == 0 else z - (nz - 1 - s)
            target = me_r + 2 if way == 0 else me_r - 2

            @pl.when((zz >= 1) & (zz <= s))
            def _():
                here = landing(way, s - 1, z)
                there = landing(way, s, z + 1 if way == 0 else z - 1)
                at_here, at_there = (u1.at[here], u2.at[here]), there
                u_copies(*at_here, way, s - 1, target, here)[which].wait_recv()
                for rows in pieces[which]:
                    value = u[here, rows, :].astype(F32) + v[dest, rows, :].astype(F32)
                    u[here, rows, :] = value.astype(BF)
                u_copies(*at_here, way, s, target, at_there)[which].start()

    prepare(0)
    load_w2.wait()
    load_w1.wait()
    cells(0, nz, at_peer(0))
    for k in range(1, n):
        prepare(k)
    for k in range(1, n):
        to_peer(xs.at[at_peer(k), :], xr.at[at_peer(n - k), :], x_sem, k).wait_send()
        to_peer(xs.at[at_peer(n - k), :], xr.at[at_peer(k), :], x_sem, n - k).wait_recv()
    cells(0, 1, others)
    other_grads(0)
    own_grads(0)
    cells(1, nz, others)
    lax.fori_loop(0, d // 256, back_rows, 0)
    if nz > 2:
        z_round(1, 1)
    column = lax.fori_loop(
        0, d // 256, back_results, jnp.zeros((sz.all_slots, 1), F32)
    )
    for k in range(n):
        line = jnp.where(square, column[at_peer(k), :], 0.0)
        qs[k] = jnp.broadcast_to(jnp.sum(line, 0, keepdims=True), (8, sz.slots))
    qr[me] = qs[0]
    ret[slots_me, :] = res_send[at_peer(0), :]
    for k in range(1, n):
        to_peer(qs.at[k], qr.at[me], q_sem, k).start()
    for k in range(1, n):
        to_peer(res_send.at[at_peer(k), :], ret.at[slots_me, :], ret_sem, k).start()

    def slice_step(i, carry):
        other_grads(i)
        own_grads(i)
        return carry

    lax.fori_loop(1, nz, slice_step, 0)
    if nz > 2:
        z_round(1, 0)
    dense_load = pltpu.make_async_copy(o_save, dw, wsem.at[0])
    dense_load.start()

    for k in range(1, n):
        src = lax.rem(me + n - k, n)
        for c in range(d // 256):
            row_copy(c, k, rows_at(src, sz.slots)).wait()
        to_peer(qs.at[k], qr.at[src], q_sem, k).wait()
    mixed = sgrad = wide2
    lane = iota((sz.rows, sz.small), 1)
    weighted = jnp.zeros((sz.rows, sz.small), F32)
    for e in range(sz.experts):
        q = jnp.sum(comb[e].astype(F32) * qr[e, 0:1, :], 1, keepdims=True)
        weighted = jnp.where(lane == 8 + e, q, weighted)
    total = jnp.sum(weighted, 1, keepdims=True)
    logit_low = (weighted - probs[...] * total).astype(BF)
    sgrad[...] = mm(logit_low, smf[...].astype(BF))
    for e in range(sz.experts):
        sgrad[...] += mm(comb[e], bck[e * sz.slots : (e + 1) * sz.slots, :])
    back2, gain2, shift2 = normalize_back(resid[...], smf[1:2, :], sgrad[...])
    rgrad = wide1
    rgrad[...] = gpad[...].astype(F32) + back2
    low = rgrad[...].astype(BF)
    bias_out = jnp.sum(low.astype(F32), 0, keepdims=True)

    dense = w2
    wide = d // 2
    keep = pl.ds(pl.multiple_of(core * wide, 128), wide)
    give = pl.ds(pl.multiple_of((1 - core) * wide, 128), wide)

    def chunk_rows(j, start, size):
        return pl.ds(pl.multiple_of(j * d + start, 16), size)

    def parked(j):
        cols = pl.ds(pl.multiple_of(lax.rem(j, 2) * wide, 128), wide)
        return acts.at[lax.div(j, 2), 0:d, cols]

    def to_sibling(j):
        return remote(
            dense.at[chunk_rows(j, 0, d), give],
            parked(j),
            d1_sem.at[0, j],
            d1_sem.at[1, j],
            sibling,
            me,
        )

    def to_owner(j, k):
        e = lax.rem(me + k, n)
        return remote(
            dense.at[chunk_rows(j, e * sz.shard, sz.shard), keep],
            r2.at[k - 1, pl.ds(pl.multiple_of(j * sz.shard, 16), sz.shard), :],
            d2_sem.at[0, j, k],
            d2_sem.at[1, j, k],
            me_r,
            e,
        )

    outer = (z == 0) | (z == nz - 1)
    across = me_r - 2 + 4 * odd

    def inward(j):
        return remote(
            z1.at[j], z2.at[0, j], z1_sem.at[0, 0, j], z1_sem.at[1, 0, j], partner, me
        )

    def swap(j):
        return remote(
            z1.at[j], z2.at[1, j], z1_sem.at[0, 1, j], z1_sem.at[1, 1, j], across, me
        )

    def outward(j):
        piece = od.at[j, :, keep]
        return remote(piece, piece, z2_sem.at[0, j], z2_sem.at[1, j], partner, me)

    def to_twin(j, cols):
        piece = od.at[j, :, cols]
        return remote(piece, piece, z3_sem.at[0, j], z3_sem.at[1, j], sibling, me)

    def stage1(j):
        to_sibling(j).wait()
        rows = chunk_rows(j, 0, d)
        dense[rows, keep] = (dense[rows, keep].astype(F32) + parked(j)[...].astype(F32)).astype(BF)
        for k in range(1, n):
            to_owner(j, k).start()

    def stage2(j):
        acc = dense[chunk_rows(j, me * sz.shard, sz.shard), keep].astype(F32)
        for k in range(1, n):
            to_owner(j, k).wait()
            acc = acc + r2[k - 1, j * sz.shard : (j + 1) * sz.shard, :].astype(F32)
        z1[j] = acc.astype(BF)
        pl.when(outer)(lambda: inward(j).start())

    def stage3(j):
        @pl.when(jnp.logical_not(outer))
        def _():
            inward(j).wait_recv()
            z1[j] = (z1[j].astype(F32) + z2[0, j].astype(F32)).astype(BF)
            swap(j).start()

    def stage4(j):
        @pl.when(jnp.logical_not(outer))
        def _():
            swap(j).wait()
            od[j, :, keep] = (z1[j].astype(F32) + z2[1, j].astype(F32)).astype(BF)
            outward(j).start()
            to_twin(j, keep).start()

    def stage5(j):
        @pl.when(outer)
        def _():
            inward(j).wait_send()
            outward(j).wait_recv()
            to_twin(j, keep).start()

    def stage6(j):
        pl.when(jnp.logical_not(outer))(lambda: outward(j).wait_send())
        to_twin(j, keep).wait_send()
        to_twin(j, give).wait_recv()
        pltpu.make_async_copy(od.at[j], o_dense.at[j], isem.at[j]).start()

    dense[chunk_rows(0, 0, d), :] = mm(ctx_t[...], low).astype(BF)
    to_sibling(0).start()
    dense_load.wait()
    for k in range(1, n):
        theirs = rows_at(lax.rem(me + n - k, n), sz.slots)
        to_peer(res_send.at[at_peer(k), :], ret.at[theirs, :], ret_sem, k).wait()
    cgrad = sends.at[3 * sz.rows : 4 * sz.rows, :]

    def load_probs(pair):
        slot = lax.rem(pair, 2)
        return pltpu.make_async_copy(o_probs.at[pair], pbuf.at[slot], psem.at[slot])

    load_probs(0).start()
    cgrad[...] = mm_nt(low, dw[:, 3 * d : 4 * d]).astype(BF)
    sm[...] = mm_tn(logit_low, second[...])

    scale = 1.0 / math.sqrt(HEAD_DIM)
    half_lane = iota((sz.seq, 128), 1)

    def pair_step(pair, carry):
        load_probs(pair).wait()

        @pl.when(pair + 1 < sz.pairs)
        def _():
            load_probs(pair + 1).start()

        for image in range(sz.images):
            rows = slice(image * sz.seq, (image + 1) * sz.seq)
            q2, k2, v2_ = (qkv[rows, pair_cols(pair, j)] for j in range(3))
            c2 = cgrad[rows, pl.ds(pl.multiple_of(pair * 128, 128), 128)]
            there = pl.ds(
                pl.multiple_of(lax.div(pair, 2) * sz.rows + image * sz.seq, 16), sz.seq
            )
            dq = jnp.zeros((sz.seq, 128), F32)
            dk = jnp.zeros((sz.seq, 128), F32)
            dv = jnp.zeros((sz.seq, 128), F32)
            for half in range(2):
                mask = (half_lane >= half * 64) & (half_lane < half * 64 + 64)
                zero = jnp.zeros_like(q2)
                ch = jnp.where(mask, c2, zero)
                p = pbuf[lax.rem(pair, 2), image * 2 + half]
                dv = dv + mm_tn(p, ch)
                pb = mm_nt(ch, v2_)
                p32 = p.astype(F32)
                mix = jnp.sum(pb * p32, -1, keepdims=True)
                ds = (p32 * (pb - mix)).astype(BF)
                dq = dq + mm(ds, jnp.where(mask, k2, zero))
                dk = dk + mm_tn(ds, jnp.where(mask, q2, zero))
            sends[there, pair_cols(pair, 0, 0)] = (dq * scale).astype(BF)
            sends[there, pair_cols(pair, 1, 0)] = (dk * scale).astype(BF)
            sends[there, pair_cols(pair, 2, 0)] = dv.astype(BF)
        return carry

    def group_step(g, carry):
        lax.fori_loop(2 * g, 2 * g + 2, pair_step, 0)
        dense[chunk_rows(g + 1, 0, d), :] = mm(
            normed_t[...], sends[rows_at(g, sz.rows), :]
        ).astype(BF)
        to_sibling(g + 1).start()
        stage1(g)

        @pl.when(g == sz.groups - 2)
        def _():
            for s in range(2, nz - 1):
                z_round(s, 1)

        return carry

    lax.fori_loop(0, sz.groups, group_step, 0)
    for s in range(2, nz - 1):
        z_round(s, 0)
    stage1(sz.groups)

    ngrad = sgrad
    ngrad[...] = mm_nt(sends[0 : sz.rows, :], dw[:, 0:d])
    for g in range(1, sz.groups):
        grads = sends[g * sz.rows : (g + 1) * sz.rows, :]
        ngrad[...] += mm_nt(grads, dw[:, g * d : (g + 1) * d])
    stage2(0)
    x = mm(pad_matrix(sz), tok_ref[...])
    back1, gain1, shift1 = normalize_back(x, smf[0:1, :], ngrad[...])
    stage[...] = mm(unpad_matrix(sz), (rgrad[...] + back1).astype(BF)).astype(BF)
    store = pltpu.make_async_copy(stage, o_gin, wsem.at[2])
    store.start()
    sums = [
        jnp.sum(sends[g * sz.rows : (g + 1) * sz.rows, :].astype(F32), 0, keepdims=True)
        for g in range(sz.groups)
    ]
    bias_q = jnp.concatenate([total[:, 0:256] for total in sums], 1)
    bias_v = jnp.concatenate([total[:, 512:768] for total in sums], 1)
    row = iota((sz.small, d), 0)
    small = sm[...]
    for i, value in enumerate((gain1, gain2, shift1, bias_q, bias_v, bias_out, shift2)):
        small = jnp.where(row == i, value, small)
    sm[...] = small
    smb = sme.at[n]
    smb[...] = small.astype(BF)
    s_first = remote(smb, smr, s1_sem.at[0], s1_sem.at[1], sibling, me)
    s_first.start()

    stage2(1)
    stage3(0)
    mixed[...] = resid[...]
    for e in range(sz.experts):
        block = slice(e * sz.slots, (e + 1) * sz.slots)
        mixed[...] += probs[:, 8 + e : 9 + e] * mm(comb[e], ret[block, :])
    store.wait()
    stage[...] = mm(unpad_matrix(sz), mixed[...].astype(BF)).astype(BF)
    store = pltpu.make_async_copy(stage, o_out, wsem.at[2])
    store.start()

    s_first.wait()
    chip_small = (sm[...] + smr[...].astype(F32)).astype(BF)
    for e in range(n):
        r = iota((sz.shard_pad, d), 0)
        c = iota((sz.shard_pad, d), 1)
        pick = ((c == r + e * sz.shard) & (r < sz.shard)).astype(F32).astype(BF)
        sme[e, :, 0 : sz.shard_pad] = mm_nt(chip_small, pick).astype(BF)

    def small_peer(k):
        piece = sme.at[lax.rem(me + k, n), :, 0 : sz.shard_pad]
        return to_peer(piece, sme_r.at[k], s2_sem, k)

    for k in range(1, n):
        small_peer(k).start()
    stage2(2)
    stage3(1)
    stage4(0)
    acc = sme[me, :, 0 : sz.shard_pad].astype(F32)
    for k in range(1, n):
        small_peer(k).wait()
        acc = acc + sme_r[k].astype(F32)
    smz_r[0] = acc.astype(BF)
    for k in range(1, nz):
        to_z(smz_r.at[0], smz_r.at[k], s3_sem, k).start()
    stage2(3)
    stage3(2)
    stage4(1)

    for way in range(2):
        zz = z if way == 0 else nz - 1 - z
        target = me_r + 2 if way == 0 else me_r - 2

        @pl.when(zz >= 1)
        def _():
            here = landing(way, nz - 2, z)
            for cp in u_copies(u1.at[here], u2.at[here], way, nz - 2, target, here):
                cp.wait_recv()
            v1[z] = (v1[z].astype(F32) + u1[here].astype(F32)).astype(BF)
            v2[z] = (v2[z].astype(F32) + u2[here].astype(F32)).astype(BF)

    stores = [
        pltpu.make_async_copy(v1.at[z], o_w1, wsem.at[0]),
        pltpu.make_async_copy(v2.at[z], o_w2, wsem.at[1]),
    ]
    for cp in stores:
        cp.start()
    stage3(3)
    stage4(2)
    acc = smz_r[0].astype(F32)
    for k in range(1, nz):
        to_z(smz_r.at[0], smz_r.at[k], s3_sem, k).wait()
        acc = acc + smz_r[k].astype(F32)
    o_small[...] = acc
    stage4(3)
    for j in range(sz.chunks):
        stage5(j)
    for j in range(sz.chunks):
        stage6(j)
    for j in range(sz.chunks):
        pltpu.make_async_copy(od.at[j], o_dense.at[j], isem.at[j]).wait()

    for cp in stores:
        cp.wait()
    store.wait()
    for s in range(nz - 1):
        for way in range(2):
            zz = z if way == 0 else nz - 1 - z
            target = me_r + 2 if way == 0 else me_r - 2

            @pl.when(zz <= s)
            def _():
                for cp in u_copies(v1.at[0], v2.at[0], way, s, target, 0):
                    cp.wait_send()
    for k in range(1, n):
        for cp in small_sends(k):
            cp.wait_send()


def block(sz, tokens, routes, router, gains, biases, b1, b2, grad, wq, wp, w1, w2):
    vmem = pl.BlockSpec(memory_space=pltpu.VMEM)
    hbm = pl.BlockSpec(memory_space=pl.ANY)
    rows, d, slots, fs, nz, n = sz.rows, sz.d, sz.all_slots, sz.fs, sz.nz, sz.n_exp
    half = d // 2
    dma = pltpu.SemaphoreType.DMA
    outs = [
        ((sz.chunks, sz.shard, d), BF),
        ((sz.small, sz.shard_pad), F32),
        ((sz.tok, d), BF),
        ((sz.tok, d), BF),
        ((d, fs), BF),
        ((sz.fs_rows, d), BF),
        ((sz.pairs, sz.images * 2, sz.seq, sz.seq), BF),
        ((d, 4 * d), BF),
    ]
    buffers = [
        (tokens.shape, BF),
        (b1.shape, BF),
        (b2.shape, BF),
        ((sz.chunks, sz.shard, d), BF),
        ((d, 4 * d), BF),
        (w2.shape, BF),
        ((sz.tok, d), BF),
        ((slots, d), BF),
        ((slots, d), BF),
        ((rows, 3 * d), BF),
        ((d, rows), BF),
        ((rows, d), F32),
        ((rows, d), BF),
        ((d, rows), BF),
        ((rows, sz.small), F32),
        ((sz.small, d), F32),
        ((rows, d), BF),
        ((sz.experts, rows, sz.slots), BF),
        ((n, sz.ep, sz.slots), F32),
        ((n, sz.ep, sz.slots), F32),
        ((n, *router.shape), BF),
        ((n, *gains.shape), BF),
        ((n, *biases.shape), BF),
        ((1, d), F32),
        ((d, slots - d), BF),
        ((d, d), BF),
        ((nz, slots, 2 * fs), BF),
        ((nz, slots, 2 * fs), BF),
        ((rows, d), F32),
        ((rows, d), F32),
        ((2 * slots, d), BF),
        ((slots, d), BF),
        ((slots, d), BF),
        ((n, 8, sz.slots), F32),
        ((n, 8, sz.slots), F32),
        ((sz.fs_rows, d), BF),
        ((nz, d, fs), BF),
        ((nz, sz.fs_rows, d), BF),
        ((nz + 1, d, fs), BF),
        ((nz + 1, sz.fs_rows, d), BF),
        ((2, 2 * sz.images, sz.seq, sz.seq), BF),
        ((n - 1, d, half), BF),
        ((sz.chunks, sz.shard, half), BF),
        ((2, sz.chunks, sz.shard, half), BF),
        ((sz.small, d), F32),
        ((sz.small, d), BF),
        ((n + 1, sz.small, d), BF),
        ((n, sz.small, sz.shard_pad), BF),
        ((nz, sz.small, sz.shard_pad), BF),
    ]
    sems = (
        [dma((7,)), dma((4,)), dma((2,))]
        + [dma((2, sz.chunks, 2, n)), dma((2, sz.chunks, n))]
        + [dma((2, sz.chunks, 2, n)), dma((sz.chunks, 3))]
        + [dma((3, 2, n))]
        + [dma((2, n))] * 3
        + [dma((2, 2, nz)), dma((2, 2, 2, nz - 1))]
        + [dma((2, n)), dma((2, d // 256, n)), dma((2, n))]
        + [dma((2, sz.chunks)), dma((2, sz.chunks, n))]
        + [dma((2, 2, sz.chunks)), dma((2, sz.chunks))]
        + [dma((2, sz.chunks)), dma((2,)), dma((2, n)), dma((2, nz))]
    )
    return pl.pallas_call(
        partial(block_kernel, sz),
        name="block",
        out_shape=[jax.ShapeDtypeStruct(s, t) for s, t in outs],
        in_specs=[hbm] * 12,
        out_specs=[hbm, vmem] + [hbm] * 6,
        scratch_shapes=[pltpu.VMEM(s, t) for s, t in buffers[:1]]
        + [pltpu.VMEM(routes.shape, jnp.int32)]
        + [pltpu.VMEM(s, t) for s, t in buffers[1:]]
        + sems,
        compiler_params=pltpu.CompilerParams(
            collective_id=1, has_side_effects=True, vmem_limit_bytes=62 << 20
        ),
    )(tokens, routes, router, gains, biases, b1, b2, grad, wq, wp, w1, w2)


def plain_rest(sz, state, tokens, w1, b1, w2, b2):
    xr, dres, qkv, pall, ctx_t, resid, second, normed_t, probs, wq, wp, smf, gpad, comb = state
    d, n = sz.d, sz.experts
    scale = 1.0 / math.sqrt(HEAD_DIM)
    h = mm(xr, w1) + b1
    cdf, pdf = gelu_parts(h)
    act = (h * cdf).astype(BF)
    result = (mm(act, w2) + b2).astype(BF)
    dhid = (mm_nt(dres, w2) * (cdf + h * pdf)).astype(BF)
    row_grad = mm_nt(dhid, w1).astype(BF)
    swap = partial(
        lax.all_to_all, axis_name="exp", split_axis=0, concat_axis=0, tiled=True
    )
    ret = swap(result).reshape(n, sz.slots, d)
    bck = swap(row_grad).reshape(n, sz.slots, d)
    g32 = gpad.astype(F32)
    p = probs[:, 8 : 8 + n]
    picked = jnp.einsum("ets,esd->etd", comb, ret, preferred_element_type=F32)
    mixed = resid + jnp.einsum("te,etd->td", p, picked, precision="highest")
    pg = jnp.sum(g32[None] * picked, -1).T
    lg = (p * (pg - jnp.sum(pg * p, 1, keepdims=True))).astype(BF)
    sgrad = mm(lg, smf[8 : 8 + n].astype(BF))
    sgrad = sgrad + jnp.einsum("ets,esd->td", comb, bck, preferred_element_type=F32)
    back2, gain2, shift2 = normalize_back(resid, smf[1:2], sgrad)
    rgrad = g32 + back2
    low = rgrad.astype(BF)
    cgrad = mm_nt(low, wp).astype(BF)
    four = (sz.images, sz.seq, d // HEAD_DIM, HEAD_DIM)
    q, k, v, c = (
        a.reshape(four)
        for a in (qkv[:, :d], qkv[:, d : 2 * d], qkv[:, 2 * d :], cgrad)
    )
    prob = pall.reshape(sz.pairs, sz.images, 2, sz.seq, sz.seq)
    prob = prob.transpose(1, 0, 2, 3, 4).reshape(sz.images, -1, sz.seq, sz.seq)
    product = partial(jnp.einsum, preferred_element_type=F32)
    dv = product("ihst,ishd->ithd", prob, c).astype(BF)
    pb = product("ishd,ithd->ihst", c, v)
    p32 = prob.astype(F32)
    ds = (p32 * (pb - jnp.sum(pb * p32, -1, keepdims=True))).astype(BF)
    dq = (product("ihst,ithd->ishd", ds, k) * scale).astype(BF)
    dk = (product("ihst,ishd->ithd", ds, q) * scale).astype(BF)
    dqkv = jnp.concatenate([a.reshape(sz.rows, d) for a in (dq, dk, dv)], 1)
    x = mm(pad_matrix(sz), tokens)
    back1, gain1, shift1 = normalize_back(x, smf[0:1], mm_nt(dqkv, wq))
    gin = (rgrad + back1).astype(BF)
    sums = jnp.sum(dqkv.astype(F32), 0, keepdims=True)
    small = jnp.concatenate(
        [gain1, gain2, shift1, sums[:, :d], sums[:, 2 * d :]]
        + [jnp.sum(low.astype(F32), 0, keepdims=True), shift2, mm_tn(lg, second)]
    )

    def dense(grad, dim):
        total = lax.psum(grad.astype(BF), "rep")
        total = lax.psum_scatter(total, "exp", scatter_dimension=dim, tiled=True)
        return total.astype(F32)

    def owned(grad, dim):
        total = lax.psum_scatter(
            grad[None].astype(BF), "rep", scatter_dimension=dim, tiled=True
        )
        return total.astype(F32)

    def unpad(rows):
        return rows.reshape(sz.images, sz.seq, d)[:, :SEQ].reshape(sz.tok, d)

    sums = dense(small, 1)
    return (
        unpad(mixed.astype(BF)),
        unpad(gin),
        dense(mm(normed_t, dqkv), 0),
        dense(mm(ctx_t, low), 0),
        sums[7:].T,
        sums[0:2],
        sums[2:7],
        owned(mm_tn(xr, dhid), 2),
        owned(jnp.sum(dhid.astype(F32), 0), 1),
        owned(mm_tn(act, dres), 1),
        owned(jnp.sum(dres.astype(F32), 0), 1),
    )


def on_device(
    mesh,
    tokens,
    routes,
    out_grad,
    attn_qkv,
    attn_out,
    router,
    norm_gains,
    dense_biases,
    expert_in,
    expert_in_bias,
    expert_out,
    expert_out_bias,
):
    sz = Sizes(mesh, tokens.shape[0], tokens.shape[1], expert_in.shape[2])
    d, fs = sz.d, sz.fs
    w1, w2 = expert_in[0], expert_out[0]
    small = (router.T, norm_gains, dense_biases)
    if (sz.nz, sz.chunks * sz.shard, 2 * fs) != (4, d, d) or sz.all_slots < 2 * sz.rows:
        state = front(sz, tokens, out_grad, routes.T, attn_qkv, attn_out, *small)
        bias1, bias2 = expert_in_bias.astype(F32), expert_out_bias.astype(F32)
        return plain_rest(sz, state, tokens, w1, bias1, w2, bias2)
    dense, sums, out, gin, g1, g2, _, _ = block(
        sz,
        tokens,
        routes.T,
        *small,
        expert_in_bias,
        expert_out_bias,
        out_grad,
        attn_qkv,
        attn_out,
        w1,
        w2,
    )
    return finish(sz, out, gin, g1, g2, dense, sums)


def solution(mesh):
    both = P(("rep", "exp"), None)
    rows = P("exp", None)
    cols = P(None, "exp")
    cube = P("exp", None, None)
    in_specs = (both, both, both, rows, rows, rows, cols, cols, cube, rows, cube, rows)
    out_specs = (
        both,
        both,
        rows,
        rows,
        rows,
        cols,
        cols,
        P("exp", None, "rep"),
        P("exp", "rep"),
        P("exp", "rep", None),
        P("exp", "rep"),
    )
    return jax.shard_map(
        partial(on_device, mesh),
        mesh=mesh,
        in_specs=in_specs,
        out_specs=out_specs,
        check_vma=False,
    )
```
